32 devices in a mesh: shard: 2 (over x), ctx: 4 (over z), tp: 4 (over y, core).
Axes of the slice: x: 2, y: 2, z: 4, core: 2. Of those that a mesh axis runs over, the one named last changes fastest.
Arguments:
- hidden: bfloat16 [2, 4096, 1024], P('shard', ('ctx', 'tp')), may hold values from -6 to 6
- segments: int32 [2, 4096], P('shard'), may hold values from 0 to 7, never falling along the last dimension, each value on 1 to 2048 neighbouring positions
- cotangent: bfloat16 [2, 4096, 1024], P('shard', ('ctx', 'tp')), may hold values from -6 to 6
- attn_gain: bfloat16 [1024], P('shard'), may hold values from 0.25 to 1.75
- w_query: bfloat16 [1024, 2048], P('shard', 'tp'), may hold values from -0.1875 to 0.1875
- key_weight_matrix: bfloat16 [1024, 1024], P('shard', 'tp'), may hold values from -0.1875 to 0.1875
- value_weight_matrix: bfloat16 [1024, 1024], P('shard', 'tp'), may hold values from -0.1875 to 0.1875
- query_gain: bfloat16 [128], P('shard'), may hold values from 0.25 to 1.75
- key_gain: bfloat16 [128], P('shard'), may hold values from 0.25 to 1.75
- mixer_exit_coefficients: bfloat16 [2048, 1024], P('tp', 'shard'), may hold values from -0.5 to 0.5
- mlp_gain: bfloat16 [1024], P('shard'), may hold values from 0.25 to 1.75
- w_gate: bfloat16 [1024, 3072], P('shard', 'tp'), may hold values from -0.1875 to 0.1875
- w_up: bfloat16 [1024, 3072], P('shard', 'tp'), may hold values from -0.1875 to 0.1875
- w_down: bfloat16 [3072, 1024], P('tp', 'shard'), may hold values from -0.109375 to 0.109375
Outputs:
- out_hidden: bfloat16 [2, 4096, 1024], P('shard', ('ctx', 'tp'))
- grad_hidden: float32 [2, 4096, 1024], P('shard', ('ctx', 'tp'))
- grad_attn_gain: float32 [1024], P('shard')
- grad_w_query: float32 [1024, 2048], P('shard', 'tp')
- grad_w_key: float32 [1024, 1024], P('shard', 'tp')
- grad_w_value: float32 [1024, 1024], P('shard', 'tp')
- grad_query_gain: float32 [128], P('shard')
- grad_key_gain: float32 [128], P('shard')
- grad_w_output: float32 [2048, 1024], P('tp', 'shard')
- grad_mlp_gain: float32 [1024], P('shard')
- grad_w_gate: float32 [1024, 3072], P('shard', 'tp')
- grad_w_up: float32 [1024, 3072], P('shard', 'tp')
- grad_w_down: float32 [3072, 1024], P('tp', 'shard')
The draws below stay inside these ranges and needn't reach their ends.
Inputs may be any that keep to these rules, and one draw needn't show every extreme that they name: `segments`: along each sequence the segment numbers never fall and every number from 0 to 7 occurs; a document has 1 to 2048 tokens, and one has exactly 2048.
All inputs are finite; a program needn't handle non-finite values.
Results may differ from the reference program's by a relative error of at most 0.022.
Values may be sent and summed in bfloat16 or wider, within the bound.
A program may use at most 192 MiB of HBM per device.

```python
import math
import jax
import jax.numpy as jnp
import numpy as np
from jax import lax

MODEL_WIDTH = 1024
QUERY_HEADS = 16
KEY_VALUE_HEADS = 8
HEAD_SIZE = 128
FF = 3072
LEN = 4096
NDOC = 8
MOSTDOC = 2048
NSEQ = 2


def levels(own_key, shape, pieces, low, high):
    def one(axis_at, blocks):
        heights = jax.random.uniform(jax.random.fold_in(jax.random.fold_in(own_key, 6), axis_at), (blocks,), jnp.float32, low / len(pieces), high / len(pieces))
        return jnp.repeat(jnp.exp(heights), shape[axis_at] // blocks).reshape((-1,) + (1,) * (len(shape) - axis_at - 1))

    level = one(*pieces[0])
    for cut in pieces[1:]:
        level = level * one(*cut)
    return level


def profile(count, total, most, slope):
    weights = [(1 << 20) // math.isqrt(grade ** slope) + 1 for grade in range(2, count + 1)]
    rest, holding = total - most - (count - 1), [1] * (count - 1)
    while rest > 0:
        movable = [i for i in range(count - 1) if holding[i] < most]
        pool, left = sum([weights[i] for i in movable]), rest
        for i in movable:
            extra = min(most - holding[i], max(1, left * weights[i] // pool), rest)
            holding[i] = holding[i] + extra
            rest = rest - extra
    return np.array([most] + holding)


def ragged(key, number_of, total, bound, skew):
    if number_of == 2:
        one = jax.random.randint(key, (), max(1, total - bound), min(bound, total - 1) + 1)
        return jnp.stack([one, total - one])
    sizes = jnp.asarray(profile(number_of, total, bound, skew), jnp.int32)
    couples = (number_of - 1) // 2
    giver, taker = sizes[1:1 + 2 * couples:2], sizes[2:2 + 2 * couples:2]
    room = jnp.minimum(giver - 1, bound - taker)
    moved = jax.random.randint(jax.random.fold_in(key, 1), (couples,), 0, 1 << 20) % (room + 1)
    sizes = sizes.at[1:1 + 2 * couples:2].set(giver - moved).at[2:2 + 2 * couples:2].set(taker + moved)
    return sizes[jax.random.permutation(jax.random.fold_in(key, 2), number_of)]


def gaussian(own_key, extent, spread, bound, pieces=(), kind=jnp.bfloat16):
    gain = levels(own_key, extent, pieces, -0.22, 0.18) if pieces else 1.0
    array = jax.random.normal(own_key, extent, jnp.float32) * spread * gain
    return jnp.minimum(jnp.maximum(array, -bound), bound).astype(kind)


def setup_inputs(seed: int = 0) -> dict:
    arg_keys = jax.random.split(jax.random.key(seed), 15)
    hidden = gaussian(arg_keys[0], (NSEQ, LEN, MODEL_WIDTH), 1.0, 6.0, ((0, 2), (1, 16)))
    segments = jax.vmap(lambda own: jnp.searchsorted(jnp.cumsum(ragged(own, NDOC, LEN, MOSTDOC, 2)), jnp.arange(LEN), side="right"))(jax.random.split(arg_keys[1], NSEQ)).reshape((NSEQ, LEN)).astype(jnp.int32)
    cotangent = gaussian(arg_keys[2], (NSEQ, LEN, MODEL_WIDTH), 1.0, 6.0, ((0, 2), (1, 16)))
    attn_gain = jnp.clip(1.0 + 0.15 * jax.random.normal(arg_keys[3], (MODEL_WIDTH,), jnp.float32), 0.25, 1.75).astype(jnp.bfloat16)
    w_query = gaussian(arg_keys[4], (MODEL_WIDTH, QUERY_HEADS * HEAD_SIZE), MODEL_WIDTH ** -0.5, 0.1875, ((0, 2), (1, 4)))
    key_weight_matrix = gaussian(arg_keys[5], (MODEL_WIDTH, KEY_VALUE_HEADS * HEAD_SIZE), MODEL_WIDTH ** -0.5, 0.1875, ((0, 2), (1, 4)))
    value_weight_matrix = gaussian(arg_keys[6], (MODEL_WIDTH, KEY_VALUE_HEADS * HEAD_SIZE), MODEL_WIDTH ** -0.5, 0.1875, ((0, 2), (1, 4)))
    query_gain = jnp.clip(1.0 + 0.15 * jax.random.normal(arg_keys[7], (HEAD_SIZE,), jnp.float32), 0.25, 1.75).astype(jnp.bfloat16)
    key_gain = jnp.clip(1.0 + 0.15 * jax.random.normal(arg_keys[8], (HEAD_SIZE,), jnp.float32), 0.25, 1.75).astype(jnp.bfloat16)
    mixer_exit_coefficients = gaussian(arg_keys[9], (QUERY_HEADS * HEAD_SIZE, MODEL_WIDTH), (QUERY_HEADS * HEAD_SIZE // 16) ** -0.5, 0.5, ((0, 4), (1, 2)))
    mlp_gain = jnp.clip(1.0 + 0.15 * jax.random.normal(arg_keys[10], (MODEL_WIDTH,), jnp.float32), 0.25, 1.75).astype(jnp.bfloat16)
    w_gate = gaussian(arg_keys[11], (MODEL_WIDTH, FF), MODEL_WIDTH ** -0.5, 0.1875, ((0, 2), (1, 4)))
    w_up = gaussian(arg_keys[12], (MODEL_WIDTH, FF), MODEL_WIDTH ** -0.5, 0.1875, ((0, 2), (1, 4)))
    w_down = gaussian(arg_keys[13], (FF, MODEL_WIDTH), FF ** -0.5, 0.109375, ((0, 4), (1, 2)))
    return dict(hidden=hidden, segments=segments, cotangent=cotangent, attn_gain=attn_gain, w_query=w_query, key_weight_matrix=key_weight_matrix, value_weight_matrix=value_weight_matrix, query_gain=query_gain, key_gain=key_gain, mixer_exit_coefficients=mixer_exit_coefficients, mlp_gain=mlp_gain, w_gate=w_gate, w_up=w_up, w_down=w_down)


norm_eps = 1e-06
rope_base = 1000000.0
masked_fill = -1e+30
highest = lax.Precision.HIGHEST

@jax.custom_vjp
def reduced_precision(v):
    return lax.optimization_barrier(v.astype(jnp.bfloat16)).astype(jnp.float32)

@jax.custom_vjp
def reduced_precision_backward(v):
    return v

def low_keep(v):
    return (reduced_precision(v), None)

def low_pass(kept, grad):
    return (grad,)

def back_keep(v):
    return (v, None)

def back_low(kept, grad):
    return (reduced_precision(grad),)
reduced_precision.defvjp(low_keep, low_pass)
reduced_precision_backward.defvjp(back_keep, back_low)

def rms_scale(values):
    return lax.rsqrt(lax.optimization_barrier(jnp.mean(values * values, axis=-1, keepdims=True)) + norm_eps)

def doc_positions(segments):
    seq_width = segments.shape[-1]
    labels = jnp.arange(NDOC, dtype=jnp.int32)
    onehot = (segments[..., None] == labels).astype(jnp.int32)
    counts = lax.optimization_barrier(jnp.sum(onehot, axis=-2))
    starts = jnp.cumsum(counts, axis=-1) - counts
    first_row = lax.optimization_barrier(jnp.sum(onehot * starts[..., None, :], axis=-1))
    return jnp.arange(seq_width, dtype=jnp.int32) - first_row

def rope_tables(positions):
    exponents = jnp.arange(0, HEAD_SIZE, 2).astype(jnp.float32) / HEAD_SIZE
    angle_rates = jnp.power(jnp.float32(rope_base), -exponents)
    angles = positions.astype(jnp.float32)[..., None] * angle_rates
    angles = jnp.concatenate([angles, angles], axis=-1)[..., None, :]
    return (jnp.cos(angles), jnp.sin(angles))

def rotate(inputs, cosine, sine_part):
    half_dim = inputs.shape[-1] // 2
    turned = jnp.concatenate([-inputs[..., half_dim:], inputs[..., :half_dim]], axis=-1)
    return inputs * cosine + turned * sine_part

def matrix_product(left_op, second_operand):
    return jnp.dot(left_op, second_operand, precision=highest)

def attention(query_rows_input, keys, values, segs):
    sequence_length = query_rows_input.shape[0]
    query_group_width = QUERY_HEADS // KEY_VALUE_HEADS
    grouped_queries = query_rows_input.reshape(sequence_length, KEY_VALUE_HEADS, query_group_width, HEAD_SIZE)
    rows_block = math.gcd(sequence_length, 512)
    key_index = jnp.arange(sequence_length, dtype=jnp.int32)

    def one_block(block_index):
        first_row = block_index * rows_block
        query_part = lax.dynamic_slice_in_dim(grouped_queries, first_row, rows_block, 0)
        query_pos = first_row + jnp.arange(rows_block, dtype=jnp.int32)
        query_seg = lax.dynamic_slice_in_dim(segs, first_row, rows_block, 0)
        scores = reduced_precision_backward(jnp.einsum('qhgd,khd->hgqk', query_part, keys, precision=highest) * HEAD_SIZE ** (-0.5))
        allowed = ((key_index[None, :] <= query_pos[:, None]) & (segs[None, :] == query_seg[:, None]))[None, None]
        masked = jnp.where(allowed, scores, masked_fill)
        row_max = lax.optimization_barrier(jnp.max(masked, axis=-1, keepdims=True))
        weights = jnp.where(allowed, jnp.exp(masked - row_max), 0.0)
        probs = reduced_precision(weights / lax.optimization_barrier(jnp.sum(weights, axis=-1, keepdims=True)))
        return jnp.einsum('hgqk,khd->qhgd', probs, values, precision=highest)
    blocks = lax.map(jax.checkpoint(one_block), jnp.arange(sequence_length // rows_block, dtype=jnp.int32))
    return blocks.reshape(sequence_length, QUERY_HEADS * HEAD_SIZE)

def layer(inputs, segs, layer_coefficients):
    gain_attn, w_query, key_weight_matrix, value_weight_matrix, gain_query, gain_key, mixer_exit_coefficients, gain_mlp, w_gate, w_up, w_down = layer_coefficients
    sequence_length = inputs.shape[0]
    cosine, sine_part = rope_tables(doc_positions(segs))
    attention_input = reduced_precision(inputs * rms_scale(inputs) * gain_attn)
    q_proj = reduced_precision_backward(matrix_product(attention_input, w_query)).reshape(sequence_length, QUERY_HEADS, HEAD_SIZE)
    key_projected = reduced_precision_backward(matrix_product(attention_input, key_weight_matrix)).reshape(sequence_length, KEY_VALUE_HEADS, HEAD_SIZE)
    value_projected = reduced_precision(reduced_precision_backward(matrix_product(attention_input, value_weight_matrix))).reshape(sequence_length, KEY_VALUE_HEADS, HEAD_SIZE)
    query_rows_input = reduced_precision(rotate(q_proj * rms_scale(q_proj) * gain_query, cosine, sine_part))
    keys = reduced_precision(rotate(key_projected * rms_scale(key_projected) * gain_key, cosine, sine_part))
    attended = reduced_precision(reduced_precision_backward(attention(query_rows_input, keys, value_projected, segs)))
    middle = inputs + reduced_precision_backward(matrix_product(attended, mixer_exit_coefficients))
    mlp_in = reduced_precision(middle * rms_scale(middle) * gain_mlp)
    gate = reduced_precision_backward(matrix_product(mlp_in, w_gate))
    upward = reduced_precision_backward(matrix_product(mlp_in, w_up))
    activated = reduced_precision(jax.nn.silu(gate) * upward)
    return middle + reduced_precision_backward(matrix_product(activated, w_down))

def add_arrays(first_arr, second_arr):
    return first_arr + second_arr

def reference(hidden, segments, cotangent, attn_gain, w_query, key_weight_matrix, value_weight_matrix, query_gain, key_gain, mixer_exit_coefficients, mlp_gain, w_gate, w_up, w_down):
    layer_coefficients = (attn_gain.astype(jnp.float32), w_query.astype(jnp.float32), key_weight_matrix.astype(jnp.float32), value_weight_matrix.astype(jnp.float32), query_gain.astype(jnp.float32), key_gain.astype(jnp.float32), mixer_exit_coefficients.astype(jnp.float32), mlp_gain.astype(jnp.float32), w_gate.astype(jnp.float32), w_up.astype(jnp.float32), w_down.astype(jnp.float32))

    def one_sequence(totals, batch_item):
        seq_in, seq_segs, seq_cot = batch_item

        def forward(layer_in, layer_params):
            return layer(layer_in, seq_segs, layer_params)
        result, pullback = jax.vjp(forward, seq_in.astype(jnp.float32), layer_coefficients)
        grad_in, grad_params = pullback(seq_cot.astype(jnp.float32))
        totals = jax.tree.map(add_arrays, totals, grad_params)
        return (totals, (result.astype(jnp.bfloat16), grad_in))
    zero_grads = jax.tree.map(jnp.zeros_like, layer_coefficients)
    totals, (outputs, input_grads) = lax.scan(one_sequence, zero_grads, (hidden, segments, cotangent))
    return (outputs, input_grads, totals[0], totals[1], totals[2], totals[3], totals[4], totals[5], totals[6], totals[7], totals[8], totals[9], totals[10])
```

```python
import math

import jax
import jax.numpy as jnp
from jax import lax
from jax.experimental import pallas as pl
from jax.experimental.pallas import tpu as pltpu
from jax.sharding import PartitionSpec as P

SHARD_AXIS, CTX_AXIS, TP_AXIS = "shard", "ctx", "tp"
HEAD_SIZE = 128
NDOC = 8


norm_eps = 1e-06
rope_base = 1000000.0
masked_fill = -1e30


def rms_scale(values):
    return lax.rsqrt(jnp.mean(values * values, axis=-1, keepdims=True) + norm_eps)


def rms_back(grad_out, values, row_scale, gain_vec):
    scaled = grad_out * gain_vec
    inner_sum = jnp.mean(scaled * values, axis=-1, keepdims=True)
    return row_scale * scaled - values * (row_scale * row_scale * row_scale) * inner_sum


def doc_positions(segments):
    seq_width = segments.shape[-1]
    labels = jnp.arange(NDOC, dtype=jnp.int32)
    onehot = (segments[..., None] == labels).astype(jnp.int32)
    counts = jnp.sum(onehot, axis=-2)
    starts = jnp.cumsum(counts, axis=-1) - counts
    first_row = jnp.sum(onehot * starts[..., None, :], axis=-1)
    return jnp.arange(seq_width, dtype=jnp.int32) - first_row


def rope_tables(positions):
    exponents = jnp.arange(0, HEAD_SIZE, 2).astype(jnp.float32) / HEAD_SIZE
    angle_rates = jnp.power(jnp.float32(rope_base), -exponents)
    angles = positions.astype(jnp.float32)[..., None] * angle_rates
    angles = jnp.concatenate([angles, angles], axis=-1)[..., None, :]
    return (jnp.cos(angles), jnp.sin(angles))


def rotate(inputs, cosine, sine_part):
    half_dim = inputs.shape[-1] // 2
    turned = jnp.concatenate([-inputs[..., half_dim:], inputs[..., :half_dim]], axis=-1)
    return inputs * cosine + turned * sine_part


def rotate_back(grads, cosine, sine_part):
    half_dim = grads.shape[-1] // 2
    moved = grads * sine_part
    turned = jnp.concatenate([moved[..., half_dim:], -moved[..., :half_dim]], axis=-1)
    return grads * cosine + turned


def tp_rows(local_part):
    return lax.all_gather(local_part, TP_AXIS, axis=1, tiled=True)


def tp_total(partial_sum):
    return lax.psum_scatter(
        partial_sum.astype(jnp.bfloat16), TP_AXIS, scatter_dimension=1, tiled=True
    ).astype(jnp.float32)


def key_block(segments, key_first, step_rows, query_pos, query_seg):
    key_pos = key_first + jnp.arange(step_rows, dtype=jnp.int32)
    key_seg = lax.dynamic_slice_in_dim(segments, key_first, step_rows, 1)
    allowed = (key_pos[None, None, :] <= query_pos[None, :, None]) & (
        key_seg[:, None, :] == query_seg[:, :, None]
    )
    return allowed[:, None, None]


def keep_state(state):
    return state


MESH_ID = pl.DeviceIdType.MESH
ANY_SPEC = pl.BlockSpec(memory_space=pl.ANY)
VMEM_SPEC = pl.BlockSpec(memory_space=pltpu.VMEM)
SCORE_STEP = HEAD_SIZE ** (-0.5) * math.log2(math.e)
APART = 16384.0


def enter(peers):
    barrier = pltpu.get_barrier_semaphore()
    for peer in peers:
        pl.semaphore_signal(barrier, inc=1, device_id=peer, device_id_type=MESH_ID)
    pl.semaphore_wait(barrier, len(peers))


def last_dot(left, right):
    return lax.dot_general(
        left, right, (((1,), (1,)), ((), ())), preferred_element_type=jnp.float32
    )


def flat_dot(left, right):
    return jnp.dot(left, right, preferred_element_type=jnp.float32)


def first_dot(left, right):
    return lax.dot_general(
        left, right, (((0,), (0,)), ((), ())), preferred_element_type=jnp.float32
    )


def spin(values, cosine, sine_signed):
    return values * cosine + pltpu.roll(values, HEAD_SIZE // 2, 1) * sine_signed


def forward_kernel(
    hidden, cotangent, gains_in, cosine, sine, marks, wq, wk, wv, wo,
    gains_out, rows_out, q_out, k_out, query_out, keys_out, values_out,
    attended_out, low_out, wo_out, wqkv_out, crows_out,
    gains, rows, wqkv, q_proj, k_proj, qaug, kaug, vaug, acc, low,
    crows, gains_land, send, recv, local,
):
    s, c, t = lax.axis_index(SHARD_AXIS), lax.axis_index(CTX_AXIS), lax.axis_index(TP_AXIS)
    nctx = lax.axis_size(CTX_AXIS)
    part = hidden.shape[0]
    block = 4 * part
    half = wq.shape[0]
    other = 1 - s
    side, across = {TP_AXIS: t ^ 1}, {TP_AXIS: t ^ 2}
    mate = {SHARD_AXIS: other}
    nxt, prv = {CTX_AXIS: lax.rem(c + 1, nctx)}, {CTX_AXIS: lax.rem(c + nctx - 1, nctx)}
    enter([side, across, mate, nxt, prv])

    def remote(number, src, dst, device):
        return pltpu.make_async_remote_copy(
            src_ref=src, dst_ref=dst, send_sem=send.at[number], recv_sem=recv.at[number],
            device_id=device, device_id_type=MESH_ID,
        )

    def piece(owner):
        return pl.ds(pl.multiple_of(owner * part, part), part)

    mine = pl.ds(pl.multiple_of(s * half, half), half)
    gains_copy = remote(0, gains_in, gains_land, mate)
    wk_copy = remote(1, wk, wqkv.at[mine, 512:768], mate)
    wv_copy = remote(2, wv, wqkv.at[mine, 768:1024], mate)
    wq_copy = remote(3, wq, wqkv.at[mine, 0:512], mate)
    wo_copy = remote(4, wo, wo_out.at[:, mine], mate)
    c_side = remote(5, cotangent, crows.at[piece(t), :], side)
    c_over = remote(6, cotangent, crows.at[piece(t), :], across)
    c_on = remote(7, crows.at[piece(t ^ 2), :], crows.at[piece(t ^ 2), :], side)
    own_copies = [
        pltpu.make_async_copy(a, b, local.at[n])
        for n, (a, b) in enumerate(
            (
                (wk, wqkv.at[mine, 512:768]),
                (wv, wqkv.at[mine, 768:1024]),
                (wq, wqkv.at[mine, 0:512]),
                (wo, wo_out.at[:, mine]),
                (cotangent, crows.at[piece(t), :]),
            )
        )
    ]
    gains_copy.start()
    wk_copy.start()
    wv_copy.start()
    for copy in own_copies:
        copy.start()

    def to_across(b):
        return remote(8 + 3 * b, rows.at[b, piece(t)], rows.at[b, piece(t)], across)

    def to_side(b):
        return remote(9 + 3 * b, rows.at[b, piece(t)], rows.at[b, piece(t)], side)

    def on_to_side(b):
        return remote(10 + 3 * b, rows.at[b, piece(t ^ 2)], rows.at[b, piece(t ^ 2)], side)

    def to_next(b):
        return remote(17 + b, rows.at[b, piece(t)], rows.at[b + 1, piece(t)], nxt)

    x = hidden[...].astype(jnp.float32)
    scale = lax.rsqrt(jnp.mean(x * x, axis=-1, keepdims=True) + norm_eps)
    gains_copy.wait()
    gains[...] = gains_in[...] + gains_land[...]
    rows[0, piece(t), :] = (x * scale * gains[0:1, :]).astype(jnp.bfloat16)
    to_across(0).start()
    to_side(0).start()

    @pl.when(c < nctx - 1)
    def _():
        to_next(0).start()

    wq_copy.start()
    c_side.start()
    for b in range(3):
        for g in range(2):
            kaug[b, g, :, 128:256] = 1 - marks[b]
            vaug[b, g, :, 128:256] = jnp.ones((block, 128), jnp.bfloat16)
    for h in range(4):
        qaug[h, :, 128:256] = marks[0] * jnp.bfloat16(-APART)
    q_gain = gains[2:3, 0:HEAD_SIZE]
    k_gain = gains[3:4, 0:HEAD_SIZE]

    def project_kv(b, owner):
        at = piece(owner)
        got = flat_dot(rows[b, at, :], wqkv[:, 512:1024])
        k_proj[b, at, :] = got[:, 0:256]
        for g in range(2):
            u = got[:, g * 128 : g * 128 + 128]
            r = lax.rsqrt(jnp.mean(u * u, axis=-1, keepdims=True) + norm_eps)
            turned = spin(u * r * k_gain, cosine[b, at, :], sine[b, at, :])
            kaug[b, g, at, 0:128] = turned.astype(jnp.bfloat16)
            vaug[b, g, at, 0:128] = got[:, 256 + g * 128 : 384 + g * 128].astype(jnp.bfloat16)

    def project_q(owner):
        at = piece(owner)
        got = flat_dot(rows[0, at, :], wqkv[:, 0:512])
        q_proj[at, :] = got
        for h in range(4):
            u = got[:, h * 128 : h * 128 + 128]
            r = lax.rsqrt(jnp.mean(u * u, axis=-1, keepdims=True) + norm_eps)
            turned = spin(u * r * q_gain, cosine[0, at, :], sine[0, at, :])
            qaug[h, at, 0:128] = turned.astype(jnp.bfloat16)

    def weights(b, g, r, k0, size, triangle):
        at = pl.ds(pl.multiple_of(r * 256, 256), 256)
        keys_at = pl.ds(pl.multiple_of(k0, 256), size)
        kk = kaug[b, g, keys_at, :]
        vv = vaug[b, g, keys_at, :]
        found = []
        for hh in range(2):
            scores = last_dot(qaug[2 * g + hh, at, :], kk)
            p = jnp.exp2(scores * SCORE_STEP)
            if triangle:
                p = jnp.where(
                    lax.broadcasted_iota(jnp.int32, p.shape, 0)
                    >= lax.broadcasted_iota(jnp.int32, p.shape, 1),
                    p,
                    0.0,
                )
            found.append(flat_dot(p.astype(jnp.bfloat16), vv))
        return at, found

    def add(b, g, r, k0, size):
        at, found = weights(b, g, r, k0, size, False)
        for hh in range(2):
            acc[2 * g + hh, at, :] += found[hh]

    wk_copy.wait()
    wv_copy.wait()
    own_copies[0].wait()
    own_copies[1].wait()
    to_side(0).wait_recv()

    @pl.loop(0, 2)
    def _(n):
        project_kv(0, t ^ n)

    to_across(0).wait_recv()
    on_to_side(0).start()

    @pl.when(c >= 1)
    def _():
        to_next(0).wait_recv()
        to_across(1).start()
        to_side(1).start()

        @pl.when(c < nctx - 1)
        def _():
            to_next(1).start()

    on_to_side(0).wait_recv()

    @pl.loop(2, 4)
    def _(n):
        project_kv(0, t ^ n)

    wq_copy.wait()
    own_copies[2].wait()
    wo_copy.start()

    @pl.loop(0, 4)
    def _(n):
        project_q(n)

    @pl.when(c >= 1)
    def _():
        to_side(1).wait_recv()
        to_across(1).wait_recv()
        on_to_side(1).start()

        @pl.when(c >= 2)
        def _():
            to_next(1).wait_recv()
            to_across(2).start()
            to_side(2).start()

    @pl.loop(0, 8)
    def _(n):
        g, r = n // 4, lax.rem(n, 4)
        at, found = weights(0, g, r, r * 256, 256, True)
        for hh in range(2):
            acc[2 * g + hh, at, :] = found[hh]

        @pl.loop(0, r)
        def _(k):
            add(0, g, r, k * 256, 256)

    @pl.when(c >= 1)
    def _():
        on_to_side(1).wait_recv()

        @pl.loop(0, 4)
        def _(n):
            project_kv(1, n)

        @pl.loop(0, 8)
        def _(n):
            g, r = n // 4, lax.rem(n, 4)
            for k in range(2):
                add(1, g, r, k * 512, 512)

    @pl.when(c >= 2)
    def _():
        to_side(2).wait_recv()
        to_across(2).wait_recv()
        on_to_side(2).start()

    c_over.start()

    @pl.when(c >= 2)
    def _():
        on_to_side(2).wait_recv()

        @pl.loop(0, 4)
        def _(n):
            project_kv(2, n)

        @pl.loop(0, 8)
        def _(n):
            g, r = n // 4, lax.rem(n, 4)

            @pl.loop(r, 4)
            def _(k):
                add(2, g, r, k * 256, 256)

    @pl.loop(0, 16)
    def _(n):
        h, r = n // 4, lax.rem(n, 4)
        at = pl.ds(pl.multiple_of(r * 256, 256), 256)
        total = acc[h, at, 128:256]
        value = acc[h, at, 0:128] / total
        acc[h, at, 0:128] = value
        shift = jnp.log(total) * -(HEAD_SIZE**0.5)
        top = shift.astype(jnp.bfloat16).astype(jnp.float32)
        mid = (shift - top).astype(jnp.bfloat16).astype(jnp.float32)
        lane = lax.broadcasted_iota(jnp.int32, shift.shape, 1)
        parts = jnp.where(lane == NDOC, top, 0.0)
        parts = jnp.where(lane == NDOC + 1, mid, parts)
        parts = jnp.where(lane == NDOC + 2, shift - top - mid, parts)
        qaug[h, at, 128:256] = qaug[h, at, 128:256] + parts.astype(jnp.bfloat16)
        low[h, at, :] = value.astype(jnp.bfloat16)

    c_over.wait_recv()
    c_on.start()
    outs = [
        (gains, gains_out), (rows, rows_out), (q_proj, q_out), (k_proj, k_out),
        (qaug, query_out), (kaug, keys_out), (vaug, values_out), (wqkv, wqkv_out),
    ]
    outs += [(low.at[h], low_out.at[:, h * 128 : h * 128 + 128]) for h in range(4)]
    outs += [
        (acc.at[h, :, 0:128], attended_out.at[:, h * 128 : h * 128 + 128]) for h in range(4)
    ]
    out_copies = [
        pltpu.make_async_copy(a, b, local.at[5 + n]) for n, (a, b) in enumerate(outs)
    ]
    for copy in out_copies:
        copy.start()

    to_across(0).wait_send()
    to_side(0).wait_send()
    on_to_side(0).wait_send()

    @pl.when(c < nctx - 1)
    def _():
        to_next(0).wait_send()

    @pl.when(c >= 1)
    def _():
        to_across(1).wait_send()
        to_side(1).wait_send()
        on_to_side(1).wait_send()

        @pl.when(c < nctx - 1)
        def _():
            to_next(1).wait_send()

    @pl.when(c >= 2)
    def _():
        to_across(2).wait_send()
        to_side(2).wait_send()
        on_to_side(2).wait_send()

    wo_copy.wait()
    for copy in own_copies[3:]:
        copy.wait()
    c_side.wait()
    c_over.wait_send()
    c_on.wait()
    crows_copy = pltpu.make_async_copy(crows, crows_out, local.at[21])
    crows_copy.start()
    for copy in out_copies:
        copy.wait()
    crows_copy.wait()


def forward_call(hidden, cotangent, gains, cosine, sine, marks, wq, wk, wv, wo):
    part, width = hidden.shape
    block = 4 * part
    f32, bf16 = jnp.float32, jnp.bfloat16
    shape = jax.ShapeDtypeStruct
    outs = (
        shape(gains.shape, f32),
        shape((3, block, width), bf16),
        shape((block, 512), f32),
        shape((3, block, 256), f32),
        shape((4, block, 256), bf16),
        shape((3, 2, block, 256), bf16),
        shape((3, 2, block, 256), bf16),
        shape((block, 512), f32),
        shape((block, 512), bf16),
        shape((wo.shape[0], 2 * wo.shape[1]), bf16),
        shape((width, 1024), bf16),
        shape((block, width), bf16),
    )
    return pl.pallas_call(
        forward_kernel,
        name="forward",
        out_shape=outs,
        in_specs=[VMEM_SPEC] * 6 + [ANY_SPEC] * 4,
        out_specs=[ANY_SPEC] * len(outs),
        scratch_shapes=[
            pltpu.VMEM(gains.shape, f32),
            pltpu.VMEM((3, block, width), bf16),
            pltpu.VMEM((width, 1024), bf16),
            pltpu.VMEM((block, 512), f32),
            pltpu.VMEM((3, block, 256), f32),
            pltpu.VMEM((4, block, 256), bf16),
            pltpu.VMEM((3, 2, block, 256), bf16),
            pltpu.VMEM((3, 2, block, 256), bf16),
            pltpu.VMEM((4, block, 256), f32),
            pltpu.VMEM((4, block, 128), bf16),
            pltpu.VMEM((block, width), bf16),
            pltpu.VMEM(gains.shape, f32),
            pltpu.SemaphoreType.DMA((19,)),
            pltpu.SemaphoreType.DMA((19,)),
            pltpu.SemaphoreType.DMA((22,)),
        ],
        compiler_params=pltpu.CompilerParams(
            collective_id=0, has_side_effects=True, vmem_limit_bytes=56 << 20
        ),
    )(hidden, cotangent, gains, cosine, sine, marks, wq, wk, wv, wo)


class Links:
    def __init__(self, send, recv):
        self.send, self.recv, self.used = send, recv, 0

    def copy(self, src, dst, device):
        number = self.used
        self.used += 1
        return pltpu.make_async_remote_copy(
            src_ref=src, dst_ref=dst, send_sem=self.send.at[number],
            recv_sem=self.recv.at[number], device_id=device, device_id_type=MESH_ID,
        )


class Locals:
    def __init__(self, sems):
        self.sems, self.used, self.open = sems, 0, []

    def start(self, src, dst):
        copy = pltpu.make_async_copy(src, dst, self.sems.at[self.used])
        self.used += 1
        copy.start()
        self.open.append(copy)
        return copy

    def wait(self, copy):
        copy.wait()
        self.open.remove(copy)

    def finish(self):
        for copy in self.open:
            copy.wait()


class Scatter:
    def __init__(self, links, bufs, side, across):
        self.bufs = bufs
        self.far = links.copy(bufs.at[0], bufs.at[3], side)
        self.over = links.copy(bufs.at[1], bufs.at[4], across)
        self.near = links.copy(bufs.at[2], bufs.at[5], side)

    def put_far(self, value):
        self.bufs[0] = value.astype(jnp.bfloat16)
        self.far.start()

    def put_over(self, value):
        self.far.wait_recv()
        self.bufs[1] = (value + self.bufs[3].astype(jnp.float32)).astype(jnp.bfloat16)
        self.over.start()

    def put_near(self, value):
        self.bufs[2] = value.astype(jnp.bfloat16)
        self.near.start()

    def total(self, value):
        self.near.wait_recv()
        self.over.wait_recv()
        return value + self.bufs[5].astype(jnp.float32) + self.bufs[4].astype(jnp.float32)

    def close(self):
        self.far.wait_send()
        self.over.wait_send()
        self.near.wait_send()


def mlp_kernel(
    low, wo, attended, hidden, crows, gains, wg, wu, wd,
    hidden_out, d_middle_out, gain_out, dout_out, down_out, gate_out, up_own_out, up_mate_out,
    o_own_out, o_mate_out,
    wgf, wuf, wdf, mrows, act, dgate, dup, brows, dout, kept, middle, bufs, give, take, own, up_own,
    result, last, o_own, o_mate, send, recv, local,
):
    s, c, t = lax.axis_index(SHARD_AXIS), lax.axis_index(CTX_AXIS), lax.axis_index(TP_AXIS)
    part = hidden.shape[0]
    half = wg.shape[0]
    side, across = {TP_AXIS: t ^ 1}, {TP_AXIS: t ^ 2}
    mate, pair = {SHARD_AXIS: 1 - s}, {CTX_AXIS: c ^ 1}
    enter([side, across, mate, pair])
    links, locals_ = Links(send, recv), Locals(local)

    def piece(owner):
        return pl.ds(pl.multiple_of(owner * part, part), part)

    mine = pl.ds(pl.multiple_of(s * half, half), half)
    low_bit = c & 1

    def rows_of(shard, count, size):
        return pl.ds(pl.multiple_of(shard * count + low_bit * size, size), size)

    quarter = half // 2
    third = wd.shape[0] // 2
    theirs = pl.ds(pl.multiple_of((1 - s) * half, half), half)
    shared = []
    for src, dst in ((wg, wgf), (wu, wuf)):
        first = links.copy(
            src.at[rows_of(0, half, quarter), :], dst.at[rows_of(s, half, quarter), :], mate
        )
        got = dst.at[rows_of(1 - s, half, quarter), :]
        shared.append((first, links.copy(got, got, pair)))
    first = links.copy(
        wd.at[rows_of(0, 0, third), :], wdf.at[rows_of(0, 0, third), mine], mate
    )
    got = wdf.at[rows_of(0, 0, third), theirs]
    shared.append((first, links.copy(got, got, pair)))
    for first, _ in shared:
        first.start()
    own_weights = [
        locals_.start(wg, wgf.at[mine, :]),
        locals_.start(wu, wuf.at[mine, :]),
        locals_.start(wd, wdf.at[:, mine]),
    ]

    branch = Scatter(links, bufs.at[0], side, across)
    back = Scatter(links, bufs.at[1], side, across)
    out = Scatter(links, bufs.at[2], side, across)

    def branch_part(owner):
        return flat_dot(low[piece(owner), :], wo[...])

    branch.put_far(branch_part(t ^ 3))
    value = branch_part(t ^ 2)
    branch.put_over(value)
    branch.put_near(branch_part(t ^ 1))
    middle[...] = hidden[...].astype(jnp.float32) + branch_part(t)
    for first, on in shared[:2]:
        first.wait_recv()
        on.start()
    middle[...] = branch.total(middle[...])
    m = middle[...]
    scale = lax.rsqrt(jnp.mean(m * m, axis=-1, keepdims=True) + norm_eps)
    gain = gains[1:2, :]
    mrows[piece(t), :] = (m * scale * gain).astype(jnp.bfloat16)
    here, there = mrows.at[piece(t), :], mrows.at[piece(t ^ 2), :]
    m_over, m_near = links.copy(here, here, across), links.copy(here, here, side)
    m_on = links.copy(there, there, side)
    m_over.start()
    m_near.start()
    shared[2][0].wait_recv()
    shared[2][1].start()
    for copy in own_weights:
        locals_.wait(copy)
    for _, on in shared:
        on.wait_recv()

    def mlp(owner):
        at = piece(owner)
        rows = mrows[at, :]
        gate = flat_dot(rows, wgf[...])
        upward = flat_dot(rows, wuf[...])
        d_act = last_dot(crows[at, :], wdf[...])
        sig = 1.0 / (1.0 + jnp.exp(-gate))
        silu = gate * sig
        act[at, :] = (silu * upward).astype(jnp.bfloat16)
        dup[at, :] = (d_act * silu).astype(jnp.bfloat16)
        dgate[at, :] = (d_act * upward * sig * (1.0 + gate * (1.0 - sig))).astype(jnp.bfloat16)

    def out_part(owner):
        return flat_dot(act[piece(owner), :], wdf[...])

    def back_part(owner):
        at = piece(owner)
        return last_dot(dgate[at, :], wgf[...]) + last_dot(dup[at, :], wuf[...])

    mlp(t)
    kept[0] = back_part(t)
    kept[1] = out_part(t)
    m_near.wait_recv()
    mlp(t ^ 1)
    back.put_near(back_part(t ^ 1))
    m_over.wait_recv()
    m_on.start()
    m_on.wait_recv()
    mlp(t ^ 3)
    back.put_far(back_part(t ^ 3))
    mlp(t ^ 2)
    back.put_over(back_part(t ^ 2))
    out.put_far(out_part(t ^ 3))
    out.put_over(out_part(t ^ 2))
    out.put_near(out_part(t ^ 1))

    down_copy = links.copy(give.at[0:768, 0:512], take.at[0:768, 0:512], mate)
    gate_copy = links.copy(give.at[768:1280, 0:768], take.at[768:1280, 0:768], mate)
    give[0:768, 0:512] = first_dot(act[...], crows[:, theirs]).astype(jnp.bfloat16)
    down_copy.start()
    give[768:1280, 0:768] = first_dot(mrows[:, theirs], dgate[...]).astype(jnp.bfloat16)
    gate_copy.start()
    give[1280:1792, 0:768] = first_dot(mrows[:, theirs], dup[...]).astype(jnp.bfloat16)
    locals_.start(give.at[1280:1792, 0:768], up_mate_out)

    d_mlp = back.total(kept[0])
    m = middle[...]
    scale = lax.rsqrt(jnp.mean(m * m, axis=-1, keepdims=True) + norm_eps)
    scaled = d_mlp * gain
    inner = jnp.mean(scaled * m, axis=-1, keepdims=True)
    d_middle = (
        crows[piece(t), :].astype(jnp.float32) + scale * scaled - m * (scale * scale * scale) * inner
    )
    kept[0] = d_middle
    gain_grad = jnp.sum(d_mlp * m * scale, axis=0, keepdims=True)
    brows[piece(t), :] = d_middle.astype(jnp.bfloat16)
    here, there = brows.at[piece(t), :], brows.at[piece(t ^ 2), :]
    b_over, b_near = links.copy(here, here, across), links.copy(here, here, side)
    b_on = links.copy(there, there, side)
    b_over.start()
    b_near.start()
    locals_.start(kept.at[0], d_middle_out)
    result[...] = jnp.broadcast_to(gain_grad, (8, gain_grad.shape[1]))
    locals_.start(result, gain_out)

    own[0:768, 0:512] = first_dot(act[...], crows[:, mine])
    own[768:1280, 0:768] = first_dot(mrows[:, mine], dgate[...])
    up_own[...] = first_dot(mrows[:, mine], dup[...]).astype(jnp.bfloat16)
    locals_.start(up_own, up_own_out)

    def attended_back(owner):
        at = piece(owner)
        got = last_dot(brows[at, :], wo[...]).astype(jnp.bfloat16)
        for h in range(4):
            mine_h = got[:, h * 128 : h * 128 + 128]
            delta = -jnp.sum(
                mine_h.astype(jnp.float32) * attended[at, h * 128 : h * 128 + 128],
                axis=1,
                keepdims=True,
            )
            top = delta.astype(jnp.bfloat16).astype(jnp.float32)
            lane = lax.broadcasted_iota(jnp.int32, (part, HEAD_SIZE), 1)
            parts = jnp.where(lane == 0, top, jnp.where(lane == 1, delta - top, 0.0))
            dout[h, at, 0:128] = mine_h
            dout[h, at, 128:256] = parts.astype(jnp.bfloat16)

    attended_back(t)
    b_near.wait_recv()
    attended_back(t ^ 1)
    last[...] = (out.total(kept[1]) + middle[...]).astype(jnp.bfloat16)
    locals_.start(last, hidden_out)
    b_over.wait_recv()
    b_on.start()
    attended_back(t ^ 2)
    b_on.wait_recv()
    attended_back(t ^ 3)
    out.close()
    locals_.start(dout, dout_out)
    o_mate[...] = first_dot(low[...], brows[:, theirs]).astype(jnp.bfloat16)
    locals_.start(o_mate, o_mate_out)
    o_own[...] = first_dot(low[...], brows[:, mine]).astype(jnp.bfloat16)
    locals_.start(o_own, o_own_out)
    down_copy.wait()
    gate_copy.wait()
    give[0:768, 0:512] = (
        own[0:768, 0:512] + take[0:768, 0:512].astype(jnp.float32)
    ).astype(jnp.bfloat16)
    give[768:1280, 0:768] = (
        own[768:1280, 0:768] + take[768:1280, 0:768].astype(jnp.float32)
    ).astype(jnp.bfloat16)
    locals_.start(give.at[0:768, 0:512], down_out)
    locals_.start(give.at[768:1280, 0:768], gate_out)
    for first, on in shared:
        first.wait_send()
        on.wait_send()
    branch.close()
    back.close()
    for copy in (m_over, m_near, m_on, b_over, b_near, b_on):
        copy.wait_send()
    locals_.finish()


def mlp_call(low, wo, attended, hidden, crows, gains, wg, wu, wd):
    part, width = hidden.shape
    block = 4 * part
    units = wg.shape[1]
    half = wg.shape[0]
    f32, bf16 = jnp.float32, jnp.bfloat16
    shape = jax.ShapeDtypeStruct
    outs = (
        shape((part, width), bf16),
        shape((part, width), f32),
        shape((8, width), f32),
        shape((4, block, 256), bf16),
        shape((units, half), bf16),
        shape((half, units), bf16),
        shape((half, units), bf16),
        shape((half, units), bf16),
        shape((512, half), bf16),
        shape((512, half), bf16),
    )
    return pl.pallas_call(
        mlp_kernel,
        name="mlp",
        out_shape=outs,
        in_specs=[VMEM_SPEC] * 6 + [ANY_SPEC] * 3,
        out_specs=[ANY_SPEC] * len(outs),
        scratch_shapes=[
            pltpu.VMEM((width, units), bf16),
            pltpu.VMEM((width, units), bf16),
            pltpu.VMEM((units, width), bf16),
            pltpu.VMEM((block, width), bf16),
            pltpu.VMEM((block, units), bf16),
            pltpu.VMEM((block, units), bf16),
            pltpu.VMEM((block, units), bf16),
            pltpu.VMEM((block, width), bf16),
            pltpu.VMEM((4, block, 256), bf16),
            pltpu.VMEM((2, part, width), f32),
            pltpu.VMEM((part, width), f32),
            pltpu.VMEM((3, 6, part, width), bf16),
            pltpu.VMEM((1792, 768), bf16),
            pltpu.VMEM((1280, 768), bf16),
            pltpu.VMEM((1280, 768), f32),
            pltpu.VMEM((half, units), bf16),
            pltpu.VMEM((8, width), f32),
            pltpu.VMEM((part, width), bf16),
            pltpu.VMEM((512, half), bf16),
            pltpu.VMEM((512, half), bf16),
            pltpu.SemaphoreType.DMA((23,)),
            pltpu.SemaphoreType.DMA((23,)),
            pltpu.SemaphoreType.DMA((13,)),
        ],
        compiler_params=pltpu.CompilerParams(
            collective_id=1, has_side_effects=True, vmem_limit_bytes=58 << 20
        ),
    )(low, wo, attended, hidden, crows, gains, wg, wu, wd)


class LineSum:
    def __init__(self, links, own, landed, summed, outer, near, opposite):
        self.own, self.landed, self.summed, self.outer = own, landed, summed, outer
        self.inward = links.copy(own, landed, near)
        self.cross = links.copy(landed, summed, opposite)
        self.outward = links.copy(summed, landed, near)

    def first(self):
        pl.when(self.outer)(self.inward.start)

    def second(self):
        @pl.when(jnp.logical_not(self.outer))
        def _():
            self.inward.wait_recv()
            self.landed[...] = (
                self.own[...].astype(jnp.float32) + self.landed[...].astype(jnp.float32)
            ).astype(jnp.bfloat16)
            self.cross.start()

    def third(self):
        @pl.when(jnp.logical_not(self.outer))
        def _():
            self.cross.wait_recv()
            self.summed[...] = (
                self.landed[...].astype(jnp.float32) + self.summed[...].astype(jnp.float32)
            ).astype(jnp.bfloat16)
            self.outward.start()

    def finish(self, out, sem):
        @pl.when(self.outer)
        def _():
            self.outward.wait_recv()
            copy = pltpu.make_async_copy(self.landed, out, sem)
            copy.start()
            self.inward.wait_send()
            copy.wait()

        @pl.when(jnp.logical_not(self.outer))
        def _():
            copy = pltpu.make_async_copy(self.summed, out, sem)
            copy.start()
            self.cross.wait_send()
            self.outward.wait_send()
            copy.wait()


def backward_kernel(
    query, dout, q_proj, wqkv, hidden, d_middle, gains, mlp_gain_grad,
    down_in, gate_in, up_own, up_mate, o_own, o_mate,
    keys, values, k_proj, cosine, sine, rows,
    hidden_grad, gains_out, down_out, gate_out, up_out, o_out, kv_out, q_out,
    kbuf, vbuf, kpbuf, cosbuf, sinbuf, rowbuf, dq, dk, dv, dkv, dqp, gkv, kept, bufs,
    up_sum, o_sum, kv_sum, q_sum, up_land, o_land, kv_land, q_land, kv_give, q_give,
    down_b, down_s, gate_b, gate_s, up_b, up_s, o_b, o_s, kv_b, kv_s, q_b, q_s,
    far_send, far_land, mid_send, mid_land, gsum, gland, send, recv, local, blocksem,
):
    s, c, t = lax.axis_index(SHARD_AXIS), lax.axis_index(CTX_AXIS), lax.axis_index(TP_AXIS)
    nctx = lax.axis_size(CTX_AXIS)
    part = hidden.shape[0]
    half = rows.shape[2] // 2
    f32, bf16 = jnp.float32, jnp.bfloat16
    side, across, mate = {TP_AXIS: t ^ 1}, {TP_AXIS: t ^ 2}, {SHARD_AXIS: 1 - s}
    near, opposite = {CTX_AXIS: c ^ 1}, {CTX_AXIS: c ^ 3}
    previous = {CTX_AXIS: lax.rem(c + nctx - 1, nctx)}
    outer = (c == 0) | (c == nctx - 1)
    enter([side, across, mate, near, opposite])
    links, locals_ = Links(send, recv), Locals(local)
    scale = HEAD_SIZE ** (-0.5)

    def piece(owner):
        return pl.ds(pl.multiple_of(owner * part, part), part)

    mine = pl.ds(pl.multiple_of(s * half, half), half)
    theirs = pl.ds(pl.multiple_of((1 - s) * half, half), half)

    def block_copies(b):
        slot = b & 1
        pairs = (
            (keys.at[b], kbuf.at[slot]), (values.at[b], vbuf.at[slot]),
            (k_proj.at[b], kpbuf.at[slot]), (cosine.at[b], cosbuf.at[slot]),
            (sine.at[b], sinbuf.at[slot]),
        )
        return [
            pltpu.make_async_copy(a, d, blocksem.at[6 * b + n]) for n, (a, d) in enumerate(pairs)
        ]

    def row_copy(b):
        return pltpu.make_async_copy(rows.at[b], rowbuf, blocksem.at[6 * b + 5])

    def fetch(b):
        for copy in block_copies(b):
            copy.start()

    def fetched(b):
        for copy in block_copies(b):
            copy.wait()

    up_copy = links.copy(up_mate, up_land, mate)
    o_copy = links.copy(o_mate, o_land, mate)
    kv_copy = links.copy(kv_give, kv_land, mate)
    q_copy = links.copy(q_give, q_land, mate)
    up_copy.start()
    o_copy.start()
    line = [
        LineSum(links, own, landed, summed, outer, near, opposite)
        for own, landed, summed in (
            (down_in, down_b, down_s), (gate_in, gate_b, gate_s), (up_sum, up_b, up_s),
            (o_sum, o_b, o_s), (kv_sum, kv_b, kv_s), (q_sum, q_b, q_s),
        )
    ]
    line[0].first()
    line[1].first()
    scatters = [
        Scatter(links, bufs.at[0], side, across),
        Scatter(links, bufs.at[1], side, across),
        Scatter(links, bufs.at[0], side, across),
    ]
    far_copy = links.copy(far_send, far_land, previous)
    mid_copy = links.copy(mid_send, mid_land, previous)

    @pl.when(c >= 2)
    def _():
        fetch(2)
        row_copy(2).start()

    @pl.when(c >= 1)
    def _():
        fetch(1)

    @pl.when(c == 1)
    def _():
        row_copy(1).start()

    @pl.when(c <= 1)
    def _():
        fetch(0)

    @pl.when(c == 0)
    def _():
        row_copy(0).start()

    dq[...] = jnp.zeros(dq.shape, f32)
    gkv[...] = jnp.zeros(gkv.shape, f32)
    gsum[...] = jnp.zeros(gsum.shape, f32)
    gsum[1:2, :] = mlp_gain_grad[0:1, :]
    q_gain = gains[2:3, 0:HEAD_SIZE]
    k_gain = gains[3:4, 0:HEAD_SIZE]

    def tile(b, g, r, k0, size, triangle):
        slot = b & 1
        q_at = pl.ds(pl.multiple_of(r * 256, 256), 256)
        k_at = pl.ds(pl.multiple_of(k0, 256), size)
        kk, vv = kbuf[slot, g, k_at, :], vbuf[slot, g, k_at, :]
        dv_new, dk_new = [], []
        for hh in range(2):
            h = 2 * g + hh
            qq, do = query[h, q_at, :], dout[h, q_at, :]
            p = jnp.exp2(last_dot(kk, qq) * SCORE_STEP)
            if triangle:
                p = jnp.where(
                    lax.broadcasted_iota(jnp.int32, p.shape, 0)
                    <= lax.broadcasted_iota(jnp.int32, p.shape, 1),
                    p,
                    0.0,
                )
            ds = (p * last_dot(vv, do)).astype(bf16)
            dv_new.append(flat_dot(p.astype(bf16), do[:, 0:HEAD_SIZE]))
            dk_new.append(flat_dot(ds, qq[:, 0:HEAD_SIZE]))
            dq[h, q_at, :] += first_dot(ds, kk[:, 0:HEAD_SIZE])
        dv[g, k_at, :] += dv_new[0] + dv_new[1]
        dk[g, k_at, :] += dk_new[0] + dk_new[1]

    def clear():
        dk[...] = jnp.zeros(dk.shape, f32)
        dv[...] = jnp.zeros(dv.shape, f32)

    def norm_back(grad, u, gain, cos, sin, row):
        turned = grad * cos - pltpu.roll(grad, HEAD_SIZE // 2, 1) * sin
        r = lax.rsqrt(jnp.mean(u * u, axis=-1, keepdims=True) + norm_eps)
        gsum[row : row + 1, 0:HEAD_SIZE] += jnp.sum(turned * u * r, axis=0, keepdims=True)
        scaled = turned * gain
        inner = jnp.mean(scaled * u, axis=-1, keepdims=True)
        return (r * scaled - u * (r * r * r) * inner).astype(bf16)

    def finish_kv(b):
        slot = b & 1

        @pl.loop(0, 4)
        def _(n):
            at = piece(n)
            cos, sin = cosbuf[slot, at, :], sinbuf[slot, at, :]
            for g in range(2):
                lanes = slice(g * 128, g * 128 + 128)
                u = kpbuf[slot, at, lanes]
                dkv[at, lanes] = norm_back(dk[g, at, :] * scale, u, k_gain, cos, sin, 3)
                dkv[at, 256 + g * 128 : 384 + g * 128] = dv[g, at, :].astype(bf16)

        row_copy(b).wait()

        @pl.loop(0, 4)
        def _(n):
            at = piece(n)
            gkv[at, :] += first_dot(rowbuf[:, at], dkv[...])

    def kv_part(owner):
        return last_dot(dkv[piece(owner), :], wqkv[:, 512:1024])

    def all_part(owner):
        return kv_part(owner) + last_dot(dqp[piece(owner), :], wqkv[:, 0:512])

    def scatter(which, slot, partial):
        which.put_far(partial(t ^ 3))
        which.put_over(partial(t ^ 2))
        which.put_near(partial(t ^ 1))
        kept[slot] = partial(t)

    @pl.when(c >= 2)
    def _():
        fetched(2)
        clear()

        @pl.loop(0, 8)
        def _(n):
            g, r = n // 4, lax.rem(n, 4)

            @pl.loop(r, 4)
            def _(k):
                tile(2, g, r, k * 256, 256, False)

        finish_kv(2)
        fetch(0)
        row_copy(1).start()
        scatter(scatters[2], 0, kv_part)

    @pl.when(c >= 1)
    def _():
        fetched(1)
        clear()

        @pl.loop(0, 8)
        def _(n):
            g, r = n // 4, lax.rem(n, 4)

            @pl.loop(0, 2)
            def _(k):
                tile(1, g, r, k * 512, 512, False)

        finish_kv(1)
        row_copy(0).start()

    @pl.when(c >= 2)
    def _():
        far_send[...] = scatters[2].total(kept[0]).astype(bf16)
        far_copy.start()
        scatters[2].close()

    @pl.when(c >= 1)
    def _():
        scatter(scatters[1], 1, kv_part)

    up_copy.wait()
    up_sum[...] = (up_own[...].astype(f32) + up_land[...].astype(f32)).astype(bf16)
    line[2].first()
    o_copy.wait()
    o_sum[...] = (o_own[...].astype(f32) + o_land[...].astype(f32)).astype(bf16)
    line[3].first()
    line[0].second()
    line[1].second()

    fetched(0)
    clear()

    @pl.loop(0, 8)
    def _(n):
        g, r = n // 4, lax.rem(n, 4)
        tile(0, g, r, r * 256, 256, True)

        @pl.loop(0, r)
        def _(k):
            tile(0, g, r, k * 256, 256, False)

    finish_kv(0)

    @pl.loop(0, 4)
    def _(n):
        at = piece(n)
        cos, sin = cosbuf[0, at, :], sinbuf[0, at, :]
        for h in range(4):
            lanes = slice(h * 128, h * 128 + 128)
            u = q_proj[at, lanes]
            dqp[at, lanes] = norm_back(dq[h, at, :] * scale, u, q_gain, cos, sin, 2)

    kv_give[...] = gkv[theirs, :].astype(bf16)
    kv_copy.start()
    for n in range(2):
        lanes = pl.ds(pl.multiple_of((1 - s) * half + n * 256, 256), 256)
        q_give[n * 256 : n * 256 + 256, :] = first_dot(rowbuf[:, lanes], dqp[...]).astype(bf16)
    q_copy.start()

    @pl.when((c >= 1) & (c < nctx - 1))
    def _():
        far_copy.wait_recv()
        kept[1] += far_land[...].astype(f32)

    @pl.when(c >= 1)
    def _():
        mid_send[...] = scatters[1].total(kept[1]).astype(bf16)
        mid_copy.start()
        scatters[1].close()

    scatter(scatters[0], 0, all_part)
    line[0].third()
    line[1].third()
    line[2].second()
    line[3].second()

    kv_copy.wait()
    kv_sum[...] = (gkv[mine, :] + kv_land[...].astype(f32)).astype(bf16)
    line[4].first()
    q_copy.wait()
    for n in range(2):
        lanes = pl.ds(pl.multiple_of(s * half + n * 256, 256), 256)
        at = slice(n * 256, n * 256 + 256)
        q_sum[at, :] = (first_dot(rowbuf[:, lanes], dqp[...]) + q_land[at, :].astype(f32)).astype(
            bf16
        )
    line[5].first()
    line[2].third()
    line[3].third()

    @pl.when(c < nctx - 1)
    def _():
        mid_copy.wait_recv()
        kept[0] += mid_land[...].astype(f32)

    kept[0] = scatters[0].total(kept[0])
    x = hidden[...].astype(f32)
    r = lax.rsqrt(jnp.mean(x * x, axis=-1, keepdims=True) + norm_eps)
    d_in = kept[0]
    gsum[0:1, :] = jnp.sum(d_in * x * r, axis=0, keepdims=True)
    scaled = d_in * gains[0:1, :]
    inner = jnp.mean(scaled * x, axis=-1, keepdims=True)
    kept[1] = d_middle[...] + r * scaled - x * (r * r * r) * inner
    locals_.start(kept.at[1], hidden_grad)
    scatters[0].close()
    line[4].second()
    line[5].second()
    for n, device in enumerate((side, across, mate, near, opposite)):
        copy = links.copy(gsum, gland.at[n], device)
        copy.start()
        copy.wait()
        gsum[...] += gland[n]
    locals_.start(gsum, gains_out)
    line[4].third()
    line[5].third()

    @pl.when(c >= 2)
    def _():
        far_copy.wait_send()

    @pl.when(c >= 1)
    def _():
        mid_copy.wait_send()

    for n, (item, out) in enumerate(
        zip(line, (down_out, gate_out, up_out, o_out, kv_out, q_out), strict=True)
    ):
        item.finish(out, local.at[2 + n])
    locals_.finish()


def backward_call(vmem_args, any_args):
    query, dout, q_proj, wqkv, hidden, d_middle, gains = vmem_args[:7]
    keys, values, k_proj, cosine, sine, rows = any_args
    part, width = hidden.shape
    block = 4 * part
    f32, bf16 = jnp.float32, jnp.bfloat16
    shape = jax.ShapeDtypeStruct
    sizes = ((768, 512), (512, 768), (512, 768), (512, 512), (512, 512), (512, 512))
    outs = [shape((part, width), f32), shape((8, width), f32)] + [shape(z, bf16) for z in sizes]
    sums = [pltpu.VMEM(z, bf16) for z in sizes[2:]]
    pairs = [pltpu.VMEM(z, bf16) for z in sizes for _ in range(2)]
    tile = pltpu.VMEM((part, width), bf16)
    return pl.pallas_call(
        backward_kernel,
        name="backward",
        out_shape=outs,
        in_specs=[VMEM_SPEC] * 14 + [ANY_SPEC] * 6,
        out_specs=[ANY_SPEC] * len(outs),
        scratch_shapes=[
            pltpu.VMEM((2, 2, block, 256), bf16),
            pltpu.VMEM((2, 2, block, 256), bf16),
            pltpu.VMEM((2, block, 256), f32),
            pltpu.VMEM((2, block, HEAD_SIZE), f32),
            pltpu.VMEM((2, block, HEAD_SIZE), f32),
            pltpu.VMEM((block, width), bf16),
            pltpu.VMEM((4, block, HEAD_SIZE), f32),
            pltpu.VMEM((2, block, HEAD_SIZE), f32),
            pltpu.VMEM((2, block, HEAD_SIZE), f32),
            pltpu.VMEM((block, 512), bf16),
            pltpu.VMEM((block, 512), bf16),
            pltpu.VMEM((width, 512), f32),
            pltpu.VMEM((2, part, width), f32),
            pltpu.VMEM((2, 6, part, width), bf16),
        ]
        + sums
        + sums
        + sums[2:]
        + pairs
        + [
            tile, tile, tile, tile,
            pltpu.VMEM((8, width), f32),
            pltpu.VMEM((5, 8, width), f32),
            pltpu.SemaphoreType.DMA((38,)),
            pltpu.SemaphoreType.DMA((38,)),
            pltpu.SemaphoreType.DMA((8,)),
            pltpu.SemaphoreType.DMA((18,)),
        ],
        compiler_params=pltpu.CompilerParams(
            collective_id=2, has_side_effects=True, vmem_limit_bytes=60 << 20
        ),
    )(*vmem_args, *any_args)


def tables(segments, ctx_index, block):
    length = segments.shape[0]
    labels = jnp.arange(NDOC, dtype=jnp.int32)
    before = jnp.sum((segments[:, None] < labels).astype(jnp.int32), axis=0)
    half_lane = lax.rem(jnp.arange(HEAD_SIZE, dtype=jnp.int32), HEAD_SIZE // 2)
    rates = jnp.power(
        jnp.float32(rope_base), -(2 * half_lane).astype(jnp.float32) / HEAD_SIZE
    )
    cosines, sines, marks = [], [], []
    for back in range(3):
        start = jnp.maximum(ctx_index - back, 0) * block
        seg = lax.dynamic_slice_in_dim(segments, start, block, 0)
        first = jnp.sum(jnp.where(seg[:, None] == labels, before, 0), axis=1)
        pos = start + jnp.arange(block, dtype=jnp.int32) - first
        angles = pos.astype(jnp.float32)[:, None] * rates
        cosines.append(jnp.cos(angles))
        sines.append(jnp.where(jnp.arange(HEAD_SIZE) < HEAD_SIZE // 2, -1.0, 1.0) * jnp.sin(angles))
        marks.append(
            (seg[:, None] == jnp.arange(HEAD_SIZE, dtype=jnp.int32)).astype(jnp.bfloat16)
        )
    return jnp.stack(cosines), jnp.stack(sines), jnp.stack(marks)


def pack_gains(attn_gain, mlp_gain, query_gain, key_gain):
    shard = lax.axis_index(SHARD_AXIS)

    def row(gain, width):
        spread = jnp.tile(gain.astype(jnp.float32), width // gain.shape[0])
        own = jnp.arange(width) // gain.shape[0] == shard
        return jnp.where(own, spread, 0.0)

    width = attn_gain.shape[0] * lax.axis_size(SHARD_AXIS)
    small = [
        jnp.pad(row(gain, HEAD_SIZE), (0, width - HEAD_SIZE)) for gain in (query_gain, key_gain)
    ]
    rows = [row(attn_gain, width), row(mlp_gain, width)] + small
    return jnp.stack(rows + [jnp.zeros((width,), jnp.float32)] * 4)


def fast_device(
    hidden,
    segments,
    cotangent,
    attn_gain,
    w_query,
    key_weight_matrix,
    value_weight_matrix,
    query_gain,
    key_gain,
    mixer_exit_coefficients,
    mlp_gain,
    w_gate,
    w_up,
    w_down,
):
    block_rows = hidden.shape[1] * lax.axis_size(TP_AXIS)
    cosine, sine, marks = tables(segments[0], lax.axis_index(CTX_AXIS), block_rows)
    gains_in = pack_gains(attn_gain, mlp_gain, query_gain, key_gain)
    gains, rows, q_proj, k_proj, query, keys, values, attended, low, wo, wqkv, crows = forward_call(
        hidden[0], cotangent[0], gains_in, cosine, sine, marks, w_query, key_weight_matrix,
        value_weight_matrix, mixer_exit_coefficients,
    )
    out_hidden, d_middle, mlp_gain_grad, dout, down, gate, up_own, up_mate, o_own, o_mate = mlp_call(
        low, wo, attended, hidden[0], crows, gains, w_gate, w_up, w_down
    )
    grad_hidden, sums, down, gate, up, o, kv, q = backward_call(
        (query, dout, q_proj, wqkv, hidden[0], d_middle, gains, mlp_gain_grad,
         down, gate, up_own, up_mate, o_own, o_mate),
        (keys, values, k_proj, cosine, sine, rows),
    )
    shard = lax.axis_index(SHARD_AXIS)

    def own(row, count):
        return lax.dynamic_slice_in_dim(sums[row], shard * count, count, 0)

    f32 = jnp.float32
    kv_width = key_weight_matrix.shape[1]
    return (
        out_hidden[None],
        grad_hidden[None],
        own(0, attn_gain.shape[0]),
        q.astype(f32),
        kv[:, :kv_width].astype(f32),
        kv[:, kv_width:].astype(f32),
        own(2, query_gain.shape[0]),
        own(3, key_gain.shape[0]),
        o.astype(f32),
        own(1, mlp_gain.shape[0]),
        gate.astype(f32),
        up.astype(f32),
        down.astype(f32),
    )


def per_device(
    hidden,
    segments,
    cotangent,
    attn_gain,
    w_query,
    key_weight_matrix,
    value_weight_matrix,
    query_gain,
    key_gain,
    mixer_exit_coefficients,
    mlp_gain,
    w_gate,
    w_up,
    w_down,
):
    collected_rows = (
        lax.all_gather(attn_gain, SHARD_AXIS, axis=0, tiled=True),
        lax.all_gather(w_query, SHARD_AXIS, axis=0, tiled=True),
        lax.all_gather(key_weight_matrix, SHARD_AXIS, axis=0, tiled=True),
        lax.all_gather(value_weight_matrix, SHARD_AXIS, axis=0, tiled=True),
        lax.all_gather(query_gain, SHARD_AXIS, axis=0, tiled=True),
        lax.all_gather(key_gain, SHARD_AXIS, axis=0, tiled=True),
        lax.all_gather(mixer_exit_coefficients, SHARD_AXIS, axis=1, tiled=True),
        lax.all_gather(mlp_gain, SHARD_AXIS, axis=0, tiled=True),
        lax.all_gather(w_gate, SHARD_AXIS, axis=0, tiled=True),
        lax.all_gather(w_up, SHARD_AXIS, axis=0, tiled=True),
        lax.all_gather(w_down, SHARD_AXIS, axis=1, tiled=True),
    )
    gain_attn = collected_rows[0].astype(jnp.float32)
    gain_query = collected_rows[4].astype(jnp.float32)
    gain_key = collected_rows[5].astype(jnp.float32)
    gain_mlp = collected_rows[7].astype(jnp.float32)
    seq_count = hidden.shape[0]
    block_rows = hidden.shape[1] * lax.axis_size(TP_AXIS)
    seq_length = segments.shape[1]
    ctx_index = lax.axis_index(CTX_AXIS)
    heads_local = w_query.shape[1] // HEAD_SIZE
    kv_local = key_weight_matrix.shape[1] // HEAD_SIZE
    query_group_width = heads_local // kv_local
    score_scale = HEAD_SIZE ** (-0.5)
    block_start = ctx_index * block_rows
    query_pos = block_start + jnp.arange(block_rows, dtype=jnp.int32)
    query_seg = lax.dynamic_slice_in_dim(segments, block_start, block_rows, 1)
    positions = lax.dynamic_slice_in_dim(doc_positions(segments), block_start, block_rows, 1)
    cosine, sine_part = rope_tables(positions)

    def counting_keys(key_first, step_rows):
        early = key_first <= block_start + block_rows - 1
        last_seg = lax.dynamic_slice_in_dim(segments, key_first + step_rows - 1, 1, 1)[:, 0]
        return early & jnp.any(last_seg >= query_seg[:, 0])

    inputs = hidden.astype(jnp.float32)
    scale_one = rms_scale(inputs)
    attention_input = (inputs * scale_one * gain_attn).astype(jnp.bfloat16)
    attention_rows = tp_rows(attention_input)
    q_proj = jnp.einsum(
        "zjr,rm->zjm", attention_rows, collected_rows[1], preferred_element_type=jnp.float32
    ).reshape(seq_count, block_rows, heads_local, HEAD_SIZE)
    key_projected = jnp.einsum(
        "zjr,rm->zjm", attention_rows, collected_rows[2], preferred_element_type=jnp.float32
    ).reshape(seq_count, block_rows, kv_local, HEAD_SIZE)
    value_projected = jnp.einsum(
        "zjr,rm->zjm", attention_rows, collected_rows[3], preferred_element_type=jnp.float32
    )
    q_scale = rms_scale(q_proj)
    k_scale = rms_scale(key_projected)
    query_rows_input = (
        rotate(q_proj * q_scale * gain_query, cosine, sine_part)
        .astype(jnp.bfloat16)
        .reshape(seq_count, block_rows, kv_local, query_group_width, HEAD_SIZE)
    )
    keys = rotate(key_projected * k_scale * gain_key, cosine, sine_part).astype(jnp.bfloat16)
    values = value_projected.astype(jnp.bfloat16).reshape(
        seq_count, block_rows, kv_local, HEAD_SIZE
    )
    stat_shape = (seq_count, kv_local, query_group_width, block_rows)
    start_state = (
        jnp.full(stat_shape, masked_fill, jnp.float32),
        jnp.zeros(stat_shape, jnp.float32),
        jnp.zeros(stat_shape + (HEAD_SIZE,), jnp.float32),
    )
    piece_keys = lax.all_gather(keys, CTX_AXIS, axis=1, tiled=True)
    piece_values = lax.all_gather(values, CTX_AXIS, axis=1, tiled=True)
    piece_rows = piece_keys.shape[1]
    step_rows = math.gcd(piece_rows, 1024)

    def attend_one_step(number, loop_state):
        offset = number * step_rows
        key_first = offset

        def attend_compute(state):
            row_max, row_total, summed = state
            key_part = lax.dynamic_slice_in_dim(piece_keys, offset, step_rows, 1)
            value_part = lax.dynamic_slice_in_dim(piece_values, offset, step_rows, 1)
            allowed = key_block(segments, key_first, step_rows, query_pos, query_seg)
            scores = (
                jnp.einsum(
                    "sqhgd,skhd->shgqk",
                    query_rows_input,
                    key_part,
                    preferred_element_type=jnp.float32,
                )
                * score_scale
            )
            masked = jnp.where(allowed, scores, masked_fill)
            new_max = jnp.maximum(row_max, jnp.max(masked, axis=-1))
            weights = jnp.where(allowed, jnp.exp(masked - new_max[..., None]), 0.0)
            decay_factor = jnp.exp(row_max - new_max)
            row_total = row_total * decay_factor + jnp.sum(weights, axis=-1)
            summed = summed * decay_factor[..., None] + jnp.einsum(
                "shgqk,skhd->shgqd",
                weights.astype(jnp.bfloat16),
                value_part,
                preferred_element_type=jnp.float32,
            )
            return (new_max, row_total, summed)

        return lax.cond(counting_keys(key_first, step_rows), attend_compute, keep_state, loop_state)

    row_max, row_total, summed = lax.fori_loop(
        0, piece_rows // step_rows, attend_one_step, start_state
    )
    attended = summed / row_total[..., None]
    log_total = row_max + jnp.log(row_total)
    attended_reduced_copy = (
        attended.transpose(0, 3, 1, 2, 4)
        .reshape(seq_count, block_rows, heads_local * HEAD_SIZE)
        .astype(jnp.bfloat16)
    )
    branch = tp_total(
        jnp.einsum(
            "vkq,qy->vky",
            attended_reduced_copy,
            collected_rows[6],
            preferred_element_type=jnp.float32,
        )
    )
    middle = inputs + branch
    scale_two = rms_scale(middle)
    mlp_in = (middle * scale_two * gain_mlp).astype(jnp.bfloat16)
    mlp_rows = tp_rows(mlp_in)
    gate = jnp.einsum(
        "snd,df->snf", mlp_rows, collected_rows[8], preferred_element_type=jnp.float32
    )
    upward = jnp.einsum(
        "snd,df->snf", mlp_rows, collected_rows[9], preferred_element_type=jnp.float32
    )
    activated = (jax.nn.silu(gate) * upward).astype(jnp.bfloat16)
    out_hidden = (
        middle
        + tp_total(
            jnp.einsum(
                "snf,fd->snd", activated, collected_rows[10], preferred_element_type=jnp.float32
            )
        )
    ).astype(jnp.bfloat16)
    again = (
        lax.all_gather(attn_gain, SHARD_AXIS, axis=0, tiled=True),
        lax.all_gather(w_query, SHARD_AXIS, axis=0, tiled=True),
        lax.all_gather(key_weight_matrix, SHARD_AXIS, axis=0, tiled=True),
        lax.all_gather(value_weight_matrix, SHARD_AXIS, axis=0, tiled=True),
        lax.all_gather(query_gain, SHARD_AXIS, axis=0, tiled=True),
        lax.all_gather(key_gain, SHARD_AXIS, axis=0, tiled=True),
        lax.all_gather(mixer_exit_coefficients, SHARD_AXIS, axis=1, tiled=True),
        lax.all_gather(mlp_gain, SHARD_AXIS, axis=0, tiled=True),
        lax.all_gather(w_gate, SHARD_AXIS, axis=0, tiled=True),
        lax.all_gather(w_up, SHARD_AXIS, axis=0, tiled=True),
        lax.all_gather(w_down, SHARD_AXIS, axis=1, tiled=True),
    )
    query_backward = again[1]
    lookup_pullback = again[2]
    value_backward = again[3]
    output_backward = again[6]
    back_gate = again[8]
    back_up = again[9]
    back_down = again[10]
    d_out = cotangent.astype(jnp.float32)
    d_rows = tp_rows(cotangent)
    grad_down = jnp.einsum("snf,snd->fd", activated, d_rows, preferred_element_type=jnp.float32)
    d_act = jnp.einsum("snd,fd->snf", d_rows, back_down, preferred_element_type=jnp.float32)
    sigmoid_gate = jax.nn.sigmoid(gate)
    d_upward = (d_act * jax.nn.silu(gate)).astype(jnp.bfloat16)
    d_gate = (d_act * upward * sigmoid_gate * (1.0 + gate * (1.0 - sigmoid_gate))).astype(
        jnp.bfloat16
    )
    grad_gate = jnp.einsum("snd,snf->df", mlp_rows, d_gate, preferred_element_type=jnp.float32)
    grad_up = jnp.einsum("snd,snf->df", mlp_rows, d_upward, preferred_element_type=jnp.float32)
    d_mlp_in = tp_total(
        jnp.einsum("snf,df->snd", d_gate, back_gate, preferred_element_type=jnp.float32)
        + jnp.einsum("snf,df->snd", d_upward, back_up, preferred_element_type=jnp.float32)
    )
    grad_mlp_gain = jnp.sum(d_mlp_in * middle * scale_two, axis=(0, 1))
    d_middle = d_out + rms_back(d_mlp_in, middle, scale_two, gain_mlp)
    d_branch = d_middle.astype(jnp.bfloat16)
    residual_branch_rows = tp_rows(d_branch)
    result_cotangent = jnp.einsum(
        "xbj,xbk->jk",
        attended_reduced_copy,
        residual_branch_rows,
        preferred_element_type=jnp.float32,
    )
    d_attended = (
        jnp.einsum(
            "miv,cv->mic", residual_branch_rows, output_backward, preferred_element_type=jnp.float32
        )
        .astype(jnp.bfloat16)
        .reshape(seq_count, block_rows, kv_local, query_group_width, HEAD_SIZE)
    )
    delta = jnp.sum(d_attended.astype(jnp.float32).transpose(0, 2, 3, 1, 4) * attended, axis=-1)
    query_zeros = jnp.zeros(
        (seq_count, block_rows, kv_local, query_group_width, HEAD_SIZE), jnp.float32
    )
    back_state = (
        query_zeros,
        jnp.zeros((seq_count, seq_length, kv_local, HEAD_SIZE), jnp.float32),
        jnp.zeros((seq_count, seq_length, kv_local, HEAD_SIZE), jnp.float32),
    )
    back_piece_keys = lax.all_gather(keys, CTX_AXIS, axis=1, tiled=True)
    back_piece_values = lax.all_gather(values, CTX_AXIS, axis=1, tiled=True)
    piece_rows = back_piece_keys.shape[1]
    back_step_rows = math.gcd(piece_rows, 1024)

    def back_one_step(number, loop_state):
        offset = number * back_step_rows
        key_first = offset
        write_at = offset

        def back_compute(state):
            d_query, d_keys, d_values = state
            key_part = lax.dynamic_slice_in_dim(back_piece_keys, offset, back_step_rows, 1)
            value_part = lax.dynamic_slice_in_dim(back_piece_values, offset, back_step_rows, 1)
            allowed = key_block(segments, key_first, back_step_rows, query_pos, query_seg)
            scores = (
                jnp.einsum(
                    "sqhgd,skhd->shgqk",
                    query_rows_input,
                    key_part,
                    preferred_element_type=jnp.float32,
                )
                * score_scale
            )
            probs = jnp.where(allowed, jnp.exp(scores - log_total[..., None]), 0.0)
            d_probs = jnp.einsum(
                "sqhgd,skhd->shgqk", d_attended, value_part, preferred_element_type=jnp.float32
            )
            d_scores = (probs * (d_probs - delta[..., None])).astype(jnp.bfloat16)
            d_query = d_query + jnp.einsum(
                "shgqk,skhd->sqhgd", d_scores, key_part, preferred_element_type=jnp.float32
            )
            key_grad = jnp.einsum(
                "shgqk,sqhgd->skhd", d_scores, query_rows_input, preferred_element_type=jnp.float32
            )
            value_grad = jnp.einsum(
                "shgqk,sqhgd->skhd",
                probs.astype(jnp.bfloat16),
                d_attended,
                preferred_element_type=jnp.float32,
            )
            d_keys = lax.dynamic_update_slice_in_dim(
                d_keys,
                lax.dynamic_slice_in_dim(d_keys, write_at, back_step_rows, 1) + key_grad,
                write_at,
                1,
            )
            d_values = lax.dynamic_update_slice_in_dim(
                d_values,
                lax.dynamic_slice_in_dim(d_values, write_at, back_step_rows, 1) + value_grad,
                write_at,
                1,
            )
            return (d_query, d_keys, d_values)

        return lax.cond(
            counting_keys(key_first, back_step_rows), back_compute, keep_state, loop_state
        )

    d_query, d_keys, d_values = lax.fori_loop(
        0, piece_rows // back_step_rows, back_one_step, back_state
    )
    own_keys, own_values = (
        lax.psum_scatter(
            d_keys.astype(jnp.bfloat16), CTX_AXIS, scatter_dimension=1, tiled=True
        ).astype(jnp.float32),
        lax.psum_scatter(
            d_values.astype(jnp.bfloat16), CTX_AXIS, scatter_dimension=1, tiled=True
        ).astype(jnp.float32),
    )
    q_normed = rotate_back(
        d_query.reshape(seq_count, block_rows, heads_local, HEAD_SIZE) * score_scale,
        cosine,
        sine_part,
    )
    grad_query_gain = jnp.sum(q_normed * q_proj * q_scale, axis=(0, 1, 2))
    query_projection_gradient = (
        rms_back(q_normed, q_proj, q_scale, gain_query)
        .astype(jnp.bfloat16)
        .reshape(seq_count, block_rows, heads_local * HEAD_SIZE)
    )
    k_normed = rotate_back(own_keys * score_scale, cosine, sine_part)
    grad_key_gain = jnp.sum(k_normed * key_projected * k_scale, axis=(0, 1, 2))
    lookup_map_derivative = (
        rms_back(k_normed, key_projected, k_scale, gain_key)
        .astype(jnp.bfloat16)
        .reshape(seq_count, block_rows, kv_local * HEAD_SIZE)
    )
    value_projection_gradient = own_values.astype(jnp.bfloat16).reshape(
        seq_count, block_rows, kv_local * HEAD_SIZE
    )
    query_gradient_rows = jnp.einsum(
        "zqr,zqa->ra", attention_rows, query_projection_gradient, preferred_element_type=jnp.float32
    )
    key_gradient_rows = jnp.einsum(
        "zqr,zqa->ra", attention_rows, lookup_map_derivative, preferred_element_type=jnp.float32
    )
    value_gradient_rows = jnp.einsum(
        "zqr,zqa->ra", attention_rows, value_projection_gradient, preferred_element_type=jnp.float32
    )
    d_attn_in = tp_total(
        jnp.einsum(
            "wtl,al->wta",
            query_projection_gradient,
            query_backward,
            preferred_element_type=jnp.float32,
        )
        + jnp.einsum(
            "wtl,al->wta",
            lookup_map_derivative,
            lookup_pullback,
            preferred_element_type=jnp.float32,
        )
        + jnp.einsum(
            "wtl,al->wta",
            value_projection_gradient,
            value_backward,
            preferred_element_type=jnp.float32,
        )
    )
    grad_attn_gain = jnp.sum(d_attn_in * inputs * scale_one, axis=(0, 1))
    grad_hidden = d_middle + rms_back(d_attn_in, inputs, scale_one, gain_attn)
    reduced = (
        lax.psum_scatter(
            grad_attn_gain.astype(jnp.bfloat16), SHARD_AXIS, scatter_dimension=0, tiled=True
        ).astype(jnp.float32),
        lax.psum_scatter(
            query_gradient_rows.astype(jnp.bfloat16), SHARD_AXIS, scatter_dimension=0, tiled=True
        ).astype(jnp.float32),
        lax.psum_scatter(
            key_gradient_rows.astype(jnp.bfloat16), SHARD_AXIS, scatter_dimension=0, tiled=True
        ).astype(jnp.float32),
        lax.psum_scatter(
            value_gradient_rows.astype(jnp.bfloat16), SHARD_AXIS, scatter_dimension=0, tiled=True
        ).astype(jnp.float32),
        lax.psum_scatter(
            grad_query_gain.astype(jnp.bfloat16), SHARD_AXIS, scatter_dimension=0, tiled=True
        ).astype(jnp.float32),
        lax.psum_scatter(
            grad_key_gain.astype(jnp.bfloat16), SHARD_AXIS, scatter_dimension=0, tiled=True
        ).astype(jnp.float32),
        lax.psum_scatter(
            result_cotangent.astype(jnp.bfloat16), SHARD_AXIS, scatter_dimension=1, tiled=True
        ).astype(jnp.float32),
        lax.psum_scatter(
            grad_mlp_gain.astype(jnp.bfloat16), SHARD_AXIS, scatter_dimension=0, tiled=True
        ).astype(jnp.float32),
        lax.psum_scatter(
            grad_gate.astype(jnp.bfloat16), SHARD_AXIS, scatter_dimension=0, tiled=True
        ).astype(jnp.float32),
        lax.psum_scatter(
            grad_up.astype(jnp.bfloat16), SHARD_AXIS, scatter_dimension=0, tiled=True
        ).astype(jnp.float32),
        lax.psum_scatter(
            grad_down.astype(jnp.bfloat16), SHARD_AXIS, scatter_dimension=1, tiled=True
        ).astype(jnp.float32),
    )
    matrices = (
        lax.psum(reduced[1].astype(jnp.bfloat16), CTX_AXIS).astype(jnp.float32),
        lax.psum(reduced[2].astype(jnp.bfloat16), CTX_AXIS).astype(jnp.float32),
        lax.psum(reduced[3].astype(jnp.bfloat16), CTX_AXIS).astype(jnp.float32),
        lax.psum(reduced[6].astype(jnp.bfloat16), CTX_AXIS).astype(jnp.float32),
        lax.psum(reduced[8].astype(jnp.bfloat16), CTX_AXIS).astype(jnp.float32),
        lax.psum(reduced[9].astype(jnp.bfloat16), CTX_AXIS).astype(jnp.float32),
        lax.psum(reduced[10].astype(jnp.bfloat16), CTX_AXIS).astype(jnp.float32),
    )
    gains = lax.psum((reduced[0], reduced[4], reduced[5], reduced[7]), (CTX_AXIS, TP_AXIS))
    return (
        out_hidden,
        grad_hidden,
        gains[0],
        matrices[0],
        matrices[1],
        matrices[2],
        gains[1],
        gains[2],
        matrices[3],
        gains[3],
        matrices[4],
        matrices[5],
        matrices[6],
    )


def solution(mesh):
    in_specs = (
        P(SHARD_AXIS, (CTX_AXIS, TP_AXIS), None),
        P(SHARD_AXIS, None),
        P(SHARD_AXIS, (CTX_AXIS, TP_AXIS), None),
        P(SHARD_AXIS),
        P(SHARD_AXIS, TP_AXIS),
        P(SHARD_AXIS, TP_AXIS),
        P(SHARD_AXIS, TP_AXIS),
        P(SHARD_AXIS),
        P(SHARD_AXIS),
        P(TP_AXIS, SHARD_AXIS),
        P(SHARD_AXIS),
        P(SHARD_AXIS, TP_AXIS),
        P(SHARD_AXIS, TP_AXIS),
        P(TP_AXIS, SHARD_AXIS),
    )
    out_specs = (
        P(SHARD_AXIS, (CTX_AXIS, TP_AXIS), None),
        P(SHARD_AXIS, (CTX_AXIS, TP_AXIS), None),
        P(SHARD_AXIS),
        P(SHARD_AXIS, TP_AXIS),
        P(SHARD_AXIS, TP_AXIS),
        P(SHARD_AXIS, TP_AXIS),
        P(SHARD_AXIS),
        P(SHARD_AXIS),
        P(TP_AXIS, SHARD_AXIS),
        P(SHARD_AXIS),
        P(SHARD_AXIS, TP_AXIS),
        P(SHARD_AXIS, TP_AXIS),
        P(TP_AXIS, SHARD_AXIS),
    )
    one_block = mesh.shape[SHARD_AXIS] == 2 and mesh.shape[TP_AXIS] == 4
    return jax.shard_map(
        fast_device if one_block else per_device, mesh=mesh, in_specs=in_specs, out_specs=out_specs, check_vma=False
    )
```

```python
import math

import jax
import jax.numpy as jnp
from jax import lax
from jax.experimental import pallas as pl
from jax.experimental.pallas import tpu as pltpu
from jax.sharding import PartitionSpec as P

SHARD_AXIS, CTX_AXIS, TP_AXIS = "shard", "ctx", "tp"
HEAD_SIZE = 128
NDOC = 8


norm_eps = 1e-06
rope_base = 1000000.0
masked_fill = -1e30


def rms_scale(values):
    return lax.rsqrt(jnp.mean(values * values, axis=-1, keepdims=True) + norm_eps)


def rms_back(grad_out, values, row_scale, gain_vec):
    scaled = grad_out * gain_vec
    inner_sum = jnp.mean(scaled * values, axis=-1, keepdims=True)
    return row_scale * scaled - values * (row_scale * row_scale * row_scale) * inner_sum


def doc_positions(segments):
    seq_width = segments.shape[-1]
    labels = jnp.arange(NDOC, dtype=jnp.int32)
    onehot = (segments[..., None] == labels).astype(jnp.int32)
    counts = jnp.sum(onehot, axis=-2)
    starts = jnp.cumsum(counts, axis=-1) - counts
    first_row = jnp.sum(onehot * starts[..., None, :], axis=-1)
    return jnp.arange(seq_width, dtype=jnp.int32) - first_row


def rope_tables(positions):
    exponents = jnp.arange(0, HEAD_SIZE, 2).astype(jnp.float32) / HEAD_SIZE
    angle_rates = jnp.power(jnp.float32(rope_base), -exponents)
    angles = positions.astype(jnp.float32)[..., None] * angle_rates
    angles = jnp.concatenate([angles, angles], axis=-1)[..., None, :]
    return (jnp.cos(angles), jnp.sin(angles))


def rotate(inputs, cosine, sine_part):
    half_dim = inputs.shape[-1] // 2
    turned = jnp.concatenate([-inputs[..., half_dim:], inputs[..., :half_dim]], axis=-1)
    return inputs * cosine + turned * sine_part


def rotate_back(grads, cosine, sine_part):
    half_dim = grads.shape[-1] // 2
    moved = grads * sine_part
    turned = jnp.concatenate([moved[..., half_dim:], -moved[..., :half_dim]], axis=-1)
    return grads * cosine + turned


def tp_rows(local_part):
    return lax.all_gather(local_part, TP_AXIS, axis=1, tiled=True)


def tp_total(partial_sum):
    return lax.psum_scatter(
        partial_sum.astype(jnp.bfloat16), TP_AXIS, scatter_dimension=1, tiled=True
    ).astype(jnp.float32)


def key_block(segments, key_first, step_rows, query_pos, query_seg):
    key_pos = key_first + jnp.arange(step_rows, dtype=jnp.int32)
    key_seg = lax.dynamic_slice_in_dim(segments, key_first, step_rows, 1)
    allowed = (key_pos[None, None, :] <= query_pos[None, :, None]) & (
        key_seg[:, None, :] == query_seg[:, :, None]
    )
    return allowed[:, None, None]


def keep_state(state):
    return state


CHUNKS = 15
READY = 4
FROM_MLP = 11


MESH_ID = pl.DeviceIdType.MESH
ANY_SPEC = pl.BlockSpec(memory_space=pl.ANY)
VMEM_SPEC = pl.BlockSpec(memory_space=pltpu.VMEM)
SCORE_STEP = HEAD_SIZE ** (-0.5) * math.log2(math.e)
APART = 16384.0


def enter(peers):
    barrier = pltpu.get_barrier_semaphore()
    for peer in peers:
        pl.semaphore_signal(barrier, inc=1, device_id=peer, device_id_type=MESH_ID)
    pl.semaphore_wait(barrier, len(peers))


def last_dot(left, right):
    return lax.dot_general(
        left, right, (((1,), (1,)), ((), ())), preferred_element_type=jnp.float32
    )


def flat_dot(left, right):
    return jnp.dot(left, right, preferred_element_type=jnp.float32)


def first_dot(left, right):
    return lax.dot_general(
        left, right, (((0,), (0,)), ((), ())), preferred_element_type=jnp.float32
    )


def spin(values, cosine, sine_signed):
    return values * cosine + pltpu.roll(values, HEAD_SIZE // 2, 1) * sine_signed


class Links:
    def __init__(self, send, recv):
        self.send, self.recv, self.used = send, recv, 0

    def copy(self, src, dst, device):
        number = self.used
        self.used += 1
        return pltpu.make_async_remote_copy(
            src_ref=src, dst_ref=dst, send_sem=self.send.at[number],
            recv_sem=self.recv.at[number], device_id=device, device_id_type=MESH_ID,
        )


class Locals:
    def __init__(self, sems):
        self.sems, self.used, self.open = sems, 0, []

    def make(self, src, dst):
        copy = pltpu.make_async_copy(src, dst, self.sems.at[self.used])
        self.used += 1
        return copy

    def start(self, src, dst):
        copy = self.make(src, dst)
        copy.start()
        self.open.append(copy)
        return copy

    def wait(self, copy):
        copy.wait()
        self.open = [other for other in self.open if other is not copy]

    def finish(self):
        for copy in self.open:
            copy.wait()


def forward_kernel(
    hidden, cotangent, gains_in, places, wq, wk, wv, wo, wg, wu,
    gains_out, rows_out, q_out, k_out, query_out, keys_out, values_out, cos_out, sin_out,
    attended_out, low_out, wqkv_out, crows_out, wo_out, wg_out, wu_out,
    gains, rows, wqkv, q_proj, k_proj, qaug, kaug, vaug, cosine, sine, acc, low, crows,
    gains_land, send, recv, local,
):
    s, c, t = lax.axis_index(SHARD_AXIS), lax.axis_index(CTX_AXIS), lax.axis_index(TP_AXIS)
    nctx = lax.axis_size(CTX_AXIS)
    part = hidden.shape[0]
    block = 4 * part
    half = wq.shape[0]
    f32, bf16 = jnp.float32, jnp.bfloat16
    side, across, mate = {TP_AXIS: t ^ 1}, {TP_AXIS: t ^ 2}, {SHARD_AXIS: 1 - s}
    pair = {CTX_AXIS: c ^ 1}
    nxt, prv = {CTX_AXIS: lax.rem(c + 1, nctx)}, {CTX_AXIS: lax.rem(c + nctx - 1, nctx)}
    enter([side, across, mate, nxt, prv])
    links, locals_ = Links(send, recv), Locals(local)

    def piece(owner):
        return pl.ds(pl.multiple_of(owner * part, part), part)

    low_bit = c & 1

    def some(shard, count, size):
        return pl.ds(pl.multiple_of(shard * count + low_bit * size, size), size)

    mine = pl.ds(pl.multiple_of(s * half, half), half)
    theirs = pl.ds(pl.multiple_of((1 - s) * half, half), half)
    quarter = half // 2
    gains_copy = links.copy(gains_in, gains_land, mate)
    wk_copy = links.copy(wk, wqkv.at[mine, 512:768], mate)
    wv_copy = links.copy(wv, wqkv.at[mine, 768:1024], mate)
    wq_copy = links.copy(wq, wqkv.at[mine, 0:512], mate)
    wo_copy = links.copy(
        wo.at[some(0, 0, quarter), :], wo_out.at[some(0, 0, quarter), mine], mate
    )
    wo_got = wo_out.at[some(0, 0, quarter), theirs]
    wo_on = links.copy(wo_got, wo_got, pair)
    wg_copy = links.copy(
        wg.at[some(0, 0, quarter), :], wg_out.at[some(s, half, quarter), :], mate
    )
    wg_got = wg_out.at[some(1 - s, half, quarter), :]
    wg_on = links.copy(wg_got, wg_got, pair)
    wu_copy = links.copy(
        wu.at[some(0, 0, quarter), :], wu_out.at[some(s, half, quarter), :], mate
    )
    gains_copy.start()
    wk_copy.start()
    wv_copy.start()
    own_k = locals_.start(wk, wqkv.at[mine, 512:768])
    own_v = locals_.start(wv, wqkv.at[mine, 768:1024])
    own_q = locals_.start(wq, wqkv.at[mine, 0:512])
    locals_.start(wo, wo_out.at[:, mine])
    locals_.start(wg, wg_out.at[mine, :])
    locals_.start(wu, wu_out.at[mine, :])
    own_c = locals_.start(cotangent, crows.at[piece(t), :])

    to_across, to_side, on_to_side, to_next = [], [], [], []
    for b in range(3):
        here, there = rows.at[b, piece(t)], rows.at[b, piece(t ^ 2)]
        to_across.append(links.copy(here, here, across))
        to_side.append(links.copy(here, here, side))
        on_to_side.append(links.copy(there, there, side))
        if b < 2:
            to_next.append(links.copy(here, rows.at[b + 1, piece(t)], nxt))
    c_side = links.copy(cotangent, crows.at[piece(t), :], side)
    c_over = links.copy(cotangent, crows.at[piece(t), :], across)
    c_on = links.copy(crows.at[piece(t ^ 2), :], crows.at[piece(t ^ 2), :], side)

    x = hidden[...].astype(f32)
    scale = lax.rsqrt(jnp.mean(x * x, axis=-1, keepdims=True) + norm_eps)
    gains_copy.wait()
    gains[...] = gains_in[...] + gains_land[...]
    rows[0, piece(t), :] = (x * scale * gains[0:1, :]).astype(bf16)
    to_across[0].start()
    to_side[0].start()

    @pl.when(c < nctx - 1)
    def _():
        to_next[0].start()

    wq_copy.start()
    c_side.start()
    q_gain = gains[2:3, 0:HEAD_SIZE]
    k_gain = gains[3:4, 0:HEAD_SIZE]

    def table(b):
        start, stop, rate = places[0:1, :], places[1:2, :], places[2:3, :]
        shape = (128, HEAD_SIZE)
        lower = lax.broadcasted_iota(jnp.int32, shape, 1) < HEAD_SIZE // 2

        @pl.loop(0, 4)
        def _(n):
            found = []
            for offset in (0, 512):
                first = n * 128 + offset
                index = (lax.broadcasted_iota(jnp.int32, shape, 0) + first) + (c - b) * block
                index = index.astype(f32)
                inside = (index >= start) & (index < stop)
                marks = jnp.where(inside, 1.0, 0.0)
                begin = jnp.sum(jnp.where(inside, start, 0.0), axis=1, keepdims=True)
                at = pl.ds(pl.multiple_of(first, 128), 128)
                for g in range(2):
                    kaug[b, g, at, 128:256] = (1.0 - marks).astype(bf16)
                if b == 0:
                    for h in range(4):
                        qaug[h, at, 128:256] = (marks * -APART).astype(bf16)
                found.append((at, index - begin))
            (low_at, low_pos), (high_at, high_pos) = found
            angle = jnp.where(lower, low_pos, high_pos) * rate
            cs, sn = jnp.cos(angle), jnp.sin(angle)
            cr, sr = pltpu.roll(cs, HEAD_SIZE // 2, 1), pltpu.roll(sn, HEAD_SIZE // 2, 1)
            cosine[b, low_at, :] = jnp.where(lower, cs, cr)
            cosine[b, high_at, :] = jnp.where(lower, cr, cs)
            sine[b, low_at, :] = jnp.where(lower, -sn, sr)
            sine[b, high_at, :] = jnp.where(lower, -sr, sn)

    def project_kv(b, owner):
        at = piece(owner)
        got = flat_dot(rows[b, at, :], wqkv[:, 512:1024])
        k_proj[b, at, :] = got[:, 0:256]
        for g in range(2):
            u = got[:, g * 128 : g * 128 + 128]
            r = lax.rsqrt(jnp.mean(u * u, axis=-1, keepdims=True) + norm_eps)
            turned = spin(u * r * k_gain, cosine[b, at, :], sine[b, at, :])
            kaug[b, g, at, 0:128] = turned.astype(bf16)
            vaug[b, g, at, 0:128] = got[:, 256 + g * 128 : 384 + g * 128].astype(bf16)

    def project_q(owner):
        at = piece(owner)
        got = flat_dot(rows[0, at, :], wqkv[:, 0:512])
        q_proj[at, :] = got
        for h in range(4):
            u = got[:, h * 128 : h * 128 + 128]
            r = lax.rsqrt(jnp.mean(u * u, axis=-1, keepdims=True) + norm_eps)
            turned = spin(u * r * q_gain, cosine[0, at, :], sine[0, at, :])
            qaug[h, at, 0:128] = turned.astype(bf16)

    def unit(b, g, r, kc, bound):
        at = pl.ds(pl.multiple_of(r * 512, 512), 512)
        for hh in range(2):
            qq = qaug[2 * g + hh, at, :]
            total = None
            for j in range(2):
                keys_at = pl.ds(pl.multiple_of(kc * 512 + j * 256, 256), 256)
                p = jnp.exp2(last_dot(qq, kaug[b, g, keys_at, :]) * SCORE_STEP)
                if bound is not None:
                    ahead = lax.broadcasted_iota(jnp.int32, p.shape, 0) - lax.broadcasted_iota(
                        jnp.int32, p.shape, 1
                    )
                    p = jnp.where(ahead >= bound + j * 256, p, 0.0)
                value = flat_dot(p.astype(bf16), vaug[b, g, keys_at, :])
                total = value if total is None else total + value
            acc[2 * g + hh, at, :] += total

    def block_outs(b):
        pairs = (
            (rows, rows_out), (k_proj, k_out), (kaug, keys_out), (vaug, values_out),
            (cosine, cos_out), (sine, sin_out),
        )
        return [locals_.make(a.at[b], d.at[b]) for a, d in pairs]

    outs = [block_outs(b) for b in range(3)]

    table(0)
    vaug[:, :, :, 128:256] = jnp.ones((3, 2, block, 128), bf16)
    acc[...] = jnp.zeros(acc.shape, f32)
    locals_.wait(own_k)
    locals_.wait(own_v)
    wk_copy.wait()
    wv_copy.wait()
    to_side[0].wait_recv()

    @pl.loop(0, 2)
    def _(n):
        project_kv(0, t ^ n)

    to_across[0].wait_recv()
    on_to_side[0].start()

    @pl.when(c >= 1)
    def _():
        to_next[0].wait_recv()
        to_across[1].start()
        to_side[1].start()

        @pl.when(c < nctx - 1)
        def _():
            to_next[1].start()

    on_to_side[0].wait_recv()

    @pl.loop(2, 4)
    def _(n):
        project_kv(0, t ^ n)

    for copy in outs[0]:
        copy.start()

    @pl.when(c >= 1)
    def _():
        table(1)

    locals_.wait(own_q)
    wq_copy.wait()
    wo_copy.start()

    @pl.loop(0, 4)
    def _(n):
        project_q(n)

    locals_.start(q_proj, q_out)
    locals_.start(wqkv, wqkv_out)

    @pl.when(c >= 1)
    def _():
        to_side[1].wait_recv()
        to_across[1].wait_recv()
        on_to_side[1].start()

        @pl.when(c >= 2)
        def _():
            to_next[1].wait_recv()
            to_across[2].start()
            to_side[2].start()

    @pl.loop(0, 6)
    def _(n):
        m = lax.rem(n, 3)
        unit(0, n // 3, (m + 1) // 2, m // 2, (m & 1) * -512)

    wo_copy.wait_recv()
    wo_on.start()
    wg_copy.start()

    @pl.when(c >= 1)
    def _():
        on_to_side[1].wait_recv()

        @pl.loop(0, 4)
        def _(n):
            project_kv(1, n)

        for copy in outs[1]:
            copy.start()

        @pl.loop(0, 8)
        def _(n):
            m = lax.rem(n, 4)
            unit(1, n // 4, m // 2, m & 1, None)

    @pl.when(c >= 2)
    def _():
        table(2)

    wg_copy.wait_recv()
    wg_on.start()
    wu_copy.start()

    @pl.when(c >= 2)
    def _():
        to_side[2].wait_recv()
        to_across[2].wait_recv()
        on_to_side[2].start()

    c_over.start()

    @pl.when(c >= 2)
    def _():
        on_to_side[2].wait_recv()

        @pl.loop(0, 4)
        def _(n):
            project_kv(2, n)

        for copy in outs[2]:
            copy.start()

        @pl.loop(0, 6)
        def _(n):
            m = lax.rem(n, 3)
            unit(2, n // 3, m // 2, (m + 1) // 2, None)

    @pl.loop(0, 16)
    def _(n):
        h, r = n // 4, lax.rem(n, 4)
        at = pl.ds(pl.multiple_of(r * 256, 256), 256)
        total = acc[h, at, 128:256]
        value = acc[h, at, 0:128] / total
        acc[h, at, 0:128] = value
        shift = jnp.log(total) * -(HEAD_SIZE**0.5)
        top = shift.astype(bf16).astype(f32)
        mid = (shift - top).astype(bf16).astype(f32)
        lane = lax.broadcasted_iota(jnp.int32, shift.shape, 1)
        parts = jnp.where(lane == NDOC, top, 0.0)
        parts = jnp.where(lane == NDOC + 1, mid, parts)
        parts = jnp.where(lane == NDOC + 2, shift - top - mid, parts)
        qaug[h, at, 128:256] = qaug[h, at, 128:256] + parts.astype(bf16)
        low[h, at, :] = value.astype(bf16)

    locals_.start(gains, gains_out)
    locals_.start(qaug, query_out)
    for h in range(4):
        lanes = slice(h * 128, h * 128 + 128)
        locals_.start(low.at[h], low_out.at[:, lanes])
        locals_.start(acc.at[h, :, 0:128], attended_out.at[:, lanes])
    locals_.wait(own_c)
    c_side.wait()
    c_over.wait()
    c_on.start()
    to_across[0].wait_send()
    to_side[0].wait_send()
    on_to_side[0].wait_send()
    for copy in outs[0]:
        copy.wait()

    @pl.when(c < nctx - 1)
    def _():
        to_next[0].wait_send()

    for b in (1, 2):

        @pl.when(c >= b)
        def _():
            to_across[b].wait_send()
            to_side[b].wait_send()
            on_to_side[b].wait_send()
            for copy in outs[b]:
                copy.wait()

    @pl.when((c >= 1) & (c < nctx - 1))
    def _():
        to_next[1].wait_send()

    wo_copy.wait_send()
    wo_on.wait()
    wg_copy.wait_send()
    wg_on.wait()
    wu_copy.wait()
    c_on.wait()
    locals_.start(crows, crows_out)
    locals_.finish()


def forward_call(hidden, cotangent, gains, places, wq, wk, wv, wo, wg, wu):
    part, width = hidden.shape
    block = 4 * part
    f32, bf16 = jnp.float32, jnp.bfloat16
    shape = jax.ShapeDtypeStruct
    outs = (
        shape(gains.shape, f32),
        shape((3, block, width), bf16),
        shape((block, 512), f32),
        shape((3, block, 256), f32),
        shape((4, block, 256), bf16),
        shape((3, 2, block, 256), bf16),
        shape((3, 2, block, 256), bf16),
        shape((3, block, HEAD_SIZE), f32),
        shape((3, block, HEAD_SIZE), f32),
        shape((block, 512), f32),
        shape((block, 512), bf16),
        shape((width, 1024), bf16),
        shape((block, width), bf16),
        shape((wo.shape[0], 2 * wo.shape[1]), bf16),
        shape((2 * wg.shape[0], wg.shape[1]), bf16),
        shape((2 * wu.shape[0], wu.shape[1]), bf16),
    )
    return pl.pallas_call(
        forward_kernel,
        name="forward",
        out_shape=outs,
        in_specs=[VMEM_SPEC] * 4 + [ANY_SPEC] * 6,
        out_specs=[ANY_SPEC] * len(outs),
        scratch_shapes=[
            pltpu.VMEM(gains.shape, f32),
            pltpu.VMEM((3, block, width), bf16),
            pltpu.VMEM((width, 1024), bf16),
            pltpu.VMEM((block, 512), f32),
            pltpu.VMEM((3, block, 256), f32),
            pltpu.VMEM((4, block, 256), bf16),
            pltpu.VMEM((3, 2, block, 256), bf16),
            pltpu.VMEM((3, 2, block, 256), bf16),
            pltpu.VMEM((3, block, HEAD_SIZE), f32),
            pltpu.VMEM((3, block, HEAD_SIZE), f32),
            pltpu.VMEM((4, block, 256), f32),
            pltpu.VMEM((4, block, 128), bf16),
            pltpu.VMEM((block, width), bf16),
            pltpu.VMEM(gains.shape, f32),
            pltpu.SemaphoreType.DMA((23,)),
            pltpu.SemaphoreType.DMA((23,)),
            pltpu.SemaphoreType.DMA((38,)),
        ],
        compiler_params=pltpu.CompilerParams(
            collective_id=0, has_side_effects=True, vmem_limit_bytes=58 << 20
        ),
    )(hidden, cotangent, gains, places, wq, wk, wv, wo, wg, wu)


class Scatter:
    def __init__(self, links, bufs, side, across):
        self.bufs = bufs
        self.far = links.copy(bufs.at[0], bufs.at[3], side)
        self.over = links.copy(bufs.at[1], bufs.at[4], across)
        self.near = links.copy(bufs.at[2], bufs.at[5], side)

    def put_far(self, value):
        self.bufs[0] = value.astype(jnp.bfloat16)
        self.far.start()

    def put_over(self, value):
        self.far.wait_recv()
        self.bufs[1] = (value + self.bufs[3].astype(jnp.float32)).astype(jnp.bfloat16)
        self.over.start()

    def put_near(self, value):
        self.bufs[2] = value.astype(jnp.bfloat16)
        self.near.start()

    def total(self, value):
        self.near.wait_recv()
        self.over.wait_recv()
        return value + self.bufs[5].astype(jnp.float32) + self.bufs[4].astype(jnp.float32)

    def close(self):
        self.far.wait_send()
        self.over.wait_send()
        self.near.wait_send()


def mlp_kernel(
    low, wo, attended, hidden, crows, gains, wgf, wu, wd,
    d_middle_out, gain_out, dout_out, own_out, give_out, parts_out, out_own_out,
    wuf, wdf, mrows, act, dgate, dup, brows, dout, kept, middle, bufs, parts, give, own, land,
    result, send, recv, local,
):
    s, c, t = lax.axis_index(SHARD_AXIS), lax.axis_index(CTX_AXIS), lax.axis_index(TP_AXIS)
    part = hidden.shape[0]
    half = wd.shape[1]
    bf16, f32 = jnp.bfloat16, jnp.float32
    side, across = {TP_AXIS: t ^ 1}, {TP_AXIS: t ^ 2}
    mate, pair = {SHARD_AXIS: 1 - s}, {CTX_AXIS: c ^ 1}
    enter([side, across, mate, pair])
    links, locals_ = Links(send, recv), Locals(local)

    def piece(owner):
        return pl.ds(pl.multiple_of(owner * part, part), part)

    mine = pl.ds(pl.multiple_of(s * half, half), half)
    theirs = pl.ds(pl.multiple_of((1 - s) * half, half), half)
    low_bit = c & 1

    def some(shard, count, size):
        return pl.ds(pl.multiple_of(shard * count + low_bit * size, size), size)

    quarter = half // 2
    third = wd.shape[0] // 2
    wu_at = some(1 - s, half, quarter)
    wu_on = links.copy(wu.at[wu_at, :], wuf.at[wu_at, :], pair)
    wd_copy = links.copy(
        wd.at[some(0, 0, third), :], wdf.at[some(0, 0, third), mine], mate
    )
    wd_got = wdf.at[some(0, 0, third), theirs]
    wd_on = links.copy(wd_got, wd_got, pair)
    wu_on.start()
    wd_copy.start()
    own_weights = [
        locals_.start(wu.at[mine, :], wuf.at[mine, :]),
        locals_.start(wu.at[wu_at, :], wuf.at[wu_at, :]),
        locals_.start(wd, wdf.at[:, mine]),
    ]

    branch = Scatter(links, bufs.at[0], side, across)
    back = Scatter(links, bufs.at[1], side, across)

    def branch_part(owner):
        return flat_dot(low[piece(owner), :], wo[...])

    branch.put_far(branch_part(t ^ 3))
    branch.put_over(branch_part(t ^ 2))
    branch.put_near(branch_part(t ^ 1))
    middle[...] = hidden[...].astype(f32) + branch_part(t)
    wd_copy.wait_recv()
    wd_on.start()
    middle[...] = branch.total(middle[...])
    m = middle[...]
    scale = lax.rsqrt(jnp.mean(m * m, axis=-1, keepdims=True) + norm_eps)
    gain = gains[1:2, :]
    mrows[piece(t), :] = (m * scale * gain).astype(bf16)
    here, there = mrows.at[piece(t), :], mrows.at[piece(t ^ 2), :]
    m_over, m_near = links.copy(here, here, across), links.copy(here, here, side)
    m_on = links.copy(there, there, side)
    m_over.start()
    m_near.start()
    for copy in own_weights:
        locals_.wait(copy)
    wu_on.wait_recv()
    wd_on.wait_recv()

    def mlp(owner):
        at = piece(owner)
        rows = mrows[at, :]
        gate = flat_dot(rows, wgf[...])
        upward = flat_dot(rows, wuf[...])
        d_act = last_dot(crows[at, :], wdf[...])
        sig = 1.0 / (1.0 + jnp.exp(-gate))
        silu = gate * sig
        act[at, :] = (silu * upward).astype(bf16)
        dup[at, :] = (d_act * silu).astype(bf16)
        dgate[at, :] = (d_act * upward * sig * (1.0 + gate * (1.0 - sig))).astype(bf16)

    def out_part(owner):
        return flat_dot(act[piece(owner), :], wdf[...])

    def back_part(owner):
        at = piece(owner)
        return last_dot(dgate[at, :], wgf[...]) + last_dot(dup[at, :], wuf[...])

    mlp(t)
    kept[0] = back_part(t)
    kept[1] = out_part(t) + middle[...]
    locals_.start(kept.at[1], out_own_out)
    m_near.wait_recv()
    mlp(t ^ 1)
    back.put_near(back_part(t ^ 1))
    m_over.wait_recv()
    m_on.start()
    m_on.wait_recv()
    mlp(t ^ 3)
    back.put_far(back_part(t ^ 3))
    mlp(t ^ 2)
    back.put_over(back_part(t ^ 2))

    def down_chunk(n, columns):
        return first_dot(act[:, n * 256 : n * 256 + 256], crows[:, columns]).astype(bf16)

    def wide_chunk(ref, grads, n, columns):
        got = first_dot(mrows[:, columns], grads[:, n * 256 : n * 256 + 256]).astype(bf16)
        ref[:, 0:256] = got[0:256]
        ref[:, 256:512] = got[256:512]

    to_mate = [links.copy(give.at[k], land.at[k], mate) for k in range(READY)]
    for k in range(3):
        give[k] = down_chunk(k, theirs)
        to_mate[k].start()
    for k in range(3):
        wide_chunk(give.at[3 + k], dgate, k, theirs)
        if 3 + k < READY:
            to_mate[3 + k].start()
    for n, owner in enumerate((3, 2, 1)):
        parts[n] = out_part(t ^ owner).astype(bf16)
    locals_.start(parts, parts_out)

    d_mlp = back.total(kept[0])
    m = middle[...]
    scale = lax.rsqrt(jnp.mean(m * m, axis=-1, keepdims=True) + norm_eps)
    scaled = d_mlp * gain
    inner = jnp.mean(scaled * m, axis=-1, keepdims=True)
    d_middle = (
        crows[piece(t), :].astype(f32) + scale * scaled - m * (scale * scale * scale) * inner
    )
    kept[0] = d_middle
    gain_grad = jnp.sum(d_mlp * m * scale, axis=0, keepdims=True)
    brows[piece(t), :] = d_middle.astype(bf16)
    here, there = brows.at[piece(t), :], brows.at[piece(t ^ 2), :]
    b_over, b_near = links.copy(here, here, across), links.copy(here, here, side)
    b_on = links.copy(there, there, side)
    b_over.start()
    b_near.start()
    locals_.start(kept.at[0], d_middle_out)
    result[...] = jnp.broadcast_to(gain_grad, (8, gain_grad.shape[1]))
    locals_.start(result, gain_out)

    for k in range(3):
        own[k] = down_chunk(k, mine)
        wide_chunk(own.at[3 + k], dgate, k, mine)
        wide_chunk(give.at[6 + k], dup, k, theirs)
        wide_chunk(own.at[6 + k], dup, k, mine)

    def attended_back(owner):
        at = piece(owner)
        got = last_dot(brows[at, :], wo[...]).astype(bf16)
        for h in range(4):
            head = got[:, h * 128 : h * 128 + 128]
            delta = -jnp.sum(
                head.astype(f32) * attended[at, h * 128 : h * 128 + 128], axis=1, keepdims=True
            )
            top = delta.astype(bf16).astype(f32)
            lane = lax.broadcasted_iota(jnp.int32, (part, HEAD_SIZE), 1)
            extra = jnp.where(lane == 0, top, jnp.where(lane == 1, delta - top, 0.0))
            dout[h, at, 0:128] = head
            dout[h, at, 128:256] = extra.astype(bf16)

    attended_back(t)
    b_near.wait_recv()
    attended_back(t ^ 1)
    b_over.wait_recv()
    b_on.start()
    attended_back(t ^ 2)
    b_on.wait_recv()
    attended_back(t ^ 3)
    locals_.start(dout, dout_out)
    for n in range(2):
        at = slice(n * 256, n * 256 + 256)
        give[9 + n] = first_dot(low[:, at], brows[:, theirs]).astype(bf16)
        own[9 + n] = first_dot(low[:, at], brows[:, mine]).astype(bf16)
    locals_.start(give.at[READY:FROM_MLP], give_out)
    locals_.start(own.at[READY:FROM_MLP], own_out.at[READY:FROM_MLP])
    for k in range(READY):
        to_mate[k].wait_recv()
        own[k] = own[k] + land[k]
    locals_.start(own.at[0:READY], own_out.at[0:READY])
    for k in range(READY):
        to_mate[k].wait_send()
    wu_on.wait_send()
    wd_copy.wait_send()
    wd_on.wait_send()
    branch.close()
    back.close()
    for copy in (m_over, m_near, m_on, b_over, b_near, b_on):
        copy.wait_send()
    locals_.finish()


def mlp_call(low, wo, attended, hidden, crows, gains, wgf, wu, wd):
    part, width = hidden.shape
    block = 4 * part
    units = wgf.shape[1]
    f32, bf16 = jnp.float32, jnp.bfloat16
    shape = jax.ShapeDtypeStruct
    outs = (
        shape((part, width), f32),
        shape((8, width), f32),
        shape((4, block, 256), bf16),
        shape((FROM_MLP, 256, 512), bf16),
        shape((FROM_MLP - READY, 256, 512), bf16),
        shape((3, part, width), bf16),
        shape((part, width), f32),
    )
    return pl.pallas_call(
        mlp_kernel,
        name="mlp",
        out_shape=outs,
        in_specs=[VMEM_SPEC] * 7 + [ANY_SPEC] * 2,
        out_specs=[ANY_SPEC] * len(outs),
        scratch_shapes=[
            pltpu.VMEM((width, units), bf16),
            pltpu.VMEM((units, width), bf16),
            pltpu.VMEM((block, width), bf16),
            pltpu.VMEM((block, units), bf16),
            pltpu.VMEM((block, units), bf16),
            pltpu.VMEM((block, units), bf16),
            pltpu.VMEM((block, width), bf16),
            pltpu.VMEM((4, block, 256), bf16),
            pltpu.VMEM((2, part, width), f32),
            pltpu.VMEM((part, width), f32),
            pltpu.VMEM((2, 6, part, width), bf16),
            pltpu.VMEM((3, part, width), bf16),
            pltpu.VMEM((FROM_MLP, 256, 512), bf16),
            pltpu.VMEM((FROM_MLP, 256, 512), bf16),
            pltpu.VMEM((READY, 256, 512), bf16),
            pltpu.VMEM((8, width), f32),
            pltpu.SemaphoreType.DMA((15 + READY,)),
            pltpu.SemaphoreType.DMA((15 + READY,)),
            pltpu.SemaphoreType.DMA((11,)),
        ],
        compiler_params=pltpu.CompilerParams(
            collective_id=1, has_side_effects=True, vmem_limit_bytes=58 << 20
        ),
    )(low, wo, attended, hidden, crows, gains, wgf, wu, wd)


class Pump:
    def __init__(self, refs, sems, mate, near, opposite, outer, out, first_mate, count):
        self.own, self.mated, self.landed, self.summed = refs
        self.send, self.recv, self.local = sems
        self.mate, self.near, self.opposite, self.outer = mate, near, opposite, outer
        self.out, self.first_mate, self.count = out, first_mate, count

    def remote(self, stage, k, src, dst, device):
        return pltpu.make_async_remote_copy(
            src_ref=src, dst_ref=dst, send_sem=self.send.at[stage, k],
            recv_sem=self.recv.at[stage, k], device_id=device, device_id_type=MESH_ID,
        )

    def to_mate(self, k, src):
        return self.remote(0, k, src, self.mated.at[k - self.first_mate], self.mate)

    def inward(self, k):
        return self.remote(1, k, self.own.at[k], self.landed.at[k], self.near)

    def cross(self, k):
        return self.remote(2, k, self.landed.at[k], self.summed.at[k], self.opposite)

    def outward(self, k):
        return self.remote(3, k, self.summed.at[k], self.landed.at[k], self.near)

    def write(self, k, ref):
        return pltpu.make_async_copy(ref.at[k], self.out.at[k], self.local.at[k])

    def bring(self, k):
        self.to_mate(k, self.own.at[k]).wait_recv()
        self.own[k] = self.own[k] + self.mated[k - self.first_mate]

    def slot(self, k):
        def run(condition, body):
            if isinstance(condition, bool):
                if condition:
                    body()
            else:
                pl.when(condition)(body)

        def begin():
            run(k >= self.first_mate, lambda: self.bring(k))
            pl.when(self.outer)(lambda: self.inward(k).start())

        def second():
            @pl.when(jnp.logical_not(self.outer))
            def _():
                self.inward(k - 1).wait_recv()
                self.landed[k - 1] = self.own[k - 1] + self.landed[k - 1]
                self.cross(k - 1).start()

        def third():
            @pl.when(jnp.logical_not(self.outer))
            def _():
                self.cross(k - 2).wait_recv()
                self.summed[k - 2] = self.landed[k - 2] + self.summed[k - 2]
                self.outward(k - 2).start()
                self.write(k - 2, self.summed).start()

        def fourth():
            @pl.when(self.outer)
            def _():
                self.outward(k - 3).wait_recv()
                self.write(k - 3, self.landed).start()

        run(k < self.count, begin)
        run((k >= 1) & (k < self.count + 1), second)
        run((k >= 2) & (k < self.count + 2), third)
        run((k >= 3) & (k < self.count + 3), fourth)

    def close(self):
        @pl.loop(0, self.count)
        def _(k):
            @pl.when(self.outer)
            def _():
                self.inward(k).wait_send()

            @pl.when(jnp.logical_not(self.outer))
            def _():
                self.cross(k).wait_send()
                self.outward(k).wait_send()

            self.write(k, self.summed).wait()


def backward_kernel(
    query, dout, q_proj, wqkv, hidden, gains, mlp_gain_grad, d_middle,
    own_in, give, parts, out_own, keys, values, k_proj, cosine, sine, rows,
    hidden_out, hidden_grad, gains_out, sums_out,
    kbuf, vbuf, kpbuf, cosbuf, sinbuf, rowbuf, dq, dk, dv, dkv, dqp, gkv, kept, bufs,
    own, mated, landed, summed, late_give, far_land, mid_land, out_buf,
    gsum, gland, send, recv, pump_send, pump_recv, pump_local, local, blocksem,
):
    s, c, t = lax.axis_index(SHARD_AXIS), lax.axis_index(CTX_AXIS), lax.axis_index(TP_AXIS)
    nctx = lax.axis_size(CTX_AXIS)
    part = hidden.shape[0]
    half = rows.shape[2] // 2
    f32, bf16 = jnp.float32, jnp.bfloat16
    side, across, mate = {TP_AXIS: t ^ 1}, {TP_AXIS: t ^ 2}, {SHARD_AXIS: 1 - s}
    near, opposite = {CTX_AXIS: c ^ 1}, {CTX_AXIS: c ^ 3}
    previous = {CTX_AXIS: lax.rem(c + nctx - 1, nctx)}
    outer = (c == 0) | (c == nctx - 1)
    links, locals_ = Links(send, recv), Locals(local)
    scale = HEAD_SIZE ** (-0.5)
    pump = Pump(
        (own, mated, landed, summed), (pump_send, pump_recv, pump_local),
        mate, near, opposite, outer, sums_out, READY, CHUNKS,
    )

    def piece(owner):
        return pl.ds(pl.multiple_of(owner * part, part), part)

    def half_at(ref_shard, n, size):
        return pl.ds(pl.multiple_of(ref_shard * half + n * size, size), size)

    def block_copies(b):
        slot = b & 1
        pairs = (
            (keys.at[b], kbuf.at[slot]), (values.at[b], vbuf.at[slot]),
            (k_proj.at[b], kpbuf.at[slot]), (cosine.at[b], cosbuf.at[slot]),
            (sine.at[b], sinbuf.at[slot]),
        )
        return [
            pltpu.make_async_copy(a, d, blocksem.at[6 * b + n]) for n, (a, d) in enumerate(pairs)
        ]

    def row_copy(b):
        return pltpu.make_async_copy(rows.at[b], rowbuf, blocksem.at[6 * b + 5])

    def fetch(b):
        for copy in block_copies(b):
            copy.start()

    def fetched(b):
        for copy in block_copies(b):
            copy.wait()

    first_loads = [
        locals_.start(own_in, own.at[0:FROM_MLP]),
        locals_.start(parts.at[1], out_buf.at[0]),
        locals_.start(out_own, kept.at[1]),
    ]

    @pl.when(c >= 2)
    def _():
        fetch(2)
        row_copy(2).start()

    @pl.when(c >= 1)
    def _():
        fetch(1)

    @pl.when(c == 1)
    def _():
        row_copy(1).start()

    @pl.when(c <= 1)
    def _():
        fetch(0)

    @pl.when(c == 0)
    def _():
        row_copy(0).start()

    enter([side, across, mate, near, opposite])

    @pl.loop(READY, FROM_MLP)
    def _(k):
        pump.to_mate(k, give.at[k - READY]).start()

    out_far = links.copy(parts.at[0], out_buf.at[1], side)
    out_over = links.copy(out_buf.at[0], out_buf.at[2], across)
    out_near = links.copy(parts.at[2], out_buf.at[3], side)
    out_far.start()
    out_near.start()
    scatters = [
        Scatter(links, bufs.at[0], side, across),
        Scatter(links, bufs.at[1], side, across),
        Scatter(links, bufs.at[0], side, across),
    ]
    far_copy = links.copy(out_buf.at[0], far_land, previous)
    mid_copy = links.copy(out_buf.at[1], mid_land, previous)
    for copy in first_loads:
        locals_.wait(copy)
    pump.slot(0)
    dq[...] = jnp.zeros(dq.shape, f32)
    gkv[...] = jnp.zeros(gkv.shape, f32)
    gsum[...] = jnp.zeros(gsum.shape, f32)
    gsum[1:2, :] = mlp_gain_grad[0:1, :]
    q_gain = gains[2:3, 0:HEAD_SIZE]
    k_gain = gains[3:4, 0:HEAD_SIZE]
    out_far.wait_recv()
    out_buf[0] = out_buf[0] + out_buf[1]
    out_over.start()

    def tile(b, g, r, kc, bound):
        slot = b & 1
        q_at = pl.ds(pl.multiple_of(r * 512, 512), 512)
        k_at = pl.ds(pl.multiple_of(kc * 512, 512), 512)
        kk, vv = kbuf[slot, g, k_at, :], vbuf[slot, g, k_at, :]
        dv_new, dk_new = [], []
        for hh in range(2):
            h = 2 * g + hh
            qq, do = query[h, q_at, :], dout[h, q_at, :]
            p = jnp.exp2(last_dot(qq, kk) * SCORE_STEP)
            if bound is not None:
                ahead = lax.broadcasted_iota(jnp.int32, p.shape, 0) - lax.broadcasted_iota(
                    jnp.int32, p.shape, 1
                )
                p = jnp.where(ahead >= bound, p, 0.0)
            ds = (p * last_dot(do, vv)).astype(bf16)
            dv_new.append(first_dot(do[:, 0:HEAD_SIZE], p.astype(bf16)))
            dk_new.append(first_dot(qq[:, 0:HEAD_SIZE], ds))
            dq[h, q_at, :] += flat_dot(ds, kk[:, 0:HEAD_SIZE])
        dv[g, :, k_at] += dv_new[0] + dv_new[1]
        dk[g, :, k_at] += dk_new[0] + dk_new[1]

    def clear():
        dk[...] = jnp.zeros(dk.shape, f32)
        dv[...] = jnp.zeros(dv.shape, f32)

    def norm_back(grad, u, gain, cos, sin, row):
        turned = grad * cos - pltpu.roll(grad, HEAD_SIZE // 2, 1) * sin
        r = lax.rsqrt(jnp.mean(u * u, axis=-1, keepdims=True) + norm_eps)
        gsum[row : row + 1, 0:HEAD_SIZE] += jnp.sum(turned * u * r, axis=0, keepdims=True)
        scaled = turned * gain
        inner = jnp.mean(scaled * u, axis=-1, keepdims=True)
        return (r * scaled - u * (r * r * r) * inner).astype(bf16)

    def finish_kv(b):
        slot = b & 1

        @pl.loop(0, 4)
        def _(n):
            at = piece(n)
            cos, sin = cosbuf[slot, at, :], sinbuf[slot, at, :]
            for g in range(2):
                lanes = slice(g * 128, g * 128 + 128)
                u = kpbuf[slot, at, lanes]
                dkv[at, lanes] = norm_back(dk[g, :, at].T * scale, u, k_gain, cos, sin, 3)
                dkv[at, 256 + g * 128 : 384 + g * 128] = dv[g, :, at].T.astype(bf16)

        row_copy(b).wait()

        @pl.loop(0, 4)
        def _(n):
            at = piece(n)
            gkv[at, :] += first_dot(rowbuf[:, at], dkv[...])

    def kv_part(owner):
        return last_dot(dkv[piece(owner), :], wqkv[:, 512:1024])

    def all_part(owner):
        return kv_part(owner) + last_dot(dqp[piece(owner), :], wqkv[:, 0:512])

    def scatter(which, slot, partial):
        which.put_far(partial(t ^ 3))
        which.put_over(partial(t ^ 2))
        which.put_near(partial(t ^ 1))
        kept[slot] = partial(t)

    @pl.when(c >= 2)
    def _():
        fetched(2)
        clear()

    @pl.loop(0, 6)
    def _(n):
        m = lax.rem(n, 3)

        @pl.when(c >= 2)
        def _():
            tile(2, n // 3, m // 2, (m + 1) // 2, None)

        @pl.when(m == 2)
        def _():
            pump.slot(1 + n // 3)

    @pl.when(c >= 2)
    def _():
        finish_kv(2)
        fetch(0)
        row_copy(1).start()
        scatter(scatters[2], 0, kv_part)

    out_near.wait_recv()
    out_over.wait_recv()
    out_buf[3] = (kept[1] + out_buf[2].astype(f32) + out_buf[3].astype(f32)).astype(bf16)
    locals_.start(out_buf.at[3], hidden_out)
    out_far.wait_send()
    out_over.wait_send()
    out_near.wait_send()
    pump.slot(3)

    @pl.when(c >= 1)
    def _():
        fetched(1)
        clear()

    @pl.loop(0, 8)
    def _(n):
        m = lax.rem(n, 4)

        @pl.when(c >= 1)
        def _():
            tile(1, n // 4, m // 2, m & 1, None)

        @pl.when(m == 3)
        def _():
            pump.slot(4 + n // 4)

    @pl.when(c >= 1)
    def _():
        finish_kv(1)
        row_copy(0).start()

    @pl.when(c >= 2)
    def _():
        out_buf[0] = scatters[2].total(kept[0]).astype(bf16)
        far_copy.start()
        scatters[2].close()

    @pl.when(c >= 1)
    def _():
        scatter(scatters[1], 1, kv_part)

    pump.slot(6)
    fetched(0)
    clear()

    @pl.loop(0, 6)
    def _(n):
        m = lax.rem(n, 3)
        tile(0, n // 3, (m + 1) // 2, m // 2, (m & 1) * -512)

        @pl.when(m == 2)
        def _():
            pump.slot(7 + n // 3)

    finish_kv(0)

    @pl.loop(0, 4)
    def _(n):
        at = piece(n)
        cos, sin = cosbuf[0, at, :], sinbuf[0, at, :]
        for h in range(4):
            lanes = slice(h * 128, h * 128 + 128)
            u = q_proj[at, lanes]
            dqp[at, lanes] = norm_back(dq[h, at, :] * scale, u, q_gain, cos, sin, 2)

    for n in range(2):
        late_give[n] = gkv[half_at(1 - s, n, 256), :].astype(bf16)
        pump.to_mate(FROM_MLP + n, late_give.at[n]).start()
    for n in range(2):
        late_give[2 + n] = first_dot(rowbuf[:, half_at(1 - s, n, 256)], dqp[...]).astype(bf16)
        pump.to_mate(FROM_MLP + 2 + n, late_give.at[2 + n]).start()
    pump.slot(9)

    @pl.when((c >= 1) & (c < nctx - 1))
    def _():
        far_copy.wait_recv()
        kept[1] += far_land[...].astype(f32)

    @pl.when(c >= 1)
    def _():
        out_buf[1] = scatters[1].total(kept[1]).astype(bf16)
        mid_copy.start()
        scatters[1].close()

    base = locals_.start(d_middle, kept.at[1])
    scatter(scatters[0], 0, all_part)
    pump.slot(10)
    for n in range(2):
        own[FROM_MLP + n] = gkv[half_at(s, n, 256), :].astype(bf16)
        own[FROM_MLP + 2 + n] = first_dot(rowbuf[:, half_at(s, n, 256)], dqp[...]).astype(bf16)

    @pl.loop(11, 13)
    def _(k):
        pump.slot(k)

    @pl.when(c < nctx - 1)
    def _():
        mid_copy.wait_recv()
        kept[0] += mid_land[...].astype(f32)

    kept[0] = scatters[0].total(kept[0])
    x = hidden[...].astype(f32)
    r = lax.rsqrt(jnp.mean(x * x, axis=-1, keepdims=True) + norm_eps)
    d_in = kept[0]
    gsum[0:1, :] = jnp.sum(d_in * x * r, axis=0, keepdims=True)
    scaled = d_in * gains[0:1, :]
    inner = jnp.mean(scaled * x, axis=-1, keepdims=True)
    locals_.wait(base)
    kept[1] += r * scaled - x * (r * r * r) * inner
    locals_.start(kept.at[1], hidden_grad)
    scatters[0].close()
    for n, device in enumerate((side, across, mate, near, opposite)):
        copy = links.copy(gsum, gland.at[n], device)
        copy.start()
        pump.slot(13 + n)
        copy.wait()
        gsum[...] += gland[n]
    locals_.start(gsum, gains_out)

    @pl.when(c >= 2)
    def _():
        far_copy.wait_send()

    @pl.when(c >= 1)
    def _():
        mid_copy.wait_send()

    @pl.loop(READY, FROM_MLP)
    def _(k):
        pump.to_mate(k, give.at[k - READY]).wait_send()

    for n in range(4):
        pump.to_mate(FROM_MLP + n, late_give.at[n]).wait_send()
    pump.close()
    locals_.finish()


def backward_call(vmem_args, any_args):
    hidden = vmem_args[4]
    part, width = hidden.shape
    block = 4 * part
    f32, bf16 = jnp.float32, jnp.bfloat16
    shape = jax.ShapeDtypeStruct
    outs = (
        shape((part, width), bf16),
        shape((part, width), f32),
        shape((8, width), f32),
        shape((CHUNKS, 256, 512), bf16),
    )
    tile = pltpu.VMEM((part, width), bf16)
    chunks = pltpu.VMEM((CHUNKS, 256, 512), bf16)
    return pl.pallas_call(
        backward_kernel,
        name="backward",
        out_shape=outs,
        in_specs=[VMEM_SPEC] * len(vmem_args) + [ANY_SPEC] * len(any_args),
        out_specs=[ANY_SPEC] * len(outs),
        scratch_shapes=[
            pltpu.VMEM((2, 2, block, 256), bf16),
            pltpu.VMEM((2, 2, block, 256), bf16),
            pltpu.VMEM((2, block, 256), f32),
            pltpu.VMEM((2, block, HEAD_SIZE), f32),
            pltpu.VMEM((2, block, HEAD_SIZE), f32),
            pltpu.VMEM((block, width), bf16),
            pltpu.VMEM((4, block, HEAD_SIZE), f32),
            pltpu.VMEM((2, HEAD_SIZE, block), f32),
            pltpu.VMEM((2, HEAD_SIZE, block), f32),
            pltpu.VMEM((block, 512), bf16),
            pltpu.VMEM((block, 512), bf16),
            pltpu.VMEM((width, 512), f32),
            pltpu.VMEM((2, part, width), f32),
            pltpu.VMEM((2, 6, part, width), bf16),
            chunks,
            pltpu.VMEM((CHUNKS - READY, 256, 512), bf16),
            chunks,
            chunks,
            pltpu.VMEM((4, 256, 512), bf16),
            tile, tile,
            pltpu.VMEM((4, part, width), bf16),
            pltpu.VMEM((8, width), f32),
            pltpu.VMEM((5, 8, width), f32),
            pltpu.SemaphoreType.DMA((19,)),
            pltpu.SemaphoreType.DMA((19,)),
            pltpu.SemaphoreType.DMA((4, CHUNKS)),
            pltpu.SemaphoreType.DMA((4, CHUNKS)),
            pltpu.SemaphoreType.DMA((CHUNKS,)),
            pltpu.SemaphoreType.DMA((7,)),
            pltpu.SemaphoreType.DMA((18,)),
        ],
        compiler_params=pltpu.CompilerParams(
            collective_id=2, has_side_effects=True, vmem_limit_bytes=60 << 20
        ),
    )(*vmem_args, *any_args)


def result_kernel(
    chunks_in, gains, grad_in, hidden_in,
    grad_out, hidden_out, attn, wq, wk, wv, q_gain, k_gain, wo, mlp, wg, wu, wd,
    buf, q, k, v, o, gate, up, down, inside, outside,
):
    shard = lax.axis_index(SHARD_AXIS)
    count = buf.shape[0]
    whole = [
        pltpu.make_async_copy(grad_in, grad_out, outside.at[count]),
        pltpu.make_async_copy(hidden_in, hidden_out, outside.at[count + 1]),
    ]
    loads = [pltpu.make_async_copy(chunks_in.at[n], buf.at[n], inside.at[n]) for n in range(count)]
    for copy in loads + whole:
        copy.start()
    stores = []

    def put(n, ref, out, row, lanes):
        at = (slice(row, row + 256), lanes)
        stores.append(pltpu.make_async_copy(ref.at[at], out.at[at], outside.at[len(stores)]))
        stores[-1].start()

    for n in range(count):
        loads[n].wait()
        values = buf[n].astype(jnp.float32)
        every = slice(0, 512)
        if n < 3:
            down[n * 256 : n * 256 + 256, :] = values
            put(n, down, wd, n * 256, every)
        elif n < 9:
            ref, out, j = (gate, wg, n - 3) if n < 6 else (up, wu, n - 6)
            lanes = slice(j * 256, j * 256 + 256)
            ref[0:256, lanes] = values[:, 0:256]
            ref[256:512, lanes] = values[:, 256:512]
            at = (slice(0, 512), lanes)
            stores.append(pltpu.make_async_copy(ref.at[at], out.at[at], outside.at[len(stores)]))
            stores[-1].start()
        elif n < 11:
            o[(n - 9) * 256 : (n - 8) * 256, :] = values
            put(n, o, wo, (n - 9) * 256, every)
        elif n < 13:
            row = (n - 11) * 256
            k[row : row + 256, :] = values[:, 0:256]
            v[row : row + 256, :] = values[:, 256:512]
        else:
            q[(n - 13) * 256 : (n - 12) * 256, :] = values
            put(n, q, wq, (n - 13) * 256, every)
    for ref, out in ((k, wk), (v, wv)):
        stores.append(pltpu.make_async_copy(ref, out, outside.at[len(stores)]))
        stores[-1].start()
    wide, small = attn.shape[1], q_gain.shape[1]
    first = shard == 0
    attn[...] = jnp.where(first, gains[0:1, 0:wide], gains[0:1, wide : 2 * wide])
    mlp[...] = jnp.where(first, gains[1:2, 0:wide], gains[1:2, wide : 2 * wide])
    q_gain[...] = jnp.where(first, gains[2:3, 0:small], gains[2:3, small : 2 * small])
    k_gain[...] = jnp.where(first, gains[3:4, 0:small], gains[3:4, small : 2 * small])
    for copy in stores + whole:
        copy.wait()


def result_call(chunks, gains, grad_hidden, out_hidden):
    part, width = grad_hidden.shape
    f32 = jnp.float32
    shape = jax.ShapeDtypeStruct
    half = width // 2
    q, k, v, o = (half, 512), (half, 256), (half, 256), (512, half)
    gate, up, down = (half, 768), (half, 768), (768, half)
    sizes = [q, k, v, (1, 64), (1, 64), o, (1, half), gate, up, down]
    outs = [shape((part, width), f32), shape((part, width), out_hidden.dtype), shape((1, half), f32)]
    outs += [shape(z, f32) for z in sizes]
    specs = [ANY_SPEC] * 2 + [VMEM_SPEC] + [ANY_SPEC] * 3 + [VMEM_SPEC] * 2 + [ANY_SPEC, VMEM_SPEC]
    return pl.pallas_call(
        result_kernel,
        name="result",
        out_shape=outs,
        in_specs=[ANY_SPEC, VMEM_SPEC, ANY_SPEC, ANY_SPEC],
        out_specs=specs + [ANY_SPEC] * 3,
        scratch_shapes=[pltpu.VMEM((CHUNKS, 256, 512), jnp.bfloat16)]
        + [pltpu.VMEM(z, f32) for z in (q, k, v, o, gate, up, down)]
        + [pltpu.SemaphoreType.DMA((CHUNKS,)), pltpu.SemaphoreType.DMA((CHUNKS + 2,))],
        compiler_params=pltpu.CompilerParams(vmem_limit_bytes=40 << 20),
    )(chunks, gains, grad_hidden, out_hidden)


def place_rows(segments):
    label = jnp.arange(HEAD_SIZE, dtype=jnp.int32)
    begin = jnp.sum((segments[:, None] < label).astype(jnp.float32), axis=0)
    end = jnp.sum((segments[:, None] <= label).astype(jnp.float32), axis=0)
    exponents = 2 * lax.rem(label, HEAD_SIZE // 2)
    rates = jnp.power(jnp.float32(rope_base), -exponents.astype(jnp.float32) / HEAD_SIZE)
    return jnp.stack([begin, end, rates] + [jnp.zeros_like(begin)] * 5)


def pack_gains(attn_gain, mlp_gain, query_gain, key_gain):
    shard = lax.axis_index(SHARD_AXIS)

    def row(gain, width):
        spread = jnp.tile(gain.astype(jnp.float32), width // gain.shape[0])
        own = jnp.arange(width) // gain.shape[0] == shard
        return jnp.where(own, spread, 0.0)

    width = attn_gain.shape[0] * lax.axis_size(SHARD_AXIS)
    small = [
        jnp.pad(row(gain, HEAD_SIZE), (0, width - HEAD_SIZE)) for gain in (query_gain, key_gain)
    ]
    rows = [row(attn_gain, width), row(mlp_gain, width)] + small
    return jnp.stack(rows + [jnp.zeros((width,), jnp.float32)] * 4)


def fast_device(
    hidden,
    segments,
    cotangent,
    attn_gain,
    w_query,
    key_weight_matrix,
    value_weight_matrix,
    query_gain,
    key_gain,
    mixer_exit_coefficients,
    mlp_gain,
    w_gate,
    w_up,
    w_down,
):
    places = place_rows(segments[0])
    gains_in = pack_gains(attn_gain, mlp_gain, query_gain, key_gain)
    (gains, rows, q_proj, k_proj, query, keys, values, cosine, sine, attended, low, wqkv, crows,
     wo, wg, wu) = forward_call(
        hidden[0], cotangent[0], gains_in, places, w_query, key_weight_matrix,
        value_weight_matrix, mixer_exit_coefficients, w_gate, w_up,
    )
    d_middle, mlp_gain_grad, dout, own, give, parts, out_own = mlp_call(
        low, wo, attended, hidden[0], crows, gains, wg, wu, w_down
    )
    out_hidden, grad_hidden, sums, chunks = backward_call(
        (query, dout, q_proj, wqkv, hidden[0], gains, mlp_gain_grad),
        (d_middle, own, give, parts, out_own, keys, values, k_proj, cosine, sine, rows),
    )
    (grad_hidden, out_hidden, attn, wq, wk, wv, q_gain, k_gain, wo, mlp, wg, wu, wd) = result_call(
        chunks, sums, grad_hidden, out_hidden
    )
    return (
        out_hidden[None], grad_hidden[None], attn[0], wq, wk, wv, q_gain[0], k_gain[0], wo, mlp[0],
        wg, wu, wd,
    )


def per_device(
    hidden,
    segments,
    cotangent,
    attn_gain,
    w_query,
    key_weight_matrix,
    value_weight_matrix,
    query_gain,
    key_gain,
    mixer_exit_coefficients,
    mlp_gain,
    w_gate,
    w_up,
    w_down,
):
    collected_rows = (
        lax.all_gather(attn_gain, SHARD_AXIS, axis=0, tiled=True),
        lax.all_gather(w_query, SHARD_AXIS, axis=0, tiled=True),
        lax.all_gather(key_weight_matrix, SHARD_AXIS, axis=0, tiled=True),
        lax.all_gather(value_weight_matrix, SHARD_AXIS, axis=0, tiled=True),
        lax.all_gather(query_gain, SHARD_AXIS, axis=0, tiled=True),
        lax.all_gather(key_gain, SHARD_AXIS, axis=0, tiled=True),
        lax.all_gather(mixer_exit_coefficients, SHARD_AXIS, axis=1, tiled=True),
        lax.all_gather(mlp_gain, SHARD_AXIS, axis=0, tiled=True),
        lax.all_gather(w_gate, SHARD_AXIS, axis=0, tiled=True),
        lax.all_gather(w_up, SHARD_AXIS, axis=0, tiled=True),
        lax.all_gather(w_down, SHARD_AXIS, axis=1, tiled=True),
    )
    gain_attn = collected_rows[0].astype(jnp.float32)
    gain_query = collected_rows[4].astype(jnp.float32)
    gain_key = collected_rows[5].astype(jnp.float32)
    gain_mlp = collected_rows[7].astype(jnp.float32)
    seq_count = hidden.shape[0]
    block_rows = hidden.shape[1] * lax.axis_size(TP_AXIS)
    seq_length = segments.shape[1]
    ctx_index = lax.axis_index(CTX_AXIS)
    heads_local = w_query.shape[1] // HEAD_SIZE
    kv_local = key_weight_matrix.shape[1] // HEAD_SIZE
    query_group_width = heads_local // kv_local
    score_scale = HEAD_SIZE ** (-0.5)
    block_start = ctx_index * block_rows
    query_pos = block_start + jnp.arange(block_rows, dtype=jnp.int32)
    query_seg = lax.dynamic_slice_in_dim(segments, block_start, block_rows, 1)
    positions = lax.dynamic_slice_in_dim(doc_positions(segments), block_start, block_rows, 1)
    cosine, sine_part = rope_tables(positions)

    def counting_keys(key_first, step_rows):
        early = key_first <= block_start + block_rows - 1
        last_seg = lax.dynamic_slice_in_dim(segments, key_first + step_rows - 1, 1, 1)[:, 0]
        return early & jnp.any(last_seg >= query_seg[:, 0])

    inputs = hidden.astype(jnp.float32)
    scale_one = rms_scale(inputs)
    attention_input = (inputs * scale_one * gain_attn).astype(jnp.bfloat16)
    attention_rows = tp_rows(attention_input)
    q_proj = jnp.einsum(
        "zjr,rm->zjm", attention_rows, collected_rows[1], preferred_element_type=jnp.float32
    ).reshape(seq_count, block_rows, heads_local, HEAD_SIZE)
    key_projected = jnp.einsum(
        "zjr,rm->zjm", attention_rows, collected_rows[2], preferred_element_type=jnp.float32
    ).reshape(seq_count, block_rows, kv_local, HEAD_SIZE)
    value_projected = jnp.einsum(
        "zjr,rm->zjm", attention_rows, collected_rows[3], preferred_element_type=jnp.float32
    )
    q_scale = rms_scale(q_proj)
    k_scale = rms_scale(key_projected)
    query_rows_input = (
        rotate(q_proj * q_scale * gain_query, cosine, sine_part)
        .astype(jnp.bfloat16)
        .reshape(seq_count, block_rows, kv_local, query_group_width, HEAD_SIZE)
    )
    keys = rotate(key_projected * k_scale * gain_key, cosine, sine_part).astype(jnp.bfloat16)
    values = value_projected.astype(jnp.bfloat16).reshape(
        seq_count, block_rows, kv_local, HEAD_SIZE
    )
    stat_shape = (seq_count, kv_local, query_group_width, block_rows)
    start_state = (
        jnp.full(stat_shape, masked_fill, jnp.float32),
        jnp.zeros(stat_shape, jnp.float32),
        jnp.zeros(stat_shape + (HEAD_SIZE,), jnp.float32),
    )
    piece_keys = lax.all_gather(keys, CTX_AXIS, axis=1, tiled=True)
    piece_values = lax.all_gather(values, CTX_AXIS, axis=1, tiled=True)
    piece_rows = piece_keys.shape[1]
    step_rows = math.gcd(piece_rows, 1024)

    def attend_one_step(number, loop_state):
        offset = number * step_rows
        key_first = offset

        def attend_compute(state):
            row_max, row_total, summed = state
            key_part = lax.dynamic_slice_in_dim(piece_keys, offset, step_rows, 1)
            value_part = lax.dynamic_slice_in_dim(piece_values, offset, step_rows, 1)
            allowed = key_block(segments, key_first, step_rows, query_pos, query_seg)
            scores = (
                jnp.einsum(
                    "sqhgd,skhd->shgqk",
                    query_rows_input,
                    key_part,
                    preferred_element_type=jnp.float32,
                )
                * score_scale
            )
            masked = jnp.where(allowed, scores, masked_fill)
            new_max = jnp.maximum(row_max, jnp.max(masked, axis=-1))
            weights = jnp.where(allowed, jnp.exp(masked - new_max[..., None]), 0.0)
            decay_factor = jnp.exp(row_max - new_max)
            row_total = row_total * decay_factor + jnp.sum(weights, axis=-1)
            summed = summed * decay_factor[..., None] + jnp.einsum(
                "shgqk,skhd->shgqd",
                weights.astype(jnp.bfloat16),
                value_part,
                preferred_element_type=jnp.float32,
            )
            return (new_max, row_total, summed)

        return lax.cond(counting_keys(key_first, step_rows), attend_compute, keep_state, loop_state)

    row_max, row_total, summed = lax.fori_loop(
        0, piece_rows // step_rows, attend_one_step, start_state
    )
    attended = summed / row_total[..., None]
    log_total = row_max + jnp.log(row_total)
    attended_reduced_copy = (
        attended.transpose(0, 3, 1, 2, 4)
        .reshape(seq_count, block_rows, heads_local * HEAD_SIZE)
        .astype(jnp.bfloat16)
    )
    branch = tp_total(
        jnp.einsum(
            "vkq,qy->vky",
            attended_reduced_copy,
            collected_rows[6],
            preferred_element_type=jnp.float32,
        )
    )
    middle = inputs + branch
    scale_two = rms_scale(middle)
    mlp_in = (middle * scale_two * gain_mlp).astype(jnp.bfloat16)
    mlp_rows = tp_rows(mlp_in)
    gate = jnp.einsum(
        "snd,df->snf", mlp_rows, collected_rows[8], preferred_element_type=jnp.float32
    )
    upward = jnp.einsum(
        "snd,df->snf", mlp_rows, collected_rows[9], preferred_element_type=jnp.float32
    )
    activated = (jax.nn.silu(gate) * upward).astype(jnp.bfloat16)
    out_hidden = (
        middle
        + tp_total(
            jnp.einsum(
                "snf,fd->snd", activated, collected_rows[10], preferred_element_type=jnp.float32
            )
        )
    ).astype(jnp.bfloat16)
    again = (
        lax.all_gather(attn_gain, SHARD_AXIS, axis=0, tiled=True),
        lax.all_gather(w_query, SHARD_AXIS, axis=0, tiled=True),
        lax.all_gather(key_weight_matrix, SHARD_AXIS, axis=0, tiled=True),
        lax.all_gather(value_weight_matrix, SHARD_AXIS, axis=0, tiled=True),
        lax.all_gather(query_gain, SHARD_AXIS, axis=0, tiled=True),
        lax.all_gather(key_gain, SHARD_AXIS, axis=0, tiled=True),
        lax.all_gather(mixer_exit_coefficients, SHARD_AXIS, axis=1, tiled=True),
        lax.all_gather(mlp_gain, SHARD_AXIS, axis=0, tiled=True),
        lax.all_gather(w_gate, SHARD_AXIS, axis=0, tiled=True),
        lax.all_gather(w_up, SHARD_AXIS, axis=0, tiled=True),
        lax.all_gather(w_down, SHARD_AXIS, axis=1, tiled=True),
    )
    query_backward = again[1]
    lookup_pullback = again[2]
    value_backward = again[3]
    output_backward = again[6]
    back_gate = again[8]
    back_up = again[9]
    back_down = again[10]
    d_out = cotangent.astype(jnp.float32)
    d_rows = tp_rows(cotangent)
    grad_down = jnp.einsum("snf,snd->fd", activated, d_rows, preferred_element_type=jnp.float32)
    d_act = jnp.einsum("snd,fd->snf", d_rows, back_down, preferred_element_type=jnp.float32)
    sigmoid_gate = jax.nn.sigmoid(gate)
    d_upward = (d_act * jax.nn.silu(gate)).astype(jnp.bfloat16)
    d_gate = (d_act * upward * sigmoid_gate * (1.0 + gate * (1.0 - sigmoid_gate))).astype(
        jnp.bfloat16
    )
    grad_gate = jnp.einsum("snd,snf->df", mlp_rows, d_gate, preferred_element_type=jnp.float32)
    grad_up = jnp.einsum("snd,snf->df", mlp_rows, d_upward, preferred_element_type=jnp.float32)
    d_mlp_in = tp_total(
        jnp.einsum("snf,df->snd", d_gate, back_gate, preferred_element_type=jnp.float32)
        + jnp.einsum("snf,df->snd", d_upward, back_up, preferred_element_type=jnp.float32)
    )
    grad_mlp_gain = jnp.sum(d_mlp_in * middle * scale_two, axis=(0, 1))
    d_middle = d_out + rms_back(d_mlp_in, middle, scale_two, gain_mlp)
    d_branch = d_middle.astype(jnp.bfloat16)
    residual_branch_rows = tp_rows(d_branch)
    result_cotangent = jnp.einsum(
        "xbj,xbk->jk",
        attended_reduced_copy,
        residual_branch_rows,
        preferred_element_type=jnp.float32,
    )
    d_attended = (
        jnp.einsum(
            "miv,cv->mic", residual_branch_rows, output_backward, preferred_element_type=jnp.float32
        )
        .astype(jnp.bfloat16)
        .reshape(seq_count, block_rows, kv_local, query_group_width, HEAD_SIZE)
    )
    delta = jnp.sum(d_attended.astype(jnp.float32).transpose(0, 2, 3, 1, 4) * attended, axis=-1)
    query_zeros = jnp.zeros(
        (seq_count, block_rows, kv_local, query_group_width, HEAD_SIZE), jnp.float32
    )
    back_state = (
        query_zeros,
        jnp.zeros((seq_count, seq_length, kv_local, HEAD_SIZE), jnp.float32),
        jnp.zeros((seq_count, seq_length, kv_local, HEAD_SIZE), jnp.float32),
    )
    back_piece_keys = lax.all_gather(keys, CTX_AXIS, axis=1, tiled=True)
    back_piece_values = lax.all_gather(values, CTX_AXIS, axis=1, tiled=True)
    piece_rows = back_piece_keys.shape[1]
    back_step_rows = math.gcd(piece_rows, 1024)

    def back_one_step(number, loop_state):
        offset = number * back_step_rows
        key_first = offset
        write_at = offset

        def back_compute(state):
            d_query, d_keys, d_values = state
            key_part = lax.dynamic_slice_in_dim(back_piece_keys, offset, back_step_rows, 1)
            value_part = lax.dynamic_slice_in_dim(back_piece_values, offset, back_step_rows, 1)
            allowed = key_block(segments, key_first, back_step_rows, query_pos, query_seg)
            scores = (
                jnp.einsum(
                    "sqhgd,skhd->shgqk",
                    query_rows_input,
                    key_part,
                    preferred_element_type=jnp.float32,
                )
                * score_scale
            )
            probs = jnp.where(allowed, jnp.exp(scores - log_total[..., None]), 0.0)
            d_probs = jnp.einsum(
                "sqhgd,skhd->shgqk", d_attended, value_part, preferred_element_type=jnp.float32
            )
            d_scores = (probs * (d_probs - delta[..., None])).astype(jnp.bfloat16)
            d_query = d_query + jnp.einsum(
                "shgqk,skhd->sqhgd", d_scores, key_part, preferred_element_type=jnp.float32
            )
            key_grad = jnp.einsum(
                "shgqk,sqhgd->skhd", d_scores, query_rows_input, preferred_element_type=jnp.float32
            )
            value_grad = jnp.einsum(
                "shgqk,sqhgd->skhd",
                probs.astype(jnp.bfloat16),
                d_attended,
                preferred_element_type=jnp.float32,
            )
            d_keys = lax.dynamic_update_slice_in_dim(
                d_keys,
                lax.dynamic_slice_in_dim(d_keys, write_at, back_step_rows, 1) + key_grad,
                write_at,
                1,
            )
            d_values = lax.dynamic_update_slice_in_dim(
                d_values,
                lax.dynamic_slice_in_dim(d_values, write_at, back_step_rows, 1) + value_grad,
                write_at,
                1,
            )
            return (d_query, d_keys, d_values)

        return lax.cond(
            counting_keys(key_first, back_step_rows), back_compute, keep_state, loop_state
        )

    d_query, d_keys, d_values = lax.fori_loop(
        0, piece_rows // back_step_rows, back_one_step, back_state
    )
    own_keys, own_values = (
        lax.psum_scatter(
            d_keys.astype(jnp.bfloat16), CTX_AXIS, scatter_dimension=1, tiled=True
        ).astype(jnp.float32),
        lax.psum_scatter(
            d_values.astype(jnp.bfloat16), CTX_AXIS, scatter_dimension=1, tiled=True
        ).astype(jnp.float32),
    )
    q_normed = rotate_back(
        d_query.reshape(seq_count, block_rows, heads_local, HEAD_SIZE) * score_scale,
        cosine,
        sine_part,
    )
    grad_query_gain = jnp.sum(q_normed * q_proj * q_scale, axis=(0, 1, 2))
    query_projection_gradient = (
        rms_back(q_normed, q_proj, q_scale, gain_query)
        .astype(jnp.bfloat16)
        .reshape(seq_count, block_rows, heads_local * HEAD_SIZE)
    )
    k_normed = rotate_back(own_keys * score_scale, cosine, sine_part)
    grad_key_gain = jnp.sum(k_normed * key_projected * k_scale, axis=(0, 1, 2))
    lookup_map_derivative = (
        rms_back(k_normed, key_projected, k_scale, gain_key)
        .astype(jnp.bfloat16)
        .reshape(seq_count, block_rows, kv_local * HEAD_SIZE)
    )
    value_projection_gradient = own_values.astype(jnp.bfloat16).reshape(
        seq_count, block_rows, kv_local * HEAD_SIZE
    )
    query_gradient_rows = jnp.einsum(
        "zqr,zqa->ra", attention_rows, query_projection_gradient, preferred_element_type=jnp.float32
    )
    key_gradient_rows = jnp.einsum(
        "zqr,zqa->ra", attention_rows, lookup_map_derivative, preferred_element_type=jnp.float32
    )
    value_gradient_rows = jnp.einsum(
        "zqr,zqa->ra", attention_rows, value_projection_gradient, preferred_element_type=jnp.float32
    )
    d_attn_in = tp_total(
        jnp.einsum(
            "wtl,al->wta",
            query_projection_gradient,
            query_backward,
            preferred_element_type=jnp.float32,
        )
        + jnp.einsum(
            "wtl,al->wta",
            lookup_map_derivative,
            lookup_pullback,
            preferred_element_type=jnp.float32,
        )
        + jnp.einsum(
            "wtl,al->wta",
            value_projection_gradient,
            value_backward,
            preferred_element_type=jnp.float32,
        )
    )
    grad_attn_gain = jnp.sum(d_attn_in * inputs * scale_one, axis=(0, 1))
    grad_hidden = d_middle + rms_back(d_attn_in, inputs, scale_one, gain_attn)
    reduced = (
        lax.psum_scatter(
            grad_attn_gain.astype(jnp.bfloat16), SHARD_AXIS, scatter_dimension=0, tiled=True
        ).astype(jnp.float32),
        lax.psum_scatter(
            query_gradient_rows.astype(jnp.bfloat16), SHARD_AXIS, scatter_dimension=0, tiled=True
        ).astype(jnp.float32),
        lax.psum_scatter(
            key_gradient_rows.astype(jnp.bfloat16), SHARD_AXIS, scatter_dimension=0, tiled=True
        ).astype(jnp.float32),
        lax.psum_scatter(
            value_gradient_rows.astype(jnp.bfloat16), SHARD_AXIS, scatter_dimension=0, tiled=True
        ).astype(jnp.float32),
        lax.psum_scatter(
            grad_query_gain.astype(jnp.bfloat16), SHARD_AXIS, scatter_dimension=0, tiled=True
        ).astype(jnp.float32),
        lax.psum_scatter(
            grad_key_gain.astype(jnp.bfloat16), SHARD_AXIS, scatter_dimension=0, tiled=True
        ).astype(jnp.float32),
        lax.psum_scatter(
            result_cotangent.astype(jnp.bfloat16), SHARD_AXIS, scatter_dimension=1, tiled=True
        ).astype(jnp.float32),
        lax.psum_scatter(
            grad_mlp_gain.astype(jnp.bfloat16), SHARD_AXIS, scatter_dimension=0, tiled=True
        ).astype(jnp.float32),
        lax.psum_scatter(
            grad_gate.astype(jnp.bfloat16), SHARD_AXIS, scatter_dimension=0, tiled=True
        ).astype(jnp.float32),
        lax.psum_scatter(
            grad_up.astype(jnp.bfloat16), SHARD_AXIS, scatter_dimension=0, tiled=True
        ).astype(jnp.float32),
        lax.psum_scatter(
            grad_down.astype(jnp.bfloat16), SHARD_AXIS, scatter_dimension=1, tiled=True
        ).astype(jnp.float32),
    )
    matrices = (
        lax.psum(reduced[1].astype(jnp.bfloat16), CTX_AXIS).astype(jnp.float32),
        lax.psum(reduced[2].astype(jnp.bfloat16), CTX_AXIS).astype(jnp.float32),
        lax.psum(reduced[3].astype(jnp.bfloat16), CTX_AXIS).astype(jnp.float32),
        lax.psum(reduced[6].astype(jnp.bfloat16), CTX_AXIS).astype(jnp.float32),
        lax.psum(reduced[8].astype(jnp.bfloat16), CTX_AXIS).astype(jnp.float32),
        lax.psum(reduced[9].astype(jnp.bfloat16), CTX_AXIS).astype(jnp.float32),
        lax.psum(reduced[10].astype(jnp.bfloat16), CTX_AXIS).astype(jnp.float32),
    )
    gains = lax.psum((reduced[0], reduced[4], reduced[5], reduced[7]), (CTX_AXIS, TP_AXIS))
    return (
        out_hidden,
        grad_hidden,
        gains[0],
        matrices[0],
        matrices[1],
        matrices[2],
        gains[1],
        gains[2],
        matrices[3],
        gains[3],
        matrices[4],
        matrices[5],
        matrices[6],
    )


def solution(mesh):
    in_specs = (
        P(SHARD_AXIS, (CTX_AXIS, TP_AXIS), None),
        P(SHARD_AXIS, None),
        P(SHARD_AXIS, (CTX_AXIS, TP_AXIS), None),
        P(SHARD_AXIS),
        P(SHARD_AXIS, TP_AXIS),
        P(SHARD_AXIS, TP_AXIS),
        P(SHARD_AXIS, TP_AXIS),
        P(SHARD_AXIS),
        P(SHARD_AXIS),
        P(TP_AXIS, SHARD_AXIS),
        P(SHARD_AXIS),
        P(SHARD_AXIS, TP_AXIS),
        P(SHARD_AXIS, TP_AXIS),
        P(TP_AXIS, SHARD_AXIS),
    )
    out_specs = (
        P(SHARD_AXIS, (CTX_AXIS, TP_AXIS), None),
        P(SHARD_AXIS, (CTX_AXIS, TP_AXIS), None),
        P(SHARD_AXIS),
        P(SHARD_AXIS, TP_AXIS),
        P(SHARD_AXIS, TP_AXIS),
        P(SHARD_AXIS, TP_AXIS),
        P(SHARD_AXIS),
        P(SHARD_AXIS),
        P(TP_AXIS, SHARD_AXIS),
        P(SHARD_AXIS),
        P(SHARD_AXIS, TP_AXIS),
        P(SHARD_AXIS, TP_AXIS),
        P(TP_AXIS, SHARD_AXIS),
    )
    shape = mesh.shape
    fast = shape[SHARD_AXIS] == 2 and shape[CTX_AXIS] == 4 and shape[TP_AXIS] == 4
    return jax.shard_map(
        fast_device if fast else per_device, mesh=mesh, in_specs=in_specs, out_specs=out_specs, check_vma=False
    )
```

```python
import functools
import math

import jax
import jax.numpy as jnp
import numpy as np
from jax import lax
from jax.experimental import pallas as pl
from jax.experimental.pallas import tpu as pltpu
from jax.sharding import PartitionSpec as P

SHARD_AXIS, CTX_AXIS, TP_AXIS = "shard", "ctx", "tp"
HEAD_SIZE = 128
NDOC = 8


norm_eps = 1e-06
rope_base = 1000000.0
masked_fill = -1e30


def rms_scale(values):
    return lax.rsqrt(jnp.mean(values * values, axis=-1, keepdims=True) + norm_eps)


def rms_back(grad_out, values, row_scale, gain_vec):
    scaled = grad_out * gain_vec
    inner_sum = jnp.mean(scaled * values, axis=-1, keepdims=True)
    return row_scale * scaled - values * (row_scale * row_scale * row_scale) * inner_sum


def doc_positions(segments):
    seq_width = segments.shape[-1]
    labels = jnp.arange(NDOC, dtype=jnp.int32)
    onehot = (segments[..., None] == labels).astype(jnp.int32)
    counts = jnp.sum(onehot, axis=-2)
    starts = jnp.cumsum(counts, axis=-1) - counts
    first_row = jnp.sum(onehot * starts[..., None, :], axis=-1)
    return jnp.arange(seq_width, dtype=jnp.int32) - first_row


def rope_tables(positions):
    exponents = jnp.arange(0, HEAD_SIZE, 2).astype(jnp.float32) / HEAD_SIZE
    angle_rates = jnp.power(jnp.float32(rope_base), -exponents)
    angles = positions.astype(jnp.float32)[..., None] * angle_rates
    angles = jnp.concatenate([angles, angles], axis=-1)[..., None, :]
    return (jnp.cos(angles), jnp.sin(angles))


def rotate(inputs, cosine, sine_part):
    half_dim = inputs.shape[-1] // 2
    turned = jnp.concatenate([-inputs[..., half_dim:], inputs[..., :half_dim]], axis=-1)
    return inputs * cosine + turned * sine_part


def rotate_back(grads, cosine, sine_part):
    half_dim = grads.shape[-1] // 2
    moved = grads * sine_part
    turned = jnp.concatenate([moved[..., half_dim:], -moved[..., :half_dim]], axis=-1)
    return grads * cosine + turned


def tp_rows(local_part):
    return lax.all_gather(local_part, TP_AXIS, axis=1, tiled=True)


def tp_total(partial_sum):
    return lax.psum_scatter(
        partial_sum.astype(jnp.bfloat16), TP_AXIS, scatter_dimension=1, tiled=True
    ).astype(jnp.float32)


def key_block(segments, key_first, step_rows, query_pos, query_seg):
    key_pos = key_first + jnp.arange(step_rows, dtype=jnp.int32)
    key_seg = lax.dynamic_slice_in_dim(segments, key_first, step_rows, 1)
    allowed = (key_pos[None, None, :] <= query_pos[None, :, None]) & (
        key_seg[:, None, :] == query_seg[:, :, None]
    )
    return allowed[:, None, None]


def keep_state(state):
    return state


CHUNKS = 15
FROM_MLP = 9
READY = 2
UNITS, EARLY, MATED, LATE = 2 * CHUNKS, 2 * FROM_MLP, 2 * READY, 22


MESH_ID = pl.DeviceIdType.MESH
ANY_SPEC = pl.BlockSpec(memory_space=pl.ANY)
VMEM_SPEC = pl.BlockSpec(memory_space=pltpu.VMEM)
SCORE_STEP = HEAD_SIZE ** (-0.5) * math.log2(math.e)
APART = 16384.0


def enter(peers):
    barrier = pltpu.get_barrier_semaphore()
    for peer in peers:
        pl.semaphore_signal(barrier, inc=1, device_id=peer, device_id_type=MESH_ID)
    pl.semaphore_wait(barrier, len(peers))


def last_dot(left, right):
    return lax.dot_general(
        left, right, (((1,), (1,)), ((), ())), preferred_element_type=jnp.float32
    )


def flat_dot(left, right):
    return jnp.dot(left, right, preferred_element_type=jnp.float32)


def first_dot(left, right):
    return lax.dot_general(
        left, right, (((0,), (0,)), ((), ())), preferred_element_type=jnp.float32
    )


def spin(values, cosine, sine_signed):
    return values * cosine + pltpu.roll(values, HEAD_SIZE // 2, 1) * sine_signed


class Links:
    def __init__(self, send, recv):
        self.send, self.recv, self.used = send, recv, 0

    def copy(self, src, dst, device):
        number = self.used
        self.used += 1
        return pltpu.make_async_remote_copy(
            src_ref=src, dst_ref=dst, send_sem=self.send.at[number],
            recv_sem=self.recv.at[number], device_id=device, device_id_type=MESH_ID,
        )


class Locals:
    def __init__(self, sems):
        self.sems, self.used, self.open = sems, 0, []

    def make(self, src, dst):
        copy = pltpu.make_async_copy(src, dst, self.sems.at[self.used])
        self.used += 1
        return copy

    def start(self, src, dst):
        copy = self.make(src, dst)
        copy.start()
        self.open.append(copy)
        return copy

    def wait(self, copy):
        copy.wait()
        self.open = [other for other in self.open if other is not copy]

    def finish(self):
        for copy in self.open:
            copy.wait()


def forward_kernel(
    hidden, cotangent, gains_own, segments, rates, wq, wk, wv, wo, wg, wu,
    gains_out, rows_out, q_out, k_out, query_out, keys_out, values_out, cos_out, sin_out,
    attended_out, low_out, wqkv_out, crows_out, wo_out, wg_out, wu_out,
    gains, raw, rows, wqkv, q_proj, k_proj, qaug, kaug, vaug, cosine, sine, acc, low, crows,
    gains_in, gains_land, places, send, recv, local,
):
    s, c, t = lax.axis_index(SHARD_AXIS), lax.axis_index(CTX_AXIS), lax.axis_index(TP_AXIS)
    nctx = lax.axis_size(CTX_AXIS)
    part = hidden.shape[0]
    block = 4 * part
    half = wq.shape[0]
    f32, bf16 = jnp.float32, jnp.bfloat16
    side, across, mate = {TP_AXIS: t ^ 1}, {TP_AXIS: t ^ 2}, {SHARD_AXIS: 1 - s}
    pair = {CTX_AXIS: c ^ 1}
    nxt, prv = {CTX_AXIS: lax.rem(c + 1, nctx)}, {CTX_AXIS: lax.rem(c + nctx - 1, nctx)}
    gains_in[...] = jnp.zeros(gains_in.shape, f32)
    for row in range(2):
        own_gain = gains_own[:, row * half : row * half + half].astype(f32)
        gains_in[row : row + 1, pl.ds(pl.multiple_of(s * half, half), half)] = own_gain
    small = jnp.broadcast_to(gains_own[:, 2 * half : 2 * half + HEAD_SIZE], (16, HEAD_SIZE))
    square = (HEAD_SIZE, HEAD_SIZE)
    source_lane = lax.broadcasted_iota(jnp.int32, square, 0)
    target_lane = lax.broadcasted_iota(jnp.int32, square, 1) - s * (HEAD_SIZE // 2)
    for row, first in ((2, 0), (3, HEAD_SIZE // 2)):
        chosen = (source_lane - first == target_lane) & (source_lane >= first)
        chosen = chosen & (source_lane < first + HEAD_SIZE // 2)
        placed = flat_dot(small, jnp.where(chosen, 1.0, 0.0).astype(bf16))
        gains_in[row : row + 1, 0:HEAD_SIZE] = placed[0:1]
    enter([side, across, mate, nxt, prv])
    links, locals_ = Links(send, recv), Locals(local)

    def piece(owner):
        return pl.ds(pl.multiple_of(owner * part, part), part)

    low_bit = c & 1

    def some(shard, count, size):
        return pl.ds(pl.multiple_of(shard * count + low_bit * size, size), size)

    mine = pl.ds(pl.multiple_of(s * half, half), half)
    quarter = half // 2
    gains_copy = links.copy(gains_in, gains_land, mate)
    wk_copy = links.copy(wk, wqkv.at[mine, 512:768], mate)
    wv_copy = links.copy(wv, wqkv.at[mine, 768:1024], mate)
    wq_copy = links.copy(wq, wqkv.at[mine, 0:512], mate)
    wo_copy = links.copy(
        wo.at[some(0, 0, quarter), :], wo_out.at[some(0, 0, quarter), :], mate
    )
    wo_got = wo_out.at[some(0, 0, quarter), :]
    wo_on = links.copy(wo_got, wo_got, pair)
    wg_copy = links.copy(
        wg.at[some(0, 0, quarter), :], wg_out.at[some(0, 0, quarter), :], mate
    )
    wg_got = wg_out.at[some(0, 0, quarter), :]
    wg_on = links.copy(wg_got, wg_got, pair)
    wu_copy = links.copy(
        wu.at[some(0, 0, quarter), :], wu_out.at[some(0, 0, quarter), :], mate
    )
    gains_copy.start()
    wk_copy.start()
    wv_copy.start()
    own_k = locals_.start(wk, wqkv.at[mine, 512:768])
    own_v = locals_.start(wv, wqkv.at[mine, 768:1024])
    own_q = locals_.start(wq, wqkv.at[mine, 0:512])
    own_c = locals_.start(cotangent, crows.at[piece(t), :])

    def source(b, owner):
        return hidden if b == 0 else raw.at[b, piece(owner)]

    to_across, to_side, on_to_side, to_next = [], [], [], []
    for b in range(3):
        there = raw.at[b, piece(t ^ 2)]
        to_side.append(links.copy(source(b, t), raw.at[b, piece(t)], side))
        on_to_side.append(links.copy(there, there, side))
        if b < 2:
            to_across.append(links.copy(source(b, t), raw.at[b, piece(t)], across))
            to_next.append(links.copy(source(b, t), raw.at[b + 1, piece(t)], nxt))
    far_to_next = links.copy(raw.at[1, piece(t ^ 2)], raw.at[2, piece(t ^ 2)], nxt)
    c_side = links.copy(cotangent, crows.at[piece(t), :], side)
    c_over = links.copy(cotangent, crows.at[piece(t), :], across)
    c_on = links.copy(crows.at[piece(t ^ 2), :], crows.at[piece(t ^ 2), :], side)
    to_across[0].start()
    to_side[0].start()

    @pl.when(c < nctx - 1)
    def _():
        to_next[0].start()

    c_side.start()
    raw[0, piece(t), :] = hidden[...]
    gains_copy.wait()
    gains[...] = gains_in[...] + gains_land[...]
    q_gain = gains[2:3, 0:HEAD_SIZE]
    k_gain = gains[3:4, 0:HEAD_SIZE]

    def table(b):
        start, stop, rate = places[0:1, :], places[1:2, :], rates[...]
        shape = (128, HEAD_SIZE)
        lower = lax.broadcasted_iota(jnp.int32, shape, 1) < HEAD_SIZE // 2

        @pl.loop(0, 4)
        def _(n):
            found = []
            for offset in (0, 512):
                first = n * 128 + offset
                index = (lax.broadcasted_iota(jnp.int32, shape, 0) + first) + (c - b) * block
                index = index.astype(f32)
                inside = (index >= start) & (index < stop)
                marks = jnp.where(inside, 1.0, 0.0)
                begin = jnp.sum(jnp.where(inside, start, 0.0), axis=1, keepdims=True)
                at = pl.ds(pl.multiple_of(first, 128), 128)
                for g in range(2):
                    kaug[b, g, at, 128:256] = (1.0 - marks).astype(bf16)
                if b == 0:
                    for h in range(4):
                        qaug[h, at, 128:256] = (marks * -APART).astype(bf16)
                found.append((at, index - begin))
            (low_at, low_pos), (high_at, high_pos) = found
            angle = jnp.where(lower, low_pos, high_pos) * rate
            cs, sn = jnp.cos(angle), jnp.sin(angle)
            cr, sr = pltpu.roll(cs, HEAD_SIZE // 2, 1), pltpu.roll(sn, HEAD_SIZE // 2, 1)
            cosine[b, low_at, :] = jnp.where(lower, cs, cr)
            cosine[b, high_at, :] = jnp.where(lower, cr, cs)
            sine[b, low_at, :] = jnp.where(lower, -sn, sr)
            sine[b, high_at, :] = jnp.where(lower, -sr, sn)

    def project_kv(b, owner):
        at = piece(owner)
        x = raw[b, at, :].astype(f32)
        scale = lax.rsqrt(jnp.mean(x * x, axis=-1, keepdims=True) + norm_eps)
        rows[b, at, :] = (x * scale * gains[0:1, :]).astype(bf16)
        got = flat_dot(rows[b, at, :], wqkv[:, 512:1024])
        k_proj[b, at, :] = got[:, 0:256]
        for g in range(2):
            u = got[:, g * 128 : g * 128 + 128]
            r = lax.rsqrt(jnp.mean(u * u, axis=-1, keepdims=True) + norm_eps)
            turned = spin(u * r * k_gain, cosine[b, at, :], sine[b, at, :])
            kaug[b, g, at, 0:128] = turned.astype(bf16)
            vaug[b, g, at, 0:128] = got[:, 256 + g * 128 : 384 + g * 128].astype(bf16)

    def project_q(owner):
        at = piece(owner)
        got = flat_dot(rows[0, at, :], wqkv[:, 0:512])
        q_proj[at, :] = got
        for h in range(4):
            u = got[:, h * 128 : h * 128 + 128]
            r = lax.rsqrt(jnp.mean(u * u, axis=-1, keepdims=True) + norm_eps)
            turned = spin(u * r * q_gain, cosine[0, at, :], sine[0, at, :])
            qaug[h, at, 0:128] = turned.astype(bf16)

    def unit(b, g, r, kc, bound):
        at = pl.ds(pl.multiple_of(r * 512, 512), 512)
        for hh in range(2):
            qq = qaug[2 * g + hh, at, :]
            total = None
            for j in range(2):
                keys_at = pl.ds(pl.multiple_of(kc * 512 + j * 256, 256), 256)
                p = jnp.exp2(last_dot(qq, kaug[b, g, keys_at, :]) * SCORE_STEP)
                if bound is not None:
                    ahead = lax.broadcasted_iota(jnp.int32, p.shape, 0) - lax.broadcasted_iota(
                        jnp.int32, p.shape, 1
                    )
                    p = jnp.where(ahead >= bound + j * 256, p, 0.0)
                value = flat_dot(p.astype(bf16), vaug[b, g, keys_at, :])
                total = value if total is None else total + value
            acc[2 * g + hh, at, :] += total

    def block_outs(b):
        pairs = (
            (rows, rows_out), (k_proj, k_out), (kaug, keys_out), (vaug, values_out),
            (cosine, cos_out), (sine, sin_out),
        )
        return [locals_.make(a.at[b], d.at[b]) for a, d in pairs]

    outs = [block_outs(b) for b in range(3)]

    lane = lax.broadcasted_iota(jnp.int32, (1, HEAD_SIZE), 1)
    begin = jnp.full((1, HEAD_SIZE), float(nctx * block), f32)
    end = begin
    for label in range(NDOC):
        before = jnp.where(segments[...] < label, 1.0, 0.0)
        before = jnp.sum(before, axis=(0, 1), keepdims=True)
        begin = jnp.where(lane == label, before, begin)
        end = jnp.where(lane == label - 1, before, end)
    places[0:1, :] = begin
    places[1:2, :] = end
    table(0)
    vaug[:, :, :, 128:256] = jnp.ones((3, 2, block, 128), bf16)
    acc[...] = jnp.zeros(acc.shape, f32)
    locals_.wait(own_k)
    locals_.wait(own_v)
    wk_copy.wait()
    wv_copy.wait()
    wq_copy.start()
    to_across[0].wait_recv()
    on_to_side[0].start()

    @pl.when(c >= 1)
    def _():
        to_next[0].wait_recv()
        to_across[1].start()
        to_side[1].start()

        @pl.when(c < nctx - 1)
        def _():
            to_next[1].start()

    to_side[0].wait_recv()
    on_to_side[0].wait_recv()

    @pl.loop(0, 4)
    def _(n):
        project_kv(0, n)

    for copy in outs[0]:
        copy.start()

    @pl.when(c >= 1)
    def _():
        table(1)
        to_side[1].wait_recv()

        @pl.loop(0, 2)
        def _(n):
            project_kv(1, t ^ n)

    @pl.when(c >= 2)
    def _():
        table(2)

    locals_.wait(own_q)
    wq_copy.wait()
    wo_copy.start()

    @pl.when(c >= 1)
    def _():
        to_across[1].wait_recv()
        on_to_side[1].start()

        @pl.when(c < nctx - 1)
        def _():
            far_to_next.start()

        @pl.when(c >= 2)
        def _():
            to_next[1].wait_recv()
            to_side[2].start()

    c_over.start()

    @pl.loop(0, 4)
    def _(n):
        project_q(n)

    locals_.start(q_proj, q_out)
    locals_.start(wqkv, wqkv_out)

    @pl.loop(0, 6)
    def _(n):
        m = lax.rem(n, 3)
        unit(0, n // 3, (m + 1) // 2, m // 2, (m & 1) * -512)

    wo_copy.wait_recv()
    wo_on.start()
    wg_copy.start()

    @pl.when(c >= 1)
    def _():
        on_to_side[1].wait_recv()

        @pl.loop(2, 4)
        def _(n):
            project_kv(1, t ^ n)

        for copy in outs[1]:
            copy.start()

        @pl.loop(0, 8)
        def _(n):
            m = lax.rem(n, 4)
            unit(1, n // 4, m // 2, m & 1, None)

    wg_copy.wait_recv()
    wg_on.start()
    wu_copy.start()

    c_over.wait_recv()
    c_on.start()

    @pl.when(c >= 2)
    def _():
        far_to_next.wait_recv()
        on_to_side[2].start()
        to_side[2].wait_recv()
        on_to_side[2].wait_recv()

        @pl.loop(0, 4)
        def _(n):
            project_kv(2, n)

        for copy in outs[2]:
            copy.start()

        @pl.loop(0, 6)
        def _(n):
            m = lax.rem(n, 3)
            unit(2, n // 3, m // 2, (m + 1) // 2, None)

    for h in range(4):

        @pl.loop(0, 4)
        def _(r):
            at = pl.ds(pl.multiple_of(r * 256, 256), 256)
            total = acc[h, at, 128:256]
            value = acc[h, at, 0:128] / total
            acc[h, at, 0:128] = value
            shift = jnp.log(total) * -(HEAD_SIZE**0.5)
            top = shift.astype(bf16).astype(f32)
            mid = (shift - top).astype(bf16).astype(f32)
            lane = lax.broadcasted_iota(jnp.int32, shift.shape, 1)
            parts = jnp.where(lane == NDOC, top, 0.0)
            parts = jnp.where(lane == NDOC + 1, mid, parts)
            parts = jnp.where(lane == NDOC + 2, shift - top - mid, parts)
            qaug[h, at, 128:256] = qaug[h, at, 128:256] + parts.astype(bf16)
            low[h, at, :] = value.astype(bf16)

        lanes = slice(h * 128, h * 128 + 128)
        locals_.start(low.at[h], low_out.at[:, lanes])
        locals_.start(acc.at[h, :, 0:128], attended_out.at[:, lanes])
        locals_.start(qaug.at[h], query_out.at[h])

    locals_.start(gains, gains_out)
    locals_.wait(own_c)
    c_side.wait()
    c_on.wait()
    locals_.start(crows, crows_out)
    c_over.wait_send()
    to_across[0].wait_send()
    to_side[0].wait_send()
    on_to_side[0].wait_send()
    for copy in outs[0]:
        copy.wait()

    @pl.when(c < nctx - 1)
    def _():
        to_next[0].wait_send()

    for b in (1, 2):

        @pl.when(c >= b)
        def _():
            if b < 2:
                to_across[b].wait_send()
            to_side[b].wait_send()
            on_to_side[b].wait_send()
            for copy in outs[b]:
                copy.wait()

    @pl.when((c >= 1) & (c < nctx - 1))
    def _():
        to_next[1].wait_send()
        far_to_next.wait_send()

    wo_copy.wait_send()
    wo_on.wait()
    wg_copy.wait_send()
    wg_on.wait()
    wu_copy.wait()
    locals_.finish()


def forward_call(hidden, cotangent, gains, segments, rates, wq, wk, wv, wo, wg, wu):
    part, width = hidden.shape
    block = 4 * part
    f32, bf16 = jnp.float32, jnp.bfloat16
    shape = jax.ShapeDtypeStruct
    outs = (
        shape((8, width), f32),
        shape((3, block, width), bf16),
        shape((block, 512), f32),
        shape((3, block, 256), f32),
        shape((4, block, 256), bf16),
        shape((3, 2, block, 256), bf16),
        shape((3, 2, block, 256), bf16),
        shape((3, block, HEAD_SIZE), f32),
        shape((3, block, HEAD_SIZE), f32),
        shape((block, 512), f32),
        shape((block, 512), bf16),
        shape((width, 1024), bf16),
        shape((block, width), bf16),
        shape(wo.shape, bf16),
        shape(wg.shape, bf16),
        shape(wu.shape, bf16),
    )
    return pl.pallas_call(
        forward_kernel,
        name="forward",
        out_shape=outs,
        in_specs=[VMEM_SPEC] * 5 + [ANY_SPEC] * 6,
        out_specs=[ANY_SPEC] * len(outs),
        scratch_shapes=[
            pltpu.VMEM((8, width), f32),
            pltpu.VMEM((3, block, width), bf16),
            pltpu.VMEM((3, block, width), bf16),
            pltpu.VMEM((width, 1024), bf16),
            pltpu.VMEM((block, 512), f32),
            pltpu.VMEM((3, block, 256), f32),
            pltpu.VMEM((4, block, 256), bf16),
            pltpu.VMEM((3, 2, block, 256), bf16),
            pltpu.VMEM((3, 2, block, 256), bf16),
            pltpu.VMEM((3, block, HEAD_SIZE), f32),
            pltpu.VMEM((3, block, HEAD_SIZE), f32),
            pltpu.VMEM((4, block, 256), f32),
            pltpu.VMEM((4, block, 128), bf16),
            pltpu.VMEM((block, width), bf16),
            pltpu.VMEM((8, width), f32),
            pltpu.VMEM((8, width), f32),
            pltpu.VMEM((8, HEAD_SIZE), f32),
            pltpu.SemaphoreType.DMA((23,)),
            pltpu.SemaphoreType.DMA((23,)),
            pltpu.SemaphoreType.DMA((38,)),
        ],
        compiler_params=pltpu.CompilerParams(
            collective_id=0, has_side_effects=True, vmem_limit_bytes=58 << 20
        ),
    )(hidden, cotangent, gains, segments, rates, wq, wk, wv, wo, wg, wu)


class Scatter:
    def __init__(self, links, bufs, side, across):
        self.bufs = bufs
        self.far = links.copy(bufs.at[0], bufs.at[3], side)
        self.over = links.copy(bufs.at[1], bufs.at[4], across)
        self.near = links.copy(bufs.at[2], bufs.at[5], side)

    def put_far(self, value):
        self.bufs[0] = value.astype(jnp.bfloat16)
        self.far.start()

    def put_over(self, value):
        self.far.wait_recv()
        self.bufs[1] = (value + self.bufs[3].astype(jnp.float32)).astype(jnp.bfloat16)
        self.over.start()

    def put_near(self, value):
        self.bufs[2] = value.astype(jnp.bfloat16)
        self.near.start()

    def total(self, value):
        self.near.wait_recv()
        self.over.wait_recv()
        return value + self.bufs[5].astype(jnp.float32) + self.bufs[4].astype(jnp.float32)

    def close(self):
        self.far.wait_send()
        self.over.wait_send()
        self.near.wait_send()


def mlp_kernel(
    low, hidden, gains, crows_in, wo_own, wo_got, wg_own, wg_got, wu_own, wu_got,
    wd,
    d_middle_out, gain_out, brow_out, own_out, give_out, parts_out, out_own_out,
    wo, wgf, wuf, wdf, mrows, act, dgate, dup, brow, kept, middle, bufs, parts, give, own, land,
    crows, result, send, recv, local,
):
    s, c, t = lax.axis_index(SHARD_AXIS), lax.axis_index(CTX_AXIS), lax.axis_index(TP_AXIS)
    part = hidden.shape[0]
    half = wd.shape[1]
    bf16, f32 = jnp.bfloat16, jnp.float32
    side, across = {TP_AXIS: t ^ 1}, {TP_AXIS: t ^ 2}
    mate, pair = {SHARD_AXIS: 1 - s}, {CTX_AXIS: c ^ 1}
    links, locals_ = Links(send, recv), Locals(local)

    def piece(owner):
        return pl.ds(pl.multiple_of(owner * part, part), part)

    mine = pl.ds(pl.multiple_of(s * half, half), half)
    theirs = pl.ds(pl.multiple_of((1 - s) * half, half), half)
    low_bit = c & 1

    def some(shard, count, size):
        return pl.ds(pl.multiple_of(shard * count + low_bit * size, size), size)

    quarter = half // 2
    third = wd.shape[0] // 2
    wu_at = some(1 - s, half, quarter)
    wu_on = links.copy(wu_got.at[some(0, 0, quarter), :], wuf.at[wu_at, :], pair)
    wd_copy = links.copy(
        wd.at[some(0, 0, third), :], wdf.at[some(0, 0, third), mine], mate
    )
    wd_got = wdf.at[some(0, 0, third), theirs]
    wd_on = links.copy(wd_got, wd_got, pair)
    wo_loads = [
        locals_.start(wo_own, wo.at[:, mine]),
        locals_.start(wo_got, wo.at[:, theirs]),
    ]
    enter([side, across, mate, pair])
    wu_on.start()
    wd_copy.start()
    own_weights = [
        locals_.start(wg_own, wgf.at[mine, :]),
        locals_.start(wg_got, wgf.at[theirs, :]),
        locals_.start(wu_own, wuf.at[mine, :]),
        locals_.start(wu_got.at[some(0, 0, quarter), :], wuf.at[wu_at, :]),
        locals_.start(wd, wdf.at[:, mine]),
        locals_.start(crows_in, crows),
    ]
    for copy in wo_loads:
        locals_.wait(copy)

    branch = Scatter(links, bufs.at[0], side, across)
    back = Scatter(links, bufs.at[1], side, across)

    def branch_part(owner):
        return flat_dot(low[piece(owner), :], wo[...])

    branch.put_far(branch_part(t ^ 3))
    branch.put_over(branch_part(t ^ 2))
    branch.put_near(branch_part(t ^ 1))
    middle[...] = hidden[...].astype(f32) + branch_part(t)
    wd_copy.wait_recv()
    wd_on.start()
    middle[...] = branch.total(middle[...])
    m = middle[...]
    scale = lax.rsqrt(jnp.mean(m * m, axis=-1, keepdims=True) + norm_eps)
    gain = gains[1:2, :]
    mrows[piece(t), :] = (m * scale * gain).astype(bf16)
    here, there = mrows.at[piece(t), :], mrows.at[piece(t ^ 2), :]
    m_over, m_near = links.copy(here, here, across), links.copy(here, here, side)
    m_on = links.copy(there, there, side)
    m_over.start()
    m_near.start()
    for copy in own_weights:
        locals_.wait(copy)
    wu_on.wait_recv()
    wd_on.wait_recv()

    def mlp(owner):
        at = piece(owner)
        rows = mrows[at, :]
        gate = flat_dot(rows, wgf[...])
        upward = flat_dot(rows, wuf[...])
        d_act = last_dot(crows[at, :], wdf[...])
        sig = 1.0 / (1.0 + jnp.exp(-gate))
        silu = gate * sig
        act[at, :] = (silu * upward).astype(bf16)
        dup[at, :] = (d_act * silu).astype(bf16)
        dgate[at, :] = (d_act * upward * sig * (1.0 + gate * (1.0 - sig))).astype(bf16)

    def out_part(owner):
        return flat_dot(act[piece(owner), :], wdf[...])

    def back_part(owner):
        at = piece(owner)
        return last_dot(dgate[at, :], wgf[...]) + last_dot(dup[at, :], wuf[...])

    mlp(t)
    kept[0] = back_part(t)
    kept[1] = out_part(t) + middle[...]
    locals_.start(kept.at[1], out_own_out)
    m_near.wait_recv()
    mlp(t ^ 1)
    back.put_near(back_part(t ^ 1))
    m_over.wait_recv()
    m_on.start()
    m_on.wait_recv()
    mlp(t ^ 3)
    back.put_far(back_part(t ^ 3))
    mlp(t ^ 2)
    back.put_over(back_part(t ^ 2))

    def down_chunk(n, columns):
        return first_dot(act[:, n * 256 : n * 256 + 256], crows[:, columns]).astype(bf16)

    def wide_chunk(ref, grads, n, columns):
        got = first_dot(mrows[:, columns], grads[:, n * 256 : n * 256 + 256]).astype(bf16)
        ref[:, 0:256] = got[0:256]
        ref[:, 256:512] = got[256:512]

    to_mate = [links.copy(give.at[k], land.at[k], mate) for k in range(READY)]
    for k in range(3):
        give[k] = down_chunk(k, theirs)
        if k < READY:
            to_mate[k].start()
    for k in range(3):
        wide_chunk(give.at[3 + k], dgate, k, theirs)
    for k in range(3):
        own[k] = down_chunk(k, mine)
        wide_chunk(own.at[3 + k], dgate, k, mine)
    for n, owner in enumerate((3, 2, 1)):
        parts[n] = out_part(t ^ owner).astype(bf16)
    locals_.start(parts, parts_out)
    for k in range(3):
        wide_chunk(give.at[6 + k], dup, k, theirs)
        wide_chunk(own.at[6 + k], dup, k, mine)
    locals_.start(give.at[READY:FROM_MLP], give_out)
    locals_.start(own.at[READY:FROM_MLP], own_out.at[READY:FROM_MLP])

    d_mlp = back.total(kept[0])
    m = middle[...]
    scale = lax.rsqrt(jnp.mean(m * m, axis=-1, keepdims=True) + norm_eps)
    scaled = d_mlp * gain
    inner = jnp.mean(scaled * m, axis=-1, keepdims=True)
    d_middle = (
        crows[piece(t), :].astype(f32) + scale * scaled - m * (scale * scale * scale) * inner
    )
    kept[0] = d_middle
    gain_grad = jnp.sum(d_mlp * m * scale, axis=0, keepdims=True)
    brow[...] = d_middle.astype(bf16)
    locals_.start(brow, brow_out)
    locals_.start(kept.at[0], d_middle_out)
    result[...] = jnp.broadcast_to(gain_grad, (8, gain_grad.shape[1]))
    locals_.start(result, gain_out)

    for k in range(READY):
        to_mate[k].wait_recv()
        own[k] = own[k] + land[k]
    locals_.start(own.at[0:READY], own_out.at[0:READY])
    for k in range(READY):
        to_mate[k].wait_send()
    wu_on.wait_send()
    wd_copy.wait_send()
    wd_on.wait_send()
    branch.close()
    back.close()
    for copy in (m_over, m_near, m_on):
        copy.wait_send()
    locals_.finish()


def mlp_call(vmem_args, any_args):
    low, hidden, gains = vmem_args
    wo, wd = any_args[1], any_args[-1]
    part, width = hidden.shape
    block = 4 * part
    units = wd.shape[0]
    f32, bf16 = jnp.float32, jnp.bfloat16
    shape = jax.ShapeDtypeStruct
    outs = (
        shape((part, width), f32),
        shape((8, width), f32),
        shape((part, width), bf16),
        shape((FROM_MLP, 256, 512), bf16),
        shape((FROM_MLP - READY, 256, 512), bf16),
        shape((3, part, width), bf16),
        shape((part, width), f32),
    )
    return pl.pallas_call(
        mlp_kernel,
        name="mlp",
        out_shape=outs,
        in_specs=[VMEM_SPEC] * 3 + [ANY_SPEC] * 8,
        out_specs=[ANY_SPEC] * len(outs),
        scratch_shapes=[
            pltpu.VMEM((wo.shape[0], width), bf16),
            pltpu.VMEM((width, units), bf16),
            pltpu.VMEM((width, units), bf16),
            pltpu.VMEM((units, width), bf16),
            pltpu.VMEM((block, width), bf16),
            pltpu.VMEM((block, units), bf16),
            pltpu.VMEM((block, units), bf16),
            pltpu.VMEM((block, units), bf16),
            pltpu.VMEM((part, width), bf16),
            pltpu.VMEM((2, part, width), f32),
            pltpu.VMEM((part, width), f32),
            pltpu.VMEM((2, 6, part, width), bf16),
            pltpu.VMEM((3, part, width), bf16),
            pltpu.VMEM((FROM_MLP, 256, 512), bf16),
            pltpu.VMEM((FROM_MLP, 256, 512), bf16),
            pltpu.VMEM((READY, 256, 512), bf16),
            pltpu.VMEM((block, width), bf16),
            pltpu.VMEM((8, width), f32),
            pltpu.SemaphoreType.DMA((12 + READY,)),
            pltpu.SemaphoreType.DMA((12 + READY,)),
            pltpu.SemaphoreType.DMA((16,)),
        ],
        compiler_params=pltpu.CompilerParams(
            collective_id=1, has_side_effects=True, vmem_limit_bytes=58 << 20
        ),
    )(*vmem_args, *any_args)


class Pump:
    def __init__(self, refs, sems, mate, near, opposite, outer, out, first_mate):
        self.own, self.mated, self.landed, self.summed = refs
        self.send, self.recv, self.local = sems
        self.mate, self.near, self.opposite, self.outer = mate, near, opposite, outer
        self.inner = jnp.logical_not(outer)
        self.out, self.first_mate = out, first_mate

    def remote(self, stage, u, src, dst, device):
        return pltpu.make_async_remote_copy(
            src_ref=src, dst_ref=dst, send_sem=self.send.at[stage * UNITS + u],
            recv_sem=self.recv.at[stage * UNITS + u], device_id=device, device_id_type=MESH_ID,
        )

    def to_mate(self, u, src):
        return self.remote(0, u, src, self.mated.at[u - self.first_mate], self.mate)

    def inward(self, u):
        return self.remote(1, u, self.own.at[u], self.landed.at[u], self.near)

    def cross(self, u):
        return self.remote(2, u, self.landed.at[u], self.summed.at[u], self.opposite)

    def outward(self, u):
        return self.remote(3, u, self.summed.at[u], self.landed.at[u], self.near)

    def write(self, u, ref):
        return pltpu.make_async_copy(ref.at[u], self.out.at[u], self.local.at[u])

    def run(self, condition, body):
        if isinstance(condition, bool):
            if condition:
                body()
        else:
            pl.when(condition)(body)

    def first(self, u):
        def bring():
            self.to_mate(u, self.own.at[u]).wait_recv()
            self.own[u] = self.own[u] + self.mated[u - self.first_mate]

        self.run(u >= self.first_mate, bring)
        pl.when(self.outer)(lambda: self.inward(u).start())

    def second(self, u):
        @pl.when(self.inner)
        def _():
            self.inward(u).wait_recv()
            self.landed[u] = self.own[u] + self.landed[u]
            self.cross(u).start()

    def third(self, u):
        @pl.when(self.inner)
        def _():
            self.cross(u).wait_recv()
            self.summed[u] = self.landed[u] + self.summed[u]
            self.outward(u).start()
            self.write(u, self.summed).start()

    def fourth(self, u):
        @pl.when(self.outer)
        def _():
            self.outward(u).wait_recv()
            self.write(u, self.landed).start()

    def slot(self, k):
        for u in (2 * k, 2 * k + 1):
            self.first(u)
            self.run(k >= 1, lambda: self.second(u - 2))
            self.run(k >= 2, lambda: self.third(u - 4))

    def close(self):
        @pl.loop(0, UNITS)
        def _(u):
            pl.when(self.outer)(lambda: self.inward(u).wait_send())

            @pl.when(self.inner)
            def _():
                self.cross(u).wait_send()
                self.outward(u).wait_send()

            self.write(u, self.summed).wait()


def backward_kernel(
    query, gains, mlp_gain_grad, hidden, brow_in, low, attended, wo_own, wo_got, d_middle,
    q_proj_in, wqkv_in, own_in, give, parts, out_own, keys, values, k_proj, cosine, sine, rows,
    hidden_out, hidden_grad, gains_out, sums_out,
    kbuf, vbuf, kpbuf, cosbuf, sinbuf, rowbuf, dq, dk, dv, dkv, dqp, gkv, kept, bufs,
    own, mated, landed, summed, late_give, far_land, mid_land, out_buf,
    dout, q_proj, wqkv,
    gsum, gland, send, recv, pump_send, pump_recv, pump_local, local, blocksem,
):
    s, c, t = lax.axis_index(SHARD_AXIS), lax.axis_index(CTX_AXIS), lax.axis_index(TP_AXIS)
    nctx = lax.axis_size(CTX_AXIS)
    part = hidden.shape[0]
    half = rows.shape[2] // 2
    f32, bf16 = jnp.float32, jnp.bfloat16
    side, across, mate = {TP_AXIS: t ^ 1}, {TP_AXIS: t ^ 2}, {SHARD_AXIS: 1 - s}
    near, opposite = {CTX_AXIS: c ^ 1}, {CTX_AXIS: c ^ 3}
    previous = {CTX_AXIS: lax.rem(c + nctx - 1, nctx)}
    outer = (c == 0) | (c == nctx - 1)
    links, locals_ = Links(send, recv), Locals(local)
    scale = HEAD_SIZE ** (-0.5)
    pump = Pump(
        (own, mated, landed, summed), (pump_send, pump_recv, pump_local),
        mate, near, opposite, outer, sums_out, MATED,
    )

    def piece(owner):
        return pl.ds(pl.multiple_of(owner * part, part), part)

    mine = pl.ds(pl.multiple_of(s * half, half), half)
    theirs = pl.ds(pl.multiple_of((1 - s) * half, half), half)

    def half_at(ref_shard, n, size):
        return pl.ds(pl.multiple_of(ref_shard * half + n * size, size), size)

    def block_copies(b):
        slot = b & 1
        pairs = (
            (keys.at[b], kbuf.at[slot]), (values.at[b], vbuf.at[slot]),
        )
        return [
            pltpu.make_async_copy(a, d, blocksem.at[6 * b + n]) for n, (a, d) in enumerate(pairs)
        ]

    def row_copies(b):
        pairs = (
            (k_proj.at[b], kpbuf), (cosine.at[b], cosbuf), (sine.at[b], sinbuf),
            (rows.at[b], rowbuf),
        )
        return [
            pltpu.make_async_copy(a, d, blocksem.at[6 * b + 2 + n])
            for n, (a, d) in enumerate(pairs)
        ]

    def row_fetch(b):
        for copy in row_copies(b):
            copy.start()

    def fetch(b):
        for copy in block_copies(b):
            copy.start()

    def fetched(b):
        for copy in block_copies(b):
            copy.wait()

    brow_load = locals_.start(brow_in, rowbuf.at[piece(t), :])
    loads = [locals_.start(own_in, own.at[0:EARLY])]
    wo_loads = []
    for j in range(2):
        at = slice(j * 256, j * 256 + 256)
        wo_loads.append(locals_.start(wo_own.at[at, :], bufs.at[1, j, :, mine]))
        wo_loads.append(locals_.start(wo_got.at[at, :], bufs.at[1, j, :, theirs]))
    for h in range(4):
        wo_loads.append(locals_.start(attended.at[:, h * 128 : h * 128 + 128], dq.at[h]))
    wo_loads.append(locals_.start(low, dkv))
    out_loads = [locals_.start(parts.at[1], out_buf.at[0]), locals_.start(out_own, kept.at[1])]

    @pl.when(c >= 2)
    def _():
        fetch(2)

    @pl.when(c >= 1)
    def _():
        fetch(1)

    @pl.when(c <= 1)
    def _():
        fetch(0)

    late_loads = [locals_.start(q_proj_in, q_proj), locals_.start(wqkv_in, wqkv)]
    enter([side, across, mate, near, opposite])

    def send_early(first, count):
        for u in range(first, min(first + count, EARLY)):
            pump.to_mate(u, give.at[u - MATED]).start()

    send_early(MATED, 4)
    here, there = rowbuf.at[piece(t), :], rowbuf.at[piece(t ^ 2), :]
    b_over, b_near = links.copy(here, here, across), links.copy(here, here, side)
    b_on = links.copy(there, there, side)
    locals_.wait(brow_load)
    b_over.start()
    b_near.start()
    out_far = links.copy(parts.at[0], out_buf.at[1], side)
    out_over = links.copy(out_buf.at[0], out_buf.at[2], across)
    out_near = links.copy(parts.at[2], out_buf.at[3], side)
    out_far.start()
    out_near.start()
    scatters = [
        Scatter(links, bufs.at[0], side, across),
        Scatter(links, bufs.at[1], side, across),
        Scatter(links, bufs.at[0], side, across),
    ]
    far_copy = links.copy(out_buf.at[0], far_land, previous)
    mid_copy = links.copy(out_buf.at[1], mid_land, previous)
    for copy in loads:
        locals_.wait(copy)
    pump.slot(0)
    send_early(MATED + 4, 2)
    gkv[...] = jnp.zeros(gkv.shape, f32)
    gsum[...] = jnp.zeros(gsum.shape, f32)
    gsum[1:2, :] = mlp_gain_grad[0:1, :]
    q_gain = gains[2:3, 0:HEAD_SIZE]
    k_gain = gains[3:4, 0:HEAD_SIZE]
    def attended_back(owner):
        at = piece(owner)
        for j in range(2):
            got = last_dot(rowbuf[at, :], bufs[1, j]).astype(bf16)
            for hh in range(2):
                h = 2 * j + hh
                head = got[:, hh * 128 : hh * 128 + 128]
                delta = -jnp.sum(head.astype(f32) * dq[h, at, :], axis=1, keepdims=True)
                top = delta.astype(bf16).astype(f32)
                lane = lax.broadcasted_iota(jnp.int32, (part, HEAD_SIZE), 1)
                extra = jnp.where(lane == 0, top, jnp.where(lane == 1, delta - top, 0.0))
                dout[h, at, 0:128] = head
                dout[h, at, 128:256] = extra.astype(bf16)

    for copy in wo_loads:
        locals_.wait(copy)
    b_near.wait_recv()

    @pl.loop(0, 2)
    def _(n):
        attended_back(t ^ n)

    for copy in out_loads:
        locals_.wait(copy)
    out_far.wait_recv()
    out_buf[0] = out_buf[0] + out_buf[1]
    pump.slot(1)
    send_early(MATED + 6, 2)
    b_over.wait_recv()
    b_on.start()
    out_over.start()
    b_on.wait_recv()

    @pl.loop(2, 4)
    def _(n):
        attended_back(t ^ n)

    for copy in (b_over, b_near, b_on):
        copy.wait_send()
    for n in range(2):
        at = slice(n * 256, n * 256 + 256)
        for columns, target, first in ((theirs, late_give, 0), (mine, own, EARLY)):
            got = first_dot(dkv[:, at], rowbuf[:, columns]).astype(bf16)
            for e in range(2):
                target[first + 2 * n + e] = got[e * 128 : e * 128 + 128]
    for n in range(4):
        pump.to_mate(EARLY + n, late_give.at[n]).start()
    dq[...] = jnp.zeros(dq.shape, f32)
    for b in range(3):
        pl.when((c == b) if b < 2 else (c >= b))(functools.partial(row_fetch, b))
    pump.slot(2)
    send_early(MATED + 8, 6)

    def tile(b, g, r, kc, bound):
        slot = b & 1
        q_at = pl.ds(pl.multiple_of(r * 512, 512), 512)
        k_at = pl.ds(pl.multiple_of(kc * 512, 512), 512)
        kk, vv = kbuf[slot, g, k_at, :], vbuf[slot, g, k_at, :]
        dv_new, dk_new = [], []
        for hh in range(2):
            h = 2 * g + hh
            qq, do = query[h, q_at, :], dout[h, q_at, :]
            p = jnp.exp2(last_dot(qq, kk) * SCORE_STEP)
            if bound is not None:
                ahead = lax.broadcasted_iota(jnp.int32, p.shape, 0) - lax.broadcasted_iota(
                    jnp.int32, p.shape, 1
                )
                p = jnp.where(ahead >= bound, p, 0.0)
            ds = (p * last_dot(do, vv)).astype(bf16)
            dv_new.append(first_dot(do[:, 0:HEAD_SIZE], p.astype(bf16)))
            dk_new.append(first_dot(qq[:, 0:HEAD_SIZE], ds))
            dq[h, q_at, :] += flat_dot(ds, kk[:, 0:HEAD_SIZE])
        dv[g, :, k_at] += dv_new[0] + dv_new[1]
        dk[g, :, k_at] += dk_new[0] + dk_new[1]

    def clear():
        dk[...] = jnp.zeros(dk.shape, f32)
        dv[...] = jnp.zeros(dv.shape, f32)

    def norm_back(grad, u, gain, cos, sin, row):
        turned = grad * cos - pltpu.roll(grad, HEAD_SIZE // 2, 1) * sin
        r = lax.rsqrt(jnp.mean(u * u, axis=-1, keepdims=True) + norm_eps)
        gsum[row : row + 1, 0:HEAD_SIZE] += jnp.sum(turned * u * r, axis=0, keepdims=True)
        scaled = turned * gain
        inner = jnp.mean(scaled * u, axis=-1, keepdims=True)
        return (r * scaled - u * (r * r * r) * inner).astype(bf16)

    def finish_kv(b):
        for copy in row_copies(b)[:3]:
            copy.wait()

        @pl.loop(0, 4)
        def _(n):
            at = piece(n)
            cos, sin = cosbuf[at, :], sinbuf[at, :]
            for g in range(2):
                lanes = slice(g * 128, g * 128 + 128)
                u = kpbuf[at, lanes]
                dkv[at, lanes] = norm_back(dk[g, :, at].T * scale, u, k_gain, cos, sin, 3)
                dkv[at, 256 + g * 128 : 384 + g * 128] = dv[g, :, at].T.astype(bf16)

        row_copies(b)[3].wait()

        @pl.loop(0, 4)
        def _(n):
            at = piece(n)
            gkv[at, :] += first_dot(rowbuf[:, at], dkv[...])

    def kv_part(owner):
        return last_dot(dkv[piece(owner), :], wqkv[:, 512:1024])

    def all_part(owner):
        return kv_part(owner) + last_dot(dqp[piece(owner), :], wqkv[:, 0:512])

    def scatter(which, slot, partial):
        which.put_far(partial(t ^ 3))
        which.put_over(partial(t ^ 2))
        which.put_near(partial(t ^ 1))
        kept[slot] = partial(t)

    for copy in late_loads:
        locals_.wait(copy)

    @pl.when(c >= 2)
    def _():
        fetched(2)
        clear()

    @pl.loop(0, 6)
    def _(n):
        m = lax.rem(n, 3)

        @pl.when(c >= 2)
        def _():
            tile(2, n // 3, m // 2, (m + 1) // 2, None)

        @pl.when(m == 2)
        def _():
            pump.slot(3 + n // 3)

    @pl.when(c >= 2)
    def _():
        finish_kv(2)
        fetch(0)
        row_fetch(1)
        scatter(scatters[2], 0, kv_part)

    out_near.wait_recv()
    out_over.wait_recv()
    out_buf[3] = (kept[1] + out_buf[2].astype(f32) + out_buf[3].astype(f32)).astype(bf16)
    locals_.start(out_buf.at[3], hidden_out)
    out_far.wait_send()
    out_over.wait_send()
    out_near.wait_send()
    pump.slot(5)

    @pl.when(c >= 1)
    def _():
        fetched(1)
        clear()

    @pl.loop(0, 8)
    def _(n):
        m = lax.rem(n, 4)

        @pl.when(c >= 1)
        def _():
            tile(1, n // 4, m // 2, m & 1, None)

        @pl.when(m == 3)
        def _():
            pump.slot(6 + n // 4)

    @pl.when(c >= 1)
    def _():
        finish_kv(1)
        row_fetch(0)

    @pl.when(c >= 2)
    def _():
        out_buf[0] = scatters[2].total(kept[0]).astype(bf16)
        far_copy.start()
        scatters[2].close()

    @pl.when(c >= 1)
    def _():
        scatter(scatters[1], 1, kv_part)

    pump.slot(8)
    fetched(0)
    clear()

    @pl.loop(0, 6)
    def _(n):
        m = lax.rem(n, 3)
        tile(0, n // 3, (m + 1) // 2, m // 2, (m & 1) * -512)

        @pl.when(n == 3)
        def _():
            pump.slot(9)

    finish_kv(0)

    @pl.loop(0, 4)
    def _(n):
        at = piece(n)
        cos, sin = cosbuf[at, :], sinbuf[at, :]
        for h in range(4):
            lanes = slice(h * 128, h * 128 + 128)
            u = q_proj[at, lanes]
            dqp[at, lanes] = norm_back(dq[h, at, :] * scale, u, q_gain, cos, sin, 2)

    for n in range(4):
        late_give[4 + n] = gkv[half_at(1 - s, n, 128), :].astype(bf16)
        pump.to_mate(LATE + n, late_give.at[4 + n]).start()
    for n in range(2):
        got = first_dot(rowbuf[:, half_at(1 - s, n, 256)], dqp[...]).astype(bf16)
        for e in range(2):
            late_give[8 + 2 * n + e] = got[e * 128 : e * 128 + 128]
            pump.to_mate(LATE + 4 + 2 * n + e, late_give.at[8 + 2 * n + e]).start()
    pump.slot(10)

    @pl.when((c >= 1) & (c < nctx - 1))
    def _():
        far_copy.wait_recv()
        kept[1] += far_land[...].astype(f32)

    @pl.when(c >= 1)
    def _():
        out_buf[1] = scatters[1].total(kept[1]).astype(bf16)
        mid_copy.start()
        scatters[1].close()

    base = locals_.start(d_middle, kept.at[1])
    hidden_load = locals_.start(hidden, out_buf.at[2])
    scatter(scatters[0], 0, all_part)
    for n in range(2):
        rows_of = gkv[half_at(s, n, 256), :].astype(bf16)
        got = first_dot(rowbuf[:, half_at(s, n, 256)], dqp[...]).astype(bf16)
        for e in range(2):
            at = slice(e * 128, e * 128 + 128)
            own[LATE + 2 * n + e] = rows_of[at]
            own[LATE + 4 + 2 * n + e] = got[at]
    for u in (LATE - 2, LATE - 1):
        pump.second(u)
    for u in (LATE - 4, LATE - 3):
        pump.third(u)

    pl.loop(0, LATE - 6)(pump.fourth)

    def finish_rows():
        @pl.when(c < nctx - 1)
        def _():
            mid_copy.wait_recv()
            kept[0] += mid_land[...].astype(f32)

        kept[0] = scatters[0].total(kept[0])
        locals_.wait(hidden_load)
        locals_.wait(base)
        x = out_buf[2].astype(f32)
        r = lax.rsqrt(jnp.mean(x * x, axis=-1, keepdims=True) + norm_eps)
        d_in = kept[0]
        gsum[0:1, :] = jnp.sum(d_in * x * r, axis=0, keepdims=True)
        scaled = d_in * gains[0:1, :]
        inner = jnp.mean(scaled * x, axis=-1, keepdims=True)
        kept[1] += r * scaled - x * (r * r * r) * inner
        locals_.start(kept.at[1], hidden_grad)

    swaps = [
        links.copy(gsum, gland.at[n], device)
        for n, device in enumerate((side, across, mate, near, opposite))
    ]

    for n, u in enumerate(range(LATE, UNITS)):
        pump.first(u)
        if n >= 1:
            pump.second(u - 1)
        pump.third(u - 2)
        if n == 2:
            finish_rows()
        if n >= 3:
            swap = n - 3
            if swap > 0:
                swaps[swap - 1].wait()
                gsum[...] += gland[swap - 1]
            swaps[swap].start()
    pump.second(UNITS - 1)
    pump.third(UNITS - 2)
    swaps[4].wait()
    gsum[...] += gland[4]
    locals_.start(gsum, gains_out)
    scatters[0].close()
    pump.third(UNITS - 1)

    @pl.when(c >= 2)
    def _():
        far_copy.wait_send()

    @pl.when(c >= 1)
    def _():
        mid_copy.wait_send()

    @pl.loop(MATED, EARLY)
    def _(u):
        pump.to_mate(u, give.at[u - MATED]).wait_send()

    @pl.loop(EARLY, UNITS)
    def _(u):
        pump.to_mate(u, late_give.at[u - EARLY]).wait_send()

    pl.loop(LATE - 6, UNITS)(pump.fourth)
    pump.close()
    locals_.finish()


def backward_call(vmem_args, any_args):
    hidden = any_args[0]
    part, width = hidden.shape
    block = 4 * part
    f32, bf16 = jnp.float32, jnp.bfloat16
    shape = jax.ShapeDtypeStruct
    outs = (
        shape((part, width), bf16),
        shape((part, width), f32),
        shape((8, width), f32),
        shape((UNITS, 128, 512), bf16),
    )
    tile = pltpu.VMEM((part, width), bf16)
    units = pltpu.VMEM((UNITS, 128, 512), bf16)
    return pl.pallas_call(
        backward_kernel,
        name="backward",
        out_shape=outs,
        in_specs=[VMEM_SPEC] * 3 + [ANY_SPEC] * len(any_args),
        out_specs=[ANY_SPEC] * len(outs),
        scratch_shapes=[
            pltpu.VMEM((2, 2, block, 256), bf16),
            pltpu.VMEM((2, 2, block, 256), bf16),
            pltpu.VMEM((block, 256), f32),
            pltpu.VMEM((block, HEAD_SIZE), f32),
            pltpu.VMEM((block, HEAD_SIZE), f32),
            pltpu.VMEM((block, width), bf16),
            pltpu.VMEM((4, block, HEAD_SIZE), f32),
            pltpu.VMEM((2, HEAD_SIZE, block), f32),
            pltpu.VMEM((2, HEAD_SIZE, block), f32),
            pltpu.VMEM((block, 512), bf16),
            pltpu.VMEM((block, 512), bf16),
            pltpu.VMEM((width, 512), f32),
            pltpu.VMEM((2, part, width), f32),
            pltpu.VMEM((2, 6, part, width), bf16),
            units,
            pltpu.VMEM((UNITS - MATED, 128, 512), bf16),
            units,
            units,
            pltpu.VMEM((UNITS - EARLY, 128, 512), bf16),
            tile, tile,
            pltpu.VMEM((4, part, width), bf16),
            pltpu.VMEM((4, block, 256), bf16),
            pltpu.VMEM((block, 512), f32),
            pltpu.VMEM((width, 1024), bf16),
            pltpu.VMEM((8, width), f32),
            pltpu.VMEM((5, 8, width), f32),
            pltpu.SemaphoreType.DMA((22,)),
            pltpu.SemaphoreType.DMA((22,)),
            pltpu.SemaphoreType.DMA((4 * UNITS,)),
            pltpu.SemaphoreType.DMA((4 * UNITS,)),
            pltpu.SemaphoreType.DMA((UNITS,)),
            pltpu.SemaphoreType.DMA((20,)),
            pltpu.SemaphoreType.DMA((18,)),
        ],
        compiler_params=pltpu.CompilerParams(
            collective_id=2, has_side_effects=True, vmem_limit_bytes=60 << 20
        ),
    )(*vmem_args, *any_args)


def result_kernel(
    chunks_in, gains, grad_in, hidden_in,
    grad_out, hidden_out, attn, wq, wk, wv, q_gain, k_gain, wo, mlp, wg, wu, wd,
    buf, q, k, v, o, gate, up, down, grad, hidden, inside, outside,
):
    shard = lax.axis_index(SHARD_AXIS)
    count = buf.shape[0]
    whole = [
        pltpu.make_async_copy(grad_in, grad, inside.at[count]),
        pltpu.make_async_copy(hidden_in, hidden, inside.at[count + 1]),
    ]
    loads = [pltpu.make_async_copy(chunks_in.at[n], buf.at[n], inside.at[n]) for n in range(count)]
    for copy in whole + loads:
        copy.start()
    stores = []

    def put(n, ref, out, row, lanes):
        at = (slice(row, row + 256), lanes)
        stores.append(pltpu.make_async_copy(ref.at[at], out.at[at], outside.at[len(stores)]))
        stores[-1].start()

    for copy in whole:
        copy.wait()
    for n, (ref, out) in enumerate(((grad, grad_out), (hidden, hidden_out))):
        whole[n] = pltpu.make_async_copy(ref, out, outside.at[count + n])
        whole[n].start()
    for n in range(count):
        loads[n].wait()
        values = buf[n].astype(jnp.float32)
        every = slice(0, 512)
        if n < 3:
            down[n * 256 : n * 256 + 256, :] = values
            put(n, down, wd, n * 256, every)
        elif n < 9:
            ref, out, j = (gate, wg, n - 3) if n < 6 else (up, wu, n - 6)
            lanes = slice(j * 256, j * 256 + 256)
            ref[0:256, lanes] = values[:, 0:256]
            ref[256:512, lanes] = values[:, 256:512]
            at = (slice(0, 512), lanes)
            stores.append(pltpu.make_async_copy(ref.at[at], out.at[at], outside.at[len(stores)]))
            stores[-1].start()
        elif n < 11:
            o[(n - 9) * 256 : (n - 8) * 256, :] = values
            put(n, o, wo, (n - 9) * 256, every)
        elif n < 13:
            row = (n - 11) * 256
            k[row : row + 256, :] = values[:, 0:256]
            v[row : row + 256, :] = values[:, 256:512]
        else:
            q[(n - 13) * 256 : (n - 12) * 256, :] = values
            put(n, q, wq, (n - 13) * 256, every)
    for ref, out in ((k, wk), (v, wv)):
        stores.append(pltpu.make_async_copy(ref, out, outside.at[len(stores)]))
        stores[-1].start()
    wide, small = attn.shape[1], q_gain.shape[1]
    first = shard == 0
    attn[...] = jnp.where(first, gains[0:1, 0:wide], gains[0:1, wide : 2 * wide])
    mlp[...] = jnp.where(first, gains[1:2, 0:wide], gains[1:2, wide : 2 * wide])
    q_gain[...] = jnp.where(first, gains[2:3, 0:small], gains[2:3, small : 2 * small])
    k_gain[...] = jnp.where(first, gains[3:4, 0:small], gains[3:4, small : 2 * small])
    for copy in stores + whole:
        copy.wait()


def result_call(chunks, gains, grad_hidden, out_hidden):
    part, width = grad_hidden.shape
    f32 = jnp.float32
    shape = jax.ShapeDtypeStruct
    half = width // 2
    q, k, v, o = (half, 512), (half, 256), (half, 256), (512, half)
    gate, up, down = (half, 768), (half, 768), (768, half)
    sizes = [q, k, v, (1, 64), (1, 64), o, (1, half), gate, up, down]
    outs = [shape((part, width), f32), shape((part, width), out_hidden.dtype), shape((1, half), f32)]
    outs += [shape(z, f32) for z in sizes]
    specs = [ANY_SPEC] * 2 + [VMEM_SPEC] + [ANY_SPEC] * 3 + [VMEM_SPEC] * 2 + [ANY_SPEC, VMEM_SPEC]
    return pl.pallas_call(
        result_kernel,
        name="result",
        out_shape=outs,
        in_specs=[ANY_SPEC, VMEM_SPEC, ANY_SPEC, ANY_SPEC],
        out_specs=specs + [ANY_SPEC] * 3,
        scratch_shapes=[pltpu.VMEM((CHUNKS, 256, 512), jnp.bfloat16)]
        + [pltpu.VMEM(z, f32) for z in (q, k, v, o, gate, up, down)]
        + [pltpu.VMEM((part, width), f32), pltpu.VMEM((part, width), out_hidden.dtype)]
        + [pltpu.SemaphoreType.DMA((CHUNKS + 2,)), pltpu.SemaphoreType.DMA((CHUNKS + 2,))],
        compiler_params=pltpu.CompilerParams(vmem_limit_bytes=60 << 20),
    )(chunks, gains, grad_hidden, out_hidden)


def fast_device(
    hidden,
    segments,
    cotangent,
    attn_gain,
    w_query,
    key_weight_matrix,
    value_weight_matrix,
    query_gain,
    key_gain,
    mixer_exit_coefficients,
    mlp_gain,
    w_gate,
    w_up,
    w_down,
):
    gains_own = jnp.concatenate([attn_gain, mlp_gain, query_gain, key_gain])[None]
    exponents = 2.0 * (np.arange(HEAD_SIZE) % (HEAD_SIZE // 2)) / HEAD_SIZE
    rates = np.power(rope_base, -exponents).astype(np.float32)[None]
    labels = segments.reshape(-1, HEAD_SIZE)
    (gains, rows, q_proj, k_proj, query, keys, values, cosine, sine, attended, low, wqkv, crows,
     wo_got, wg_got, wu_got) = forward_call(
        hidden[0], cotangent[0], gains_own, labels, jnp.asarray(rates), w_query, key_weight_matrix,
        value_weight_matrix, mixer_exit_coefficients, w_gate, w_up,
    )
    def units(chunks, count):
        return chunks.reshape(count, 128, 512)

    d_middle, mlp_gain_grad, brow, own, give, parts, out_own = mlp_call(
        (low, hidden[0], gains),
        (crows, mixer_exit_coefficients, wo_got, w_gate, wg_got, w_up, wu_got, w_down),
    )
    out_hidden, grad_hidden, sums, chunks = backward_call(
        (query, gains, mlp_gain_grad),
        (hidden[0], brow, low, attended, mixer_exit_coefficients, wo_got, d_middle, q_proj, wqkv, units(own, EARLY), units(give, EARLY - MATED),
         parts, out_own, keys, values, k_proj, cosine, sine, rows),
    )
    (grad_hidden, out_hidden, attn, wq, wk, wv, q_gain, k_gain, wo, mlp, wg, wu, wd) = result_call(
        chunks.reshape(CHUNKS, 256, 512), sums, grad_hidden, out_hidden
    )
    return (
        out_hidden[None], grad_hidden[None], attn[0], wq, wk, wv, q_gain[0], k_gain[0], wo, mlp[0],
        wg, wu, wd,
    )


def per_device(
    hidden,
    segments,
    cotangent,
    attn_gain,
    w_query,
    key_weight_matrix,
    value_weight_matrix,
    query_gain,
    key_gain,
    mixer_exit_coefficients,
    mlp_gain,
    w_gate,
    w_up,
    w_down,
):
    collected_rows = (
        lax.all_gather(attn_gain, SHARD_AXIS, axis=0, tiled=True),
        lax.all_gather(w_query, SHARD_AXIS, axis=0, tiled=True),
        lax.all_gather(key_weight_matrix, SHARD_AXIS, axis=0, tiled=True),
        lax.all_gather(value_weight_matrix, SHARD_AXIS, axis=0, tiled=True),
        lax.all_gather(query_gain, SHARD_AXIS, axis=0, tiled=True),
        lax.all_gather(key_gain, SHARD_AXIS, axis=0, tiled=True),
        lax.all_gather(mixer_exit_coefficients, SHARD_AXIS, axis=1, tiled=True),
        lax.all_gather(mlp_gain, SHARD_AXIS, axis=0, tiled=True),
        lax.all_gather(w_gate, SHARD_AXIS, axis=0, tiled=True),
        lax.all_gather(w_up, SHARD_AXIS, axis=0, tiled=True),
        lax.all_gather(w_down, SHARD_AXIS, axis=1, tiled=True),
    )
    gain_attn = collected_rows[0].astype(jnp.float32)
    gain_query = collected_rows[4].astype(jnp.float32)
    gain_key = collected_rows[5].astype(jnp.float32)
    gain_mlp = collected_rows[7].astype(jnp.float32)
    seq_count = hidden.shape[0]
    block_rows = hidden.shape[1] * lax.axis_size(TP_AXIS)
    seq_length = segments.shape[1]
    ctx_index = lax.axis_index(CTX_AXIS)
    heads_local = w_query.shape[1] // HEAD_SIZE
    kv_local = key_weight_matrix.shape[1] // HEAD_SIZE
    query_group_width = heads_local // kv_local
    score_scale = HEAD_SIZE ** (-0.5)
    block_start = ctx_index * block_rows
    query_pos = block_start + jnp.arange(block_rows, dtype=jnp.int32)
    query_seg = lax.dynamic_slice_in_dim(segments, block_start, block_rows, 1)
    positions = lax.dynamic_slice_in_dim(doc_positions(segments), block_start, block_rows, 1)
    cosine, sine_part = rope_tables(positions)

    def counting_keys(key_first, step_rows):
        early = key_first <= block_start + block_rows - 1
        last_seg = lax.dynamic_slice_in_dim(segments, key_first + step_rows - 1, 1, 1)[:, 0]
        return early & jnp.any(last_seg >= query_seg[:, 0])

    inputs = hidden.astype(jnp.float32)
    scale_one = rms_scale(inputs)
    attention_input = (inputs * scale_one * gain_attn).astype(jnp.bfloat16)
    attention_rows = tp_rows(attention_input)
    q_proj = jnp.einsum(
        "zjr,rm->zjm", attention_rows, collected_rows[1], preferred_element_type=jnp.float32
    ).reshape(seq_count, block_rows, heads_local, HEAD_SIZE)
    key_projected = jnp.einsum(
        "zjr,rm->zjm", attention_rows, collected_rows[2], preferred_element_type=jnp.float32
    ).reshape(seq_count, block_rows, kv_local, HEAD_SIZE)
    value_projected = jnp.einsum(
        "zjr,rm->zjm", attention_rows, collected_rows[3], preferred_element_type=jnp.float32
    )
    q_scale = rms_scale(q_proj)
    k_scale = rms_scale(key_projected)
    query_rows_input = (
        rotate(q_proj * q_scale * gain_query, cosine, sine_part)
        .astype(jnp.bfloat16)
        .reshape(seq_count, block_rows, kv_local, query_group_width, HEAD_SIZE)
    )
    keys = rotate(key_projected * k_scale * gain_key, cosine, sine_part).astype(jnp.bfloat16)
    values = value_projected.astype(jnp.bfloat16).reshape(
        seq_count, block_rows, kv_local, HEAD_SIZE
    )
    stat_shape = (seq_count, kv_local, query_group_width, block_rows)
    start_state = (
        jnp.full(stat_shape, masked_fill, jnp.float32),
        jnp.zeros(stat_shape, jnp.float32),
        jnp.zeros(stat_shape + (HEAD_SIZE,), jnp.float32),
    )
    piece_keys = lax.all_gather(keys, CTX_AXIS, axis=1, tiled=True)
    piece_values = lax.all_gather(values, CTX_AXIS, axis=1, tiled=True)
    piece_rows = piece_keys.shape[1]
    step_rows = math.gcd(piece_rows, 1024)

    def attend_one_step(number, loop_state):
        offset = number * step_rows
        key_first = offset

        def attend_compute(state):
            row_max, row_total, summed = state
            key_part = lax.dynamic_slice_in_dim(piece_keys, offset, step_rows, 1)
            value_part = lax.dynamic_slice_in_dim(piece_values, offset, step_rows, 1)
            allowed = key_block(segments, key_first, step_rows, query_pos, query_seg)
            scores = (
                jnp.einsum(
                    "sqhgd,skhd->shgqk",
                    query_rows_input,
                    key_part,
                    preferred_element_type=jnp.float32,
                )
                * score_scale
            )
            masked = jnp.where(allowed, scores, masked_fill)
            new_max = jnp.maximum(row_max, jnp.max(masked, axis=-1))
            weights = jnp.where(allowed, jnp.exp(masked - new_max[..., None]), 0.0)
            decay_factor = jnp.exp(row_max - new_max)
            row_total = row_total * decay_factor + jnp.sum(weights, axis=-1)
            summed = summed * decay_factor[..., None] + jnp.einsum(
                "shgqk,skhd->shgqd",
                weights.astype(jnp.bfloat16),
                value_part,
                preferred_element_type=jnp.float32,
            )
            return (new_max, row_total, summed)

        return lax.cond(counting_keys(key_first, step_rows), attend_compute, keep_state, loop_state)

    row_max, row_total, summed = lax.fori_loop(
        0, piece_rows // step_rows, attend_one_step, start_state
    )
    attended = summed / row_total[..., None]
    log_total = row_max + jnp.log(row_total)
    attended_reduced_copy = (
        attended.transpose(0, 3, 1, 2, 4)
        .reshape(seq_count, block_rows, heads_local * HEAD_SIZE)
        .astype(jnp.bfloat16)
    )
    branch = tp_total(
        jnp.einsum(
            "vkq,qy->vky",
            attended_reduced_copy,
            collected_rows[6],
            preferred_element_type=jnp.float32,
        )
    )
    middle = inputs + branch
    scale_two = rms_scale(middle)
    mlp_in = (middle * scale_two * gain_mlp).astype(jnp.bfloat16)
    mlp_rows = tp_rows(mlp_in)
    gate = jnp.einsum(
        "snd,df->snf", mlp_rows, collected_rows[8], preferred_element_type=jnp.float32
    )
    upward = jnp.einsum(
        "snd,df->snf", mlp_rows, collected_rows[9], preferred_element_type=jnp.float32
    )
    activated = (jax.nn.silu(gate) * upward).astype(jnp.bfloat16)
    out_hidden = (
        middle
        + tp_total(
            jnp.einsum(
                "snf,fd->snd", activated, collected_rows[10], preferred_element_type=jnp.float32
            )
        )
    ).astype(jnp.bfloat16)
    again = (
        lax.all_gather(attn_gain, SHARD_AXIS, axis=0, tiled=True),
        lax.all_gather(w_query, SHARD_AXIS, axis=0, tiled=True),
        lax.all_gather(key_weight_matrix, SHARD_AXIS, axis=0, tiled=True),
        lax.all_gather(value_weight_matrix, SHARD_AXIS, axis=0, tiled=True),
        lax.all_gather(query_gain, SHARD_AXIS, axis=0, tiled=True),
        lax.all_gather(key_gain, SHARD_AXIS, axis=0, tiled=True),
        lax.all_gather(mixer_exit_coefficients, SHARD_AXIS, axis=1, tiled=True),
        lax.all_gather(mlp_gain, SHARD_AXIS, axis=0, tiled=True),
        lax.all_gather(w_gate, SHARD_AXIS, axis=0, tiled=True),
        lax.all_gather(w_up, SHARD_AXIS, axis=0, tiled=True),
        lax.all_gather(w_down, SHARD_AXIS, axis=1, tiled=True),
    )
    query_backward = again[1]
    lookup_pullback = again[2]
    value_backward = again[3]
    output_backward = again[6]
    back_gate = again[8]
    back_up = again[9]
    back_down = again[10]
    d_out = cotangent.astype(jnp.float32)
    d_rows = tp_rows(cotangent)
    grad_down = jnp.einsum("snf,snd->fd", activated, d_rows, preferred_element_type=jnp.float32)
    d_act = jnp.einsum("snd,fd->snf", d_rows, back_down, preferred_element_type=jnp.float32)
    sigmoid_gate = jax.nn.sigmoid(gate)
    d_upward = (d_act * jax.nn.silu(gate)).astype(jnp.bfloat16)
    d_gate = (d_act * upward * sigmoid_gate * (1.0 + gate * (1.0 - sigmoid_gate))).astype(
        jnp.bfloat16
    )
    grad_gate = jnp.einsum("snd,snf->df", mlp_rows, d_gate, preferred_element_type=jnp.float32)
    grad_up = jnp.einsum("snd,snf->df", mlp_rows, d_upward, preferred_element_type=jnp.float32)
    d_mlp_in = tp_total(
        jnp.einsum("snf,df->snd", d_gate, back_gate, preferred_element_type=jnp.float32)
        + jnp.einsum("snf,df->snd", d_upward, back_up, preferred_element_type=jnp.float32)
    )
    grad_mlp_gain = jnp.sum(d_mlp_in * middle * scale_two, axis=(0, 1))
    d_middle = d_out + rms_back(d_mlp_in, middle, scale_two, gain_mlp)
    d_branch = d_middle.astype(jnp.bfloat16)
    residual_branch_rows = tp_rows(d_branch)
    result_cotangent = jnp.einsum(
        "xbj,xbk->jk",
        attended_reduced_copy,
        residual_branch_rows,
        preferred_element_type=jnp.float32,
    )
    d_attended = (
        jnp.einsum(
            "miv,cv->mic", residual_branch_rows, output_backward, preferred_element_type=jnp.float32
        )
        .astype(jnp.bfloat16)
        .reshape(seq_count, block_rows, kv_local, query_group_width, HEAD_SIZE)
    )
    delta = jnp.sum(d_attended.astype(jnp.float32).transpose(0, 2, 3, 1, 4) * attended, axis=-1)
    query_zeros = jnp.zeros(
        (seq_count, block_rows, kv_local, query_group_width, HEAD_SIZE), jnp.float32
    )
    back_state = (
        query_zeros,
        jnp.zeros((seq_count, seq_length, kv_local, HEAD_SIZE), jnp.float32),
        jnp.zeros((seq_count, seq_length, kv_local, HEAD_SIZE), jnp.float32),
    )
    back_piece_keys = lax.all_gather(keys, CTX_AXIS, axis=1, tiled=True)
    back_piece_values = lax.all_gather(values, CTX_AXIS, axis=1, tiled=True)
    piece_rows = back_piece_keys.shape[1]
    back_step_rows = math.gcd(piece_rows, 1024)

    def back_one_step(number, loop_state):
        offset = number * back_step_rows
        key_first = offset
        write_at = offset

        def back_compute(state):
            d_query, d_keys, d_values = state
            key_part = lax.dynamic_slice_in_dim(back_piece_keys, offset, back_step_rows, 1)
            value_part = lax.dynamic_slice_in_dim(back_piece_values, offset, back_step_rows, 1)
            allowed = key_block(segments, key_first, back_step_rows, query_pos, query_seg)
            scores = (
                jnp.einsum(
                    "sqhgd,skhd->shgqk",
                    query_rows_input,
                    key_part,
                    preferred_element_type=jnp.float32,
                )
                * score_scale
            )
            probs = jnp.where(allowed, jnp.exp(scores - log_total[..., None]), 0.0)
            d_probs = jnp.einsum(
                "sqhgd,skhd->shgqk", d_attended, value_part, preferred_element_type=jnp.float32
            )
            d_scores = (probs * (d_probs - delta[..., None])).astype(jnp.bfloat16)
            d_query = d_query + jnp.einsum(
                "shgqk,skhd->sqhgd", d_scores, key_part, preferred_element_type=jnp.float32
            )
            key_grad = jnp.einsum(
                "shgqk,sqhgd->skhd", d_scores, query_rows_input, preferred_element_type=jnp.float32
            )
            value_grad = jnp.einsum(
                "shgqk,sqhgd->skhd",
                probs.astype(jnp.bfloat16),
                d_attended,
                preferred_element_type=jnp.float32,
            )
            d_keys = lax.dynamic_update_slice_in_dim(
                d_keys,
                lax.dynamic_slice_in_dim(d_keys, write_at, back_step_rows, 1) + key_grad,
                write_at,
                1,
            )
            d_values = lax.dynamic_update_slice_in_dim(
                d_values,
                lax.dynamic_slice_in_dim(d_values, write_at, back_step_rows, 1) + value_grad,
                write_at,
                1,
            )
            return (d_query, d_keys, d_values)

        return lax.cond(
            counting_keys(key_first, back_step_rows), back_compute, keep_state, loop_state
        )

    d_query, d_keys, d_values = lax.fori_loop(
        0, piece_rows // back_step_rows, back_one_step, back_state
    )
    own_keys, own_values = (
        lax.psum_scatter(
            d_keys.astype(jnp.bfloat16), CTX_AXIS, scatter_dimension=1, tiled=True
        ).astype(jnp.float32),
        lax.psum_scatter(
            d_values.astype(jnp.bfloat16), CTX_AXIS, scatter_dimension=1, tiled=True
        ).astype(jnp.float32),
    )
    q_normed = rotate_back(
        d_query.reshape(seq_count, block_rows, heads_local, HEAD_SIZE) * score_scale,
        cosine,
        sine_part,
    )
    grad_query_gain = jnp.sum(q_normed * q_proj * q_scale, axis=(0, 1, 2))
    query_projection_gradient = (
        rms_back(q_normed, q_proj, q_scale, gain_query)
        .astype(jnp.bfloat16)
        .reshape(seq_count, block_rows, heads_local * HEAD_SIZE)
    )
    k_normed = rotate_back(own_keys * score_scale, cosine, sine_part)
    grad_key_gain = jnp.sum(k_normed * key_projected * k_scale, axis=(0, 1, 2))
    lookup_map_derivative = (
        rms_back(k_normed, key_projected, k_scale, gain_key)
        .astype(jnp.bfloat16)
        .reshape(seq_count, block_rows, kv_local * HEAD_SIZE)
    )
    value_projection_gradient = own_values.astype(jnp.bfloat16).reshape(
        seq_count, block_rows, kv_local * HEAD_SIZE
    )
    query_gradient_rows = jnp.einsum(
        "zqr,zqa->ra", attention_rows, query_projection_gradient, preferred_element_type=jnp.float32
    )
    key_gradient_rows = jnp.einsum(
        "zqr,zqa->ra", attention_rows, lookup_map_derivative, preferred_element_type=jnp.float32
    )
    value_gradient_rows = jnp.einsum(
        "zqr,zqa->ra", attention_rows, value_projection_gradient, preferred_element_type=jnp.float32
    )
    d_attn_in = tp_total(
        jnp.einsum(
            "wtl,al->wta",
            query_projection_gradient,
            query_backward,
            preferred_element_type=jnp.float32,
        )
        + jnp.einsum(
            "wtl,al->wta",
            lookup_map_derivative,
            lookup_pullback,
            preferred_element_type=jnp.float32,
        )
        + jnp.einsum(
            "wtl,al->wta",
            value_projection_gradient,
            value_backward,
            preferred_element_type=jnp.float32,
        )
    )
    grad_attn_gain = jnp.sum(d_attn_in * inputs * scale_one, axis=(0, 1))
    grad_hidden = d_middle + rms_back(d_attn_in, inputs, scale_one, gain_attn)
    reduced = (
        lax.psum_scatter(
            grad_attn_gain.astype(jnp.bfloat16), SHARD_AXIS, scatter_dimension=0, tiled=True
        ).astype(jnp.float32),
        lax.psum_scatter(
            query_gradient_rows.astype(jnp.bfloat16), SHARD_AXIS, scatter_dimension=0, tiled=True
        ).astype(jnp.float32),
        lax.psum_scatter(
            key_gradient_rows.astype(jnp.bfloat16), SHARD_AXIS, scatter_dimension=0, tiled=True
        ).astype(jnp.float32),
        lax.psum_scatter(
            value_gradient_rows.astype(jnp.bfloat16), SHARD_AXIS, scatter_dimension=0, tiled=True
        ).astype(jnp.float32),
        lax.psum_scatter(
            grad_query_gain.astype(jnp.bfloat16), SHARD_AXIS, scatter_dimension=0, tiled=True
        ).astype(jnp.float32),
        lax.psum_scatter(
            grad_key_gain.astype(jnp.bfloat16), SHARD_AXIS, scatter_dimension=0, tiled=True
        ).astype(jnp.float32),
        lax.psum_scatter(
            result_cotangent.astype(jnp.bfloat16), SHARD_AXIS, scatter_dimension=1, tiled=True
        ).astype(jnp.float32),
        lax.psum_scatter(
            grad_mlp_gain.astype(jnp.bfloat16), SHARD_AXIS, scatter_dimension=0, tiled=True
        ).astype(jnp.float32),
        lax.psum_scatter(
            grad_gate.astype(jnp.bfloat16), SHARD_AXIS, scatter_dimension=0, tiled=True
        ).astype(jnp.float32),
        lax.psum_scatter(
            grad_up.astype(jnp.bfloat16), SHARD_AXIS, scatter_dimension=0, tiled=True
        ).astype(jnp.float32),
        lax.psum_scatter(
            grad_down.astype(jnp.bfloat16), SHARD_AXIS, scatter_dimension=1, tiled=True
        ).astype(jnp.float32),
    )
    matrices = (
        lax.psum(reduced[1].astype(jnp.bfloat16), CTX_AXIS).astype(jnp.float32),
        lax.psum(reduced[2].astype(jnp.bfloat16), CTX_AXIS).astype(jnp.float32),
        lax.psum(reduced[3].astype(jnp.bfloat16), CTX_AXIS).astype(jnp.float32),
        lax.psum(reduced[6].astype(jnp.bfloat16), CTX_AXIS).astype(jnp.float32),
        lax.psum(reduced[8].astype(jnp.bfloat16), CTX_AXIS).astype(jnp.float32),
        lax.psum(reduced[9].astype(jnp.bfloat16), CTX_AXIS).astype(jnp.float32),
        lax.psum(reduced[10].astype(jnp.bfloat16), CTX_AXIS).astype(jnp.float32),
    )
    gains = lax.psum((reduced[0], reduced[4], reduced[5], reduced[7]), (CTX_AXIS, TP_AXIS))
    return (
        out_hidden,
        grad_hidden,
        gains[0],
        matrices[0],
        matrices[1],
        matrices[2],
        gains[1],
        gains[2],
        matrices[3],
        gains[3],
        matrices[4],
        matrices[5],
        matrices[6],
    )


def solution(mesh):
    in_specs = (
        P(SHARD_AXIS, (CTX_AXIS, TP_AXIS), None),
        P(SHARD_AXIS, None),
        P(SHARD_AXIS, (CTX_AXIS, TP_AXIS), None),
        P(SHARD_AXIS),
        P(SHARD_AXIS, TP_AXIS),
        P(SHARD_AXIS, TP_AXIS),
        P(SHARD_AXIS, TP_AXIS),
        P(SHARD_AXIS),
        P(SHARD_AXIS),
        P(TP_AXIS, SHARD_AXIS),
        P(SHARD_AXIS),
        P(SHARD_AXIS, TP_AXIS),
        P(SHARD_AXIS, TP_AXIS),
        P(TP_AXIS, SHARD_AXIS),
    )
    out_specs = (
        P(SHARD_AXIS, (CTX_AXIS, TP_AXIS), None),
        P(SHARD_AXIS, (CTX_AXIS, TP_AXIS), None),
        P(SHARD_AXIS),
        P(SHARD_AXIS, TP_AXIS),
        P(SHARD_AXIS, TP_AXIS),
        P(SHARD_AXIS, TP_AXIS),
        P(SHARD_AXIS),
        P(SHARD_AXIS),
        P(TP_AXIS, SHARD_AXIS),
        P(SHARD_AXIS),
        P(SHARD_AXIS, TP_AXIS),
        P(SHARD_AXIS, TP_AXIS),
        P(TP_AXIS, SHARD_AXIS),
    )
    shape = mesh.shape
    fast = shape[SHARD_AXIS] == 2 and shape[CTX_AXIS] == 4 and shape[TP_AXIS] == 4
    return jax.shard_map(
        fast_device if fast else per_device, mesh=mesh, in_specs=in_specs, out_specs=out_specs, check_vma=False
    )
```

```python
import functools
import math

import jax
import jax.numpy as jnp
import numpy as np
from jax import lax
from jax.experimental import pallas as pl
from jax.experimental.pallas import tpu as pltpu
from jax.sharding import PartitionSpec as P

SHARD_AXIS, CTX_AXIS, TP_AXIS = "shard", "ctx", "tp"
HEAD_SIZE = 128
NDOC = 8


norm_eps = 1e-06
rope_base = 1000000.0
masked_fill = -1e30


def rms_scale(values):
    return lax.rsqrt(jnp.mean(values * values, axis=-1, keepdims=True) + norm_eps)


def rms_back(grad_out, values, row_scale, gain_vec):
    scaled = grad_out * gain_vec
    inner_sum = jnp.mean(scaled * values, axis=-1, keepdims=True)
    return row_scale * scaled - values * (row_scale * row_scale * row_scale) * inner_sum


def doc_positions(segments):
    seq_width = segments.shape[-1]
    labels = jnp.arange(NDOC, dtype=jnp.int32)
    onehot = (segments[..., None] == labels).astype(jnp.int32)
    counts = jnp.sum(onehot, axis=-2)
    starts = jnp.cumsum(counts, axis=-1) - counts
    first_row = jnp.sum(onehot * starts[..., None, :], axis=-1)
    return jnp.arange(seq_width, dtype=jnp.int32) - first_row


def rope_tables(positions):
    exponents = jnp.arange(0, HEAD_SIZE, 2).astype(jnp.float32) / HEAD_SIZE
    angle_rates = jnp.power(jnp.float32(rope_base), -exponents)
    angles = positions.astype(jnp.float32)[..., None] * angle_rates
    angles = jnp.concatenate([angles, angles], axis=-1)[..., None, :]
    return (jnp.cos(angles), jnp.sin(angles))


def rotate(inputs, cosine, sine_part):
    half_dim = inputs.shape[-1] // 2
    turned = jnp.concatenate([-inputs[..., half_dim:], inputs[..., :half_dim]], axis=-1)
    return inputs * cosine + turned * sine_part


def rotate_back(grads, cosine, sine_part):
    half_dim = grads.shape[-1] // 2
    moved = grads * sine_part
    turned = jnp.concatenate([moved[..., half_dim:], -moved[..., :half_dim]], axis=-1)
    return grads * cosine + turned


def tp_rows(local_part):
    return lax.all_gather(local_part, TP_AXIS, axis=1, tiled=True)


def tp_total(partial_sum):
    return lax.psum_scatter(
        partial_sum.astype(jnp.bfloat16), TP_AXIS, scatter_dimension=1, tiled=True
    ).astype(jnp.float32)


def key_block(segments, key_first, step_rows, query_pos, query_seg):
    key_pos = key_first + jnp.arange(step_rows, dtype=jnp.int32)
    key_seg = lax.dynamic_slice_in_dim(segments, key_first, step_rows, 1)
    allowed = (key_pos[None, None, :] <= query_pos[None, :, None]) & (
        key_seg[:, None, :] == query_seg[:, :, None]
    )
    return allowed[:, None, None]


def keep_state(state):
    return state


CHUNKS = 15
FROM_MLP = 9
READY = 2
UNITS, EARLY, MATED, LATE = 2 * CHUNKS, 2 * FROM_MLP, 2 * READY, 22


MESH_ID = pl.DeviceIdType.MESH
ANY_SPEC = pl.BlockSpec(memory_space=pl.ANY)
VMEM_SPEC = pl.BlockSpec(memory_space=pltpu.VMEM)
SCORE_STEP = HEAD_SIZE ** (-0.5) * math.log2(math.e)
APART = 16384.0


def enter(peers):
    barrier = pltpu.get_barrier_semaphore()
    for peer in peers:
        pl.semaphore_signal(barrier, inc=1, device_id=peer, device_id_type=MESH_ID)
    pl.semaphore_wait(barrier, len(peers))


def last_dot(left, right):
    return lax.dot_general(
        left, right, (((1,), (1,)), ((), ())), preferred_element_type=jnp.float32
    )


def flat_dot(left, right):
    return jnp.dot(left, right, preferred_element_type=jnp.float32)


def first_dot(left, right):
    return lax.dot_general(
        left, right, (((0,), (0,)), ((), ())), preferred_element_type=jnp.float32
    )


def spin(values, cosine, sine_signed):
    return values * cosine + pltpu.roll(values, HEAD_SIZE // 2, 1) * sine_signed


class Links:
    def __init__(self, send, recv):
        self.send, self.recv, self.used = send, recv, 0

    def copy(self, src, dst, device):
        number = self.used
        self.used += 1
        return pltpu.make_async_remote_copy(
            src_ref=src, dst_ref=dst, send_sem=self.send.at[number],
            recv_sem=self.recv.at[number], device_id=device, device_id_type=MESH_ID,
        )


class Locals:
    def __init__(self, sems):
        self.sems, self.used, self.open = sems, 0, []

    def make(self, src, dst):
        copy = pltpu.make_async_copy(src, dst, self.sems.at[self.used])
        self.used += 1
        return copy

    def start(self, src, dst):
        copy = self.make(src, dst)
        copy.start()
        self.open.append(copy)
        return copy

    def wait(self, copy):
        copy.wait()
        self.open = [other for other in self.open if other is not copy]

    def finish(self):
        for copy in self.open:
            copy.wait()


def forward_kernel(
    hidden, cotangent, gains_own, segments, rates, wq, wk, wv, wo, wg, wu,
    gains_out, rows_out, q_out, k_out, query_out, keys_out, values_out, cos_out, sin_out,
    attended_out, low_out, wqkv_out, crows_out, wo_out, wg_out, wu_out,
    gains, raw, rows, wqkv, q_proj, k_proj, qaug, kaug, vaug, cosine, sine, acc, low, crows,
    gains_in, gains_land, places, send, recv, local,
):
    s, c, t = lax.axis_index(SHARD_AXIS), lax.axis_index(CTX_AXIS), lax.axis_index(TP_AXIS)
    nctx = lax.axis_size(CTX_AXIS)
    part = hidden.shape[0]
    block = 4 * part
    half = wq.shape[0]
    f32, bf16 = jnp.float32, jnp.bfloat16
    side, across, mate = {TP_AXIS: t ^ 1}, {TP_AXIS: t ^ 2}, {SHARD_AXIS: 1 - s}
    pair = {CTX_AXIS: c ^ 1}
    nxt, prv = {CTX_AXIS: lax.rem(c + 1, nctx)}, {CTX_AXIS: lax.rem(c + nctx - 1, nctx)}
    gains_in[...] = jnp.zeros(gains_in.shape, f32)
    for row in range(2):
        own_gain = gains_own[:, row * half : row * half + half].astype(f32)
        gains_in[row : row + 1, pl.ds(pl.multiple_of(s * half, half), half)] = own_gain
    small = jnp.broadcast_to(gains_own[:, 2 * half : 2 * half + HEAD_SIZE], (16, HEAD_SIZE))
    square = (HEAD_SIZE, HEAD_SIZE)
    source_lane = lax.broadcasted_iota(jnp.int32, square, 0)
    target_lane = lax.broadcasted_iota(jnp.int32, square, 1) - s * (HEAD_SIZE // 2)
    for row, first in ((2, 0), (3, HEAD_SIZE // 2)):
        chosen = (source_lane - first == target_lane) & (source_lane >= first)
        chosen = chosen & (source_lane < first + HEAD_SIZE // 2)
        placed = flat_dot(small, jnp.where(chosen, 1.0, 0.0).astype(bf16))
        gains_in[row : row + 1, 0:HEAD_SIZE] = placed[0:1]
    enter([side, across, mate, nxt, prv])
    links, locals_ = Links(send, recv), Locals(local)

    def piece(owner):
        return pl.ds(pl.multiple_of(owner * part, part), part)

    low_bit = c & 1

    def some(shard, count, size):
        return pl.ds(pl.multiple_of(shard * count + low_bit * size, size), size)

    mine = pl.ds(pl.multiple_of(s * half, half), half)
    quarter = half // 2
    gains_copy = links.copy(gains_in, gains_land, mate)
    wk_copy = links.copy(wk, wqkv.at[mine, 512:768], mate)
    wv_copy = links.copy(wv, wqkv.at[mine, 768:1024], mate)
    wq_copy = links.copy(wq, wqkv.at[mine, 0:512], mate)
    wo_copy = links.copy(
        wo.at[some(0, 0, quarter), :], wo_out.at[some(0, 0, quarter), :], mate
    )
    wo_got = wo_out.at[some(0, 0, quarter), :]
    wo_on = links.copy(wo_got, wo_got, pair)
    wg_copy = links.copy(
        wg.at[some(0, 0, quarter), :], wg_out.at[some(0, 0, quarter), :], mate
    )
    wg_got = wg_out.at[some(0, 0, quarter), :]
    wg_on = links.copy(wg_got, wg_got, pair)
    wu_copy = links.copy(
        wu.at[some(0, 0, quarter), :], wu_out.at[some(0, 0, quarter), :], mate
    )
    gains_copy.start()
    wk_copy.start()
    wv_copy.start()
    wq_copy.start()
    own_k = locals_.start(wk, wqkv.at[mine, 512:768])
    own_v = locals_.start(wv, wqkv.at[mine, 768:1024])
    own_q = locals_.start(wq, wqkv.at[mine, 0:512])
    own_c = locals_.start(cotangent, crows.at[piece(t), :])

    def source(b, owner):
        return hidden if b == 0 else raw.at[b, piece(owner)]

    to_across, to_side, on_to_side, to_next = [], [], [], []
    for b in range(3):
        there = raw.at[b, piece(t ^ 2)]
        to_side.append(links.copy(source(b, t), raw.at[b, piece(t)], side))
        on_to_side.append(links.copy(there, there, side))
        if b < 2:
            to_across.append(links.copy(source(b, t), raw.at[b, piece(t)], across))
            to_next.append(links.copy(source(b, t), raw.at[b + 1, piece(t)], nxt))
    far_to_next = links.copy(raw.at[1, piece(t ^ 2)], raw.at[2, piece(t ^ 2)], nxt)
    c_side = links.copy(cotangent, crows.at[piece(t), :], side)
    c_over = links.copy(cotangent, crows.at[piece(t), :], across)
    c_on = links.copy(crows.at[piece(t ^ 2), :], crows.at[piece(t ^ 2), :], side)
    to_across[0].start()
    to_side[0].start()

    @pl.when(c < nctx - 1)
    def _():
        to_next[0].start()

    c_side.start()
    raw[0, piece(t), :] = hidden[...]
    gains_copy.wait()
    gains[...] = gains_in[...] + gains_land[...]
    q_gain = gains[2:3, 0:HEAD_SIZE]
    k_gain = gains[3:4, 0:HEAD_SIZE]

    def table(b):
        start, stop, rate = places[0:1, :], places[1:2, :], rates[...]
        shape = (128, HEAD_SIZE)
        lower = lax.broadcasted_iota(jnp.int32, shape, 1) < HEAD_SIZE // 2

        @pl.loop(0, 4)
        def _(n):
            found = []
            for offset in (0, 512):
                first = n * 128 + offset
                index = (lax.broadcasted_iota(jnp.int32, shape, 0) + first) + (c - b) * block
                index = index.astype(f32)
                inside = (index >= start) & (index < stop)
                marks = jnp.where(inside, 1.0, 0.0)
                begin = jnp.sum(jnp.where(inside, start, 0.0), axis=1, keepdims=True)
                at = pl.ds(pl.multiple_of(first, 128), 128)
                for g in range(2):
                    kaug[b, g, at, 128:256] = (1.0 - marks).astype(bf16)
                if b == 0:
                    for h in range(4):
                        qaug[h, at, 128:256] = (marks * -APART).astype(bf16)
                found.append((at, index - begin))
            (low_at, low_pos), (high_at, high_pos) = found
            angle = jnp.where(lower, low_pos, high_pos) * rate
            cs, sn = jnp.cos(angle), jnp.sin(angle)
            cr, sr = pltpu.roll(cs, HEAD_SIZE // 2, 1), pltpu.roll(sn, HEAD_SIZE // 2, 1)
            cosine[b, low_at, :] = jnp.where(lower, cs, cr)
            cosine[b, high_at, :] = jnp.where(lower, cr, cs)
            sine[b, low_at, :] = jnp.where(lower, -sn, sr)
            sine[b, high_at, :] = jnp.where(lower, -sr, sn)

    def project_kv(b, owner):
        at = piece(owner)
        x = raw[b, at, :].astype(f32)
        scale = lax.rsqrt(jnp.mean(x * x, axis=-1, keepdims=True) + norm_eps)
        rows[b, at, :] = (x * scale * gains[0:1, :]).astype(bf16)
        got = flat_dot(rows[b, at, :], wqkv[:, 512:1024])
        k_proj[b, at, :] = got[:, 0:256]
        for g in range(2):
            u = got[:, g * 128 : g * 128 + 128]
            r = lax.rsqrt(jnp.mean(u * u, axis=-1, keepdims=True) + norm_eps)
            turned = spin(u * r * k_gain, cosine[b, at, :], sine[b, at, :])
            kaug[b, g, at, 0:128] = turned.astype(bf16)
            vaug[b, g, at, 0:128] = got[:, 256 + g * 128 : 384 + g * 128].astype(bf16)

    def project_q(owner):
        at = piece(owner)
        got = flat_dot(rows[0, at, :], wqkv[:, 0:512])
        q_proj[at, :] = got
        for h in range(4):
            u = got[:, h * 128 : h * 128 + 128]
            r = lax.rsqrt(jnp.mean(u * u, axis=-1, keepdims=True) + norm_eps)
            turned = spin(u * r * q_gain, cosine[0, at, :], sine[0, at, :])
            qaug[h, at, 0:128] = turned.astype(bf16)

    def unit(b, g, r, kc, bound):
        at = pl.ds(pl.multiple_of(r * 512, 512), 512)
        for hh in range(2):
            qq = qaug[2 * g + hh, at, :]
            total = None
            for j in range(2):
                keys_at = pl.ds(pl.multiple_of(kc * 512 + j * 256, 256), 256)
                p = jnp.exp2(last_dot(qq, kaug[b, g, keys_at, :]) * SCORE_STEP)
                if bound is not None:
                    ahead = lax.broadcasted_iota(jnp.int32, p.shape, 0) - lax.broadcasted_iota(
                        jnp.int32, p.shape, 1
                    )
                    p = jnp.where(ahead >= bound + j * 256, p, 0.0)
                value = flat_dot(p.astype(bf16), vaug[b, g, keys_at, :])
                total = value if total is None else total + value
            acc[2 * g + hh, at, :] += total

    def block_outs(b):
        pairs = (
            (rows, rows_out), (k_proj, k_out), (kaug, keys_out), (vaug, values_out),
            (cosine, cos_out), (sine, sin_out),
        )
        return [locals_.make(a.at[b], d.at[b]) for a, d in pairs]

    outs = [block_outs(b) for b in range(3)]

    lane = lax.broadcasted_iota(jnp.int32, (1, HEAD_SIZE), 1)
    begin = jnp.full((1, HEAD_SIZE), float(nctx * block), f32)
    end = begin
    for label in range(NDOC):
        before = jnp.where(segments[...] < label, 1.0, 0.0)
        before = jnp.sum(before, axis=(0, 1), keepdims=True)
        begin = jnp.where(lane == label, before, begin)
        end = jnp.where(lane == label - 1, before, end)
    places[0:1, :] = begin
    places[1:2, :] = end
    table(0)
    vaug[:, :, :, 128:256] = jnp.ones((3, 2, block, 128), bf16)
    acc[...] = jnp.zeros(acc.shape, f32)
    locals_.wait(own_k)
    locals_.wait(own_v)
    wk_copy.wait()
    wv_copy.wait()
    wo_copy.start()
    to_across[0].wait_recv()
    on_to_side[0].start()

    @pl.when(c >= 1)
    def _():
        to_next[0].wait_recv()
        to_across[1].start()
        to_side[1].start()

        @pl.when(c < nctx - 1)
        def _():
            to_next[1].start()

    to_side[0].wait_recv()
    on_to_side[0].wait_recv()

    @pl.loop(0, 4)
    def _(n):
        project_kv(0, n)

    for copy in outs[0]:
        copy.start()

    @pl.when(c >= 1)
    def _():
        table(1)
        to_side[1].wait_recv()

        @pl.loop(0, 2)
        def _(n):
            project_kv(1, t ^ n)

    @pl.when(c >= 2)
    def _():
        table(2)

    locals_.wait(own_q)
    wq_copy.wait()
    wg_copy.start()

    @pl.when(c >= 1)
    def _():
        to_across[1].wait_recv()
        on_to_side[1].start()

        @pl.when(c < nctx - 1)
        def _():
            far_to_next.start()

        @pl.when(c >= 2)
        def _():
            to_next[1].wait_recv()
            to_side[2].start()

    c_over.start()

    @pl.loop(0, 4)
    def _(n):
        project_q(n)

    locals_.start(q_proj, q_out)
    locals_.start(wqkv, wqkv_out)

    @pl.loop(0, 6)
    def _(n):
        m = lax.rem(n, 3)
        unit(0, n // 3, (m + 1) // 2, m // 2, (m & 1) * -512)

    wo_copy.wait_recv()
    wo_on.start()
    wu_copy.start()

    @pl.when(c >= 1)
    def _():
        on_to_side[1].wait_recv()

        @pl.loop(2, 4)
        def _(n):
            project_kv(1, t ^ n)

        for copy in outs[1]:
            copy.start()

        @pl.loop(0, 8)
        def _(n):
            m = lax.rem(n, 4)
            unit(1, n // 4, m // 2, m & 1, None)

    wg_copy.wait_recv()
    wg_on.start()

    c_over.wait_recv()
    c_on.start()

    @pl.when(c >= 2)
    def _():
        far_to_next.wait_recv()
        on_to_side[2].start()
        to_side[2].wait_recv()
        on_to_side[2].wait_recv()

        @pl.loop(0, 4)
        def _(n):
            project_kv(2, n)

        for copy in outs[2]:
            copy.start()

        @pl.loop(0, 6)
        def _(n):
            m = lax.rem(n, 3)
            unit(2, n // 3, m // 2, (m + 1) // 2, None)

    for h in range(4):

        @pl.loop(0, 4)
        def _(r):
            at = pl.ds(pl.multiple_of(r * 256, 256), 256)
            total = acc[h, at, 128:256]
            value = acc[h, at, 0:128] / total
            acc[h, at, 0:128] = value
            shift = jnp.log(total) * -(HEAD_SIZE**0.5)
            top = shift.astype(bf16).astype(f32)
            mid = (shift - top).astype(bf16).astype(f32)
            lane = lax.broadcasted_iota(jnp.int32, shift.shape, 1)
            parts = jnp.where(lane == NDOC, top, 0.0)
            parts = jnp.where(lane == NDOC + 1, mid, parts)
            parts = jnp.where(lane == NDOC + 2, shift - top - mid, parts)
            qaug[h, at, 128:256] = qaug[h, at, 128:256] + parts.astype(bf16)
            low[h, at, :] = value.astype(bf16)

        lanes = slice(h * 128, h * 128 + 128)
        locals_.start(low.at[h], low_out.at[:, lanes])
        locals_.start(acc.at[h, :, 0:128], attended_out.at[:, lanes])
        locals_.start(qaug.at[h], query_out.at[h])

    locals_.start(gains, gains_out)
    locals_.wait(own_c)
    c_side.wait()
    c_on.wait()
    locals_.start(crows, crows_out)
    c_over.wait_send()
    to_across[0].wait_send()
    to_side[0].wait_send()
    on_to_side[0].wait_send()
    for copy in outs[0]:
        copy.wait()

    @pl.when(c < nctx - 1)
    def _():
        to_next[0].wait_send()

    for b in (1, 2):

        @pl.when(c >= b)
        def _():
            if b < 2:
                to_across[b].wait_send()
            to_side[b].wait_send()
            on_to_side[b].wait_send()
            for copy in outs[b]:
                copy.wait()

    @pl.when((c >= 1) & (c < nctx - 1))
    def _():
        to_next[1].wait_send()
        far_to_next.wait_send()

    wo_copy.wait_send()
    wo_on.wait()
    wg_copy.wait_send()
    wg_on.wait()
    wu_copy.wait()
    locals_.finish()


def forward_call(hidden, cotangent, gains, segments, rates, wq, wk, wv, wo, wg, wu):
    part, width = hidden.shape
    block = 4 * part
    f32, bf16 = jnp.float32, jnp.bfloat16
    shape = jax.ShapeDtypeStruct
    outs = (
        shape((8, width), f32),
        shape((3, block, width), bf16),
        shape((block, 512), f32),
        shape((3, block, 256), f32),
        shape((4, block, 256), bf16),
        shape((3, 2, block, 256), bf16),
        shape((3, 2, block, 256), bf16),
        shape((3, block, HEAD_SIZE), f32),
        shape((3, block, HEAD_SIZE), f32),
        shape((block, 512), f32),
        shape((block, 512), bf16),
        shape((width, 1024), bf16),
        shape((block, width), bf16),
        shape(wo.shape, bf16),
        shape(wg.shape, bf16),
        shape(wu.shape, bf16),
    )
    return pl.pallas_call(
        forward_kernel,
        name="forward",
        out_shape=outs,
        in_specs=[VMEM_SPEC] * 5 + [ANY_SPEC] * 6,
        out_specs=[ANY_SPEC] * len(outs),
        scratch_shapes=[
            pltpu.VMEM((8, width), f32),
            pltpu.VMEM((3, block, width), bf16),
            pltpu.VMEM((3, block, width), bf16),
            pltpu.VMEM((width, 1024), bf16),
            pltpu.VMEM((block, 512), f32),
            pltpu.VMEM((3, block, 256), f32),
            pltpu.VMEM((4, block, 256), bf16),
            pltpu.VMEM((3, 2, block, 256), bf16),
            pltpu.VMEM((3, 2, block, 256), bf16),
            pltpu.VMEM((3, block, HEAD_SIZE), f32),
            pltpu.VMEM((3, block, HEAD_SIZE), f32),
            pltpu.VMEM((4, block, 256), f32),
            pltpu.VMEM((4, block, 128), bf16),
            pltpu.VMEM((block, width), bf16),
            pltpu.VMEM((8, width), f32),
            pltpu.VMEM((8, width), f32),
            pltpu.VMEM((8, HEAD_SIZE), f32),
            pltpu.SemaphoreType.DMA((23,)),
            pltpu.SemaphoreType.DMA((23,)),
            pltpu.SemaphoreType.DMA((38,)),
        ],
        compiler_params=pltpu.CompilerParams(
            collective_id=0, has_side_effects=True, vmem_limit_bytes=58 << 20
        ),
    )(hidden, cotangent, gains, segments, rates, wq, wk, wv, wo, wg, wu)


class Scatter:
    def __init__(self, links, bufs, side, across):
        self.bufs = bufs
        self.far = links.copy(bufs.at[0], bufs.at[3], side)
        self.over = links.copy(bufs.at[1], bufs.at[4], across)
        self.near = links.copy(bufs.at[2], bufs.at[5], side)

    def put_far(self, value):
        self.bufs[0] = value.astype(jnp.bfloat16)
        self.far.start()

    def put_over(self, value):
        self.far.wait_recv()
        self.bufs[1] = (value + self.bufs[3].astype(jnp.float32)).astype(jnp.bfloat16)
        self.over.start()

    def put_near(self, value):
        self.bufs[2] = value.astype(jnp.bfloat16)
        self.near.start()

    def total(self, value):
        self.near.wait_recv()
        self.over.wait_recv()
        return value + self.bufs[5].astype(jnp.float32) + self.bufs[4].astype(jnp.float32)

    def close(self):
        self.far.wait_send()
        self.over.wait_send()
        self.near.wait_send()


def mlp_kernel(
    low, hidden, gains, crows_in, wo_own, wo_got, wg_own, wg_got, wu_own, wu_got,
    wd,
    d_middle_out, gain_out, brow_out, own_out, give_out, parts_out, out_own_out,
    wo, wgf, wuf, wdf, mrows, act, dgate, dup, brow, kept, middle, bufs, parts, give, own, land,
    crows, result, send, recv, local,
):
    s, c, t = lax.axis_index(SHARD_AXIS), lax.axis_index(CTX_AXIS), lax.axis_index(TP_AXIS)
    part = hidden.shape[0]
    half = wd.shape[1]
    bf16, f32 = jnp.bfloat16, jnp.float32
    side, across = {TP_AXIS: t ^ 1}, {TP_AXIS: t ^ 2}
    mate, pair = {SHARD_AXIS: 1 - s}, {CTX_AXIS: c ^ 1}
    links, locals_ = Links(send, recv), Locals(local)

    def piece(owner):
        return pl.ds(pl.multiple_of(owner * part, part), part)

    mine = pl.ds(pl.multiple_of(s * half, half), half)
    theirs = pl.ds(pl.multiple_of((1 - s) * half, half), half)
    low_bit = c & 1

    def some(shard, count, size):
        return pl.ds(pl.multiple_of(shard * count + low_bit * size, size), size)

    quarter = half // 2
    third = wd.shape[0] // 2
    wu_at = some(1 - s, half, quarter)
    wu_on = links.copy(wu_got.at[some(0, 0, quarter), :], wuf.at[wu_at, :], pair)
    wd_copy = links.copy(
        wd.at[some(0, 0, third), :], wdf.at[some(0, 0, third), mine], mate
    )
    wd_got = wdf.at[some(0, 0, third), theirs]
    wd_on = links.copy(wd_got, wd_got, pair)
    wo_loads = [
        locals_.start(wo_own, wo.at[:, mine]),
        locals_.start(wo_got, wo.at[:, theirs]),
    ]
    enter([side, across, mate, pair])
    wu_on.start()
    wd_copy.start()
    own_weights = [
        locals_.start(wg_own, wgf.at[mine, :]),
        locals_.start(wg_got, wgf.at[theirs, :]),
        locals_.start(wu_own, wuf.at[mine, :]),
        locals_.start(wu_got.at[some(0, 0, quarter), :], wuf.at[wu_at, :]),
        locals_.start(wd, wdf.at[:, mine]),
        locals_.start(crows_in, crows),
    ]
    for copy in wo_loads:
        locals_.wait(copy)

    branch = Scatter(links, bufs.at[0], side, across)
    back = Scatter(links, bufs.at[1], side, across)

    def branch_part(owner):
        return flat_dot(low[piece(owner), :], wo[...])

    @pl.loop(0, 4)
    def _(n):
        value = branch_part(t ^ (3 - n))
        pl.when(n == 0)(lambda: branch.put_far(value))
        pl.when(n == 1)(lambda: branch.put_over(value))
        pl.when(n == 2)(lambda: branch.put_near(value))

        @pl.when(n == 3)
        def _():
            middle[...] = hidden[...].astype(f32) + value

    wd_copy.wait_recv()
    wd_on.start()
    middle[...] = branch.total(middle[...])
    m = middle[...]
    scale = lax.rsqrt(jnp.mean(m * m, axis=-1, keepdims=True) + norm_eps)
    gain = gains[1:2, :]
    mrows[piece(t), :] = (m * scale * gain).astype(bf16)
    here, there = mrows.at[piece(t), :], mrows.at[piece(t ^ 2), :]
    m_over, m_near = links.copy(here, here, across), links.copy(here, here, side)
    m_on = links.copy(there, there, side)
    m_over.start()
    m_near.start()
    for copy in own_weights:
        locals_.wait(copy)
    wu_on.wait_recv()
    wd_on.wait_recv()

    def mlp(owner):
        at = piece(owner)
        rows = mrows[at, :]
        gate = flat_dot(rows, wgf[...])
        upward = flat_dot(rows, wuf[...])
        d_act = last_dot(crows[at, :], wdf[...])
        sig = 1.0 / (1.0 + jnp.exp(-gate))
        silu = gate * sig
        act[at, :] = (silu * upward).astype(bf16)
        dup[at, :] = (d_act * silu).astype(bf16)
        dgate[at, :] = (d_act * upward * sig * (1.0 + gate * (1.0 - sig))).astype(bf16)

    def out_part(owner):
        return flat_dot(act[piece(owner), :], wdf[...])

    def back_part(owner):
        at = piece(owner)
        return last_dot(dgate[at, :], wgf[...]) + last_dot(dup[at, :], wuf[...])

    m_near.wait_recv()

    @pl.loop(0, 4)
    def _(n):
        @pl.when(n == 2)
        def _():
            m_over.wait_recv()
            m_on.start()
            m_on.wait_recv()

        owner = t ^ jnp.where(n < 2, n, 5 - n)
        mlp(owner)
        value = back_part(owner)

        @pl.when(n == 0)
        def _():
            kept[0] = value

        pl.when(n == 1)(lambda: back.put_near(value))
        pl.when(n == 2)(lambda: back.put_far(value))
        pl.when(n == 3)(lambda: back.put_over(value))

    to_mate = [links.copy(give.at[k], land.at[k], mate) for k in range(READY)]

    def lanes(n):
        return pl.ds(pl.multiple_of(n * 256, 256), 256)

    def down_chunk(ref, n, columns):
        ref[n] = first_dot(act[:, lanes(n)], crows[:, columns]).astype(bf16)

    def wide_chunk(ref, k, grads, n, columns):
        got = first_dot(mrows[:, columns], grads[:, lanes(n)]).astype(bf16)
        ref[k + n, :, 0:256] = got[0:256]
        ref[k + n, :, 256:512] = got[256:512]

    @pl.loop(0, 3)
    def _(n):
        down_chunk(give, n, theirs)

    for copy in to_mate:
        copy.start()

    @pl.loop(0, 3)
    def _(n):
        down_chunk(own, n, mine)
        for k, grads in ((3, dgate), (6, dup)):
            wide_chunk(give, k, grads, n, theirs)
            wide_chunk(own, k, grads, n, mine)

    @pl.loop(0, 4)
    def _(n):
        value = out_part(t ^ (3 - n))

        @pl.when(n < 3)
        def _():
            parts[n] = value.astype(bf16)

        @pl.when(n == 3)
        def _():
            kept[1] = value + middle[...]

    locals_.start(kept.at[1], out_own_out)
    locals_.start(parts, parts_out)
    locals_.start(give.at[READY:FROM_MLP], give_out)
    locals_.start(own.at[READY:FROM_MLP], own_out.at[READY:FROM_MLP])

    d_mlp = back.total(kept[0])
    m = middle[...]
    scale = lax.rsqrt(jnp.mean(m * m, axis=-1, keepdims=True) + norm_eps)
    scaled = d_mlp * gain
    inner = jnp.mean(scaled * m, axis=-1, keepdims=True)
    d_middle = (
        crows[piece(t), :].astype(f32) + scale * scaled - m * (scale * scale * scale) * inner
    )
    kept[0] = d_middle
    gain_grad = jnp.sum(d_mlp * m * scale, axis=0, keepdims=True)
    brow[...] = d_middle.astype(bf16)
    locals_.start(brow, brow_out)
    locals_.start(kept.at[0], d_middle_out)
    result[...] = jnp.broadcast_to(gain_grad, (8, gain_grad.shape[1]))
    locals_.start(result, gain_out)

    for k in range(READY):
        to_mate[k].wait_recv()
        own[k] = own[k] + land[k]
    locals_.start(own.at[0:READY], own_out.at[0:READY])
    for k in range(READY):
        to_mate[k].wait_send()
    wu_on.wait_send()
    wd_copy.wait_send()
    wd_on.wait_send()
    branch.close()
    back.close()
    for copy in (m_over, m_near, m_on):
        copy.wait_send()
    locals_.finish()


def mlp_call(vmem_args, any_args):
    low, hidden, gains = vmem_args
    wo, wd = any_args[1], any_args[-1]
    part, width = hidden.shape
    block = 4 * part
    units = wd.shape[0]
    f32, bf16 = jnp.float32, jnp.bfloat16
    shape = jax.ShapeDtypeStruct
    outs = (
        shape((part, width), f32),
        shape((8, width), f32),
        shape((part, width), bf16),
        shape((FROM_MLP, 256, 512), bf16),
        shape((FROM_MLP - READY, 256, 512), bf16),
        shape((3, part, width), bf16),
        shape((part, width), f32),
    )
    return pl.pallas_call(
        mlp_kernel,
        name="mlp",
        out_shape=outs,
        in_specs=[VMEM_SPEC] * 3 + [ANY_SPEC] * 8,
        out_specs=[ANY_SPEC] * len(outs),
        scratch_shapes=[
            pltpu.VMEM((wo.shape[0], width), bf16),
            pltpu.VMEM((width, units), bf16),
            pltpu.VMEM((width, units), bf16),
            pltpu.VMEM((units, width), bf16),
            pltpu.VMEM((block, width), bf16),
            pltpu.VMEM((block, units), bf16),
            pltpu.VMEM((block, units), bf16),
            pltpu.VMEM((block, units), bf16),
            pltpu.VMEM((part, width), bf16),
            pltpu.VMEM((2, part, width), f32),
            pltpu.VMEM((part, width), f32),
            pltpu.VMEM((2, 6, part, width), bf16),
            pltpu.VMEM((3, part, width), bf16),
            pltpu.VMEM((FROM_MLP, 256, 512), bf16),
            pltpu.VMEM((FROM_MLP, 256, 512), bf16),
            pltpu.VMEM((READY, 256, 512), bf16),
            pltpu.VMEM((block, width), bf16),
            pltpu.VMEM((8, width), f32),
            pltpu.SemaphoreType.DMA((12 + READY,)),
            pltpu.SemaphoreType.DMA((12 + READY,)),
            pltpu.SemaphoreType.DMA((16,)),
        ],
        compiler_params=pltpu.CompilerParams(
            collective_id=1, has_side_effects=True, vmem_limit_bytes=58 << 20
        ),
    )(*vmem_args, *any_args)


class Pump:
    def __init__(self, refs, sems, mate, near, opposite, outer, out, first_mate):
        self.own, self.mated, self.landed, self.summed = refs
        self.send, self.recv, self.local = sems
        self.mate, self.near, self.opposite, self.outer = mate, near, opposite, outer
        self.inner = jnp.logical_not(outer)
        self.out, self.first_mate = out, first_mate

    def remote(self, stage, u, src, dst, device):
        return pltpu.make_async_remote_copy(
            src_ref=src, dst_ref=dst, send_sem=self.send.at[stage * UNITS + u],
            recv_sem=self.recv.at[stage * UNITS + u], device_id=device, device_id_type=MESH_ID,
        )

    def to_mate(self, u, src):
        return self.remote(0, u, src, self.mated.at[u - self.first_mate], self.mate)

    def inward(self, u):
        return self.remote(1, u, self.own.at[u], self.landed.at[u], self.near)

    def cross(self, u):
        return self.remote(2, u, self.landed.at[u], self.summed.at[u], self.opposite)

    def outward(self, u):
        return self.remote(3, u, self.summed.at[u], self.landed.at[u], self.near)

    def write(self, u, ref):
        return pltpu.make_async_copy(ref.at[u], self.out.at[u], self.local.at[u])

    def run(self, condition, body):
        if isinstance(condition, bool):
            if condition:
                body()
        else:
            pl.when(condition)(body)

    def first(self, u):
        def bring():
            self.to_mate(u, self.own.at[u]).wait_recv()
            self.own[u] = self.own[u] + self.mated[u - self.first_mate]

        self.run(u >= self.first_mate, bring)
        pl.when(self.outer)(lambda: self.inward(u).start())

    def second(self, u):
        @pl.when(self.inner)
        def _():
            self.inward(u).wait_recv()
            self.landed[u] = self.own[u] + self.landed[u]
            self.cross(u).start()

    def third(self, u):
        @pl.when(self.inner)
        def _():
            self.cross(u).wait_recv()
            self.summed[u] = self.landed[u] + self.summed[u]
            self.outward(u).start()
            self.write(u, self.summed).start()

    def fourth(self, u):
        @pl.when(self.outer)
        def _():
            self.outward(u).wait_recv()
            self.write(u, self.landed).start()

    def slot(self, k):
        for u in (2 * k, 2 * k + 1):
            self.first(u)
            self.run(k >= 2, lambda: self.second(u - 4))
            self.run(k >= 4, lambda: self.third(u - 8))

    def close(self):
        @pl.loop(0, UNITS)
        def _(u):
            pl.when(self.outer)(lambda: self.inward(u).wait_send())

            @pl.when(self.inner)
            def _():
                self.cross(u).wait_send()
                self.outward(u).wait_send()

            self.write(u, self.summed).wait()


def backward_kernel(
    query, gains, mlp_gain_grad, hidden, brow_in, low, attended, wo_own, wo_got, d_middle,
    q_proj_in, wqkv_in, own_in, give, parts, out_own, keys, values, k_proj, cosine, sine, rows,
    hidden_out, hidden_grad, gains_out, sums_out,
    kbuf, vbuf, kpbuf, cosbuf, sinbuf, rowbuf, dq, dk, dv, dkv, dqp, gkv, kept, bufs,
    own, mated, landed, summed, late_give, far_land, mid_land, out_buf,
    dout, q_proj, wqkv,
    gsum, gland, send, recv, pump_send, pump_recv, pump_local, local, blocksem,
):
    s, c, t = lax.axis_index(SHARD_AXIS), lax.axis_index(CTX_AXIS), lax.axis_index(TP_AXIS)
    nctx = lax.axis_size(CTX_AXIS)
    part = hidden.shape[0]
    half = rows.shape[2] // 2
    f32, bf16 = jnp.float32, jnp.bfloat16
    side, across, mate = {TP_AXIS: t ^ 1}, {TP_AXIS: t ^ 2}, {SHARD_AXIS: 1 - s}
    near, opposite = {CTX_AXIS: c ^ 1}, {CTX_AXIS: c ^ 3}
    previous = {CTX_AXIS: lax.rem(c + nctx - 1, nctx)}
    outer = (c == 0) | (c == nctx - 1)
    links, locals_ = Links(send, recv), Locals(local)
    scale = HEAD_SIZE ** (-0.5)
    pump = Pump(
        (own, mated, landed, summed), (pump_send, pump_recv, pump_local),
        mate, near, opposite, outer, sums_out, MATED,
    )

    def piece(owner):
        return pl.ds(pl.multiple_of(owner * part, part), part)

    mine = pl.ds(pl.multiple_of(s * half, half), half)
    theirs = pl.ds(pl.multiple_of((1 - s) * half, half), half)

    def half_at(ref_shard, n, size):
        return pl.ds(pl.multiple_of(ref_shard * half + n * size, size), size)

    def block_copies(b):
        slot = b & 1
        pairs = (
            (keys.at[b], kbuf.at[slot]), (values.at[b], vbuf.at[slot]),
        )
        return [
            pltpu.make_async_copy(a, d, blocksem.at[6 * b + n]) for n, (a, d) in enumerate(pairs)
        ]

    def row_copies(b):
        pairs = (
            (k_proj.at[b], kpbuf), (cosine.at[b], cosbuf), (sine.at[b], sinbuf),
            (rows.at[b], rowbuf),
        )
        return [
            pltpu.make_async_copy(a, d, blocksem.at[6 * b + 2 + n])
            for n, (a, d) in enumerate(pairs)
        ]

    def row_fetch(b):
        for copy in row_copies(b):
            copy.start()

    def fetch(b):
        for copy in block_copies(b):
            copy.start()

    def fetched(b):
        for copy in block_copies(b):
            copy.wait()

    brow_load = locals_.start(brow_in, rowbuf.at[piece(t), :])
    loads = [locals_.start(own_in, own.at[0:EARLY])]
    wo_loads = []
    for j in range(2):
        at = slice(j * 256, j * 256 + 256)
        wo_loads.append(locals_.start(wo_own.at[at, :], bufs.at[1, j, :, mine]))
        wo_loads.append(locals_.start(wo_got.at[at, :], bufs.at[1, j, :, theirs]))
    for h in range(4):
        wo_loads.append(locals_.start(attended.at[:, h * 128 : h * 128 + 128], dq.at[h]))
    wo_loads.append(locals_.start(low, dkv))
    out_loads = [locals_.start(parts.at[1], out_buf.at[0]), locals_.start(out_own, kept.at[1])]

    @pl.when(c >= 2)
    def _():
        fetch(2)

    @pl.when(c >= 1)
    def _():
        fetch(1)

    @pl.when(c <= 1)
    def _():
        fetch(0)

    late_loads = [locals_.start(q_proj_in, q_proj), locals_.start(wqkv_in, wqkv)]
    enter([side, across, mate, near, opposite])

    def send_early(first, count):
        for u in range(first, min(first + count, EARLY)):
            pump.to_mate(u, give.at[u - MATED]).start()

    here, there = rowbuf.at[piece(t), :], rowbuf.at[piece(t ^ 2), :]
    b_over, b_near = links.copy(here, here, across), links.copy(here, here, side)
    b_on = links.copy(there, there, side)
    locals_.wait(brow_load)
    b_over.start()
    b_near.start()
    send_early(MATED, 4)
    out_far = links.copy(parts.at[0], out_buf.at[1], side)
    out_over = links.copy(out_buf.at[0], out_buf.at[2], across)
    out_near = links.copy(parts.at[2], out_buf.at[3], side)
    out_far.start()
    out_near.start()
    scatters = [
        Scatter(links, bufs.at[0], side, across),
        Scatter(links, bufs.at[1], side, across),
        Scatter(links, bufs.at[0], side, across),
    ]
    far_copy = links.copy(out_buf.at[0], far_land, previous)
    mid_copy = links.copy(out_buf.at[1], mid_land, previous)
    for copy in loads:
        locals_.wait(copy)
    pump.slot(0)
    send_early(MATED + 4, 2)
    gkv[...] = jnp.zeros(gkv.shape, f32)
    gsum[...] = jnp.zeros(gsum.shape, f32)
    gsum[1:2, :] = mlp_gain_grad[0:1, :]
    q_gain = gains[2:3, 0:HEAD_SIZE]
    k_gain = gains[3:4, 0:HEAD_SIZE]
    def attended_back(owner):
        at = piece(owner)
        for j in range(2):
            got = last_dot(rowbuf[at, :], bufs[1, j]).astype(bf16)
            for hh in range(2):
                h = 2 * j + hh
                head = got[:, hh * 128 : hh * 128 + 128]
                delta = -jnp.sum(head.astype(f32) * dq[h, at, :], axis=1, keepdims=True)
                top = delta.astype(bf16).astype(f32)
                lane = lax.broadcasted_iota(jnp.int32, (part, HEAD_SIZE), 1)
                extra = jnp.where(lane == 0, top, jnp.where(lane == 1, delta - top, 0.0))
                dout[h, at, 0:128] = head
                dout[h, at, 128:256] = extra.astype(bf16)

    for copy in wo_loads:
        locals_.wait(copy)
    b_near.wait_recv()

    @pl.loop(0, 2)
    def _(n):
        attended_back(t ^ n)

    for copy in out_loads:
        locals_.wait(copy)
    out_far.wait_recv()
    out_buf[0] = out_buf[0] + out_buf[1]
    pump.slot(1)
    send_early(MATED + 6, 2)
    b_over.wait_recv()
    b_on.start()
    out_over.start()
    b_on.wait_recv()

    @pl.loop(2, 4)
    def _(n):
        attended_back(t ^ n)

    for copy in (b_over, b_near, b_on):
        copy.wait_send()
    @pl.loop(0, 2)
    def _(n):
        at = pl.ds(pl.multiple_of(n * 256, 256), 256)
        for columns, target, first in ((theirs, late_give, 0), (mine, own, EARLY)):
            got = first_dot(dkv[:, at], rowbuf[:, columns]).astype(bf16)
            for e in range(2):
                target[first + 2 * n + e] = got[e * 128 : e * 128 + 128]

    for n in range(4):
        pump.to_mate(EARLY + n, late_give.at[n]).start()
    dq[...] = jnp.zeros(dq.shape, f32)
    for b in range(3):
        pl.when((c == b) if b < 2 else (c >= b))(functools.partial(row_fetch, b))
    pump.slot(2)
    send_early(MATED + 8, 2)

    def tile(b, g, r, kc, bound):
        slot = b & 1
        q_at = pl.ds(pl.multiple_of(r * 512, 512), 512)
        k_at = pl.ds(pl.multiple_of(kc * 512, 512), 512)
        kk, vv = kbuf[slot, g, k_at, :], vbuf[slot, g, k_at, :]
        dv_new, dk_new = [], []
        for hh in range(2):
            h = 2 * g + hh
            qq, do = query[h, q_at, :], dout[h, q_at, :]
            p = jnp.exp2(last_dot(qq, kk) * SCORE_STEP)
            if bound is not None:
                ahead = lax.broadcasted_iota(jnp.int32, p.shape, 0) - lax.broadcasted_iota(
                    jnp.int32, p.shape, 1
                )
                p = jnp.where(ahead >= bound, p, 0.0)
            ds = (p * last_dot(do, vv)).astype(bf16)
            dv_new.append(first_dot(do[:, 0:HEAD_SIZE], p.astype(bf16)))
            dk_new.append(first_dot(qq[:, 0:HEAD_SIZE], ds))
            dq[h, q_at, :] += flat_dot(ds, kk[:, 0:HEAD_SIZE])
        dv[g, :, k_at] += dv_new[0] + dv_new[1]
        dk[g, :, k_at] += dk_new[0] + dk_new[1]

    def clear():
        dk[...] = jnp.zeros(dk.shape, f32)
        dv[...] = jnp.zeros(dv.shape, f32)

    def norm_back(grad, u, gain, cos, sin, row):
        turned = grad * cos - pltpu.roll(grad, HEAD_SIZE // 2, 1) * sin
        r = lax.rsqrt(jnp.mean(u * u, axis=-1, keepdims=True) + norm_eps)
        gsum[row : row + 1, 0:HEAD_SIZE] += jnp.sum(turned * u * r, axis=0, keepdims=True)
        scaled = turned * gain
        inner = jnp.mean(scaled * u, axis=-1, keepdims=True)
        return (r * scaled - u * (r * r * r) * inner).astype(bf16)

    def finish_kv(b):
        for copy in row_copies(b)[:3]:
            copy.wait()

        @pl.loop(0, 4)
        def _(n):
            at = piece(n)
            cos, sin = cosbuf[at, :], sinbuf[at, :]
            for g in range(2):
                lanes = slice(g * 128, g * 128 + 128)
                u = kpbuf[at, lanes]
                dkv[at, lanes] = norm_back(dk[g, :, at].T * scale, u, k_gain, cos, sin, 3)
                dkv[at, 256 + g * 128 : 384 + g * 128] = dv[g, :, at].T.astype(bf16)

        row_copies(b)[3].wait()

        gkv[...] += first_dot(rowbuf[...], dkv[...])

    def kv_part(owner):
        return last_dot(dkv[piece(owner), :], wqkv[:, 512:1024])

    def all_part(owner):
        return kv_part(owner) + last_dot(dqp[piece(owner), :], wqkv[:, 0:512])

    def scatter(which, slot, partial):
        @pl.loop(0, 4)
        def _(n):
            value = partial(t ^ (3 - n))
            pl.when(n == 0)(lambda: which.put_far(value))
            pl.when(n == 1)(lambda: which.put_over(value))
            pl.when(n == 2)(lambda: which.put_near(value))

            @pl.when(n == 3)
            def _():
                kept[slot] = value

    for copy in late_loads:
        locals_.wait(copy)

    @pl.when(c >= 2)
    def _():
        fetched(2)
        clear()

    @pl.loop(0, 6)
    def _(n):
        m = lax.rem(n, 3)

        @pl.when(c >= 2)
        def _():
            tile(2, n // 3, m // 2, (m + 1) // 2, None)

        @pl.when(m == 2)
        def _():
            pump.slot(3 + n // 3)
            for e in range(2):
                u = MATED + 10 + 2 * (n // 3) + e
                pump.to_mate(u, give.at[u - MATED]).start()

    @pl.when(c >= 2)
    def _():
        finish_kv(2)
        fetch(0)
        row_fetch(1)
        scatter(scatters[2], 0, kv_part)

    out_near.wait_recv()
    out_over.wait_recv()
    out_buf[3] = (kept[1] + out_buf[2].astype(f32) + out_buf[3].astype(f32)).astype(bf16)
    locals_.start(out_buf.at[3], hidden_out)
    out_far.wait_send()
    out_over.wait_send()
    out_near.wait_send()
    pump.slot(5)

    @pl.when(c >= 1)
    def _():
        fetched(1)
        clear()

    @pl.loop(0, 8)
    def _(n):
        m = lax.rem(n, 4)

        @pl.when(c >= 1)
        def _():
            tile(1, n // 4, m // 2, m & 1, None)

        @pl.when(m == 3)
        def _():
            pump.slot(6 + n // 4)

    @pl.when(c >= 2)
    def _():
        out_buf[0] = scatters[2].total(kept[0]).astype(bf16)
        far_copy.start()
        scatters[2].close()

    @pl.when(c >= 1)
    def _():
        finish_kv(1)
        row_fetch(0)

    @pl.when(c >= 1)
    def _():
        scatter(scatters[1], 1, kv_part)

    pump.slot(8)
    fetched(0)
    clear()

    @pl.loop(0, 6)
    def _(n):
        m = lax.rem(n, 3)
        tile(0, n // 3, (m + 1) // 2, m // 2, (m & 1) * -512)

        @pl.when(n == 3)
        def _():
            pump.slot(9)

    finish_kv(0)

    @pl.loop(0, 4)
    def _(n):
        at = piece(n)
        cos, sin = cosbuf[at, :], sinbuf[at, :]
        for h in range(4):
            lanes = slice(h * 128, h * 128 + 128)
            u = q_proj[at, lanes]
            dqp[at, lanes] = norm_back(dq[h, at, :] * scale, u, q_gain, cos, sin, 2)

    for n in range(4):
        late_give[4 + n] = gkv[half_at(1 - s, n, 128), :].astype(bf16)
        pump.to_mate(LATE + n, late_give.at[4 + n]).start()
    for n in range(2):
        got = first_dot(rowbuf[:, half_at(1 - s, n, 256)], dqp[...]).astype(bf16)
        for e in range(2):
            late_give[8 + 2 * n + e] = got[e * 128 : e * 128 + 128]
            pump.to_mate(LATE + 4 + 2 * n + e, late_give.at[8 + 2 * n + e]).start()
    pump.slot(10)

    @pl.when((c >= 1) & (c < nctx - 1))
    def _():
        far_copy.wait_recv()
        kept[1] += far_land[...].astype(f32)

    @pl.when(c >= 1)
    def _():
        out_buf[1] = scatters[1].total(kept[1]).astype(bf16)
        mid_copy.start()
        scatters[1].close()

    base = locals_.start(d_middle, kept.at[1])
    hidden_load = locals_.start(hidden, out_buf.at[2])
    scatter(scatters[0], 0, all_part)
    for n in range(2):
        rows_of = gkv[half_at(s, n, 256), :].astype(bf16)
        got = first_dot(rowbuf[:, half_at(s, n, 256)], dqp[...]).astype(bf16)
        for e in range(2):
            at = slice(e * 128, e * 128 + 128)
            own[LATE + 2 * n + e] = rows_of[at]
            own[LATE + 4 + 2 * n + e] = got[at]
    for u in range(LATE - 4, LATE):
        pump.second(u)
        pump.third(u - 4)
    pump.third(LATE - 4)
    pump.third(LATE - 3)
    pl.loop(0, LATE - 8)(pump.fourth)

    def finish_rows():
        @pl.when(c < nctx - 1)
        def _():
            mid_copy.wait_recv()
            kept[0] += mid_land[...].astype(f32)

        kept[0] = scatters[0].total(kept[0])
        locals_.wait(hidden_load)
        locals_.wait(base)
        x = out_buf[2].astype(f32)
        r = lax.rsqrt(jnp.mean(x * x, axis=-1, keepdims=True) + norm_eps)
        d_in = kept[0]
        gsum[0:1, :] = jnp.sum(d_in * x * r, axis=0, keepdims=True)
        scaled = d_in * gains[0:1, :]
        inner = jnp.mean(scaled * x, axis=-1, keepdims=True)
        kept[1] += r * scaled - x * (r * r * r) * inner
        locals_.start(kept.at[1], hidden_grad)

    swaps = [
        links.copy(gsum, gland.at[n], device)
        for n, device in enumerate((side, across, mate, near, opposite))
    ]

    def swap(n):
        if n > 0:
            swaps[n - 1].wait()
            gsum[...] += gland[n - 1]
        if n < 5:
            swaps[n].start()

    for n, u in enumerate(range(LATE, UNITS)):
        pump.first(u)
        if n >= 1:
            pump.second(u - 1)
        pump.third(u - 2)
        if n == 3:
            finish_rows()
        if n >= 3:
            swap(n - 3)
    pump.second(UNITS - 1)
    pump.third(UNITS - 2)
    swap(8 - 3)
    pump.third(UNITS - 1)
    for n in range(9 - 3, 6):
        swap(n)
    locals_.start(gsum, gains_out)
    scatters[0].close()

    @pl.when(c >= 2)
    def _():
        far_copy.wait_send()

    @pl.when(c >= 1)
    def _():
        mid_copy.wait_send()

    @pl.loop(MATED, EARLY)
    def _(u):
        pump.to_mate(u, give.at[u - MATED]).wait_send()

    @pl.loop(EARLY, UNITS)
    def _(u):
        pump.to_mate(u, late_give.at[u - EARLY]).wait_send()

    pl.loop(LATE - 8, UNITS)(pump.fourth)
    pump.close()
    locals_.finish()


def backward_call(vmem_args, any_args):
    hidden = any_args[0]
    part, width = hidden.shape
    block = 4 * part
    f32, bf16 = jnp.float32, jnp.bfloat16
    shape = jax.ShapeDtypeStruct
    outs = (
        shape((part, width), bf16),
        shape((part, width), f32),
        shape((8, width), f32),
        shape((UNITS, 128, 512), bf16),
    )
    tile = pltpu.VMEM((part, width), bf16)
    units = pltpu.VMEM((UNITS, 128, 512), bf16)
    return pl.pallas_call(
        backward_kernel,
        name="backward",
        out_shape=outs,
        in_specs=[VMEM_SPEC] * 3 + [ANY_SPEC] * len(any_args),
        out_specs=[ANY_SPEC] * len(outs),
        scratch_shapes=[
            pltpu.VMEM((2, 2, block, 256), bf16),
            pltpu.VMEM((2, 2, block, 256), bf16),
            pltpu.VMEM((block, 256), f32),
            pltpu.VMEM((block, HEAD_SIZE), f32),
            pltpu.VMEM((block, HEAD_SIZE), f32),
            pltpu.VMEM((block, width), bf16),
            pltpu.VMEM((4, block, HEAD_SIZE), f32),
            pltpu.VMEM((2, HEAD_SIZE, block), f32),
            pltpu.VMEM((2, HEAD_SIZE, block), f32),
            pltpu.VMEM((block, 512), bf16),
            pltpu.VMEM((block, 512), bf16),
            pltpu.VMEM((width, 512), f32),
            pltpu.VMEM((2, part, width), f32),
            pltpu.VMEM((2, 6, part, width), bf16),
            units,
            pltpu.VMEM((UNITS - MATED, 128, 512), bf16),
            units,
            units,
            pltpu.VMEM((UNITS - EARLY, 128, 512), bf16),
            tile, tile,
            pltpu.VMEM((4, part, width), bf16),
            pltpu.VMEM((4, block, 256), bf16),
            pltpu.VMEM((block, 512), f32),
            pltpu.VMEM((width, 1024), bf16),
            pltpu.VMEM((8, width), f32),
            pltpu.VMEM((5, 8, width), f32),
            pltpu.SemaphoreType.DMA((22,)),
            pltpu.SemaphoreType.DMA((22,)),
            pltpu.SemaphoreType.DMA((4 * UNITS,)),
            pltpu.SemaphoreType.DMA((4 * UNITS,)),
            pltpu.SemaphoreType.DMA((UNITS,)),
            pltpu.SemaphoreType.DMA((20,)),
            pltpu.SemaphoreType.DMA((18,)),
        ],
        compiler_params=pltpu.CompilerParams(
            collective_id=2, has_side_effects=True, vmem_limit_bytes=60 << 20
        ),
    )(*vmem_args, *any_args)


def result_kernel(
    chunks_in, gains, grad_in, hidden_in,
    grad_out, hidden_out, attn, wq, wk, wv, q_gain, k_gain, wo, mlp, wg, wu, wd,
    buf, q, k, v, o, gate, up, down, grad, hidden, inside, outside,
):
    shard = lax.axis_index(SHARD_AXIS)
    count = buf.shape[0]
    whole = [
        pltpu.make_async_copy(grad_in, grad, inside.at[count]),
        pltpu.make_async_copy(hidden_in, hidden, inside.at[count + 1]),
    ]
    loads = [pltpu.make_async_copy(chunks_in.at[n], buf.at[n], inside.at[n]) for n in range(count)]
    for copy in whole + loads:
        copy.start()
    stores = []

    def put(n, ref, out, row, lanes):
        at = (slice(row, row + 256), lanes)
        stores.append(pltpu.make_async_copy(ref.at[at], out.at[at], outside.at[len(stores)]))
        stores[-1].start()

    for copy in whole:
        copy.wait()
    for n, (ref, out) in enumerate(((grad, grad_out), (hidden, hidden_out))):
        whole[n] = pltpu.make_async_copy(ref, out, outside.at[count + n])
        whole[n].start()
    for n in range(count):
        loads[n].wait()
        values = buf[n].astype(jnp.float32)
        every = slice(0, 512)
        if n < 3:
            down[n * 256 : n * 256 + 256, :] = values
            put(n, down, wd, n * 256, every)
        elif n < 9:
            ref, out, j = (gate, wg, n - 3) if n < 6 else (up, wu, n - 6)
            lanes = slice(j * 256, j * 256 + 256)
            ref[0:256, lanes] = values[:, 0:256]
            ref[256:512, lanes] = values[:, 256:512]
            at = (slice(0, 512), lanes)
            stores.append(pltpu.make_async_copy(ref.at[at], out.at[at], outside.at[len(stores)]))
            stores[-1].start()
        elif n < 11:
            o[(n - 9) * 256 : (n - 8) * 256, :] = values
            put(n, o, wo, (n - 9) * 256, every)
        elif n < 13:
            row = (n - 11) * 256
            k[row : row + 256, :] = values[:, 0:256]
            v[row : row + 256, :] = values[:, 256:512]
        else:
            q[(n - 13) * 256 : (n - 12) * 256, :] = values
            put(n, q, wq, (n - 13) * 256, every)
    for ref, out in ((k, wk), (v, wv)):
        stores.append(pltpu.make_async_copy(ref, out, outside.at[len(stores)]))
        stores[-1].start()
    wide, small = attn.shape[1], q_gain.shape[1]
    first = shard == 0
    attn[...] = jnp.where(first, gains[0:1, 0:wide], gains[0:1, wide : 2 * wide])
    mlp[...] = jnp.where(first, gains[1:2, 0:wide], gains[1:2, wide : 2 * wide])
    q_gain[...] = jnp.where(first, gains[2:3, 0:small], gains[2:3, small : 2 * small])
    k_gain[...] = jnp.where(first, gains[3:4, 0:small], gains[3:4, small : 2 * small])
    for copy in stores + whole:
        copy.wait()


def result_call(chunks, gains, grad_hidden, out_hidden):
    part, width = grad_hidden.shape
    f32 = jnp.float32
    shape = jax.ShapeDtypeStruct
    half = width // 2
    q, k, v, o = (half, 512), (half, 256), (half, 256), (512, half)
    gate, up, down = (half, 768), (half, 768), (768, half)
    sizes = [q, k, v, (1, 64), (1, 64), o, (1, half), gate, up, down]
    outs = [shape((part, width), f32), shape((part, width), out_hidden.dtype), shape((1, half), f32)]
    outs += [shape(z, f32) for z in sizes]
    specs = [ANY_SPEC] * 2 + [VMEM_SPEC] + [ANY_SPEC] * 3 + [VMEM_SPEC] * 2 + [ANY_SPEC, VMEM_SPEC]
    return pl.pallas_call(
        result_kernel,
        name="result",
        out_shape=outs,
        in_specs=[ANY_SPEC, VMEM_SPEC, ANY_SPEC, ANY_SPEC],
        out_specs=specs + [ANY_SPEC] * 3,
        scratch_shapes=[pltpu.VMEM((CHUNKS, 256, 512), jnp.bfloat16)]
        + [pltpu.VMEM(z, f32) for z in (q, k, v, o, gate, up, down)]
        + [pltpu.VMEM((part, width), f32), pltpu.VMEM((part, width), out_hidden.dtype)]
        + [pltpu.SemaphoreType.DMA((CHUNKS + 2,)), pltpu.SemaphoreType.DMA((CHUNKS + 2,))],
        compiler_params=pltpu.CompilerParams(vmem_limit_bytes=60 << 20),
    )(chunks, gains, grad_hidden, out_hidden)


def fast_device(
    hidden,
    segments,
    cotangent,
    attn_gain,
    w_query,
    key_weight_matrix,
    value_weight_matrix,
    query_gain,
    key_gain,
    mixer_exit_coefficients,
    mlp_gain,
    w_gate,
    w_up,
    w_down,
):
    gains_own, at = 0, 0
    every = (attn_gain, mlp_gain, query_gain, key_gain)
    total = sum(gain.shape[0] for gain in every)
    for gain in every:
        gains_own += jnp.pad(gain[None], ((0, 0), (at, total - at - gain.shape[0])))
        at += gain.shape[0]
    exponents = 2.0 * (np.arange(HEAD_SIZE) % (HEAD_SIZE // 2)) / HEAD_SIZE
    rates = np.power(rope_base, -exponents).astype(np.float32)[None]
    labels = segments.reshape(-1, HEAD_SIZE)
    (gains, rows, q_proj, k_proj, query, keys, values, cosine, sine, attended, low, wqkv, crows,
     wo_got, wg_got, wu_got) = forward_call(
        hidden[0], cotangent[0], gains_own, labels, jnp.asarray(rates), w_query, key_weight_matrix,
        value_weight_matrix, mixer_exit_coefficients, w_gate, w_up,
    )
    def units(chunks, count):
        return chunks.reshape(count, 128, 512)

    d_middle, mlp_gain_grad, brow, own, give, parts, out_own = mlp_call(
        (low, hidden[0], gains),
        (crows, mixer_exit_coefficients, wo_got, w_gate, wg_got, w_up, wu_got, w_down),
    )
    out_hidden, grad_hidden, sums, chunks = backward_call(
        (query, gains, mlp_gain_grad),
        (hidden[0], brow, low, attended, mixer_exit_coefficients, wo_got, d_middle, q_proj, wqkv, units(own, EARLY), units(give, EARLY - MATED),
         parts, out_own, keys, values, k_proj, cosine, sine, rows),
    )
    (grad_hidden, out_hidden, attn, wq, wk, wv, q_gain, k_gain, wo, mlp, wg, wu, wd) = result_call(
        chunks.reshape(CHUNKS, 256, 512), sums, grad_hidden, out_hidden
    )
    return (
        out_hidden[None], grad_hidden[None], attn[0], wq, wk, wv, q_gain[0], k_gain[0], wo, mlp[0],
        wg, wu, wd,
    )


def per_device(
    hidden,
    segments,
    cotangent,
    attn_gain,
    w_query,
    key_weight_matrix,
    value_weight_matrix,
    query_gain,
    key_gain,
    mixer_exit_coefficients,
    mlp_gain,
    w_gate,
    w_up,
    w_down,
):
    collected_rows = (
        lax.all_gather(attn_gain, SHARD_AXIS, axis=0, tiled=True),
        lax.all_gather(w_query, SHARD_AXIS, axis=0, tiled=True),
        lax.all_gather(key_weight_matrix, SHARD_AXIS, axis=0, tiled=True),
        lax.all_gather(value_weight_matrix, SHARD_AXIS, axis=0, tiled=True),
        lax.all_gather(query_gain, SHARD_AXIS, axis=0, tiled=True),
        lax.all_gather(key_gain, SHARD_AXIS, axis=0, tiled=True),
        lax.all_gather(mixer_exit_coefficients, SHARD_AXIS, axis=1, tiled=True),
        lax.all_gather(mlp_gain, SHARD_AXIS, axis=0, tiled=True),
        lax.all_gather(w_gate, SHARD_AXIS, axis=0, tiled=True),
        lax.all_gather(w_up, SHARD_AXIS, axis=0, tiled=True),
        lax.all_gather(w_down, SHARD_AXIS, axis=1, tiled=True),
    )
    gain_attn = collected_rows[0].astype(jnp.float32)
    gain_query = collected_rows[4].astype(jnp.float32)
    gain_key = collected_rows[5].astype(jnp.float32)
    gain_mlp = collected_rows[7].astype(jnp.float32)
    seq_count = hidden.shape[0]
    block_rows = hidden.shape[1] * lax.axis_size(TP_AXIS)
    seq_length = segments.shape[1]
    ctx_index = lax.axis_index(CTX_AXIS)
    heads_local = w_query.shape[1] // HEAD_SIZE
    kv_local = key_weight_matrix.shape[1] // HEAD_SIZE
    query_group_width = heads_local // kv_local
    score_scale = HEAD_SIZE ** (-0.5)
    block_start = ctx_index * block_rows
    query_pos = block_start + jnp.arange(block_rows, dtype=jnp.int32)
    query_seg = lax.dynamic_slice_in_dim(segments, block_start, block_rows, 1)
    positions = lax.dynamic_slice_in_dim(doc_positions(segments), block_start, block_rows, 1)
    cosine, sine_part = rope_tables(positions)

    def counting_keys(key_first, step_rows):
        early = key_first <= block_start + block_rows - 1
        last_seg = lax.dynamic_slice_in_dim(segments, key_first + step_rows - 1, 1, 1)[:, 0]
        return early & jnp.any(last_seg >= query_seg[:, 0])

    inputs = hidden.astype(jnp.float32)
    scale_one = rms_scale(inputs)
    attention_input = (inputs * scale_one * gain_attn).astype(jnp.bfloat16)
    attention_rows = tp_rows(attention_input)
    q_proj = jnp.einsum(
        "zjr,rm->zjm", attention_rows, collected_rows[1], preferred_element_type=jnp.float32
    ).reshape(seq_count, block_rows, heads_local, HEAD_SIZE)
    key_projected = jnp.einsum(
        "zjr,rm->zjm", attention_rows, collected_rows[2], preferred_element_type=jnp.float32
    ).reshape(seq_count, block_rows, kv_local, HEAD_SIZE)
    value_projected = jnp.einsum(
        "zjr,rm->zjm", attention_rows, collected_rows[3], preferred_element_type=jnp.float32
    )
    q_scale = rms_scale(q_proj)
    k_scale = rms_scale(key_projected)
    query_rows_input = (
        rotate(q_proj * q_scale * gain_query, cosine, sine_part)
        .astype(jnp.bfloat16)
        .reshape(seq_count, block_rows, kv_local, query_group_width, HEAD_SIZE)
    )
    keys = rotate(key_projected * k_scale * gain_key, cosine, sine_part).astype(jnp.bfloat16)
    values = value_projected.astype(jnp.bfloat16).reshape(
        seq_count, block_rows, kv_local, HEAD_SIZE
    )
    stat_shape = (seq_count, kv_local, query_group_width, block_rows)
    start_state = (
        jnp.full(stat_shape, masked_fill, jnp.float32),
        jnp.zeros(stat_shape, jnp.float32),
        jnp.zeros(stat_shape + (HEAD_SIZE,), jnp.float32),
    )
    piece_keys = lax.all_gather(keys, CTX_AXIS, axis=1, tiled=True)
    piece_values = lax.all_gather(values, CTX_AXIS, axis=1, tiled=True)
    piece_rows = piece_keys.shape[1]
    step_rows = math.gcd(piece_rows, 1024)

    def attend_one_step(number, loop_state):
        offset = number * step_rows
        key_first = offset

        def attend_compute(state):
            row_max, row_total, summed = state
            key_part = lax.dynamic_slice_in_dim(piece_keys, offset, step_rows, 1)
            value_part = lax.dynamic_slice_in_dim(piece_values, offset, step_rows, 1)
            allowed = key_block(segments, key_first, step_rows, query_pos, query_seg)
            scores = (
                jnp.einsum(
                    "sqhgd,skhd->shgqk",
                    query_rows_input,
                    key_part,
                    preferred_element_type=jnp.float32,
                )
                * score_scale
            )
            masked = jnp.where(allowed, scores, masked_fill)
            new_max = jnp.maximum(row_max, jnp.max(masked, axis=-1))
            weights = jnp.where(allowed, jnp.exp(masked - new_max[..., None]), 0.0)
            decay_factor = jnp.exp(row_max - new_max)
            row_total = row_total * decay_factor + jnp.sum(weights, axis=-1)
            summed = summed * decay_factor[..., None] + jnp.einsum(
                "shgqk,skhd->shgqd",
                weights.astype(jnp.bfloat16),
                value_part,
                preferred_element_type=jnp.float32,
            )
            return (new_max, row_total, summed)

        return lax.cond(counting_keys(key_first, step_rows), attend_compute, keep_state, loop_state)

    row_max, row_total, summed = lax.fori_loop(
        0, piece_rows // step_rows, attend_one_step, start_state
    )
    attended = summed / row_total[..., None]
    log_total = row_max + jnp.log(row_total)
    attended_reduced_copy = (
        attended.transpose(0, 3, 1, 2, 4)
        .reshape(seq_count, block_rows, heads_local * HEAD_SIZE)
        .astype(jnp.bfloat16)
    )
    branch = tp_total(
        jnp.einsum(
            "vkq,qy->vky",
            attended_reduced_copy,
            collected_rows[6],
            preferred_element_type=jnp.float32,
        )
    )
    middle = inputs + branch
    scale_two = rms_scale(middle)
    mlp_in = (middle * scale_two * gain_mlp).astype(jnp.bfloat16)
    mlp_rows = tp_rows(mlp_in)
    gate = jnp.einsum(
        "snd,df->snf", mlp_rows, collected_rows[8], preferred_element_type=jnp.float32
    )
    upward = jnp.einsum(
        "snd,df->snf", mlp_rows, collected_rows[9], preferred_element_type=jnp.float32
    )
    activated = (jax.nn.silu(gate) * upward).astype(jnp.bfloat16)
    out_hidden = (
        middle
        + tp_total(
            jnp.einsum(
                "snf,fd->snd", activated, collected_rows[10], preferred_element_type=jnp.float32
            )
        )
    ).astype(jnp.bfloat16)
    again = (
        lax.all_gather(attn_gain, SHARD_AXIS, axis=0, tiled=True),
        lax.all_gather(w_query, SHARD_AXIS, axis=0, tiled=True),
        lax.all_gather(key_weight_matrix, SHARD_AXIS, axis=0, tiled=True),
        lax.all_gather(value_weight_matrix, SHARD_AXIS, axis=0, tiled=True),
        lax.all_gather(query_gain, SHARD_AXIS, axis=0, tiled=True),
        lax.all_gather(key_gain, SHARD_AXIS, axis=0, tiled=True),
        lax.all_gather(mixer_exit_coefficients, SHARD_AXIS, axis=1, tiled=True),
        lax.all_gather(mlp_gain, SHARD_AXIS, axis=0, tiled=True),
        lax.all_gather(w_gate, SHARD_AXIS, axis=0, tiled=True),
        lax.all_gather(w_up, SHARD_AXIS, axis=0, tiled=True),
        lax.all_gather(w_down, SHARD_AXIS, axis=1, tiled=True),
    )
    query_backward = again[1]
    lookup_pullback = again[2]
    value_backward = again[3]
    output_backward = again[6]
    back_gate = again[8]
    back_up = again[9]
    back_down = again[10]
    d_out = cotangent.astype(jnp.float32)
    d_rows = tp_rows(cotangent)
    grad_down = jnp.einsum("snf,snd->fd", activated, d_rows, preferred_element_type=jnp.float32)
    d_act = jnp.einsum("snd,fd->snf", d_rows, back_down, preferred_element_type=jnp.float32)
    sigmoid_gate = jax.nn.sigmoid(gate)
    d_upward = (d_act * jax.nn.silu(gate)).astype(jnp.bfloat16)
    d_gate = (d_act * upward * sigmoid_gate * (1.0 + gate * (1.0 - sigmoid_gate))).astype(
        jnp.bfloat16
    )
    grad_gate = jnp.einsum("snd,snf->df", mlp_rows, d_gate, preferred_element_type=jnp.float32)
    grad_up = jnp.einsum("snd,snf->df", mlp_rows, d_upward, preferred_element_type=jnp.float32)
    d_mlp_in = tp_total(
        jnp.einsum("snf,df->snd", d_gate, back_gate, preferred_element_type=jnp.float32)
        + jnp.einsum("snf,df->snd", d_upward, back_up, preferred_element_type=jnp.float32)
    )
    grad_mlp_gain = jnp.sum(d_mlp_in * middle * scale_two, axis=(0, 1))
    d_middle = d_out + rms_back(d_mlp_in, middle, scale_two, gain_mlp)
    d_branch = d_middle.astype(jnp.bfloat16)
    residual_branch_rows = tp_rows(d_branch)
    result_cotangent = jnp.einsum(
        "xbj,xbk->jk",
        attended_reduced_copy,
        residual_branch_rows,
        preferred_element_type=jnp.float32,
    )
    d_attended = (
        jnp.einsum(
            "miv,cv->mic", residual_branch_rows, output_backward, preferred_element_type=jnp.float32
        )
        .astype(jnp.bfloat16)
        .reshape(seq_count, block_rows, kv_local, query_group_width, HEAD_SIZE)
    )
    delta = jnp.sum(d_attended.astype(jnp.float32).transpose(0, 2, 3, 1, 4) * attended, axis=-1)
    query_zeros = jnp.zeros(
        (seq_count, block_rows, kv_local, query_group_width, HEAD_SIZE), jnp.float32
    )
    back_state = (
        query_zeros,
        jnp.zeros((seq_count, seq_length, kv_local, HEAD_SIZE), jnp.float32),
        jnp.zeros((seq_count, seq_length, kv_local, HEAD_SIZE), jnp.float32),
    )
    back_piece_keys = lax.all_gather(keys, CTX_AXIS, axis=1, tiled=True)
    back_piece_values = lax.all_gather(values, CTX_AXIS, axis=1, tiled=True)
    piece_rows = back_piece_keys.shape[1]
    back_step_rows = math.gcd(piece_rows, 1024)

    def back_one_step(number, loop_state):
        offset = number * back_step_rows
        key_first = offset
        write_at = offset

        def back_compute(state):
            d_query, d_keys, d_values = state
            key_part = lax.dynamic_slice_in_dim(back_piece_keys, offset, back_step_rows, 1)
            value_part = lax.dynamic_slice_in_dim(back_piece_values, offset, back_step_rows, 1)
            allowed = key_block(segments, key_first, back_step_rows, query_pos, query_seg)
            scores = (
                jnp.einsum(
                    "sqhgd,skhd->shgqk",
                    query_rows_input,
                    key_part,
                    preferred_element_type=jnp.float32,
                )
                * score_scale
            )
            probs = jnp.where(allowed, jnp.exp(scores - log_total[..., None]), 0.0)
            d_probs = jnp.einsum(
                "sqhgd,skhd->shgqk", d_attended, value_part, preferred_element_type=jnp.float32
            )
            d_scores = (probs * (d_probs - delta[..., None])).astype(jnp.bfloat16)
            d_query = d_query + jnp.einsum(
                "shgqk,skhd->sqhgd", d_scores, key_part, preferred_element_type=jnp.float32
            )
            key_grad = jnp.einsum(
                "shgqk,sqhgd->skhd", d_scores, query_rows_input, preferred_element_type=jnp.float32
            )
            value_grad = jnp.einsum(
                "shgqk,sqhgd->skhd",
                probs.astype(jnp.bfloat16),
                d_attended,
                preferred_element_type=jnp.float32,
            )
            d_keys = lax.dynamic_update_slice_in_dim(
                d_keys,
                lax.dynamic_slice_in_dim(d_keys, write_at, back_step_rows, 1) + key_grad,
                write_at,
                1,
            )
            d_values = lax.dynamic_update_slice_in_dim(
                d_values,
                lax.dynamic_slice_in_dim(d_values, write_at, back_step_rows, 1) + value_grad,
                write_at,
                1,
            )
            return (d_query, d_keys, d_values)

        return lax.cond(
            counting_keys(key_first, back_step_rows), back_compute, keep_state, loop_state
        )

    d_query, d_keys, d_values = lax.fori_loop(
        0, piece_rows // back_step_rows, back_one_step, back_state
    )
    own_keys, own_values = (
        lax.psum_scatter(
            d_keys.astype(jnp.bfloat16), CTX_AXIS, scatter_dimension=1, tiled=True
        ).astype(jnp.float32),
        lax.psum_scatter(
            d_values.astype(jnp.bfloat16), CTX_AXIS, scatter_dimension=1, tiled=True
        ).astype(jnp.float32),
    )
    q_normed = rotate_back(
        d_query.reshape(seq_count, block_rows, heads_local, HEAD_SIZE) * score_scale,
        cosine,
        sine_part,
    )
    grad_query_gain = jnp.sum(q_normed * q_proj * q_scale, axis=(0, 1, 2))
    query_projection_gradient = (
        rms_back(q_normed, q_proj, q_scale, gain_query)
        .astype(jnp.bfloat16)
        .reshape(seq_count, block_rows, heads_local * HEAD_SIZE)
    )
    k_normed = rotate_back(own_keys * score_scale, cosine, sine_part)
    grad_key_gain = jnp.sum(k_normed * key_projected * k_scale, axis=(0, 1, 2))
    lookup_map_derivative = (
        rms_back(k_normed, key_projected, k_scale, gain_key)
        .astype(jnp.bfloat16)
        .reshape(seq_count, block_rows, kv_local * HEAD_SIZE)
    )
    value_projection_gradient = own_values.astype(jnp.bfloat16).reshape(
        seq_count, block_rows, kv_local * HEAD_SIZE
    )
    query_gradient_rows = jnp.einsum(
        "zqr,zqa->ra", attention_rows, query_projection_gradient, preferred_element_type=jnp.float32
    )
    key_gradient_rows = jnp.einsum(
        "zqr,zqa->ra", attention_rows, lookup_map_derivative, preferred_element_type=jnp.float32
    )
    value_gradient_rows = jnp.einsum(
        "zqr,zqa->ra", attention_rows, value_projection_gradient, preferred_element_type=jnp.float32
    )
    d_attn_in = tp_total(
        jnp.einsum(
            "wtl,al->wta",
            query_projection_gradient,
            query_backward,
            preferred_element_type=jnp.float32,
        )
        + jnp.einsum(
            "wtl,al->wta",
            lookup_map_derivative,
            lookup_pullback,
            preferred_element_type=jnp.float32,
        )
        + jnp.einsum(
            "wtl,al->wta",
            value_projection_gradient,
            value_backward,
            preferred_element_type=jnp.float32,
        )
    )
    grad_attn_gain = jnp.sum(d_attn_in * inputs * scale_one, axis=(0, 1))
    grad_hidden = d_middle + rms_back(d_attn_in, inputs, scale_one, gain_attn)
    reduced = (
        lax.psum_scatter(
            grad_attn_gain.astype(jnp.bfloat16), SHARD_AXIS, scatter_dimension=0, tiled=True
        ).astype(jnp.float32),
        lax.psum_scatter(
            query_gradient_rows.astype(jnp.bfloat16), SHARD_AXIS, scatter_dimension=0, tiled=True
        ).astype(jnp.float32),
        lax.psum_scatter(
            key_gradient_rows.astype(jnp.bfloat16), SHARD_AXIS, scatter_dimension=0, tiled=True
        ).astype(jnp.float32),
        lax.psum_scatter(
            value_gradient_rows.astype(jnp.bfloat16), SHARD_AXIS, scatter_dimension=0, tiled=True
        ).astype(jnp.float32),
        lax.psum_scatter(
            grad_query_gain.astype(jnp.bfloat16), SHARD_AXIS, scatter_dimension=0, tiled=True
        ).astype(jnp.float32),
        lax.psum_scatter(
            grad_key_gain.astype(jnp.bfloat16), SHARD_AXIS, scatter_dimension=0, tiled=True
        ).astype(jnp.float32),
        lax.psum_scatter(
            result_cotangent.astype(jnp.bfloat16), SHARD_AXIS, scatter_dimension=1, tiled=True
        ).astype(jnp.float32),
        lax.psum_scatter(
            grad_mlp_gain.astype(jnp.bfloat16), SHARD_AXIS, scatter_dimension=0, tiled=True
        ).astype(jnp.float32),
        lax.psum_scatter(
            grad_gate.astype(jnp.bfloat16), SHARD_AXIS, scatter_dimension=0, tiled=True
        ).astype(jnp.float32),
        lax.psum_scatter(
            grad_up.astype(jnp.bfloat16), SHARD_AXIS, scatter_dimension=0, tiled=True
        ).astype(jnp.float32),
        lax.psum_scatter(
            grad_down.astype(jnp.bfloat16), SHARD_AXIS, scatter_dimension=1, tiled=True
        ).astype(jnp.float32),
    )
    matrices = (
        lax.psum(reduced[1].astype(jnp.bfloat16), CTX_AXIS).astype(jnp.float32),
        lax.psum(reduced[2].astype(jnp.bfloat16), CTX_AXIS).astype(jnp.float32),
        lax.psum(reduced[3].astype(jnp.bfloat16), CTX_AXIS).astype(jnp.float32),
        lax.psum(reduced[6].astype(jnp.bfloat16), CTX_AXIS).astype(jnp.float32),
        lax.psum(reduced[8].astype(jnp.bfloat16), CTX_AXIS).astype(jnp.float32),
        lax.psum(reduced[9].astype(jnp.bfloat16), CTX_AXIS).astype(jnp.float32),
        lax.psum(reduced[10].astype(jnp.bfloat16), CTX_AXIS).astype(jnp.float32),
    )
    gains = lax.psum((reduced[0], reduced[4], reduced[5], reduced[7]), (CTX_AXIS, TP_AXIS))
    return (
        out_hidden,
        grad_hidden,
        gains[0],
        matrices[0],
        matrices[1],
        matrices[2],
        gains[1],
        gains[2],
        matrices[3],
        gains[3],
        matrices[4],
        matrices[5],
        matrices[6],
    )


def solution(mesh):
    in_specs = (
        P(SHARD_AXIS, (CTX_AXIS, TP_AXIS), None),
        P(SHARD_AXIS, None),
        P(SHARD_AXIS, (CTX_AXIS, TP_AXIS), None),
        P(SHARD_AXIS),
        P(SHARD_AXIS, TP_AXIS),
        P(SHARD_AXIS, TP_AXIS),
        P(SHARD_AXIS, TP_AXIS),
        P(SHARD_AXIS),
        P(SHARD_AXIS),
        P(TP_AXIS, SHARD_AXIS),
        P(SHARD_AXIS),
        P(SHARD_AXIS, TP_AXIS),
        P(SHARD_AXIS, TP_AXIS),
        P(TP_AXIS, SHARD_AXIS),
    )
    out_specs = (
        P(SHARD_AXIS, (CTX_AXIS, TP_AXIS), None),
        P(SHARD_AXIS, (CTX_AXIS, TP_AXIS), None),
        P(SHARD_AXIS),
        P(SHARD_AXIS, TP_AXIS),
        P(SHARD_AXIS, TP_AXIS),
        P(SHARD_AXIS, TP_AXIS),
        P(SHARD_AXIS),
        P(SHARD_AXIS),
        P(TP_AXIS, SHARD_AXIS),
        P(SHARD_AXIS),
        P(SHARD_AXIS, TP_AXIS),
        P(SHARD_AXIS, TP_AXIS),
        P(TP_AXIS, SHARD_AXIS),
    )
    shape = mesh.shape
    fast = shape[SHARD_AXIS] == 2 and shape[CTX_AXIS] == 4 and shape[TP_AXIS] == 4
    return jax.shard_map(
        fast_device if fast else per_device, mesh=mesh, in_specs=in_specs, out_specs=out_specs, check_vma=False
    )
```

```python
import functools
import math

import jax
import jax.numpy as jnp
import numpy as np
from jax import lax
from jax.experimental import pallas as pl
from jax.experimental.pallas import tpu as pltpu
from jax.sharding import PartitionSpec as P

SHARD_AXIS, CTX_AXIS, TP_AXIS = "shard", "ctx", "tp"
HEAD_SIZE = 128
NDOC = 8


norm_eps = 1e-06
rope_base = 1000000.0
masked_fill = -1e30


def rms_scale(values):
    return lax.rsqrt(jnp.mean(values * values, axis=-1, keepdims=True) + norm_eps)


def rms_back(grad_out, values, row_scale, gain_vec):
    scaled = grad_out * gain_vec
    inner_sum = jnp.mean(scaled * values, axis=-1, keepdims=True)
    return row_scale * scaled - values * (row_scale * row_scale * row_scale) * inner_sum


def doc_positions(segments):
    seq_width = segments.shape[-1]
    labels = jnp.arange(NDOC, dtype=jnp.int32)
    onehot = (segments[..., None] == labels).astype(jnp.int32)
    counts = jnp.sum(onehot, axis=-2)
    starts = jnp.cumsum(counts, axis=-1) - counts
    first_row = jnp.sum(onehot * starts[..., None, :], axis=-1)
    return jnp.arange(seq_width, dtype=jnp.int32) - first_row


def rope_tables(positions):
    exponents = jnp.arange(0, HEAD_SIZE, 2).astype(jnp.float32) / HEAD_SIZE
    angle_rates = jnp.power(jnp.float32(rope_base), -exponents)
    angles = positions.astype(jnp.float32)[..., None] * angle_rates
    angles = jnp.concatenate([angles, angles], axis=-1)[..., None, :]
    return (jnp.cos(angles), jnp.sin(angles))


def rotate(inputs, cosine, sine_part):
    half_dim = inputs.shape[-1] // 2
    turned = jnp.concatenate([-inputs[..., half_dim:], inputs[..., :half_dim]], axis=-1)
    return inputs * cosine + turned * sine_part


def rotate_back(grads, cosine, sine_part):
    half_dim = grads.shape[-1] // 2
    moved = grads * sine_part
    turned = jnp.concatenate([moved[..., half_dim:], -moved[..., :half_dim]], axis=-1)
    return grads * cosine + turned


def tp_rows(local_part):
    return lax.all_gather(local_part, TP_AXIS, axis=1, tiled=True)


def tp_total(partial_sum):
    return lax.psum_scatter(
        partial_sum.astype(jnp.bfloat16), TP_AXIS, scatter_dimension=1, tiled=True
    ).astype(jnp.float32)


def key_block(segments, key_first, step_rows, query_pos, query_seg):
    key_pos = key_first + jnp.arange(step_rows, dtype=jnp.int32)
    key_seg = lax.dynamic_slice_in_dim(segments, key_first, step_rows, 1)
    allowed = (key_pos[None, None, :] <= query_pos[None, :, None]) & (
        key_seg[:, None, :] == query_seg[:, :, None]
    )
    return allowed[:, None, None]


def keep_state(state):
    return state


CHUNKS = 15
FROM_MLP = 9
READY = 2
UNITS, EARLY, MATED, LATE = 2 * CHUNKS, 2 * FROM_MLP, 2 * READY, 22


MESH_ID = pl.DeviceIdType.MESH
ANY_SPEC = pl.BlockSpec(memory_space=pl.ANY)
VMEM_SPEC = pl.BlockSpec(memory_space=pltpu.VMEM)
SCORE_STEP = HEAD_SIZE ** (-0.5) * math.log2(math.e)
APART = 16384.0


def enter(peers):
    barrier = pltpu.get_barrier_semaphore()
    for peer in peers:
        pl.semaphore_signal(barrier, inc=1, device_id=peer, device_id_type=MESH_ID)
    pl.semaphore_wait(barrier, len(peers))


def last_dot(left, right):
    return lax.dot_general(
        left, right, (((1,), (1,)), ((), ())), preferred_element_type=jnp.float32
    )


def flat_dot(left, right):
    return jnp.dot(left, right, preferred_element_type=jnp.float32)


def first_dot(left, right):
    return lax.dot_general(
        left, right, (((0,), (0,)), ((), ())), preferred_element_type=jnp.float32
    )


def spin(values, cosine, sine_signed):
    return values * cosine + pltpu.roll(values, HEAD_SIZE // 2, 1) * sine_signed


class Links:
    def __init__(self, send, recv):
        self.send, self.recv, self.used = send, recv, 0

    def copy(self, src, dst, device):
        number = self.used
        self.used += 1
        return pltpu.make_async_remote_copy(
            src_ref=src, dst_ref=dst, send_sem=self.send.at[number],
            recv_sem=self.recv.at[number], device_id=device, device_id_type=MESH_ID,
        )


class Locals:
    def __init__(self, sems):
        self.sems, self.used, self.open = sems, 0, []

    def make(self, src, dst):
        copy = pltpu.make_async_copy(src, dst, self.sems.at[self.used])
        self.used += 1
        return copy

    def start(self, src, dst):
        copy = self.make(src, dst)
        copy.start()
        self.open.append(copy)
        return copy

    def wait(self, copy):
        copy.wait()
        self.open = [other for other in self.open if other is not copy]

    def finish(self):
        for copy in self.open:
            copy.wait()


def forward_kernel(
    hidden, cotangent, attn_gain, mlp_gain, query_gain, key_gain, segments, rates, wq, wk, wv, wo, wg, wu,
    gains_out, rows_out, q_out, k_out, query_out, keys_out, values_out, cos_out, sin_out,
    attended_out, low_out, wqkv_out, crows_out, wo_out, wg_out, wu_out,
    gains, raw, rows, wqkv, q_proj, k_proj, qaug, kaug, vaug, cosine, sine, acc, low, crows,
    gains_in, gains_land, places, send, recv, local,
):
    s, c, t = lax.axis_index(SHARD_AXIS), lax.axis_index(CTX_AXIS), lax.axis_index(TP_AXIS)
    nctx = lax.axis_size(CTX_AXIS)
    part = hidden.shape[0]
    block = 4 * part
    half = wq.shape[0]
    f32, bf16 = jnp.float32, jnp.bfloat16
    side, across, mate = {TP_AXIS: t ^ 1}, {TP_AXIS: t ^ 2}, {SHARD_AXIS: 1 - s}
    pair = {CTX_AXIS: c ^ 1}
    nxt, prv = {CTX_AXIS: lax.rem(c + 1, nctx)}, {CTX_AXIS: lax.rem(c + nctx - 1, nctx)}
    gains_in[...] = jnp.zeros(gains_in.shape, f32)
    for row, gain in enumerate((attn_gain, mlp_gain)):
        own_gain = gain[...].astype(f32)[None, :]
        gains_in[row : row + 1, pl.ds(pl.multiple_of(s * half, half), half)] = own_gain
    small = HEAD_SIZE // 2
    source_lane = lax.broadcasted_iota(jnp.int32, (small, HEAD_SIZE), 0)
    target_lane = lax.broadcasted_iota(jnp.int32, (small, HEAD_SIZE), 1) - s * small
    chosen = jnp.where(source_lane == target_lane, 1.0, 0.0).astype(bf16)
    for row, gain in ((2, query_gain), (3, key_gain)):
        placed = flat_dot(jnp.broadcast_to(gain[...][None, :], (16, small)), chosen)
        gains_in[row : row + 1, 0:HEAD_SIZE] = placed[0:1]
    enter([side, across, mate, nxt, prv])
    links, locals_ = Links(send, recv), Locals(local)

    def piece(owner):
        return pl.ds(pl.multiple_of(owner * part, part), part)

    low_bit = c & 1

    def some(shard, count, size):
        return pl.ds(pl.multiple_of(shard * count + low_bit * size, size), size)

    mine = pl.ds(pl.multiple_of(s * half, half), half)
    quarter = half // 2
    gains_copy = links.copy(gains_in, gains_land, mate)
    wk_copy = links.copy(wk, wqkv.at[mine, 512:768], mate)
    wv_copy = links.copy(wv, wqkv.at[mine, 768:1024], mate)
    wq_copy = links.copy(wq, wqkv.at[mine, 0:512], mate)
    wo_copy = links.copy(
        wo.at[some(0, 0, quarter), :], wo_out.at[some(0, 0, quarter), :], mate
    )
    wo_got = wo_out.at[some(0, 0, quarter), :]
    wo_on = links.copy(wo_got, wo_got, pair)
    wg_copy = links.copy(
        wg.at[some(0, 0, quarter), :], wg_out.at[some(0, 0, quarter), :], mate
    )
    wg_got = wg_out.at[some(0, 0, quarter), :]
    wg_on = links.copy(wg_got, wg_got, pair)
    wu_copy = links.copy(
        wu.at[some(0, 0, quarter), :], wu_out.at[some(0, 0, quarter), :], mate
    )
    gains_copy.start()
    wk_copy.start()
    wv_copy.start()
    wq_copy.start()
    own_k = locals_.start(wk, wqkv.at[mine, 512:768])
    own_v = locals_.start(wv, wqkv.at[mine, 768:1024])
    own_q = locals_.start(wq, wqkv.at[mine, 0:512])
    own_c = locals_.start(cotangent, crows.at[piece(t), :])

    def source(b, owner):
        return hidden if b == 0 else raw.at[b, piece(owner)]

    to_across, to_side, on_to_side, to_next = [], [], [], []
    for b in range(3):
        there = raw.at[b, piece(t ^ 2)]
        to_side.append(links.copy(source(b, t), raw.at[b, piece(t)], side))
        on_to_side.append(links.copy(there, there, side))
        if b < 2:
            to_across.append(links.copy(source(b, t), raw.at[b, piece(t)], across))
            to_next.append(links.copy(source(b, t), raw.at[b + 1, piece(t)], nxt))
    far_to_next = links.copy(raw.at[1, piece(t ^ 2)], raw.at[2, piece(t ^ 2)], nxt)
    c_side = links.copy(cotangent, crows.at[piece(t), :], side)
    c_over = links.copy(cotangent, crows.at[piece(t), :], across)
    c_on = links.copy(crows.at[piece(t ^ 2), :], crows.at[piece(t ^ 2), :], side)
    to_across[0].start()
    to_side[0].start()

    @pl.when(c < nctx - 1)
    def _():
        to_next[0].start()

    c_side.start()
    raw[0, piece(t), :] = hidden[...]
    gains_copy.wait()
    gains[...] = gains_in[...] + gains_land[...]
    q_gain = gains[2:3, 0:HEAD_SIZE]
    k_gain = gains[3:4, 0:HEAD_SIZE]

    def table(b):
        start, stop, rate = places[0:1, :], places[1:2, :], rates[...]
        shape = (128, HEAD_SIZE)
        lower = lax.broadcasted_iota(jnp.int32, shape, 1) < HEAD_SIZE // 2

        @pl.loop(0, 4)
        def _(n):
            found = []
            for offset in (0, 512):
                first = n * 128 + offset
                index = (lax.broadcasted_iota(jnp.int32, shape, 0) + first) + (c - b) * block
                index = index.astype(f32)
                inside = (index >= start) & (index < stop)
                marks = jnp.where(inside, 1.0, 0.0)
                begin = jnp.sum(jnp.where(inside, start, 0.0), axis=1, keepdims=True)
                at = pl.ds(pl.multiple_of(first, 128), 128)
                for g in range(2):
                    kaug[b, g, at, 128:256] = (1.0 - marks).astype(bf16)
                if b == 0:
                    for h in range(4):
                        qaug[h, at, 128:256] = (marks * -APART).astype(bf16)
                found.append((at, index - begin))
            (low_at, low_pos), (high_at, high_pos) = found
            angle = jnp.where(lower, low_pos, high_pos) * rate
            cs, sn = jnp.cos(angle), jnp.sin(angle)
            cr, sr = pltpu.roll(cs, HEAD_SIZE // 2, 1), pltpu.roll(sn, HEAD_SIZE // 2, 1)
            cosine[b, low_at, :] = jnp.where(lower, cs, cr)
            cosine[b, high_at, :] = jnp.where(lower, cr, cs)
            sine[b, low_at, :] = jnp.where(lower, -sn, sr)
            sine[b, high_at, :] = jnp.where(lower, -sr, sn)

    def project_kv(b, owner):
        at = piece(owner)
        x = raw[b, at, :].astype(f32)
        scale = lax.rsqrt(jnp.mean(x * x, axis=-1, keepdims=True) + norm_eps)
        rows[b, at, :] = (x * scale * gains[0:1, :]).astype(bf16)
        got = flat_dot(rows[b, at, :], wqkv[:, 512:1024])
        k_proj[b, at, :] = got[:, 0:256]
        for g in range(2):
            u = got[:, g * 128 : g * 128 + 128]
            r = lax.rsqrt(jnp.mean(u * u, axis=-1, keepdims=True) + norm_eps)
            turned = spin(u * r * k_gain, cosine[b, at, :], sine[b, at, :])
            kaug[b, g, at, 0:128] = turned.astype(bf16)
            vaug[b, g, at, 0:128] = got[:, 256 + g * 128 : 384 + g * 128].astype(bf16)

    def project_q(owner):
        at = piece(owner)
        got = flat_dot(rows[0, at, :], wqkv[:, 0:512])
        q_proj[at, :] = got
        for h in range(4):
            u = got[:, h * 128 : h * 128 + 128]
            r = lax.rsqrt(jnp.mean(u * u, axis=-1, keepdims=True) + norm_eps)
            turned = spin(u * r * q_gain, cosine[0, at, :], sine[0, at, :])
            qaug[h, at, 0:128] = turned.astype(bf16)

    def unit(b, g, r, kc, bound):
        at = pl.ds(pl.multiple_of(r * 512, 512), 512)
        for hh in range(2):
            qq = qaug[2 * g + hh, at, :]
            total = None
            for j in range(2):
                keys_at = pl.ds(pl.multiple_of(kc * 512 + j * 256, 256), 256)
                p = jnp.exp2(last_dot(qq, kaug[b, g, keys_at, :]) * SCORE_STEP)
                if bound is not None:
                    ahead = lax.broadcasted_iota(jnp.int32, p.shape, 0) - lax.broadcasted_iota(
                        jnp.int32, p.shape, 1
                    )
                    p = jnp.where(ahead >= bound + j * 256, p, 0.0)
                value = flat_dot(p.astype(bf16), vaug[b, g, keys_at, :])
                total = value if total is None else total + value
            acc[2 * g + hh, at, :] += total

    def block_outs(b):
        pairs = (
            (rows, rows_out), (k_proj, k_out), (kaug, keys_out), (vaug, values_out),
            (cosine, cos_out), (sine, sin_out),
        )
        return [locals_.make(a.at[b], d.at[b]) for a, d in pairs]

    outs = [block_outs(b) for b in range(3)]

    lane = lax.broadcasted_iota(jnp.int32, (1, HEAD_SIZE), 1)
    begin = jnp.full((1, HEAD_SIZE), float(nctx * block), f32)
    end = begin
    for label in range(NDOC):
        before = jnp.where(segments[...] < label, 1.0, 0.0)
        before = jnp.sum(before, axis=(0, 1), keepdims=True)
        begin = jnp.where(lane == label, before, begin)
        end = jnp.where(lane == label - 1, before, end)
    places[0:1, :] = begin
    places[1:2, :] = end
    table(0)
    vaug[:, :, :, 128:256] = jnp.ones((3, 2, block, 128), bf16)
    acc[...] = jnp.zeros(acc.shape, f32)
    locals_.wait(own_k)
    locals_.wait(own_v)
    wk_copy.wait()
    wv_copy.wait()
    wo_copy.start()
    to_across[0].wait_recv()
    on_to_side[0].start()

    @pl.when(c >= 1)
    def _():
        to_next[0].wait_recv()
        to_across[1].start()
        to_side[1].start()

        @pl.when(c < nctx - 1)
        def _():
            to_next[1].start()

    to_side[0].wait_recv()
    on_to_side[0].wait_recv()

    @pl.loop(0, 4)
    def _(n):
        project_kv(0, n)

    for copy in outs[0]:
        copy.start()

    @pl.when(c >= 1)
    def _():
        table(1)
        to_side[1].wait_recv()

        @pl.loop(0, 2)
        def _(n):
            project_kv(1, t ^ n)

    @pl.when(c >= 2)
    def _():
        table(2)

    locals_.wait(own_q)
    wq_copy.wait()
    wg_copy.start()

    @pl.when(c >= 1)
    def _():
        to_across[1].wait_recv()
        on_to_side[1].start()

        @pl.when(c < nctx - 1)
        def _():
            far_to_next.start()

        @pl.when(c >= 2)
        def _():
            to_next[1].wait_recv()
            to_side[2].start()

    c_over.start()

    @pl.loop(0, 4)
    def _(n):
        project_q(n)

    locals_.start(q_proj, q_out)
    locals_.start(wqkv, wqkv_out)

    @pl.loop(0, 6)
    def _(n):
        m = lax.rem(n, 3)
        unit(0, n // 3, (m + 1) // 2, m // 2, (m & 1) * -512)

    wo_copy.wait_recv()
    wo_on.start()
    wu_copy.start()

    @pl.when(c >= 1)
    def _():
        on_to_side[1].wait_recv()

        @pl.loop(2, 4)
        def _(n):
            project_kv(1, t ^ n)

        for copy in outs[1]:
            copy.start()

        @pl.loop(0, 8)
        def _(n):
            m = lax.rem(n, 4)
            unit(1, n // 4, m // 2, m & 1, None)

    wg_copy.wait_recv()
    wg_on.start()

    c_over.wait_recv()
    c_on.start()

    @pl.when(c >= 2)
    def _():
        far_to_next.wait_recv()
        on_to_side[2].start()
        to_side[2].wait_recv()
        on_to_side[2].wait_recv()

        @pl.loop(0, 4)
        def _(n):
            project_kv(2, n)

        for copy in outs[2]:
            copy.start()

        @pl.loop(0, 6)
        def _(n):
            m = lax.rem(n, 3)
            unit(2, n // 3, m // 2, (m + 1) // 2, None)

    for h in range(4):

        @pl.loop(0, 4)
        def _(r):
            at = pl.ds(pl.multiple_of(r * 256, 256), 256)
            total = acc[h, at, 128:256]
            value = acc[h, at, 0:128] / total
            acc[h, at, 0:128] = value
            shift = jnp.log(total) * -(HEAD_SIZE**0.5)
            top = shift.astype(bf16).astype(f32)
            mid = (shift - top).astype(bf16).astype(f32)
            lane = lax.broadcasted_iota(jnp.int32, shift.shape, 1)
            parts = jnp.where(lane == NDOC, top, 0.0)
            parts = jnp.where(lane == NDOC + 1, mid, parts)
            parts = jnp.where(lane == NDOC + 2, shift - top - mid, parts)
            qaug[h, at, 128:256] = qaug[h, at, 128:256] + parts.astype(bf16)
            low[h, at, :] = value.astype(bf16)

        lanes = slice(h * 128, h * 128 + 128)
        locals_.start(low.at[h], low_out.at[:, lanes])
        locals_.start(acc.at[h, :, 0:128], attended_out.at[:, lanes])
        locals_.start(qaug.at[h], query_out.at[h])

    locals_.start(gains, gains_out)
    locals_.wait(own_c)
    c_side.wait()
    c_on.wait()
    locals_.start(crows, crows_out)
    c_over.wait_send()
    to_across[0].wait_send()
    to_side[0].wait_send()
    on_to_side[0].wait_send()
    for copy in outs[0]:
        copy.wait()

    @pl.when(c < nctx - 1)
    def _():
        to_next[0].wait_send()

    for b in (1, 2):

        @pl.when(c >= b)
        def _():
            if b < 2:
                to_across[b].wait_send()
            to_side[b].wait_send()
            on_to_side[b].wait_send()
            for copy in outs[b]:
                copy.wait()

    @pl.when((c >= 1) & (c < nctx - 1))
    def _():
        to_next[1].wait_send()
        far_to_next.wait_send()

    wo_copy.wait_send()
    wo_on.wait()
    wg_copy.wait_send()
    wg_on.wait()
    wu_copy.wait()
    locals_.finish()


def forward_call(hidden, cotangent, gains, segments, rates, wq, wk, wv, wo, wg, wu):
    part, width = hidden.shape
    block = 4 * part
    f32, bf16 = jnp.float32, jnp.bfloat16
    shape = jax.ShapeDtypeStruct
    outs = (
        shape((8, width), f32),
        shape((3, block, width), bf16),
        shape((block, 512), f32),
        shape((3, block, 256), f32),
        shape((4, block, 256), bf16),
        shape((3, 2, block, 256), bf16),
        shape((3, 2, block, 256), bf16),
        shape((3, block, HEAD_SIZE), f32),
        shape((3, block, HEAD_SIZE), f32),
        shape((block, 512), f32),
        shape((block, 512), bf16),
        shape((width, 1024), bf16),
        shape((block, width), bf16),
        shape(wo.shape, bf16),
        shape(wg.shape, bf16),
        shape(wu.shape, bf16),
    )
    return pl.pallas_call(
        forward_kernel,
        name="forward",
        out_shape=outs,
        in_specs=[VMEM_SPEC] * 8 + [ANY_SPEC] * 6,
        out_specs=[ANY_SPEC] * len(outs),
        scratch_shapes=[
            pltpu.VMEM((8, width), f32),
            pltpu.VMEM((3, block, width), bf16),
            pltpu.VMEM((3, block, width), bf16),
            pltpu.VMEM((width, 1024), bf16),
            pltpu.VMEM((block, 512), f32),
            pltpu.VMEM((3, block, 256), f32),
            pltpu.VMEM((4, block, 256), bf16),
            pltpu.VMEM((3, 2, block, 256), bf16),
            pltpu.VMEM((3, 2, block, 256), bf16),
            pltpu.VMEM((3, block, HEAD_SIZE), f32),
            pltpu.VMEM((3, block, HEAD_SIZE), f32),
            pltpu.VMEM((4, block, 256), f32),
            pltpu.VMEM((4, block, 128), bf16),
            pltpu.VMEM((block, width), bf16),
            pltpu.VMEM((8, width), f32),
            pltpu.VMEM((8, width), f32),
            pltpu.VMEM((8, HEAD_SIZE), f32),
            pltpu.SemaphoreType.DMA((23,)),
            pltpu.SemaphoreType.DMA((23,)),
            pltpu.SemaphoreType.DMA((38,)),
        ],
        compiler_params=pltpu.CompilerParams(
            collective_id=0, has_side_effects=True, vmem_limit_bytes=58 << 20
        ),
    )(hidden, cotangent, *gains, segments, rates, wq, wk, wv, wo, wg, wu)


class Scatter:
    def __init__(self, links, bufs, side, across):
        self.bufs = bufs
        self.far = links.copy(bufs.at[0], bufs.at[3], side)
        self.over = links.copy(bufs.at[1], bufs.at[4], across)
        self.near = links.copy(bufs.at[2], bufs.at[5], side)

    def put_far(self, value):
        self.bufs[0] = value.astype(jnp.bfloat16)
        self.far.start()

    def put_over(self, value):
        self.far.wait_recv()
        self.bufs[1] = (value + self.bufs[3].astype(jnp.float32)).astype(jnp.bfloat16)
        self.over.start()

    def put_near(self, value):
        self.bufs[2] = value.astype(jnp.bfloat16)
        self.near.start()

    def total(self, value):
        self.near.wait_recv()
        self.over.wait_recv()
        return value + self.bufs[5].astype(jnp.float32) + self.bufs[4].astype(jnp.float32)

    def close(self):
        self.far.wait_send()
        self.over.wait_send()
        self.near.wait_send()


def mlp_kernel(
    low, hidden, gains, crows_in, wo_own, wo_got, wg_own, wg_got, wu_own, wu_got,
    wd,
    d_middle_out, gain_out, brow_out, own_out, give_out, parts_out, out_own_out,
    wo, wgf, wuf, wdf, mrows, act, dgate, dup, brow, kept, middle, bufs, parts, give, own, land,
    crows, result, send, recv, local,
):
    s, c, t = lax.axis_index(SHARD_AXIS), lax.axis_index(CTX_AXIS), lax.axis_index(TP_AXIS)
    part = hidden.shape[0]
    half = wd.shape[1]
    bf16, f32 = jnp.bfloat16, jnp.float32
    side, across = {TP_AXIS: t ^ 1}, {TP_AXIS: t ^ 2}
    mate, pair = {SHARD_AXIS: 1 - s}, {CTX_AXIS: c ^ 1}
    links, locals_ = Links(send, recv), Locals(local)

    def piece(owner):
        return pl.ds(pl.multiple_of(owner * part, part), part)

    mine = pl.ds(pl.multiple_of(s * half, half), half)
    theirs = pl.ds(pl.multiple_of((1 - s) * half, half), half)
    low_bit = c & 1

    def some(shard, count, size):
        return pl.ds(pl.multiple_of(shard * count + low_bit * size, size), size)

    quarter = half // 2
    third = wd.shape[0] // 2
    wu_at = some(1 - s, half, quarter)
    wu_on = links.copy(wu_got.at[some(0, 0, quarter), :], wuf.at[wu_at, :], pair)
    wd_copy = links.copy(
        wd.at[some(0, 0, third), :], wdf.at[some(0, 0, third), mine], mate
    )
    wd_got = wdf.at[some(0, 0, third), theirs]
    wd_on = links.copy(wd_got, wd_got, pair)
    wo_loads = [
        locals_.start(wo_own, wo.at[:, mine]),
        locals_.start(wo_got, wo.at[:, theirs]),
    ]
    enter([side, across, mate, pair])
    wu_on.start()
    wd_copy.start()
    own_weights = [
        locals_.start(wg_own, wgf.at[mine, :]),
        locals_.start(wg_got, wgf.at[theirs, :]),
        locals_.start(wu_own, wuf.at[mine, :]),
        locals_.start(wu_got.at[some(0, 0, quarter), :], wuf.at[wu_at, :]),
        locals_.start(wd, wdf.at[:, mine]),
        locals_.start(crows_in, crows),
    ]
    for copy in wo_loads:
        locals_.wait(copy)

    branch = Scatter(links, bufs.at[0], side, across)
    back = Scatter(links, bufs.at[1], side, across)

    def branch_part(owner):
        return flat_dot(low[piece(owner), :], wo[...])

    @pl.loop(0, 4)
    def _(n):
        value = branch_part(t ^ (3 - n))
        pl.when(n == 0)(lambda: branch.put_far(value))
        pl.when(n == 1)(lambda: branch.put_over(value))
        pl.when(n == 2)(lambda: branch.put_near(value))

        @pl.when(n == 3)
        def _():
            middle[...] = hidden[...].astype(f32) + value

    wd_copy.wait_recv()
    wd_on.start()
    middle[...] = branch.total(middle[...])
    m = middle[...]
    scale = lax.rsqrt(jnp.mean(m * m, axis=-1, keepdims=True) + norm_eps)
    gain = gains[1:2, :]
    mrows[piece(t), :] = (m * scale * gain).astype(bf16)
    here, there = mrows.at[piece(t), :], mrows.at[piece(t ^ 2), :]
    m_over, m_near = links.copy(here, here, across), links.copy(here, here, side)
    m_on = links.copy(there, there, side)
    m_over.start()
    m_near.start()
    for copy in own_weights:
        locals_.wait(copy)
    wu_on.wait_recv()
    wd_on.wait_recv()

    def mlp(owner):
        at = piece(owner)
        rows = mrows[at, :]
        gate = flat_dot(rows, wgf[...])
        upward = flat_dot(rows, wuf[...])
        d_act = last_dot(crows[at, :], wdf[...])
        sig = 1.0 / (1.0 + jnp.exp(-gate))
        silu = gate * sig
        act[at, :] = (silu * upward).astype(bf16)
        dup[at, :] = (d_act * silu).astype(bf16)
        dgate[at, :] = (d_act * upward * sig * (1.0 + gate * (1.0 - sig))).astype(bf16)

    def out_part(owner):
        return flat_dot(act[piece(owner), :], wdf[...])

    def back_part(owner):
        at = piece(owner)
        return last_dot(dgate[at, :], wgf[...]) + last_dot(dup[at, :], wuf[...])

    m_near.wait_recv()

    @pl.loop(0, 4)
    def _(n):
        @pl.when(n == 2)
        def _():
            m_over.wait_recv()
            m_on.start()
            m_on.wait_recv()

        owner = t ^ jnp.where(n < 2, n, 5 - n)
        mlp(owner)
        value = back_part(owner)

        @pl.when(n == 0)
        def _():
            kept[0] = value

        pl.when(n == 1)(lambda: back.put_near(value))
        pl.when(n == 2)(lambda: back.put_far(value))
        pl.when(n == 3)(lambda: back.put_over(value))

    to_mate = [links.copy(give.at[k], land.at[k], mate) for k in range(READY)]

    def lanes(n):
        return pl.ds(pl.multiple_of(n * 256, 256), 256)

    def down_chunk(ref, n, columns):
        ref[n] = first_dot(act[:, lanes(n)], crows[:, columns]).astype(bf16)

    def wide_chunk(ref, k, grads, n, columns):
        got = first_dot(mrows[:, columns], grads[:, lanes(n)]).astype(bf16)
        ref[k + n, :, 0:256] = got[0:256]
        ref[k + n, :, 256:512] = got[256:512]

    @pl.loop(0, 3)
    def _(n):
        down_chunk(give, n, theirs)

    for copy in to_mate:
        copy.start()

    @pl.loop(0, 3)
    def _(n):
        down_chunk(own, n, mine)
        for k, grads in ((3, dgate), (6, dup)):
            wide_chunk(give, k, grads, n, theirs)
            wide_chunk(own, k, grads, n, mine)

    @pl.loop(0, 4)
    def _(n):
        value = out_part(t ^ (3 - n))

        @pl.when(n < 3)
        def _():
            parts[n] = value.astype(bf16)

        @pl.when(n == 3)
        def _():
            kept[1] = value + middle[...]

    locals_.start(kept.at[1], out_own_out)
    locals_.start(parts, parts_out)
    locals_.start(give.at[READY:FROM_MLP], give_out)
    locals_.start(own.at[READY:FROM_MLP], own_out.at[READY:FROM_MLP])

    d_mlp = back.total(kept[0])
    m = middle[...]
    scale = lax.rsqrt(jnp.mean(m * m, axis=-1, keepdims=True) + norm_eps)
    scaled = d_mlp * gain
    inner = jnp.mean(scaled * m, axis=-1, keepdims=True)
    d_middle = (
        crows[piece(t), :].astype(f32) + scale * scaled - m * (scale * scale * scale) * inner
    )
    kept[0] = d_middle
    gain_grad = jnp.sum(d_mlp * m * scale, axis=0, keepdims=True)
    brow[...] = d_middle.astype(bf16)
    locals_.start(brow, brow_out)
    locals_.start(kept.at[0], d_middle_out)
    result[...] = jnp.broadcast_to(gain_grad, (8, gain_grad.shape[1]))
    locals_.start(result, gain_out)

    for k in range(READY):
        to_mate[k].wait_recv()
        own[k] = own[k] + land[k]
    locals_.start(own.at[0:READY], own_out.at[0:READY])
    for k in range(READY):
        to_mate[k].wait_send()
    wu_on.wait_send()
    wd_copy.wait_send()
    wd_on.wait_send()
    branch.close()
    back.close()
    for copy in (m_over, m_near, m_on):
        copy.wait_send()
    locals_.finish()


def mlp_call(vmem_args, any_args):
    low, hidden, gains = vmem_args
    wo, wd = any_args[1], any_args[-1]
    part, width = hidden.shape
    block = 4 * part
    units = wd.shape[0]
    f32, bf16 = jnp.float32, jnp.bfloat16
    shape = jax.ShapeDtypeStruct
    outs = (
        shape((part, width), f32),
        shape((8, width), f32),
        shape((part, width), bf16),
        shape((FROM_MLP, 256, 512), bf16),
        shape((FROM_MLP - READY, 256, 512), bf16),
        shape((3, part, width), bf16),
        shape((part, width), f32),
    )
    return pl.pallas_call(
        mlp_kernel,
        name="mlp",
        out_shape=outs,
        in_specs=[VMEM_SPEC] * 3 + [ANY_SPEC] * 8,
        out_specs=[ANY_SPEC] * len(outs),
        scratch_shapes=[
            pltpu.VMEM((wo.shape[0], width), bf16),
            pltpu.VMEM((width, units), bf16),
            pltpu.VMEM((width, units), bf16),
            pltpu.VMEM((units, width), bf16),
            pltpu.VMEM((block, width), bf16),
            pltpu.VMEM((block, units), bf16),
            pltpu.VMEM((block, units), bf16),
            pltpu.VMEM((block, units), bf16),
            pltpu.VMEM((part, width), bf16),
            pltpu.VMEM((2, part, width), f32),
            pltpu.VMEM((part, width), f32),
            pltpu.VMEM((2, 6, part, width), bf16),
            pltpu.VMEM((3, part, width), bf16),
            pltpu.VMEM((FROM_MLP, 256, 512), bf16),
            pltpu.VMEM((FROM_MLP, 256, 512), bf16),
            pltpu.VMEM((READY, 256, 512), bf16),
            pltpu.VMEM((block, width), bf16),
            pltpu.VMEM((8, width), f32),
            pltpu.SemaphoreType.DMA((12 + READY,)),
            pltpu.SemaphoreType.DMA((12 + READY,)),
            pltpu.SemaphoreType.DMA((16,)),
        ],
        compiler_params=pltpu.CompilerParams(
            collective_id=1, has_side_effects=True, vmem_limit_bytes=58 << 20
        ),
    )(*vmem_args, *any_args)


class Pump:
    def __init__(self, refs, sems, mate, near, opposite, outer, out, first_mate):
        self.own, self.mated, self.landed, self.summed = refs
        self.send, self.recv, self.local = sems
        self.mate, self.near, self.opposite, self.outer = mate, near, opposite, outer
        self.inner = jnp.logical_not(outer)
        self.out, self.first_mate = out, first_mate

    def remote(self, stage, u, src, dst, device):
        return pltpu.make_async_remote_copy(
            src_ref=src, dst_ref=dst, send_sem=self.send.at[stage * UNITS + u],
            recv_sem=self.recv.at[stage * UNITS + u], device_id=device, device_id_type=MESH_ID,
        )

    def to_mate(self, u, src):
        return self.remote(0, u, src, self.mated.at[u - self.first_mate], self.mate)

    def inward(self, u):
        return self.remote(1, u, self.own.at[u], self.landed.at[u], self.near)

    def cross(self, u):
        return self.remote(2, u, self.landed.at[u], self.summed.at[u], self.opposite)

    def outward(self, u):
        return self.remote(3, u, self.summed.at[u], self.landed.at[u], self.near)

    def write(self, u, ref):
        return pltpu.make_async_copy(ref.at[u], self.out.at[u], self.local.at[u])

    def run(self, condition, body):
        if isinstance(condition, bool):
            if condition:
                body()
        else:
            pl.when(condition)(body)

    def first(self, u):
        def bring():
            self.to_mate(u, self.own.at[u]).wait_recv()
            self.own[u] = self.own[u] + self.mated[u - self.first_mate]

        self.run(u >= self.first_mate, bring)
        pl.when(self.outer)(lambda: self.inward(u).start())

    def second(self, u):
        @pl.when(self.inner)
        def _():
            self.inward(u).wait_recv()
            self.landed[u] = self.own[u] + self.landed[u]
            self.cross(u).start()

    def third(self, u):
        @pl.when(self.inner)
        def _():
            self.cross(u).wait_recv()
            self.summed[u] = self.landed[u] + self.summed[u]
            self.outward(u).start()
            self.write(u, self.summed).start()

    def fourth(self, u):
        @pl.when(self.outer)
        def _():
            self.outward(u).wait_recv()
            self.write(u, self.landed).start()

    def slot(self, k):
        for u in (2 * k, 2 * k + 1):
            self.first(u)
            self.run(k >= 2, lambda: self.second(u - 4))
            self.run(k >= 4, lambda: self.third(u - 8))

    def close(self):
        @pl.loop(0, UNITS)
        def _(u):
            pl.when(self.outer)(lambda: self.inward(u).wait_send())

            @pl.when(self.inner)
            def _():
                self.cross(u).wait_send()
                self.outward(u).wait_send()

            self.write(u, self.summed).wait()


def backward_kernel(
    gains, mlp_gain_grad, query_in, hidden, brow_in, low, attended, wo_own, wo_got, d_middle,
    q_proj_in, wqkv_in, own_in, give, parts, out_own, keys, values, k_proj, cosine, sine, rows,
    hidden_out, hidden_grad, gains_out, sums_out,
    kbuf, vbuf, kpbuf, cosbuf, sinbuf, rowbuf, dq, dk, dv, dkv, dqp, gkv, kept, bufs,
    own, mated, landed, summed, late_give, far_land, mid_land, out_buf,
    query, dout, q_proj, wqkv,
    gsum, gland, send, recv, pump_send, pump_recv, pump_local, local, blocksem,
):
    s, c, t = lax.axis_index(SHARD_AXIS), lax.axis_index(CTX_AXIS), lax.axis_index(TP_AXIS)
    nctx = lax.axis_size(CTX_AXIS)
    part = hidden.shape[0]
    half = rows.shape[2] // 2
    f32, bf16 = jnp.float32, jnp.bfloat16
    side, across, mate = {TP_AXIS: t ^ 1}, {TP_AXIS: t ^ 2}, {SHARD_AXIS: 1 - s}
    near, opposite = {CTX_AXIS: c ^ 1}, {CTX_AXIS: c ^ 3}
    previous = {CTX_AXIS: lax.rem(c + nctx - 1, nctx)}
    outer = (c == 0) | (c == nctx - 1)
    links, locals_ = Links(send, recv), Locals(local)
    scale = HEAD_SIZE ** (-0.5)
    pump = Pump(
        (own, mated, landed, summed), (pump_send, pump_recv, pump_local),
        mate, near, opposite, outer, sums_out, MATED,
    )

    def piece(owner):
        return pl.ds(pl.multiple_of(owner * part, part), part)

    mine = pl.ds(pl.multiple_of(s * half, half), half)
    theirs = pl.ds(pl.multiple_of((1 - s) * half, half), half)

    def half_at(ref_shard, n, size):
        return pl.ds(pl.multiple_of(ref_shard * half + n * size, size), size)

    def block_copies(b):
        slot = b & 1
        pairs = (
            (keys.at[b], kbuf.at[slot]), (values.at[b], vbuf.at[slot]),
        )
        return [
            pltpu.make_async_copy(a, d, blocksem.at[6 * b + n]) for n, (a, d) in enumerate(pairs)
        ]

    def row_copies(b):
        pairs = (
            (k_proj.at[b], kpbuf), (cosine.at[b], cosbuf), (sine.at[b], sinbuf),
            (rows.at[b], rowbuf),
        )
        return [
            pltpu.make_async_copy(a, d, blocksem.at[6 * b + 2 + n])
            for n, (a, d) in enumerate(pairs)
        ]

    def row_fetch(b):
        for copy in row_copies(b):
            copy.start()

    def fetch(b):
        for copy in block_copies(b):
            copy.start()

    def fetched(b):
        for copy in block_copies(b):
            copy.wait()

    brow_load = locals_.start(brow_in, rowbuf.at[piece(t), :])
    loads = [locals_.start(own_in, own.at[0:EARLY])]
    wo_loads = []
    for j in range(2):
        at = slice(j * 256, j * 256 + 256)
        wo_loads.append(locals_.start(wo_own.at[at, :], bufs.at[1, j, :, mine]))
        wo_loads.append(locals_.start(wo_got.at[at, :], bufs.at[1, j, :, theirs]))
    for h in range(4):
        wo_loads.append(locals_.start(attended.at[:, h * 128 : h * 128 + 128], dq.at[h]))
    wo_loads.append(locals_.start(low, dkv))
    out_loads = [locals_.start(parts.at[1], out_buf.at[0]), locals_.start(out_own, kept.at[1])]

    @pl.when(c >= 2)
    def _():
        fetch(2)

    @pl.when(c >= 1)
    def _():
        fetch(1)

    @pl.when(c <= 1)
    def _():
        fetch(0)

    late_loads = [
        locals_.start(query_in, query), locals_.start(q_proj_in, q_proj),
        locals_.start(wqkv_in, wqkv),
    ]
    enter([side, across, mate, near, opposite])

    def send_early(first, count):
        for u in range(first, min(first + count, EARLY)):
            pump.to_mate(u, give.at[u - MATED]).start()

    here, there = rowbuf.at[piece(t), :], rowbuf.at[piece(t ^ 2), :]
    b_over, b_near = links.copy(here, here, across), links.copy(here, here, side)
    b_on = links.copy(there, there, side)
    locals_.wait(brow_load)
    b_over.start()
    b_near.start()
    send_early(MATED, 4)
    out_far = links.copy(parts.at[0], out_buf.at[1], side)
    out_over = links.copy(out_buf.at[0], out_buf.at[2], across)
    out_near = links.copy(parts.at[2], out_buf.at[3], side)
    out_far.start()
    out_near.start()
    scatters = [
        Scatter(links, bufs.at[0], side, across),
        Scatter(links, bufs.at[1], side, across),
        Scatter(links, bufs.at[0], side, across),
    ]
    far_copy = links.copy(out_buf.at[0], far_land, previous)
    mid_copy = links.copy(out_buf.at[1], mid_land, previous)
    for copy in loads:
        locals_.wait(copy)
    pump.slot(0)
    send_early(MATED + 4, 2)
    gkv[...] = jnp.zeros(gkv.shape, f32)
    gsum[...] = jnp.zeros(gsum.shape, f32)
    gsum[1:2, :] = mlp_gain_grad[0:1, :]
    q_gain = gains[2:3, 0:HEAD_SIZE]
    k_gain = gains[3:4, 0:HEAD_SIZE]
    def attended_back(owner):
        at = piece(owner)
        for j in range(2):
            got = last_dot(rowbuf[at, :], bufs[1, j]).astype(bf16)
            for hh in range(2):
                h = 2 * j + hh
                head = got[:, hh * 128 : hh * 128 + 128]
                delta = -jnp.sum(head.astype(f32) * dq[h, at, :], axis=1, keepdims=True)
                top = delta.astype(bf16).astype(f32)
                lane = lax.broadcasted_iota(jnp.int32, (part, HEAD_SIZE), 1)
                extra = jnp.where(lane == 0, top, jnp.where(lane == 1, delta - top, 0.0))
                dout[h, at, 0:128] = head
                dout[h, at, 128:256] = extra.astype(bf16)

    for copy in wo_loads:
        locals_.wait(copy)
    b_near.wait_recv()

    @pl.loop(0, 2)
    def _(n):
        attended_back(t ^ n)

    for copy in out_loads:
        locals_.wait(copy)
    out_far.wait_recv()
    out_buf[0] = out_buf[0] + out_buf[1]
    pump.slot(1)
    send_early(MATED + 6, 2)
    b_over.wait_recv()
    b_on.start()
    out_over.start()
    b_on.wait_recv()

    @pl.loop(2, 4)
    def _(n):
        attended_back(t ^ n)

    for copy in (b_over, b_near, b_on):
        copy.wait_send()
    @pl.loop(0, 2)
    def _(n):
        at = pl.ds(pl.multiple_of(n * 256, 256), 256)
        for columns, target, first in ((theirs, late_give, 0), (mine, own, EARLY)):
            got = first_dot(dkv[:, at], rowbuf[:, columns]).astype(bf16)
            for e in range(2):
                target[first + 2 * n + e] = got[e * 128 : e * 128 + 128]

    for n in range(4):
        pump.to_mate(EARLY + n, late_give.at[n]).start()
    dq[...] = jnp.zeros(dq.shape, f32)
    for b in range(3):
        pl.when((c == b) if b < 2 else (c >= b))(functools.partial(row_fetch, b))
    pump.slot(2)
    send_early(MATED + 8, 2)

    def tile(b, g, r, kc, bound):
        slot = b & 1
        q_at = pl.ds(pl.multiple_of(r * 512, 512), 512)
        k_at = pl.ds(pl.multiple_of(kc * 512, 512), 512)
        kk, vv = kbuf[slot, g, k_at, :], vbuf[slot, g, k_at, :]
        dv_new, dk_new = [], []
        for hh in range(2):
            h = 2 * g + hh
            qq, do = query[h, q_at, :], dout[h, q_at, :]
            p = jnp.exp2(last_dot(qq, kk) * SCORE_STEP)
            if bound is not None:
                ahead = lax.broadcasted_iota(jnp.int32, p.shape, 0) - lax.broadcasted_iota(
                    jnp.int32, p.shape, 1
                )
                p = jnp.where(ahead >= bound, p, 0.0)
            ds = (p * last_dot(do, vv)).astype(bf16)
            dv_new.append(first_dot(do[:, 0:HEAD_SIZE], p.astype(bf16)))
            dk_new.append(first_dot(qq[:, 0:HEAD_SIZE], ds))
            dq[h, q_at, :] += flat_dot(ds, kk[:, 0:HEAD_SIZE])
        dv[g, :, k_at] += dv_new[0] + dv_new[1]
        dk[g, :, k_at] += dk_new[0] + dk_new[1]

    def clear():
        dk[...] = jnp.zeros(dk.shape, f32)
        dv[...] = jnp.zeros(dv.shape, f32)

    def norm_back(grad, u, gain, cos, sin, row):
        turned = grad * cos - pltpu.roll(grad, HEAD_SIZE // 2, 1) * sin
        r = lax.rsqrt(jnp.mean(u * u, axis=-1, keepdims=True) + norm_eps)
        gsum[row : row + 1, 0:HEAD_SIZE] += jnp.sum(turned * u * r, axis=0, keepdims=True)
        scaled = turned * gain
        inner = jnp.mean(scaled * u, axis=-1, keepdims=True)
        return (r * scaled - u * (r * r * r) * inner).astype(bf16)

    def finish_kv(b):
        for copy in row_copies(b)[:3]:
            copy.wait()

        @pl.loop(0, 4)
        def _(n):
            at = piece(n)
            cos, sin = cosbuf[at, :], sinbuf[at, :]
            for g in range(2):
                lanes = slice(g * 128, g * 128 + 128)
                u = kpbuf[at, lanes]
                dkv[at, lanes] = norm_back(dk[g, :, at].T * scale, u, k_gain, cos, sin, 3)
                dkv[at, 256 + g * 128 : 384 + g * 128] = dv[g, :, at].T.astype(bf16)

        row_copies(b)[3].wait()

        gkv[...] += first_dot(rowbuf[...], dkv[...])

    def kv_part(owner):
        return last_dot(dkv[piece(owner), :], wqkv[:, 512:1024])

    def all_part(owner):
        return kv_part(owner) + last_dot(dqp[piece(owner), :], wqkv[:, 0:512])

    def scatter(which, slot, partial):
        @pl.loop(0, 4)
        def _(n):
            value = partial(t ^ (3 - n))
            pl.when(n == 0)(lambda: which.put_far(value))
            pl.when(n == 1)(lambda: which.put_over(value))
            pl.when(n == 2)(lambda: which.put_near(value))

            @pl.when(n == 3)
            def _():
                kept[slot] = value

    for copy in late_loads:
        locals_.wait(copy)

    @pl.when(c >= 2)
    def _():
        fetched(2)
        clear()

    @pl.loop(0, 6)
    def _(n):
        m = lax.rem(n, 3)

        @pl.when(c >= 2)
        def _():
            tile(2, n // 3, m // 2, (m + 1) // 2, None)

        @pl.when(m == 2)
        def _():
            pump.slot(3 + n // 3)
            for e in range(2):
                u = MATED + 10 + 2 * (n // 3) + e
                pump.to_mate(u, give.at[u - MATED]).start()

    @pl.when(c >= 2)
    def _():
        finish_kv(2)
        fetch(0)
        row_fetch(1)
        scatter(scatters[2], 0, kv_part)

    out_near.wait_recv()
    out_over.wait_recv()
    out_buf[3] = (kept[1] + out_buf[2].astype(f32) + out_buf[3].astype(f32)).astype(bf16)
    locals_.start(out_buf.at[3], hidden_out)
    out_far.wait_send()
    out_over.wait_send()
    out_near.wait_send()
    pump.slot(5)

    @pl.when(c >= 1)
    def _():
        fetched(1)
        clear()

    @pl.loop(0, 8)
    def _(n):
        m = lax.rem(n, 4)

        @pl.when(c >= 1)
        def _():
            tile(1, n // 4, m // 2, m & 1, None)

        @pl.when(m == 3)
        def _():
            pump.slot(6 + n // 4)

    @pl.when(c >= 2)
    def _():
        out_buf[0] = scatters[2].total(kept[0]).astype(bf16)
        far_copy.start()
        scatters[2].close()

    @pl.when(c >= 1)
    def _():
        finish_kv(1)
        row_fetch(0)

    @pl.when(c >= 1)
    def _():
        scatter(scatters[1], 1, kv_part)

    pump.slot(8)
    fetched(0)
    clear()

    @pl.loop(0, 6)
    def _(n):
        m = lax.rem(n, 3)
        tile(0, n // 3, (m + 1) // 2, m // 2, (m & 1) * -512)

        @pl.when(n == 3)
        def _():
            pump.slot(9)

    finish_kv(0)

    @pl.loop(0, 4)
    def _(n):
        at = piece(n)
        cos, sin = cosbuf[at, :], sinbuf[at, :]
        for h in range(4):
            lanes = slice(h * 128, h * 128 + 128)
            u = q_proj[at, lanes]
            dqp[at, lanes] = norm_back(dq[h, at, :] * scale, u, q_gain, cos, sin, 2)

    for n in range(4):
        late_give[4 + n] = gkv[half_at(1 - s, n, 128), :].astype(bf16)
        pump.to_mate(LATE + n, late_give.at[4 + n]).start()
    for n in range(2):
        got = first_dot(rowbuf[:, half_at(1 - s, n, 256)], dqp[...]).astype(bf16)
        for e in range(2):
            late_give[8 + 2 * n + e] = got[e * 128 : e * 128 + 128]
            pump.to_mate(LATE + 4 + 2 * n + e, late_give.at[8 + 2 * n + e]).start()
    pump.slot(10)

    @pl.when((c >= 1) & (c < nctx - 1))
    def _():
        far_copy.wait_recv()
        kept[1] += far_land[...].astype(f32)

    @pl.when(c >= 1)
    def _():
        out_buf[1] = scatters[1].total(kept[1]).astype(bf16)
        mid_copy.start()
        scatters[1].close()

    base = locals_.start(d_middle, kept.at[1])
    hidden_load = locals_.start(hidden, out_buf.at[2])
    scatter(scatters[0], 0, all_part)
    for n in range(2):
        rows_of = gkv[half_at(s, n, 256), :].astype(bf16)
        got = first_dot(rowbuf[:, half_at(s, n, 256)], dqp[...]).astype(bf16)
        for e in range(2):
            at = slice(e * 128, e * 128 + 128)
            own[LATE + 2 * n + e] = rows_of[at]
            own[LATE + 4 + 2 * n + e] = got[at]
    for u in range(LATE - 4, LATE):
        pump.second(u)
        pump.third(u - 4)
    pump.third(LATE - 4)
    pump.third(LATE - 3)
    pl.loop(0, LATE - 8)(pump.fourth)

    def finish_rows():
        @pl.when(c < nctx - 1)
        def _():
            mid_copy.wait_recv()
            kept[0] += mid_land[...].astype(f32)

        kept[0] = scatters[0].total(kept[0])
        locals_.wait(hidden_load)
        locals_.wait(base)
        x = out_buf[2].astype(f32)
        r = lax.rsqrt(jnp.mean(x * x, axis=-1, keepdims=True) + norm_eps)
        d_in = kept[0]
        gsum[0:1, :] = jnp.sum(d_in * x * r, axis=0, keepdims=True)
        scaled = d_in * gains[0:1, :]
        inner = jnp.mean(scaled * x, axis=-1, keepdims=True)
        kept[1] += r * scaled - x * (r * r * r) * inner
        locals_.start(kept.at[1], hidden_grad)

    swaps = [
        links.copy(gsum, gland.at[n], device)
        for n, device in enumerate((side, across, mate, near, opposite))
    ]

    def swap(n):
        if n > 0:
            swaps[n - 1].wait()
            gsum[...] += gland[n - 1]
        if n < 5:
            swaps[n].start()

    for n, u in enumerate(range(LATE, UNITS)):
        pump.first(u)
        if n >= 1:
            pump.second(u - 1)
        pump.third(u - 2)
        if n == 3:
            finish_rows()
        if n >= 3:
            swap(n - 3)
    pump.second(UNITS - 1)
    pump.third(UNITS - 2)
    swap(8 - 3)
    pump.third(UNITS - 1)
    for n in range(9 - 3, 6):
        swap(n)
    locals_.start(gsum, gains_out)
    scatters[0].close()

    @pl.when(c >= 2)
    def _():
        far_copy.wait_send()

    @pl.when(c >= 1)
    def _():
        mid_copy.wait_send()

    @pl.loop(MATED, EARLY)
    def _(u):
        pump.to_mate(u, give.at[u - MATED]).wait_send()

    @pl.loop(EARLY, UNITS)
    def _(u):
        pump.to_mate(u, late_give.at[u - EARLY]).wait_send()

    pl.loop(LATE - 8, UNITS)(pump.fourth)
    pump.close()
    locals_.finish()


def backward_call(vmem_args, any_args):
    hidden = any_args[1]
    part, width = hidden.shape
    block = 4 * part
    f32, bf16 = jnp.float32, jnp.bfloat16
    shape = jax.ShapeDtypeStruct
    outs = (
        shape((part, width), bf16),
        shape((part, width), f32),
        shape((8, width), f32),
        shape((UNITS, 128, 512), bf16),
    )
    tile = pltpu.VMEM((part, width), bf16)
    units = pltpu.VMEM((UNITS, 128, 512), bf16)
    return pl.pallas_call(
        backward_kernel,
        name="backward",
        out_shape=outs,
        in_specs=[VMEM_SPEC] * 2 + [ANY_SPEC] * len(any_args),
        out_specs=[ANY_SPEC] * len(outs),
        scratch_shapes=[
            pltpu.VMEM((2, 2, block, 256), bf16),
            pltpu.VMEM((2, 2, block, 256), bf16),
            pltpu.VMEM((block, 256), f32),
            pltpu.VMEM((block, HEAD_SIZE), f32),
            pltpu.VMEM((block, HEAD_SIZE), f32),
            pltpu.VMEM((block, width), bf16),
            pltpu.VMEM((4, block, HEAD_SIZE), f32),
            pltpu.VMEM((2, HEAD_SIZE, block), f32),
            pltpu.VMEM((2, HEAD_SIZE, block), f32),
            pltpu.VMEM((block, 512), bf16),
            pltpu.VMEM((block, 512), bf16),
            pltpu.VMEM((width, 512), f32),
            pltpu.VMEM((2, part, width), f32),
            pltpu.VMEM((2, 6, part, width), bf16),
            units,
            pltpu.VMEM((UNITS - MATED, 128, 512), bf16),
            units,
            units,
            pltpu.VMEM((UNITS - EARLY, 128, 512), bf16),
            tile, tile,
            pltpu.VMEM((4, part, width), bf16),
            pltpu.VMEM((4, block, 256), bf16),
            pltpu.VMEM((4, block, 256), bf16),
            pltpu.VMEM((block, 512), f32),
            pltpu.VMEM((width, 1024), bf16),
            pltpu.VMEM((8, width), f32),
            pltpu.VMEM((5, 8, width), f32),
            pltpu.SemaphoreType.DMA((22,)),
            pltpu.SemaphoreType.DMA((22,)),
            pltpu.SemaphoreType.DMA((4 * UNITS,)),
            pltpu.SemaphoreType.DMA((4 * UNITS,)),
            pltpu.SemaphoreType.DMA((UNITS,)),
            pltpu.SemaphoreType.DMA((21,)),
            pltpu.SemaphoreType.DMA((18,)),
        ],
        compiler_params=pltpu.CompilerParams(
            collective_id=2, has_side_effects=True, vmem_limit_bytes=60 << 20
        ),
    )(*vmem_args, *any_args)


def result_kernel(
    chunks_in, gains, grad_in, hidden_in,
    grad_out, hidden_out, attn, wq, wk, wv, q_gain, k_gain, wo, mlp, wg, wu, wd,
    buf, q, k, v, o, gate, up, down, grad, hidden, inside, outside,
):
    shard = lax.axis_index(SHARD_AXIS)
    count = buf.shape[0]
    whole = [
        pltpu.make_async_copy(grad_in, grad, inside.at[count]),
        pltpu.make_async_copy(hidden_in, hidden, inside.at[count + 1]),
    ]
    loads = [pltpu.make_async_copy(chunks_in.at[n], buf.at[n], inside.at[n]) for n in range(count)]
    for copy in whole + loads:
        copy.start()
    stores = []

    def put(n, ref, out, row, lanes):
        at = (slice(row, row + 256), lanes)
        stores.append(pltpu.make_async_copy(ref.at[at], out.at[at], outside.at[len(stores)]))
        stores[-1].start()

    for copy in whole:
        copy.wait()
    for n, (ref, out) in enumerate(((grad, grad_out), (hidden, hidden_out))):
        whole[n] = pltpu.make_async_copy(ref, out, outside.at[count + n])
        whole[n].start()
    for n in range(count):
        loads[n].wait()
        values = buf[n].astype(jnp.float32)
        every = slice(0, 512)
        if n < 3:
            down[n * 256 : n * 256 + 256, :] = values
            put(n, down, wd, n * 256, every)
        elif n < 9:
            ref, out, j = (gate, wg, n - 3) if n < 6 else (up, wu, n - 6)
            lanes = slice(j * 256, j * 256 + 256)
            ref[0:256, lanes] = values[:, 0:256]
            ref[256:512, lanes] = values[:, 256:512]
            at = (slice(0, 512), lanes)
            stores.append(pltpu.make_async_copy(ref.at[at], out.at[at], outside.at[len(stores)]))
            stores[-1].start()
        elif n < 11:
            o[(n - 9) * 256 : (n - 8) * 256, :] = values
            put(n, o, wo, (n - 9) * 256, every)
        elif n < 13:
            row = (n - 11) * 256
            k[row : row + 256, :] = values[:, 0:256]
            v[row : row + 256, :] = values[:, 256:512]
        else:
            q[(n - 13) * 256 : (n - 12) * 256, :] = values
            put(n, q, wq, (n - 13) * 256, every)
    for ref, out in ((k, wk), (v, wv)):
        stores.append(pltpu.make_async_copy(ref, out, outside.at[len(stores)]))
        stores[-1].start()
    wide, small = attn.shape[1], q_gain.shape[1]
    first = shard == 0
    attn[...] = jnp.where(first, gains[0:1, 0:wide], gains[0:1, wide : 2 * wide])
    mlp[...] = jnp.where(first, gains[1:2, 0:wide], gains[1:2, wide : 2 * wide])
    q_gain[...] = jnp.where(first, gains[2:3, 0:small], gains[2:3, small : 2 * small])
    k_gain[...] = jnp.where(first, gains[3:4, 0:small], gains[3:4, small : 2 * small])
    for copy in stores + whole:
        copy.wait()


def result_call(chunks, gains, grad_hidden, out_hidden):
    part, width = grad_hidden.shape
    f32 = jnp.float32
    shape = jax.ShapeDtypeStruct
    half = width // 2
    q, k, v, o = (half, 512), (half, 256), (half, 256), (512, half)
    gate, up, down = (half, 768), (half, 768), (768, half)
    sizes = [q, k, v, (1, 64), (1, 64), o, (1, half), gate, up, down]
    outs = [shape((part, width), f32), shape((part, width), out_hidden.dtype), shape((1, half), f32)]
    outs += [shape(z, f32) for z in sizes]
    specs = [ANY_SPEC] * 2 + [VMEM_SPEC] + [ANY_SPEC] * 3 + [VMEM_SPEC] * 2 + [ANY_SPEC, VMEM_SPEC]
    return pl.pallas_call(
        result_kernel,
        name="result",
        out_shape=outs,
        in_specs=[ANY_SPEC, VMEM_SPEC, ANY_SPEC, ANY_SPEC],
        out_specs=specs + [ANY_SPEC] * 3,
        scratch_shapes=[pltpu.VMEM((CHUNKS, 256, 512), jnp.bfloat16)]
        + [pltpu.VMEM(z, f32) for z in (q, k, v, o, gate, up, down)]
        + [pltpu.VMEM((part, width), f32), pltpu.VMEM((part, width), out_hidden.dtype)]
        + [pltpu.SemaphoreType.DMA((CHUNKS + 2,)), pltpu.SemaphoreType.DMA((CHUNKS + 2,))],
        compiler_params=pltpu.CompilerParams(vmem_limit_bytes=60 << 20),
    )(chunks, gains, grad_hidden, out_hidden)


def fast_device(
    hidden,
    segments,
    cotangent,
    attn_gain,
    w_query,
    key_weight_matrix,
    value_weight_matrix,
    query_gain,
    key_gain,
    mixer_exit_coefficients,
    mlp_gain,
    w_gate,
    w_up,
    w_down,
):
    gains_own = (attn_gain, mlp_gain, query_gain, key_gain)
    exponents = 2.0 * (np.arange(HEAD_SIZE) % (HEAD_SIZE // 2)) / HEAD_SIZE
    rates = np.power(rope_base, -exponents).astype(np.float32)[None]
    labels = segments.reshape(-1, HEAD_SIZE)
    (gains, rows, q_proj, k_proj, query, keys, values, cosine, sine, attended, low, wqkv, crows,
     wo_got, wg_got, wu_got) = forward_call(
        hidden[0], cotangent[0], gains_own, labels, jnp.asarray(rates), w_query, key_weight_matrix,
        value_weight_matrix, mixer_exit_coefficients, w_gate, w_up,
    )
    def units(chunks, count):
        return chunks.reshape(count, 128, 512)

    d_middle, mlp_gain_grad, brow, own, give, parts, out_own = mlp_call(
        (low, hidden[0], gains),
        (crows, mixer_exit_coefficients, wo_got, w_gate, wg_got, w_up, wu_got, w_down),
    )
    out_hidden, grad_hidden, sums, chunks = backward_call(
        (gains, mlp_gain_grad),
        (query, hidden[0], brow, low, attended, mixer_exit_coefficients, wo_got, d_middle, q_proj, wqkv, units(own, EARLY), units(give, EARLY - MATED),
         parts, out_own, keys, values, k_proj, cosine, sine, rows),
    )
    (grad_hidden, out_hidden, attn, wq, wk, wv, q_gain, k_gain, wo, mlp, wg, wu, wd) = result_call(
        chunks.reshape(CHUNKS, 256, 512), sums, grad_hidden, out_hidden
    )
    return (
        out_hidden[None], grad_hidden[None], attn[0], wq, wk, wv, q_gain[0], k_gain[0], wo, mlp[0],
        wg, wu, wd,
    )


def per_device(
    hidden,
    segments,
    cotangent,
    attn_gain,
    w_query,
    key_weight_matrix,
    value_weight_matrix,
    query_gain,
    key_gain,
    mixer_exit_coefficients,
    mlp_gain,
    w_gate,
    w_up,
    w_down,
):
    collected_rows = (
        lax.all_gather(attn_gain, SHARD_AXIS, axis=0, tiled=True),
        lax.all_gather(w_query, SHARD_AXIS, axis=0, tiled=True),
        lax.all_gather(key_weight_matrix, SHARD_AXIS, axis=0, tiled=True),
        lax.all_gather(value_weight_matrix, SHARD_AXIS, axis=0, tiled=True),
        lax.all_gather(query_gain, SHARD_AXIS, axis=0, tiled=True),
        lax.all_gather(key_gain, SHARD_AXIS, axis=0, tiled=True),
        lax.all_gather(mixer_exit_coefficients, SHARD_AXIS, axis=1, tiled=True),
        lax.all_gather(mlp_gain, SHARD_AXIS, axis=0, tiled=True),
        lax.all_gather(w_gate, SHARD_AXIS, axis=0, tiled=True),
        lax.all_gather(w_up, SHARD_AXIS, axis=0, tiled=True),
        lax.all_gather(w_down, SHARD_AXIS, axis=1, tiled=True),
    )
    gain_attn = collected_rows[0].astype(jnp.float32)
    gain_query = collected_rows[4].astype(jnp.float32)
    gain_key = collected_rows[5].astype(jnp.float32)
    gain_mlp = collected_rows[7].astype(jnp.float32)
    seq_count = hidden.shape[0]
    block_rows = hidden.shape[1] * lax.axis_size(TP_AXIS)
    seq_length = segments.shape[1]
    ctx_index = lax.axis_index(CTX_AXIS)
    heads_local = w_query.shape[1] // HEAD_SIZE
    kv_local = key_weight_matrix.shape[1] // HEAD_SIZE
    query_group_width = heads_local // kv_local
    score_scale = HEAD_SIZE ** (-0.5)
    block_start = ctx_index * block_rows
    query_pos = block_start + jnp.arange(block_rows, dtype=jnp.int32)
    query_seg = lax.dynamic_slice_in_dim(segments, block_start, block_rows, 1)
    positions = lax.dynamic_slice_in_dim(doc_positions(segments), block_start, block_rows, 1)
    cosine, sine_part = rope_tables(positions)

    def counting_keys(key_first, step_rows):
        early = key_first <= block_start + block_rows - 1
        last_seg = lax.dynamic_slice_in_dim(segments, key_first + step_rows - 1, 1, 1)[:, 0]
        return early & jnp.any(last_seg >= query_seg[:, 0])

    inputs = hidden.astype(jnp.float32)
    scale_one = rms_scale(inputs)
    attention_input = (inputs * scale_one * gain_attn).astype(jnp.bfloat16)
    attention_rows = tp_rows(attention_input)
    q_proj = jnp.einsum(
        "zjr,rm->zjm", attention_rows, collected_rows[1], preferred_element_type=jnp.float32
    ).reshape(seq_count, block_rows, heads_local, HEAD_SIZE)
    key_projected = jnp.einsum(
        "zjr,rm->zjm", attention_rows, collected_rows[2], preferred_element_type=jnp.float32
    ).reshape(seq_count, block_rows, kv_local, HEAD_SIZE)
    value_projected = jnp.einsum(
        "zjr,rm->zjm", attention_rows, collected_rows[3], preferred_element_type=jnp.float32
    )
    q_scale = rms_scale(q_proj)
    k_scale = rms_scale(key_projected)
    query_rows_input = (
        rotate(q_proj * q_scale * gain_query, cosine, sine_part)
        .astype(jnp.bfloat16)
        .reshape(seq_count, block_rows, kv_local, query_group_width, HEAD_SIZE)
    )
    keys = rotate(key_projected * k_scale * gain_key, cosine, sine_part).astype(jnp.bfloat16)
    values = value_projected.astype(jnp.bfloat16).reshape(
        seq_count, block_rows, kv_local, HEAD_SIZE
    )
    stat_shape = (seq_count, kv_local, query_group_width, block_rows)
    start_state = (
        jnp.full(stat_shape, masked_fill, jnp.float32),
        jnp.zeros(stat_shape, jnp.float32),
        jnp.zeros(stat_shape + (HEAD_SIZE,), jnp.float32),
    )
    piece_keys = lax.all_gather(keys, CTX_AXIS, axis=1, tiled=True)
    piece_values = lax.all_gather(values, CTX_AXIS, axis=1, tiled=True)
    piece_rows = piece_keys.shape[1]
    step_rows = math.gcd(piece_rows, 1024)

    def attend_one_step(number, loop_state):
        offset = number * step_rows
        key_first = offset

        def attend_compute(state):
            row_max, row_total, summed = state
            key_part = lax.dynamic_slice_in_dim(piece_keys, offset, step_rows, 1)
            value_part = lax.dynamic_slice_in_dim(piece_values, offset, step_rows, 1)
            allowed = key_block(segments, key_first, step_rows, query_pos, query_seg)
            scores = (
                jnp.einsum(
                    "sqhgd,skhd->shgqk",
                    query_rows_input,
                    key_part,
                    preferred_element_type=jnp.float32,
                )
                * score_scale
            )
            masked = jnp.where(allowed, scores, masked_fill)
            new_max = jnp.maximum(row_max, jnp.max(masked, axis=-1))
            weights = jnp.where(allowed, jnp.exp(masked - new_max[..., None]), 0.0)
            decay_factor = jnp.exp(row_max - new_max)
            row_total = row_total * decay_factor + jnp.sum(weights, axis=-1)
            summed = summed * decay_factor[..., None] + jnp.einsum(
                "shgqk,skhd->shgqd",
                weights.astype(jnp.bfloat16),
                value_part,
                preferred_element_type=jnp.float32,
            )
            return (new_max, row_total, summed)

        return lax.cond(counting_keys(key_first, step_rows), attend_compute, keep_state, loop_state)

    row_max, row_total, summed = lax.fori_loop(
        0, piece_rows // step_rows, attend_one_step, start_state
    )
    attended = summed / row_total[..., None]
    log_total = row_max + jnp.log(row_total)
    attended_reduced_copy = (
        attended.transpose(0, 3, 1, 2, 4)
        .reshape(seq_count, block_rows, heads_local * HEAD_SIZE)
        .astype(jnp.bfloat16)
    )
    branch = tp_total(
        jnp.einsum(
            "vkq,qy->vky",
            attended_reduced_copy,
            collected_rows[6],
            preferred_element_type=jnp.float32,
        )
    )
    middle = inputs + branch
    scale_two = rms_scale(middle)
    mlp_in = (middle * scale_two * gain_mlp).astype(jnp.bfloat16)
    mlp_rows = tp_rows(mlp_in)
    gate = jnp.einsum(
        "snd,df->snf", mlp_rows, collected_rows[8], preferred_element_type=jnp.float32
    )
    upward = jnp.einsum(
        "snd,df->snf", mlp_rows, collected_rows[9], preferred_element_type=jnp.float32
    )
    activated = (jax.nn.silu(gate) * upward).astype(jnp.bfloat16)
    out_hidden = (
        middle
        + tp_total(
            jnp.einsum(
                "snf,fd->snd", activated, collected_rows[10], preferred_element_type=jnp.float32
            )
        )
    ).astype(jnp.bfloat16)
    again = (
        lax.all_gather(attn_gain, SHARD_AXIS, axis=0, tiled=True),
        lax.all_gather(w_query, SHARD_AXIS, axis=0, tiled=True),
        lax.all_gather(key_weight_matrix, SHARD_AXIS, axis=0, tiled=True),
        lax.all_gather(value_weight_matrix, SHARD_AXIS, axis=0, tiled=True),
        lax.all_gather(query_gain, SHARD_AXIS, axis=0, tiled=True),
        lax.all_gather(key_gain, SHARD_AXIS, axis=0, tiled=True),
        lax.all_gather(mixer_exit_coefficients, SHARD_AXIS, axis=1, tiled=True),
        lax.all_gather(mlp_gain, SHARD_AXIS, axis=0, tiled=True),
        lax.all_gather(w_gate, SHARD_AXIS, axis=0, tiled=True),
        lax.all_gather(w_up, SHARD_AXIS, axis=0, tiled=True),
        lax.all_gather(w_down, SHARD_AXIS, axis=1, tiled=True),
    )
    query_backward = again[1]
    lookup_pullback = again[2]
    value_backward = again[3]
    output_backward = again[6]
    back_gate = again[8]
    back_up = again[9]
    back_down = again[10]
    d_out = cotangent.astype(jnp.float32)
    d_rows = tp_rows(cotangent)
    grad_down = jnp.einsum("snf,snd->fd", activated, d_rows, preferred_element_type=jnp.float32)
    d_act = jnp.einsum("snd,fd->snf", d_rows, back_down, preferred_element_type=jnp.float32)
    sigmoid_gate = jax.nn.sigmoid(gate)
    d_upward = (d_act * jax.nn.silu(gate)).astype(jnp.bfloat16)
    d_gate = (d_act * upward * sigmoid_gate * (1.0 + gate * (1.0 - sigmoid_gate))).astype(
        jnp.bfloat16
    )
    grad_gate = jnp.einsum("snd,snf->df", mlp_rows, d_gate, preferred_element_type=jnp.float32)
    grad_up = jnp.einsum("snd,snf->df", mlp_rows, d_upward, preferred_element_type=jnp.float32)
    d_mlp_in = tp_total(
        jnp.einsum("snf,df->snd", d_gate, back_gate, preferred_element_type=jnp.float32)
        + jnp.einsum("snf,df->snd", d_upward, back_up, preferred_element_type=jnp.float32)
    )
    grad_mlp_gain = jnp.sum(d_mlp_in * middle * scale_two, axis=(0, 1))
    d_middle = d_out + rms_back(d_mlp_in, middle, scale_two, gain_mlp)
    d_branch = d_middle.astype(jnp.bfloat16)
    residual_branch_rows = tp_rows(d_branch)
    result_cotangent = jnp.einsum(
        "xbj,xbk->jk",
        attended_reduced_copy,
        residual_branch_rows,
        preferred_element_type=jnp.float32,
    )
    d_attended = (
        jnp.einsum(
            "miv,cv->mic", residual_branch_rows, output_backward, preferred_element_type=jnp.float32
        )
        .astype(jnp.bfloat16)
        .reshape(seq_count, block_rows, kv_local, query_group_width, HEAD_SIZE)
    )
    delta = jnp.sum(d_attended.astype(jnp.float32).transpose(0, 2, 3, 1, 4) * attended, axis=-1)
    query_zeros = jnp.zeros(
        (seq_count, block_rows, kv_local, query_group_width, HEAD_SIZE), jnp.float32
    )
    back_state = (
        query_zeros,
        jnp.zeros((seq_count, seq_length, kv_local, HEAD_SIZE), jnp.float32),
        jnp.zeros((seq_count, seq_length, kv_local, HEAD_SIZE), jnp.float32),
    )
    back_piece_keys = lax.all_gather(keys, CTX_AXIS, axis=1, tiled=True)
    back_piece_values = lax.all_gather(values, CTX_AXIS, axis=1, tiled=True)
    piece_rows = back_piece_keys.shape[1]
    back_step_rows = math.gcd(piece_rows, 1024)

    def back_one_step(number, loop_state):
        offset = number * back_step_rows
        key_first = offset
        write_at = offset

        def back_compute(state):
            d_query, d_keys, d_values = state
            key_part = lax.dynamic_slice_in_dim(back_piece_keys, offset, back_step_rows, 1)
            value_part = lax.dynamic_slice_in_dim(back_piece_values, offset, back_step_rows, 1)
            allowed = key_block(segments, key_first, back_step_rows, query_pos, query_seg)
            scores = (
                jnp.einsum(
                    "sqhgd,skhd->shgqk",
                    query_rows_input,
                    key_part,
                    preferred_element_type=jnp.float32,
                )
                * score_scale
            )
            probs = jnp.where(allowed, jnp.exp(scores - log_total[..., None]), 0.0)
            d_probs = jnp.einsum(
                "sqhgd,skhd->shgqk", d_attended, value_part, preferred_element_type=jnp.float32
            )
            d_scores = (probs * (d_probs - delta[..., None])).astype(jnp.bfloat16)
            d_query = d_query + jnp.einsum(
                "shgqk,skhd->sqhgd", d_scores, key_part, preferred_element_type=jnp.float32
            )
            key_grad = jnp.einsum(
                "shgqk,sqhgd->skhd", d_scores, query_rows_input, preferred_element_type=jnp.float32
            )
            value_grad = jnp.einsum(
                "shgqk,sqhgd->skhd",
                probs.astype(jnp.bfloat16),
                d_attended,
                preferred_element_type=jnp.float32,
            )
            d_keys = lax.dynamic_update_slice_in_dim(
                d_keys,
                lax.dynamic_slice_in_dim(d_keys, write_at, back_step_rows, 1) + key_grad,
                write_at,
                1,
            )
            d_values = lax.dynamic_update_slice_in_dim(
                d_values,
                lax.dynamic_slice_in_dim(d_values, write_at, back_step_rows, 1) + value_grad,
                write_at,
                1,
            )
            return (d_query, d_keys, d_values)

        return lax.cond(
            counting_keys(key_first, back_step_rows), back_compute, keep_state, loop_state
        )

    d_query, d_keys, d_values = lax.fori_loop(
        0, piece_rows // back_step_rows, back_one_step, back_state
    )
    own_keys, own_values = (
        lax.psum_scatter(
            d_keys.astype(jnp.bfloat16), CTX_AXIS, scatter_dimension=1, tiled=True
        ).astype(jnp.float32),
        lax.psum_scatter(
            d_values.astype(jnp.bfloat16), CTX_AXIS, scatter_dimension=1, tiled=True
        ).astype(jnp.float32),
    )
    q_normed = rotate_back(
        d_query.reshape(seq_count, block_rows, heads_local, HEAD_SIZE) * score_scale,
        cosine,
        sine_part,
    )
    grad_query_gain = jnp.sum(q_normed * q_proj * q_scale, axis=(0, 1, 2))
    query_projection_gradient = (
        rms_back(q_normed, q_proj, q_scale, gain_query)
        .astype(jnp.bfloat16)
        .reshape(seq_count, block_rows, heads_local * HEAD_SIZE)
    )
    k_normed = rotate_back(own_keys * score_scale, cosine, sine_part)
    grad_key_gain = jnp.sum(k_normed * key_projected * k_scale, axis=(0, 1, 2))
    lookup_map_derivative = (
        rms_back(k_normed, key_projected, k_scale, gain_key)
        .astype(jnp.bfloat16)
        .reshape(seq_count, block_rows, kv_local * HEAD_SIZE)
    )
    value_projection_gradient = own_values.astype(jnp.bfloat16).reshape(
        seq_count, block_rows, kv_local * HEAD_SIZE
    )
    query_gradient_rows = jnp.einsum(
        "zqr,zqa->ra", attention_rows, query_projection_gradient, preferred_element_type=jnp.float32
    )
    key_gradient_rows = jnp.einsum(
        "zqr,zqa->ra", attention_rows, lookup_map_derivative, preferred_element_type=jnp.float32
    )
    value_gradient_rows = jnp.einsum(
        "zqr,zqa->ra", attention_rows, value_projection_gradient, preferred_element_type=jnp.float32
    )
    d_attn_in = tp_total(
        jnp.einsum(
            "wtl,al->wta",
            query_projection_gradient,
            query_backward,
            preferred_element_type=jnp.float32,
        )
        + jnp.einsum(
            "wtl,al->wta",
            lookup_map_derivative,
            lookup_pullback,
            preferred_element_type=jnp.float32,
        )
        + jnp.einsum(
            "wtl,al->wta",
            value_projection_gradient,
            value_backward,
            preferred_element_type=jnp.float32,
        )
    )
    grad_attn_gain = jnp.sum(d_attn_in * inputs * scale_one, axis=(0, 1))
    grad_hidden = d_middle + rms_back(d_attn_in, inputs, scale_one, gain_attn)
    reduced = (
        lax.psum_scatter(
            grad_attn_gain.astype(jnp.bfloat16), SHARD_AXIS, scatter_dimension=0, tiled=True
        ).astype(jnp.float32),
        lax.psum_scatter(
            query_gradient_rows.astype(jnp.bfloat16), SHARD_AXIS, scatter_dimension=0, tiled=True
        ).astype(jnp.float32),
        lax.psum_scatter(
            key_gradient_rows.astype(jnp.bfloat16), SHARD_AXIS, scatter_dimension=0, tiled=True
        ).astype(jnp.float32),
        lax.psum_scatter(
            value_gradient_rows.astype(jnp.bfloat16), SHARD_AXIS, scatter_dimension=0, tiled=True
        ).astype(jnp.float32),
        lax.psum_scatter(
            grad_query_gain.astype(jnp.bfloat16), SHARD_AXIS, scatter_dimension=0, tiled=True
        ).astype(jnp.float32),
        lax.psum_scatter(
            grad_key_gain.astype(jnp.bfloat16), SHARD_AXIS, scatter_dimension=0, tiled=True
        ).astype(jnp.float32),
        lax.psum_scatter(
            result_cotangent.astype(jnp.bfloat16), SHARD_AXIS, scatter_dimension=1, tiled=True
        ).astype(jnp.float32),
        lax.psum_scatter(
            grad_mlp_gain.astype(jnp.bfloat16), SHARD_AXIS, scatter_dimension=0, tiled=True
        ).astype(jnp.float32),
        lax.psum_scatter(
            grad_gate.astype(jnp.bfloat16), SHARD_AXIS, scatter_dimension=0, tiled=True
        ).astype(jnp.float32),
        lax.psum_scatter(
            grad_up.astype(jnp.bfloat16), SHARD_AXIS, scatter_dimension=0, tiled=True
        ).astype(jnp.float32),
        lax.psum_scatter(
            grad_down.astype(jnp.bfloat16), SHARD_AXIS, scatter_dimension=1, tiled=True
        ).astype(jnp.float32),
    )
    matrices = (
        lax.psum(reduced[1].astype(jnp.bfloat16), CTX_AXIS).astype(jnp.float32),
        lax.psum(reduced[2].astype(jnp.bfloat16), CTX_AXIS).astype(jnp.float32),
        lax.psum(reduced[3].astype(jnp.bfloat16), CTX_AXIS).astype(jnp.float32),
        lax.psum(reduced[6].astype(jnp.bfloat16), CTX_AXIS).astype(jnp.float32),
        lax.psum(reduced[8].astype(jnp.bfloat16), CTX_AXIS).astype(jnp.float32),
        lax.psum(reduced[9].astype(jnp.bfloat16), CTX_AXIS).astype(jnp.float32),
        lax.psum(reduced[10].astype(jnp.bfloat16), CTX_AXIS).astype(jnp.float32),
    )
    gains = lax.psum((reduced[0], reduced[4], reduced[5], reduced[7]), (CTX_AXIS, TP_AXIS))
    return (
        out_hidden,
        grad_hidden,
        gains[0],
        matrices[0],
        matrices[1],
        matrices[2],
        gains[1],
        gains[2],
        matrices[3],
        gains[3],
        matrices[4],
        matrices[5],
        matrices[6],
    )


def solution(mesh):
    in_specs = (
        P(SHARD_AXIS, (CTX_AXIS, TP_AXIS), None),
        P(SHARD_AXIS, None),
        P(SHARD_AXIS, (CTX_AXIS, TP_AXIS), None),
        P(SHARD_AXIS),
        P(SHARD_AXIS, TP_AXIS),
        P(SHARD_AXIS, TP_AXIS),
        P(SHARD_AXIS, TP_AXIS),
        P(SHARD_AXIS),
        P(SHARD_AXIS),
        P(TP_AXIS, SHARD_AXIS),
        P(SHARD_AXIS),
        P(SHARD_AXIS, TP_AXIS),
        P(SHARD_AXIS, TP_AXIS),
        P(TP_AXIS, SHARD_AXIS),
    )
    out_specs = (
        P(SHARD_AXIS, (CTX_AXIS, TP_AXIS), None),
        P(SHARD_AXIS, (CTX_AXIS, TP_AXIS), None),
        P(SHARD_AXIS),
        P(SHARD_AXIS, TP_AXIS),
        P(SHARD_AXIS, TP_AXIS),
        P(SHARD_AXIS, TP_AXIS),
        P(SHARD_AXIS),
        P(SHARD_AXIS),
        P(TP_AXIS, SHARD_AXIS),
        P(SHARD_AXIS),
        P(SHARD_AXIS, TP_AXIS),
        P(SHARD_AXIS, TP_AXIS),
        P(TP_AXIS, SHARD_AXIS),
    )
    shape = mesh.shape
    fast = shape[SHARD_AXIS] == 2 and shape[CTX_AXIS] == 4 and shape[TP_AXIS] == 4
    return jax.shard_map(
        fast_device if fast else per_device, mesh=mesh, in_specs=in_specs, out_specs=out_specs, check_vma=False
    )
```

```python
import functools
import math

import jax
import jax.numpy as jnp
import numpy as np
from jax import lax
from jax.experimental import pallas as pl
from jax.experimental.pallas import tpu as pltpu
from jax.sharding import PartitionSpec as P

SHARD_AXIS, CTX_AXIS, TP_AXIS = "shard", "ctx", "tp"
HEAD_SIZE = 128
NDOC = 8


norm_eps = 1e-06
rope_base = 1000000.0
masked_fill = -1e30


def rms_scale(values):
    return lax.rsqrt(jnp.mean(values * values, axis=-1, keepdims=True) + norm_eps)


def rms_back(grad_out, values, row_scale, gain_vec):
    scaled = grad_out * gain_vec
    inner_sum = jnp.mean(scaled * values, axis=-1, keepdims=True)
    return row_scale * scaled - values * (row_scale * row_scale * row_scale) * inner_sum


def doc_positions(segments):
    seq_width = segments.shape[-1]
    labels = jnp.arange(NDOC, dtype=jnp.int32)
    onehot = (segments[..., None] == labels).astype(jnp.int32)
    counts = jnp.sum(onehot, axis=-2)
    starts = jnp.cumsum(counts, axis=-1) - counts
    first_row = jnp.sum(onehot * starts[..., None, :], axis=-1)
    return jnp.arange(seq_width, dtype=jnp.int32) - first_row


def rope_tables(positions):
    exponents = jnp.arange(0, HEAD_SIZE, 2).astype(jnp.float32) / HEAD_SIZE
    angle_rates = jnp.power(jnp.float32(rope_base), -exponents)
    angles = positions.astype(jnp.float32)[..., None] * angle_rates
    angles = jnp.concatenate([angles, angles], axis=-1)[..., None, :]
    return (jnp.cos(angles), jnp.sin(angles))


def rotate(inputs, cosine, sine_part):
    half_dim = inputs.shape[-1] // 2
    turned = jnp.concatenate([-inputs[..., half_dim:], inputs[..., :half_dim]], axis=-1)
    return inputs * cosine + turned * sine_part


def rotate_back(grads, cosine, sine_part):
    half_dim = grads.shape[-1] // 2
    moved = grads * sine_part
    turned = jnp.concatenate([moved[..., half_dim:], -moved[..., :half_dim]], axis=-1)
    return grads * cosine + turned


def tp_rows(local_part):
    return lax.all_gather(local_part, TP_AXIS, axis=1, tiled=True)


def tp_total(partial_sum):
    return lax.psum_scatter(
        partial_sum.astype(jnp.bfloat16), TP_AXIS, scatter_dimension=1, tiled=True
    ).astype(jnp.float32)


def key_block(segments, key_first, step_rows, query_pos, query_seg):
    key_pos = key_first + jnp.arange(step_rows, dtype=jnp.int32)
    key_seg = lax.dynamic_slice_in_dim(segments, key_first, step_rows, 1)
    allowed = (key_pos[None, None, :] <= query_pos[None, :, None]) & (
        key_seg[:, None, :] == query_seg[:, :, None]
    )
    return allowed[:, None, None]


def keep_state(state):
    return state


CHUNKS = 15
FROM_MLP = 9
READY = 2
UNITS, EARLY, MATED, LATE = 2 * CHUNKS, 2 * FROM_MLP, 2 * READY, 22


MESH_ID = pl.DeviceIdType.MESH
ANY_SPEC = pl.BlockSpec(memory_space=pl.ANY)
VMEM_SPEC = pl.BlockSpec(memory_space=pltpu.VMEM)
SCORE_STEP = HEAD_SIZE ** (-0.5) * math.log2(math.e)
APART = 16384.0


def enter(peers):
    barrier = pltpu.get_barrier_semaphore()
    for peer in peers:
        pl.semaphore_signal(barrier, inc=1, device_id=peer, device_id_type=MESH_ID)
    pl.semaphore_wait(barrier, len(peers))


def last_dot(left, right):
    return lax.dot_general(
        left, right, (((1,), (1,)), ((), ())), preferred_element_type=jnp.float32
    )


def flat_dot(left, right):
    return jnp.dot(left, right, preferred_element_type=jnp.float32)


def first_dot(left, right):
    return lax.dot_general(
        left, right, (((0,), (0,)), ((), ())), preferred_element_type=jnp.float32
    )


def spin(values, cosine, sine_signed):
    return values * cosine + pltpu.roll(values, HEAD_SIZE // 2, 1) * sine_signed


class Links:
    def __init__(self, send, recv):
        self.send, self.recv, self.used = send, recv, 0

    def copy(self, src, dst, device):
        number = self.used
        self.used += 1
        return pltpu.make_async_remote_copy(
            src_ref=src, dst_ref=dst, send_sem=self.send.at[number],
            recv_sem=self.recv.at[number], device_id=device, device_id_type=MESH_ID,
        )


class Locals:
    def __init__(self, sems):
        self.sems, self.used, self.open = sems, 0, []

    def make(self, src, dst):
        copy = pltpu.make_async_copy(src, dst, self.sems.at[self.used])
        self.used += 1
        return copy

    def start(self, src, dst):
        copy = self.make(src, dst)
        copy.start()
        self.open.append(copy)
        return copy

    def wait(self, copy):
        copy.wait()
        self.open = [other for other in self.open if other is not copy]

    def finish(self):
        for copy in self.open:
            copy.wait()


def forward_kernel(
    hidden, cotangent, attn_gain, mlp_gain, query_gain, key_gain, segments, rates, wq, wk, wv, wo, wg, wu,
    gains_out, rows_out, q_out, k_out, query_out, keys_out, values_out, cos_out, sin_out,
    attended_out, low_out, wqkv_out, crows_out, wo_out, wg_out, wu_out,
    gains, raw, rows, wqkv, q_proj, k_proj, qaug, kaug, vaug, cosine, sine, acc, low, crows,
    gains_in, gains_land, places, send, recv, local,
):
    s, c, t = lax.axis_index(SHARD_AXIS), lax.axis_index(CTX_AXIS), lax.axis_index(TP_AXIS)
    nctx = lax.axis_size(CTX_AXIS)
    part = hidden.shape[0]
    block = 4 * part
    half = wq.shape[0]
    f32, bf16 = jnp.float32, jnp.bfloat16
    side, across, mate = {TP_AXIS: t ^ 1}, {TP_AXIS: t ^ 2}, {SHARD_AXIS: 1 - s}
    pair = {CTX_AXIS: c ^ 1}
    nxt, prv = {CTX_AXIS: lax.rem(c + 1, nctx)}, {CTX_AXIS: lax.rem(c + nctx - 1, nctx)}
    gains_in[...] = jnp.zeros(gains_in.shape, f32)
    for row, gain in enumerate((attn_gain, mlp_gain)):
        own_gain = gain[...].astype(f32)[None, :]
        gains_in[row : row + 1, pl.ds(pl.multiple_of(s * half, half), half)] = own_gain
    small = HEAD_SIZE // 2
    source_lane = lax.broadcasted_iota(jnp.int32, (small, HEAD_SIZE), 0)
    target_lane = lax.broadcasted_iota(jnp.int32, (small, HEAD_SIZE), 1) - s * small
    chosen = jnp.where(source_lane == target_lane, 1.0, 0.0).astype(bf16)
    for row, gain in ((2, query_gain), (3, key_gain)):
        placed = flat_dot(jnp.broadcast_to(gain[...][None, :], (16, small)), chosen)
        gains_in[row : row + 1, 0:HEAD_SIZE] = placed[0:1]
    enter([side, across, mate, nxt, prv])
    links, locals_ = Links(send, recv), Locals(local)

    def piece(owner):
        return pl.ds(pl.multiple_of(owner * part, part), part)

    low_bit = c & 1

    def some(shard, count, size):
        return pl.ds(pl.multiple_of(shard * count + low_bit * size, size), size)

    mine = pl.ds(pl.multiple_of(s * half, half), half)
    quarter = half // 2
    gains_copy = links.copy(gains_in, gains_land, mate)
    wk_copy = links.copy(wk, wqkv.at[mine, 512:768], mate)
    wv_copy = links.copy(wv, wqkv.at[mine, 768:1024], mate)
    wq_copy = links.copy(wq, wqkv.at[mine, 0:512], mate)
    wo_copy = links.copy(
        wo.at[some(0, 0, quarter), :], wo_out.at[some(0, 0, quarter), :], mate
    )
    wo_got = wo_out.at[some(0, 0, quarter), :]
    wo_on = links.copy(wo_got, wo_got, pair)
    wg_copy = links.copy(
        wg.at[some(0, 0, quarter), :], wg_out.at[some(0, 0, quarter), :], mate
    )
    wg_got = wg_out.at[some(0, 0, quarter), :]
    wg_on = links.copy(wg_got, wg_got, pair)
    wu_copy = links.copy(
        wu.at[some(0, 0, quarter), :], wu_out.at[some(0, 0, quarter), :], mate
    )
    gains_copy.start()
    wk_copy.start()
    wv_copy.start()
    wq_copy.start()
    own_k = locals_.start(wk, wqkv.at[mine, 512:768])
    own_v = locals_.start(wv, wqkv.at[mine, 768:1024])
    own_q = locals_.start(wq, wqkv.at[mine, 0:512])
    own_c = locals_.start(cotangent, crows.at[piece(t), :])

    def source(b, owner):
        return hidden if b == 0 else raw.at[b, piece(owner)]

    to_across, to_side, on_to_side, to_next = [], [], [], []
    for b in range(3):
        there = raw.at[b, piece(t ^ 2)]
        to_side.append(links.copy(source(b, t), raw.at[b, piece(t)], side))
        on_to_side.append(links.copy(there, there, side))
        if b < 2:
            to_across.append(links.copy(source(b, t), raw.at[b, piece(t)], across))
            to_next.append(links.copy(source(b, t), raw.at[b + 1, piece(t)], nxt))
    far_to_next = links.copy(raw.at[1, piece(t ^ 2)], raw.at[2, piece(t ^ 2)], nxt)
    c_side = links.copy(cotangent, crows.at[piece(t), :], side)
    c_over = links.copy(cotangent, crows.at[piece(t), :], across)
    c_on = links.copy(crows.at[piece(t ^ 2), :], crows.at[piece(t ^ 2), :], side)
    to_across[0].start()
    to_side[0].start()

    @pl.when(c < nctx - 1)
    def _():
        to_next[0].start()

    c_side.start()
    raw[0, piece(t), :] = hidden[...]
    gains_copy.wait()
    gains[...] = gains_in[...] + gains_land[...]
    q_gain = gains[2:3, 0:HEAD_SIZE]
    k_gain = gains[3:4, 0:HEAD_SIZE]

    def table(b):
        start, stop, rate = places[0:1, :], places[1:2, :], rates[...]
        shape = (128, HEAD_SIZE)
        lower = lax.broadcasted_iota(jnp.int32, shape, 1) < HEAD_SIZE // 2

        @pl.loop(0, 4)
        def _(n):
            found = []
            for offset in (0, 512):
                first = n * 128 + offset
                index = (lax.broadcasted_iota(jnp.int32, shape, 0) + first) + (c - b) * block
                index = index.astype(f32)
                inside = (index >= start) & (index < stop)
                marks = jnp.where(inside, 1.0, 0.0)
                begin = jnp.sum(jnp.where(inside, start, 0.0), axis=1, keepdims=True)
                at = pl.ds(pl.multiple_of(first, 128), 128)
                for g in range(2):
                    kaug[b, g, at, 128:256] = (1.0 - marks).astype(bf16)
                if b == 0:
                    for h in range(4):
                        qaug[h, at, 128:256] = (marks * -APART).astype(bf16)
                found.append((at, index - begin))
            (low_at, low_pos), (high_at, high_pos) = found
            angle = jnp.where(lower, low_pos, high_pos) * rate
            cs, sn = jnp.cos(angle), jnp.sin(angle)
            cr, sr = pltpu.roll(cs, HEAD_SIZE // 2, 1), pltpu.roll(sn, HEAD_SIZE // 2, 1)
            cosine[b, low_at, :] = jnp.where(lower, cs, cr)
            cosine[b, high_at, :] = jnp.where(lower, cr, cs)
            sine[b, low_at, :] = jnp.where(lower, -sn, sr)
            sine[b, high_at, :] = jnp.where(lower, -sr, sn)

    def project_kv(b, owner):
        at = piece(owner)
        x = raw[b, at, :].astype(f32)
        scale = lax.rsqrt(jnp.mean(x * x, axis=-1, keepdims=True) + norm_eps)
        rows[b, at, :] = (x * scale * gains[0:1, :]).astype(bf16)
        got = flat_dot(rows[b, at, :], wqkv[:, 512:1024])
        k_proj[b, at, :] = got[:, 0:256]
        for g in range(2):
            u = got[:, g * 128 : g * 128 + 128]
            r = lax.rsqrt(jnp.mean(u * u, axis=-1, keepdims=True) + norm_eps)
            turned = spin(u * r * k_gain, cosine[b, at, :], sine[b, at, :])
            kaug[b, g, at, 0:128] = turned.astype(bf16)
            vaug[b, g, at, 0:128] = got[:, 256 + g * 128 : 384 + g * 128].astype(bf16)

    def project_q(owner):
        at = piece(owner)
        got = flat_dot(rows[0, at, :], wqkv[:, 0:512])
        q_proj[at, :] = got
        for h in range(4):
            u = got[:, h * 128 : h * 128 + 128]
            r = lax.rsqrt(jnp.mean(u * u, axis=-1, keepdims=True) + norm_eps)
            turned = spin(u * r * q_gain, cosine[0, at, :], sine[0, at, :])
            qaug[h, at, 0:128] = turned.astype(bf16)

    def unit(b, g, r, kc, bound):
        at = pl.ds(pl.multiple_of(r * 512, 512), 512)
        for hh in range(2):
            qq = qaug[2 * g + hh, at, :]
            total = None
            for j in range(2):
                keys_at = pl.ds(pl.multiple_of(kc * 512 + j * 256, 256), 256)
                p = jnp.exp2(last_dot(qq, kaug[b, g, keys_at, :]) * SCORE_STEP)
                if bound is not None:
                    ahead = lax.broadcasted_iota(jnp.int32, p.shape, 0) - lax.broadcasted_iota(
                        jnp.int32, p.shape, 1
                    )
                    p = jnp.where(ahead >= bound + j * 256, p, 0.0)
                value = flat_dot(p.astype(bf16), vaug[b, g, keys_at, :])
                total = value if total is None else total + value
            acc[2 * g + hh, at, :] += total

    def block_outs(b):
        pairs = (
            (rows, rows_out), (k_proj, k_out), (kaug, keys_out), (vaug, values_out),
            (cosine, cos_out), (sine, sin_out),
        )
        return [locals_.make(a.at[b], d.at[b]) for a, d in pairs]

    outs = [block_outs(b) for b in range(3)]

    lane = lax.broadcasted_iota(jnp.int32, (1, HEAD_SIZE), 1)
    begin = jnp.full((1, HEAD_SIZE), float(nctx * block), f32)
    end = begin
    for label in range(NDOC):
        before = jnp.where(segments[...] < label, 1.0, 0.0)
        before = jnp.sum(before, axis=(0, 1), keepdims=True)
        begin = jnp.where(lane == label, before, begin)
        end = jnp.where(lane == label - 1, before, end)
    places[0:1, :] = begin
    places[1:2, :] = end
    table(0)
    vaug[:, :, :, 128:256] = jnp.ones((3, 2, block, 128), bf16)
    acc[...] = jnp.zeros(acc.shape, f32)
    locals_.wait(own_k)
    locals_.wait(own_v)
    wk_copy.wait()
    wv_copy.wait()
    wo_copy.start()
    to_across[0].wait_recv()
    on_to_side[0].start()

    @pl.when(c >= 1)
    def _():
        to_next[0].wait_recv()
        to_across[1].start()
        to_side[1].start()

        @pl.when(c < nctx - 1)
        def _():
            to_next[1].start()

    to_side[0].wait_recv()
    on_to_side[0].wait_recv()

    @pl.loop(0, 4)
    def _(n):
        project_kv(0, n)

    for copy in outs[0]:
        copy.start()

    @pl.when(c >= 1)
    def _():
        table(1)
        to_side[1].wait_recv()

        @pl.loop(0, 2)
        def _(n):
            project_kv(1, t ^ n)

    @pl.when(c >= 2)
    def _():
        table(2)

    locals_.wait(own_q)
    wq_copy.wait()
    wg_copy.start()

    @pl.when(c >= 1)
    def _():
        to_across[1].wait_recv()
        on_to_side[1].start()

        @pl.when(c < nctx - 1)
        def _():
            far_to_next.start()

        @pl.when(c >= 2)
        def _():
            to_next[1].wait_recv()
            to_side[2].start()

    c_over.start()

    @pl.loop(0, 4)
    def _(n):
        project_q(n)

    locals_.start(q_proj, q_out)
    locals_.start(wqkv, wqkv_out)

    @pl.loop(0, 6)
    def _(n):
        m = lax.rem(n, 3)
        unit(0, n // 3, (m + 1) // 2, m // 2, (m & 1) * -512)

    wo_copy.wait_recv()
    wo_on.start()
    wu_copy.start()

    @pl.when(c >= 1)
    def _():
        on_to_side[1].wait_recv()

        @pl.loop(2, 4)
        def _(n):
            project_kv(1, t ^ n)

        for copy in outs[1]:
            copy.start()

        @pl.loop(0, 8)
        def _(n):
            m = lax.rem(n, 4)
            unit(1, n // 4, m // 2, m & 1, None)

    wg_copy.wait_recv()
    wg_on.start()

    c_over.wait_recv()
    c_on.start()

    @pl.when(c >= 2)
    def _():
        far_to_next.wait_recv()
        on_to_side[2].start()
        to_side[2].wait_recv()
        on_to_side[2].wait_recv()

        @pl.loop(0, 4)
        def _(n):
            project_kv(2, n)

        for copy in outs[2]:
            copy.start()

        @pl.loop(0, 6)
        def _(n):
            m = lax.rem(n, 3)
            unit(2, n // 3, m // 2, (m + 1) // 2, None)

    for h in range(4):

        @pl.loop(0, 4)
        def _(r):
            at = pl.ds(pl.multiple_of(r * 256, 256), 256)
            total = acc[h, at, 128:256]
            value = acc[h, at, 0:128] / total
            acc[h, at, 0:128] = value
            shift = jnp.log(total) * -(HEAD_SIZE**0.5)
            top = shift.astype(bf16).astype(f32)
            mid = (shift - top).astype(bf16).astype(f32)
            lane = lax.broadcasted_iota(jnp.int32, shift.shape, 1)
            parts = jnp.where(lane == NDOC, top, 0.0)
            parts = jnp.where(lane == NDOC + 1, mid, parts)
            parts = jnp.where(lane == NDOC + 2, shift - top - mid, parts)
            qaug[h, at, 128:256] = qaug[h, at, 128:256] + parts.astype(bf16)
            low[h, at, :] = value.astype(bf16)

        lanes = slice(h * 128, h * 128 + 128)
        locals_.start(low.at[h], low_out.at[:, lanes])
        locals_.start(acc.at[h, :, 0:128], attended_out.at[:, lanes])
        locals_.start(qaug.at[h], query_out.at[h])

    locals_.start(gains, gains_out)
    locals_.wait(own_c)
    c_side.wait()
    c_on.wait()
    locals_.start(crows, crows_out)
    c_over.wait_send()
    to_across[0].wait_send()
    to_side[0].wait_send()
    on_to_side[0].wait_send()
    for copy in outs[0]:
        copy.wait()

    @pl.when(c < nctx - 1)
    def _():
        to_next[0].wait_send()

    for b in (1, 2):

        @pl.when(c >= b)
        def _():
            if b < 2:
                to_across[b].wait_send()
            to_side[b].wait_send()
            on_to_side[b].wait_send()
            for copy in outs[b]:
                copy.wait()

    @pl.when((c >= 1) & (c < nctx - 1))
    def _():
        to_next[1].wait_send()
        far_to_next.wait_send()

    wo_copy.wait_send()
    wo_on.wait()
    wg_copy.wait_send()
    wg_on.wait()
    wu_copy.wait()
    locals_.finish()


def forward_call(hidden, cotangent, gains, segments, rates, wq, wk, wv, wo, wg, wu):
    part, width = hidden.shape
    block = 4 * part
    f32, bf16 = jnp.float32, jnp.bfloat16
    shape = jax.ShapeDtypeStruct
    outs = (
        shape((8, width), f32),
        shape((3, block, width), bf16),
        shape((block, 512), f32),
        shape((3, block, 256), f32),
        shape((4, block, 256), bf16),
        shape((3, 2, block, 256), bf16),
        shape((3, 2, block, 256), bf16),
        shape((3, block, HEAD_SIZE), f32),
        shape((3, block, HEAD_SIZE), f32),
        shape((block, 512), f32),
        shape((block, 512), bf16),
        shape((width, 1024), bf16),
        shape((block, width), bf16),
        shape(wo.shape, bf16),
        shape(wg.shape, bf16),
        shape(wu.shape, bf16),
    )
    return pl.pallas_call(
        forward_kernel,
        name="forward",
        out_shape=outs,
        in_specs=[VMEM_SPEC] * 8 + [ANY_SPEC] * 6,
        out_specs=[ANY_SPEC] * len(outs),
        scratch_shapes=[
            pltpu.VMEM((8, width), f32),
            pltpu.VMEM((3, block, width), bf16),
            pltpu.VMEM((3, block, width), bf16),
            pltpu.VMEM((width, 1024), bf16),
            pltpu.VMEM((block, 512), f32),
            pltpu.VMEM((3, block, 256), f32),
            pltpu.VMEM((4, block, 256), bf16),
            pltpu.VMEM((3, 2, block, 256), bf16),
            pltpu.VMEM((3, 2, block, 256), bf16),
            pltpu.VMEM((3, block, HEAD_SIZE), f32),
            pltpu.VMEM((3, block, HEAD_SIZE), f32),
            pltpu.VMEM((4, block, 256), f32),
            pltpu.VMEM((4, block, 128), bf16),
            pltpu.VMEM((block, width), bf16),
            pltpu.VMEM((8, width), f32),
            pltpu.VMEM((8, width), f32),
            pltpu.VMEM((8, HEAD_SIZE), f32),
            pltpu.SemaphoreType.DMA((23,)),
            pltpu.SemaphoreType.DMA((23,)),
            pltpu.SemaphoreType.DMA((38,)),
        ],
        compiler_params=pltpu.CompilerParams(
            collective_id=0, has_side_effects=True, vmem_limit_bytes=58 << 20
        ),
    )(hidden, cotangent, *gains, segments, rates, wq, wk, wv, wo, wg, wu)


class Scatter:
    def __init__(self, links, bufs, side, across):
        self.bufs = bufs
        self.far = links.copy(bufs.at[0], bufs.at[3], side)
        self.over = links.copy(bufs.at[1], bufs.at[4], across)
        self.near = links.copy(bufs.at[2], bufs.at[5], side)

    def put_far(self, value):
        self.bufs[0] = value.astype(jnp.bfloat16)
        self.far.start()

    def put_over(self, value):
        self.far.wait_recv()
        self.bufs[1] = (value + self.bufs[3].astype(jnp.float32)).astype(jnp.bfloat16)
        self.over.start()

    def put_near(self, value):
        self.bufs[2] = value.astype(jnp.bfloat16)
        self.near.start()

    def total(self, value):
        self.near.wait_recv()
        self.over.wait_recv()
        return value + self.bufs[5].astype(jnp.float32) + self.bufs[4].astype(jnp.float32)

    def close(self):
        self.far.wait_send()
        self.over.wait_send()
        self.near.wait_send()


def mlp_kernel(
    low, hidden, gains, crows_in, wo_own, wo_got, wg_own, wg_got, wu_own, wu_got,
    wd,
    d_middle_out, gain_out, brow_out, own_out, give_out, parts_out, out_own_out,
    wo, wgf, wuf, wdf, mrows, act, dgate, dup, brow, kept, middle, bufs, parts, give, own, land,
    crows, result, send, recv, local,
):
    s, c, t = lax.axis_index(SHARD_AXIS), lax.axis_index(CTX_AXIS), lax.axis_index(TP_AXIS)
    part = hidden.shape[0]
    half = wd.shape[1]
    bf16, f32 = jnp.bfloat16, jnp.float32
    side, across = {TP_AXIS: t ^ 1}, {TP_AXIS: t ^ 2}
    mate, pair = {SHARD_AXIS: 1 - s}, {CTX_AXIS: c ^ 1}
    links, locals_ = Links(send, recv), Locals(local)

    def piece(owner):
        return pl.ds(pl.multiple_of(owner * part, part), part)

    mine = pl.ds(pl.multiple_of(s * half, half), half)
    theirs = pl.ds(pl.multiple_of((1 - s) * half, half), half)
    low_bit = c & 1

    def some(shard, count, size):
        return pl.ds(pl.multiple_of(shard * count + low_bit * size, size), size)

    quarter = half // 2
    third = wd.shape[0] // 2
    wu_at = some(1 - s, half, quarter)
    wu_on = links.copy(wu_got.at[some(0, 0, quarter), :], wuf.at[wu_at, :], pair)
    wd_copy = links.copy(
        wd.at[some(0, 0, third), :], wdf.at[some(0, 0, third), mine], mate
    )
    wd_got = wdf.at[some(0, 0, third), theirs]
    wd_on = links.copy(wd_got, wd_got, pair)
    wo_loads = [
        locals_.start(wo_own, wo.at[:, mine]),
        locals_.start(wo_got, wo.at[:, theirs]),
    ]
    enter([side, across, mate, pair])
    wu_on.start()
    wd_copy.start()
    own_weights = [
        locals_.start(wg_own, wgf.at[mine, :]),
        locals_.start(wg_got, wgf.at[theirs, :]),
        locals_.start(wu_own, wuf.at[mine, :]),
        locals_.start(wu_got.at[some(0, 0, quarter), :], wuf.at[wu_at, :]),
        locals_.start(wd, wdf.at[:, mine]),
        locals_.start(crows_in, crows),
    ]
    for copy in wo_loads:
        locals_.wait(copy)

    branch = Scatter(links, bufs.at[0], side, across)
    back = Scatter(links, bufs.at[1], side, across)

    def branch_part(owner):
        return flat_dot(low[piece(owner), :], wo[...])

    @pl.loop(0, 4)
    def _(n):
        value = branch_part(t ^ (3 - n))
        pl.when(n == 0)(lambda: branch.put_far(value))
        pl.when(n == 1)(lambda: branch.put_over(value))
        pl.when(n == 2)(lambda: branch.put_near(value))

        @pl.when(n == 3)
        def _():
            middle[...] = hidden[...].astype(f32) + value

    wd_copy.wait_recv()
    wd_on.start()
    middle[...] = branch.total(middle[...])
    m = middle[...]
    scale = lax.rsqrt(jnp.mean(m * m, axis=-1, keepdims=True) + norm_eps)
    gain = gains[1:2, :]
    mrows[piece(t), :] = (m * scale * gain).astype(bf16)
    here, there = mrows.at[piece(t), :], mrows.at[piece(t ^ 2), :]
    m_over, m_near = links.copy(here, here, across), links.copy(here, here, side)
    m_on = links.copy(there, there, side)
    m_over.start()
    m_near.start()
    for copy in own_weights:
        locals_.wait(copy)
    wu_on.wait_recv()
    wd_on.wait_recv()

    def mlp(owner):
        at = piece(owner)
        rows = mrows[at, :]
        gate = flat_dot(rows, wgf[...])
        upward = flat_dot(rows, wuf[...])
        d_act = last_dot(crows[at, :], wdf[...])
        sig = 1.0 / (1.0 + jnp.exp(-gate))
        silu = gate * sig
        act[at, :] = (silu * upward).astype(bf16)
        dup[at, :] = (d_act * silu).astype(bf16)
        dgate[at, :] = (d_act * upward * sig * (1.0 + gate * (1.0 - sig))).astype(bf16)

    def out_part(owner):
        return flat_dot(act[piece(owner), :], wdf[...])

    def back_part(owner):
        at = piece(owner)
        return last_dot(dgate[at, :], wgf[...]) + last_dot(dup[at, :], wuf[...])

    m_near.wait_recv()

    @pl.loop(0, 4)
    def _(n):
        @pl.when(n == 2)
        def _():
            m_over.wait_recv()
            m_on.start()
            m_on.wait_recv()

        owner = t ^ jnp.where(n < 2, n, 5 - n)
        mlp(owner)
        value = back_part(owner)

        @pl.when(n == 0)
        def _():
            kept[0] = value

        pl.when(n == 1)(lambda: back.put_near(value))
        pl.when(n == 2)(lambda: back.put_far(value))
        pl.when(n == 3)(lambda: back.put_over(value))

    to_mate = [links.copy(give.at[k], land.at[k], mate) for k in range(READY)]

    def lanes(n):
        return pl.ds(pl.multiple_of(n * 256, 256), 256)

    def down_chunk(ref, n, columns):
        ref[n] = first_dot(act[:, lanes(n)], crows[:, columns]).astype(bf16)

    def wide_chunk(ref, k, grads, n, columns):
        got = first_dot(mrows[:, columns], grads[:, lanes(n)]).astype(bf16)
        ref[k + n, :, 0:256] = got[0:256]
        ref[k + n, :, 256:512] = got[256:512]

    @pl.loop(0, 3)
    def _(n):
        down_chunk(give, n, theirs)

    for copy in to_mate:
        copy.start()

    @pl.loop(0, 3)
    def _(n):
        down_chunk(own, n, mine)
        for k, grads in ((3, dgate), (6, dup)):
            wide_chunk(give, k, grads, n, theirs)
            wide_chunk(own, k, grads, n, mine)

    @pl.loop(0, 4)
    def _(n):
        value = out_part(t ^ (3 - n))

        @pl.when(n < 3)
        def _():
            parts[n] = value.astype(bf16)

        @pl.when(n == 3)
        def _():
            kept[1] = value + middle[...]

    locals_.start(kept.at[1], out_own_out)
    locals_.start(parts, parts_out)
    locals_.start(give.at[READY:FROM_MLP], give_out)
    locals_.start(own.at[READY:FROM_MLP], own_out.at[READY:FROM_MLP])

    d_mlp = back.total(kept[0])
    m = middle[...]
    scale = lax.rsqrt(jnp.mean(m * m, axis=-1, keepdims=True) + norm_eps)
    scaled = d_mlp * gain
    inner = jnp.mean(scaled * m, axis=-1, keepdims=True)
    d_middle = (
        crows[piece(t), :].astype(f32) + scale * scaled - m * (scale * scale * scale) * inner
    )
    kept[0] = d_middle
    gain_grad = jnp.sum(d_mlp * m * scale, axis=0, keepdims=True)
    brow[...] = d_middle.astype(bf16)
    locals_.start(brow, brow_out)
    locals_.start(kept.at[0], d_middle_out)
    result[...] = jnp.broadcast_to(gain_grad, (8, gain_grad.shape[1]))
    locals_.start(result, gain_out)

    for k in range(READY):
        to_mate[k].wait_recv()
        own[k] = own[k] + land[k]
    locals_.start(own.at[0:READY], own_out.at[0:READY])
    for k in range(READY):
        to_mate[k].wait_send()
    wu_on.wait_send()
    wd_copy.wait_send()
    wd_on.wait_send()
    branch.close()
    back.close()
    for copy in (m_over, m_near, m_on):
        copy.wait_send()
    locals_.finish()


def mlp_call(vmem_args, any_args):
    low, hidden, gains = vmem_args
    wo, wd = any_args[1], any_args[-1]
    part, width = hidden.shape
    block = 4 * part
    units = wd.shape[0]
    f32, bf16 = jnp.float32, jnp.bfloat16
    shape = jax.ShapeDtypeStruct
    outs = (
        shape((part, width), f32),
        shape((8, width), f32),
        shape((part, width), bf16),
        shape((FROM_MLP, 256, 512), bf16),
        shape((FROM_MLP - READY, 256, 512), bf16),
        shape((3, part, width), bf16),
        shape((part, width), f32),
    )
    return pl.pallas_call(
        mlp_kernel,
        name="mlp",
        out_shape=outs,
        in_specs=[VMEM_SPEC] * 3 + [ANY_SPEC] * 8,
        out_specs=[ANY_SPEC] * len(outs),
        scratch_shapes=[
            pltpu.VMEM((wo.shape[0], width), bf16),
            pltpu.VMEM((width, units), bf16),
            pltpu.VMEM((width, units), bf16),
            pltpu.VMEM((units, width), bf16),
            pltpu.VMEM((block, width), bf16),
            pltpu.VMEM((block, units), bf16),
            pltpu.VMEM((block, units), bf16),
            pltpu.VMEM((block, units), bf16),
            pltpu.VMEM((part, width), bf16),
            pltpu.VMEM((2, part, width), f32),
            pltpu.VMEM((part, width), f32),
            pltpu.VMEM((2, 6, part, width), bf16),
            pltpu.VMEM((3, part, width), bf16),
            pltpu.VMEM((FROM_MLP, 256, 512), bf16),
            pltpu.VMEM((FROM_MLP, 256, 512), bf16),
            pltpu.VMEM((READY, 256, 512), bf16),
            pltpu.VMEM((block, width), bf16),
            pltpu.VMEM((8, width), f32),
            pltpu.SemaphoreType.DMA((12 + READY,)),
            pltpu.SemaphoreType.DMA((12 + READY,)),
            pltpu.SemaphoreType.DMA((16,)),
        ],
        compiler_params=pltpu.CompilerParams(
            collective_id=1, has_side_effects=True, vmem_limit_bytes=58 << 20
        ),
    )(*vmem_args, *any_args)


class Pump:
    def __init__(self, refs, sems, mate, near, opposite, outer, out, first_mate):
        self.own, self.mated, self.landed, self.summed = refs
        self.send, self.recv, self.local = sems
        self.mate, self.near, self.opposite, self.outer = mate, near, opposite, outer
        self.inner = jnp.logical_not(outer)
        self.out, self.first_mate = out, first_mate

    def remote(self, stage, u, src, dst, device):
        return pltpu.make_async_remote_copy(
            src_ref=src, dst_ref=dst, send_sem=self.send.at[stage * UNITS + u],
            recv_sem=self.recv.at[stage * UNITS + u], device_id=device, device_id_type=MESH_ID,
        )

    def to_mate(self, u, src):
        return self.remote(0, u, src, self.mated.at[u - self.first_mate], self.mate)

    def inward(self, u):
        return self.remote(1, u, self.own.at[u], self.landed.at[u], self.near)

    def cross(self, u):
        return self.remote(2, u, self.landed.at[u], self.summed.at[u], self.opposite)

    def outward(self, u):
        return self.remote(3, u, self.summed.at[u], self.landed.at[u], self.near)

    def write(self, u, ref):
        return pltpu.make_async_copy(ref.at[u], self.out.at[u], self.local.at[u])

    def run(self, condition, body):
        if isinstance(condition, bool):
            if condition:
                body()
        else:
            pl.when(condition)(body)

    def first(self, u):
        def bring():
            self.to_mate(u, self.own.at[u]).wait_recv()
            self.own[u] = self.own[u] + self.mated[u - self.first_mate]

        self.run(u >= self.first_mate, bring)
        pl.when(self.outer)(lambda: self.inward(u).start())

    def second(self, u):
        @pl.when(self.inner)
        def _():
            self.inward(u).wait_recv()
            self.landed[u] = self.own[u] + self.landed[u]
            self.cross(u).start()

    def third(self, u):
        @pl.when(self.inner)
        def _():
            self.cross(u).wait_recv()
            self.summed[u] = self.landed[u] + self.summed[u]
            self.outward(u).start()
            self.write(u, self.summed).start()

    def fourth(self, u):
        @pl.when(self.outer)
        def _():
            self.outward(u).wait_recv()
            self.write(u, self.landed).start()

    def slot(self, k):
        for u in (2 * k, 2 * k + 1):
            self.run(k < LATE // 2, lambda: self.first(u))
            self.run(k >= 2, lambda: self.second(u - 4))
            self.run(k >= 4, lambda: self.third(u - 8))

    def close(self):
        @pl.loop(0, UNITS)
        def _(u):
            pl.when(self.outer)(lambda: self.inward(u).wait_send())

            @pl.when(self.inner)
            def _():
                self.cross(u).wait_send()
                self.outward(u).wait_send()

            self.write(u, self.summed).wait()


def backward_kernel(
    gains, mlp_gain_grad, query_in, hidden, brow_in, low, attended, wo_own, wo_got, d_middle,
    q_proj_in, wqkv_in, own_in, give, parts, out_own, keys, values, k_proj, cosine, sine, rows,
    hidden_out, hidden_grad, gains_out, sums_out,
    kbuf, vbuf, kpbuf, cosbuf, sinbuf, rowbuf, dq, dk, dv, dkv, dqp, gkv, kept, bufs,
    own, mated, landed, summed, late_give, far_land, mid_land, out_buf,
    query, dout, q_proj, wqkv,
    gsum, gland, send, recv, pump_send, pump_recv, pump_local, local, blocksem,
):
    s, c, t = lax.axis_index(SHARD_AXIS), lax.axis_index(CTX_AXIS), lax.axis_index(TP_AXIS)
    nctx = lax.axis_size(CTX_AXIS)
    part = hidden.shape[0]
    half = rows.shape[2] // 2
    f32, bf16 = jnp.float32, jnp.bfloat16
    side, across, mate = {TP_AXIS: t ^ 1}, {TP_AXIS: t ^ 2}, {SHARD_AXIS: 1 - s}
    near, opposite = {CTX_AXIS: c ^ 1}, {CTX_AXIS: c ^ 3}
    previous = {CTX_AXIS: lax.rem(c + nctx - 1, nctx)}
    outer = (c == 0) | (c == nctx - 1)
    links, locals_ = Links(send, recv), Locals(local)
    scale = HEAD_SIZE ** (-0.5)
    pump = Pump(
        (own, mated, landed, summed), (pump_send, pump_recv, pump_local),
        mate, near, opposite, outer, sums_out, MATED,
    )

    def piece(owner):
        return pl.ds(pl.multiple_of(owner * part, part), part)

    mine = pl.ds(pl.multiple_of(s * half, half), half)
    theirs = pl.ds(pl.multiple_of((1 - s) * half, half), half)

    def half_at(ref_shard, n, size):
        return pl.ds(pl.multiple_of(ref_shard * half + n * size, size), size)

    def block_copies(b):
        slot = b & 1
        pairs = (
            (keys.at[b], kbuf.at[slot]), (values.at[b], vbuf.at[slot]),
        )
        return [
            pltpu.make_async_copy(a, d, blocksem.at[6 * b + n]) for n, (a, d) in enumerate(pairs)
        ]

    def row_copies(b):
        pairs = (
            (k_proj.at[b], kpbuf), (cosine.at[b], cosbuf), (sine.at[b], sinbuf),
            (rows.at[b], rowbuf),
        )
        return [
            pltpu.make_async_copy(a, d, blocksem.at[6 * b + 2 + n])
            for n, (a, d) in enumerate(pairs)
        ]

    def row_fetch(b):
        for copy in row_copies(b):
            copy.start()

    def fetch(b):
        for copy in block_copies(b):
            copy.start()

    def fetched(b):
        for copy in block_copies(b):
            copy.wait()

    brow_load = locals_.start(brow_in, rowbuf.at[piece(t), :])
    loads = [locals_.start(own_in.at[0:MATED], own.at[0:MATED])]
    own_load = locals_.start(own_in.at[MATED:EARLY], own.at[MATED:EARLY])
    wo_loads = []
    for j in range(2):
        at = slice(j * 256, j * 256 + 256)
        wo_loads.append(locals_.start(wo_own.at[at, :], bufs.at[1, j, :, mine]))
        wo_loads.append(locals_.start(wo_got.at[at, :], bufs.at[1, j, :, theirs]))
    for h in range(4):
        wo_loads.append(locals_.start(attended.at[:, h * 128 : h * 128 + 128], dq.at[h]))
    wo_loads.append(locals_.start(low, dkv))
    out_loads = [locals_.start(parts.at[1], out_buf.at[0]), locals_.start(out_own, kept.at[1])]

    @pl.when(c >= 2)
    def _():
        fetch(2)

    @pl.when(c >= 1)
    def _():
        fetch(1)

    @pl.when(c <= 1)
    def _():
        fetch(0)

    late_loads = [
        locals_.start(query_in, query), locals_.start(q_proj_in, q_proj),
        locals_.start(wqkv_in, wqkv),
    ]
    enter([side, across, mate, near, opposite])

    def send_early(first, count):
        for u in range(first, min(first + count, EARLY)):
            pump.to_mate(u, give.at[u - MATED]).start()

    here, there = rowbuf.at[piece(t), :], rowbuf.at[piece(t ^ 2), :]
    b_over, b_near = links.copy(here, here, across), links.copy(here, here, side)
    b_on = links.copy(there, there, side)
    locals_.wait(brow_load)
    b_over.start()
    b_near.start()
    send_early(MATED, 4)
    out_far = links.copy(parts.at[0], out_buf.at[1], side)
    out_over = links.copy(out_buf.at[0], out_buf.at[2], across)
    out_near = links.copy(parts.at[2], out_buf.at[3], side)
    out_far.start()
    out_near.start()
    scatters = [
        Scatter(links, bufs.at[0], side, across),
        Scatter(links, bufs.at[1], side, across),
        Scatter(links, bufs.at[0], side, across),
    ]
    far_copy = links.copy(out_buf.at[0], far_land, previous)
    mid_copy = links.copy(out_buf.at[1], mid_land, previous)
    for copy in loads:
        locals_.wait(copy)
    pump.slot(0)
    pump.slot(1)
    send_early(MATED + 4, 4)
    locals_.wait(own_load)
    gkv[...] = jnp.zeros(gkv.shape, f32)
    gsum[...] = jnp.zeros(gsum.shape, f32)
    gsum[1:2, :] = mlp_gain_grad[0:1, :]
    q_gain = gains[2:3, 0:HEAD_SIZE]
    k_gain = gains[3:4, 0:HEAD_SIZE]
    def attended_back(owner):
        at = piece(owner)
        for j in range(2):
            got = last_dot(rowbuf[at, :], bufs[1, j]).astype(bf16)
            for hh in range(2):
                h = 2 * j + hh
                head = got[:, hh * 128 : hh * 128 + 128]
                delta = -jnp.sum(head.astype(f32) * dq[h, at, :], axis=1, keepdims=True)
                top = delta.astype(bf16).astype(f32)
                lane = lax.broadcasted_iota(jnp.int32, (part, HEAD_SIZE), 1)
                extra = jnp.where(lane == 0, top, jnp.where(lane == 1, delta - top, 0.0))
                dout[h, at, 0:128] = head
                dout[h, at, 128:256] = extra.astype(bf16)

    for copy in wo_loads:
        locals_.wait(copy)
    b_near.wait_recv()

    @pl.loop(0, 2)
    def _(n):
        attended_back(t ^ n)

    for copy in out_loads:
        locals_.wait(copy)
    out_far.wait_recv()
    out_buf[0] = out_buf[0] + out_buf[1]
    b_over.wait_recv()
    b_on.start()
    out_over.start()
    b_on.wait_recv()

    @pl.loop(2, 4)
    def _(n):
        attended_back(t ^ n)

    for copy in (b_over, b_near, b_on):
        copy.wait_send()
    @pl.loop(0, 2)
    def _(n):
        at = pl.ds(pl.multiple_of(n * 256, 256), 256)
        for columns, target, first in ((theirs, late_give, 0), (mine, own, EARLY)):
            got = first_dot(dkv[:, at], rowbuf[:, columns]).astype(bf16)
            for e in range(2):
                target[first + 2 * n + e] = got[e * 128 : e * 128 + 128]

    for n in range(4):
        pump.to_mate(EARLY + n, late_give.at[n]).start()
    dq[...] = jnp.zeros(dq.shape, f32)
    for b in range(3):
        pl.when((c == b) if b < 2 else (c >= b))(functools.partial(row_fetch, b))
    pump.slot(2)
    send_early(MATED + 8, 2)

    def tile(b, g, r, kc, bound):
        slot = b & 1
        q_at = pl.ds(pl.multiple_of(r * 512, 512), 512)
        k_at = pl.ds(pl.multiple_of(kc * 512, 512), 512)
        kk, vv = kbuf[slot, g, k_at, :], vbuf[slot, g, k_at, :]
        dv_new, dk_new = [], []
        for hh in range(2):
            h = 2 * g + hh
            qq, do = query[h, q_at, :], dout[h, q_at, :]
            p = jnp.exp2(last_dot(qq, kk) * SCORE_STEP)
            if bound is not None:
                ahead = lax.broadcasted_iota(jnp.int32, p.shape, 0) - lax.broadcasted_iota(
                    jnp.int32, p.shape, 1
                )
                p = jnp.where(ahead >= bound, p, 0.0)
            ds = (p * last_dot(do, vv)).astype(bf16)
            dv_new.append(first_dot(do[:, 0:HEAD_SIZE], p.astype(bf16)))
            dk_new.append(first_dot(qq[:, 0:HEAD_SIZE], ds))
            dq[h, q_at, :] += flat_dot(ds, kk[:, 0:HEAD_SIZE])
        dv[g, :, k_at] += dv_new[0] + dv_new[1]
        dk[g, :, k_at] += dk_new[0] + dk_new[1]

    def clear():
        dk[...] = jnp.zeros(dk.shape, f32)
        dv[...] = jnp.zeros(dv.shape, f32)

    def norm_back(grad, u, gain, cos, sin, row):
        turned = grad * cos - pltpu.roll(grad, HEAD_SIZE // 2, 1) * sin
        r = lax.rsqrt(jnp.mean(u * u, axis=-1, keepdims=True) + norm_eps)
        gsum[row : row + 1, 0:HEAD_SIZE] += jnp.sum(turned * u * r, axis=0, keepdims=True)
        scaled = turned * gain
        inner = jnp.mean(scaled * u, axis=-1, keepdims=True)
        return (r * scaled - u * (r * r * r) * inner).astype(bf16)

    def finish_kv(b):
        for copy in row_copies(b)[:3]:
            copy.wait()

        @pl.loop(0, 4)
        def _(n):
            at = piece(n)
            cos, sin = cosbuf[at, :], sinbuf[at, :]
            for g in range(2):
                lanes = slice(g * 128, g * 128 + 128)
                u = kpbuf[at, lanes]
                dkv[at, lanes] = norm_back(dk[g, :, at].T * scale, u, k_gain, cos, sin, 3)
                dkv[at, 256 + g * 128 : 384 + g * 128] = dv[g, :, at].T.astype(bf16)

        row_copies(b)[3].wait()

        gkv[...] += first_dot(rowbuf[...], dkv[...])

    def kv_part(owner):
        return last_dot(dkv[piece(owner), :], wqkv[:, 512:1024])

    def all_part(owner):
        return kv_part(owner) + last_dot(dqp[piece(owner), :], wqkv[:, 0:512])

    def scatter(which, slot, partial):
        @pl.loop(0, 4)
        def _(n):
            value = partial(t ^ (3 - n))
            pl.when(n == 0)(lambda: which.put_far(value))
            pl.when(n == 1)(lambda: which.put_over(value))
            pl.when(n == 2)(lambda: which.put_near(value))

            @pl.when(n == 3)
            def _():
                kept[slot] = value

    for copy in late_loads:
        locals_.wait(copy)

    @pl.when(c >= 2)
    def _():
        fetched(2)
        clear()

    @pl.loop(0, 6)
    def _(n):
        m = lax.rem(n, 3)

        @pl.when(c >= 2)
        def _():
            tile(2, n // 3, m // 2, (m + 1) // 2, None)

        @pl.when((n & 1) == 1)
        def _():
            pump.slot(3 + n // 2)

        @pl.when(m == 2)
        def _():
            for e in range(2):
                u = MATED + 10 + 2 * (n // 3) + e
                pump.to_mate(u, give.at[u - MATED]).start()

    @pl.when(c >= 2)
    def _():
        finish_kv(2)
        fetch(0)
        row_fetch(1)
        scatter(scatters[2], 0, kv_part)

    out_near.wait_recv()
    out_over.wait_recv()
    out_buf[3] = (kept[1] + out_buf[2].astype(f32) + out_buf[3].astype(f32)).astype(bf16)
    locals_.start(out_buf.at[3], hidden_out)
    out_far.wait_send()
    out_over.wait_send()
    out_near.wait_send()

    @pl.when(c >= 1)
    def _():
        fetched(1)
        clear()

    @pl.loop(0, 8)
    def _(n):
        m = lax.rem(n, 4)

        @pl.when(c >= 1)
        def _():
            tile(1, n // 4, m // 2, m & 1, None)

        @pl.when((n & 1) == 1)
        def _():
            pump.slot(6 + n // 2)

    @pl.when(c >= 2)
    def _():
        out_buf[0] = scatters[2].total(kept[0]).astype(bf16)
        far_copy.start()
        scatters[2].close()

    @pl.when(c >= 1)
    def _():
        finish_kv(1)
        row_fetch(0)

    @pl.when(c >= 1)
    def _():
        scatter(scatters[1], 1, kv_part)

    pump.slot(10)
    fetched(0)
    clear()

    @pl.loop(0, 6)
    def _(n):
        m = lax.rem(n, 3)
        tile(0, n // 3, (m + 1) // 2, m // 2, (m & 1) * -512)

        @pl.when(n == 3)
        def _():
            pump.slot(11)

    finish_kv(0)

    @pl.loop(0, 4)
    def _(n):
        at = piece(n)
        cos, sin = cosbuf[at, :], sinbuf[at, :]
        for h in range(4):
            lanes = slice(h * 128, h * 128 + 128)
            u = q_proj[at, lanes]
            dqp[at, lanes] = norm_back(dq[h, at, :] * scale, u, q_gain, cos, sin, 2)

    for n in range(4):
        late_give[4 + n] = gkv[half_at(1 - s, n, 128), :].astype(bf16)
        pump.to_mate(LATE + n, late_give.at[4 + n]).start()
    for n in range(2):
        got = first_dot(rowbuf[:, half_at(1 - s, n, 256)], dqp[...]).astype(bf16)
        for e in range(2):
            late_give[8 + 2 * n + e] = got[e * 128 : e * 128 + 128]
            pump.to_mate(LATE + 4 + 2 * n + e, late_give.at[8 + 2 * n + e]).start()
    pump.slot(12)

    @pl.when((c >= 1) & (c < nctx - 1))
    def _():
        far_copy.wait_recv()
        kept[1] += far_land[...].astype(f32)

    @pl.when(c >= 1)
    def _():
        out_buf[1] = scatters[1].total(kept[1]).astype(bf16)
        mid_copy.start()
        scatters[1].close()

    base = locals_.start(d_middle, kept.at[1])
    hidden_load = locals_.start(hidden, out_buf.at[2])
    scatter(scatters[0], 0, all_part)
    for n in range(2):
        rows_of = gkv[half_at(s, n, 256), :].astype(bf16)
        got = first_dot(rowbuf[:, half_at(s, n, 256)], dqp[...]).astype(bf16)
        for e in range(2):
            at = slice(e * 128, e * 128 + 128)
            own[LATE + 2 * n + e] = rows_of[at]
            own[LATE + 4 + 2 * n + e] = got[at]
    pump.third(LATE - 4)
    pump.third(LATE - 3)
    pl.loop(0, LATE - 8)(pump.fourth)

    def finish_rows():
        @pl.when(c < nctx - 1)
        def _():
            mid_copy.wait_recv()
            kept[0] += mid_land[...].astype(f32)

        kept[0] = scatters[0].total(kept[0])
        locals_.wait(hidden_load)
        locals_.wait(base)
        x = out_buf[2].astype(f32)
        r = lax.rsqrt(jnp.mean(x * x, axis=-1, keepdims=True) + norm_eps)
        d_in = kept[0]
        gsum[0:1, :] = jnp.sum(d_in * x * r, axis=0, keepdims=True)
        scaled = d_in * gains[0:1, :]
        inner = jnp.mean(scaled * x, axis=-1, keepdims=True)
        kept[1] += r * scaled - x * (r * r * r) * inner
        locals_.start(kept.at[1], hidden_grad)

    swaps = [
        links.copy(gsum, gland.at[n], device)
        for n, device in enumerate((side, across, mate, near, opposite))
    ]

    def swap(n):
        if n > 0:
            swaps[n - 1].wait()
            gsum[...] += gland[n - 1]
        if n < 5:
            swaps[n].start()

    for n, u in enumerate(range(LATE, UNITS)):
        pump.first(u)
        if n >= 1:
            pump.second(u - 1)
        pump.third(u - 2)
        if n == 3:
            finish_rows()
        if n >= 3:
            swap(n - 3)
    pump.second(UNITS - 1)
    pump.third(UNITS - 2)
    swap(8 - 3)
    pump.third(UNITS - 1)
    for n in range(9 - 3, 6):
        swap(n)
    locals_.start(gsum, gains_out)
    scatters[0].close()

    @pl.when(c >= 2)
    def _():
        far_copy.wait_send()

    @pl.when(c >= 1)
    def _():
        mid_copy.wait_send()

    @pl.loop(MATED, EARLY)
    def _(u):
        pump.to_mate(u, give.at[u - MATED]).wait_send()

    @pl.loop(EARLY, UNITS)
    def _(u):
        pump.to_mate(u, late_give.at[u - EARLY]).wait_send()

    pl.loop(LATE - 8, UNITS)(pump.fourth)
    pump.close()
    locals_.finish()


def backward_call(vmem_args, any_args):
    hidden = any_args[1]
    part, width = hidden.shape
    block = 4 * part
    f32, bf16 = jnp.float32, jnp.bfloat16
    shape = jax.ShapeDtypeStruct
    outs = (
        shape((part, width), bf16),
        shape((part, width), f32),
        shape((8, width), f32),
        shape((UNITS, 128, 512), bf16),
    )
    tile = pltpu.VMEM((part, width), bf16)
    units = pltpu.VMEM((UNITS, 128, 512), bf16)
    return pl.pallas_call(
        backward_kernel,
        name="backward",
        out_shape=outs,
        in_specs=[VMEM_SPEC] * 2 + [ANY_SPEC] * len(any_args),
        out_specs=[ANY_SPEC] * len(outs),
        scratch_shapes=[
            pltpu.VMEM((2, 2, block, 256), bf16),
            pltpu.VMEM((2, 2, block, 256), bf16),
            pltpu.VMEM((block, 256), f32),
            pltpu.VMEM((block, HEAD_SIZE), f32),
            pltpu.VMEM((block, HEAD_SIZE), f32),
            pltpu.VMEM((block, width), bf16),
            pltpu.VMEM((4, block, HEAD_SIZE), f32),
            pltpu.VMEM((2, HEAD_SIZE, block), f32),
            pltpu.VMEM((2, HEAD_SIZE, block), f32),
            pltpu.VMEM((block, 512), bf16),
            pltpu.VMEM((block, 512), bf16),
            pltpu.VMEM((width, 512), f32),
            pltpu.VMEM((2, part, width), f32),
            pltpu.VMEM((2, 6, part, width), bf16),
            units,
            pltpu.VMEM((UNITS - MATED, 128, 512), bf16),
            units,
            units,
            pltpu.VMEM((UNITS - EARLY, 128, 512), bf16),
            tile, tile,
            pltpu.VMEM((4, part, width), bf16),
            pltpu.VMEM((4, block, 256), bf16),
            pltpu.VMEM((4, block, 256), bf16),
            pltpu.VMEM((block, 512), f32),
            pltpu.VMEM((width, 1024), bf16),
            pltpu.VMEM((8, width), f32),
            pltpu.VMEM((5, 8, width), f32),
            pltpu.SemaphoreType.DMA((22,)),
            pltpu.SemaphoreType.DMA((22,)),
            pltpu.SemaphoreType.DMA((4 * UNITS,)),
            pltpu.SemaphoreType.DMA((4 * UNITS,)),
            pltpu.SemaphoreType.DMA((UNITS,)),
            pltpu.SemaphoreType.DMA((22,)),
            pltpu.SemaphoreType.DMA((18,)),
        ],
        compiler_params=pltpu.CompilerParams(
            collective_id=2, has_side_effects=True, vmem_limit_bytes=60 << 20
        ),
    )(*vmem_args, *any_args)


def result_kernel(
    chunks_in, gains, grad_in, hidden_in,
    grad_out, hidden_out, attn, wq, wk, wv, q_gain, k_gain, wo, mlp, wg, wu, wd,
    buf, q, k, v, o, gate, up, down, grad, hidden, inside, outside,
):
    shard = lax.axis_index(SHARD_AXIS)
    count = buf.shape[0]
    whole = [
        pltpu.make_async_copy(grad_in, grad, inside.at[count]),
        pltpu.make_async_copy(hidden_in, hidden, inside.at[count + 1]),
    ]
    loads = [pltpu.make_async_copy(chunks_in.at[n], buf.at[n], inside.at[n]) for n in range(count)]
    for copy in whole + loads:
        copy.start()
    stores = []

    def put(n, ref, out, row, lanes):
        at = (slice(row, row + 256), lanes)
        stores.append(pltpu.make_async_copy(ref.at[at], out.at[at], outside.at[len(stores)]))
        stores[-1].start()

    for copy in whole:
        copy.wait()
    for n, (ref, out) in enumerate(((grad, grad_out), (hidden, hidden_out))):
        whole[n] = pltpu.make_async_copy(ref, out, outside.at[count + n])
        whole[n].start()
    for n in range(count):
        loads[n].wait()
        values = buf[n].astype(jnp.float32)
        every = slice(0, 512)
        if n < 3:
            down[n * 256 : n * 256 + 256, :] = values
            put(n, down, wd, n * 256, every)
        elif n < 9:
            ref, out, j = (gate, wg, n - 3) if n < 6 else (up, wu, n - 6)
            lanes = slice(j * 256, j * 256 + 256)
            ref[0:256, lanes] = values[:, 0:256]
            ref[256:512, lanes] = values[:, 256:512]
            at = (slice(0, 512), lanes)
            stores.append(pltpu.make_async_copy(ref.at[at], out.at[at], outside.at[len(stores)]))
            stores[-1].start()
        elif n < 11:
            o[(n - 9) * 256 : (n - 8) * 256, :] = values
            put(n, o, wo, (n - 9) * 256, every)
        elif n < 13:
            row = (n - 11) * 256
            k[row : row + 256, :] = values[:, 0:256]
            v[row : row + 256, :] = values[:, 256:512]
        else:
            q[(n - 13) * 256 : (n - 12) * 256, :] = values
            put(n, q, wq, (n - 13) * 256, every)
    for ref, out in ((k, wk), (v, wv)):
        stores.append(pltpu.make_async_copy(ref, out, outside.at[len(stores)]))
        stores[-1].start()
    wide, small = attn.shape[1], q_gain.shape[1]
    first = shard == 0
    attn[...] = jnp.where(first, gains[0:1, 0:wide], gains[0:1, wide : 2 * wide])
    mlp[...] = jnp.where(first, gains[1:2, 0:wide], gains[1:2, wide : 2 * wide])
    q_gain[...] = jnp.where(first, gains[2:3, 0:small], gains[2:3, small : 2 * small])
    k_gain[...] = jnp.where(first, gains[3:4, 0:small], gains[3:4, small : 2 * small])
    for copy in stores + whole:
        copy.wait()


def result_call(chunks, gains, grad_hidden, out_hidden):
    part, width = grad_hidden.shape
    f32 = jnp.float32
    shape = jax.ShapeDtypeStruct
    half = width // 2
    q, k, v, o = (half, 512), (half, 256), (half, 256), (512, half)
    gate, up, down = (half, 768), (half, 768), (768, half)
    sizes = [q, k, v, (1, 64), (1, 64), o, (1, half), gate, up, down]
    outs = [shape((part, width), f32), shape((part, width), out_hidden.dtype), shape((1, half), f32)]
    outs += [shape(z, f32) for z in sizes]
    specs = [ANY_SPEC] * 2 + [VMEM_SPEC] + [ANY_SPEC] * 3 + [VMEM_SPEC] * 2 + [ANY_SPEC, VMEM_SPEC]
    return pl.pallas_call(
        result_kernel,
        name="result",
        out_shape=outs,
        in_specs=[ANY_SPEC, VMEM_SPEC, ANY_SPEC, ANY_SPEC],
        out_specs=specs + [ANY_SPEC] * 3,
        scratch_shapes=[pltpu.VMEM((CHUNKS, 256, 512), jnp.bfloat16)]
        + [pltpu.VMEM(z, f32) for z in (q, k, v, o, gate, up, down)]
        + [pltpu.VMEM((part, width), f32), pltpu.VMEM((part, width), out_hidden.dtype)]
        + [pltpu.SemaphoreType.DMA((CHUNKS + 2,)), pltpu.SemaphoreType.DMA((CHUNKS + 2,))],
        compiler_params=pltpu.CompilerParams(vmem_limit_bytes=60 << 20),
    )(chunks, gains, grad_hidden, out_hidden)


def fast_device(
    hidden,
    segments,
    cotangent,
    attn_gain,
    w_query,
    key_weight_matrix,
    value_weight_matrix,
    query_gain,
    key_gain,
    mixer_exit_coefficients,
    mlp_gain,
    w_gate,
    w_up,
    w_down,
):
    gains_own = (attn_gain, mlp_gain, query_gain, key_gain)
    exponents = 2.0 * (np.arange(HEAD_SIZE) % (HEAD_SIZE // 2)) / HEAD_SIZE
    rates = np.power(rope_base, -exponents).astype(np.float32)[None]
    labels = segments.reshape(-1, HEAD_SIZE)
    (gains, rows, q_proj, k_proj, query, keys, values, cosine, sine, attended, low, wqkv, crows,
     wo_got, wg_got, wu_got) = forward_call(
        hidden[0], cotangent[0], gains_own, labels, jnp.asarray(rates), w_query, key_weight_matrix,
        value_weight_matrix, mixer_exit_coefficients, w_gate, w_up,
    )
    def units(chunks, count):
        return chunks.reshape(count, 128, 512)

    d_middle, mlp_gain_grad, brow, own, give, parts, out_own = mlp_call(
        (low, hidden[0], gains),
        (crows, mixer_exit_coefficients, wo_got, w_gate, wg_got, w_up, wu_got, w_down),
    )
    out_hidden, grad_hidden, sums, chunks = backward_call(
        (gains, mlp_gain_grad),
        (query, hidden[0], brow, low, attended, mixer_exit_coefficients, wo_got, d_middle, q_proj, wqkv, units(own, EARLY), units(give, EARLY - MATED),
         parts, out_own, keys, values, k_proj, cosine, sine, rows),
    )
    (grad_hidden, out_hidden, attn, wq, wk, wv, q_gain, k_gain, wo, mlp, wg, wu, wd) = result_call(
        chunks.reshape(CHUNKS, 256, 512), sums, grad_hidden, out_hidden
    )
    return (
        out_hidden[None], grad_hidden[None], attn[0], wq, wk, wv, q_gain[0], k_gain[0], wo, mlp[0],
        wg, wu, wd,
    )


def per_device(
    hidden,
    segments,
    cotangent,
    attn_gain,
    w_query,
    key_weight_matrix,
    value_weight_matrix,
    query_gain,
    key_gain,
    mixer_exit_coefficients,
    mlp_gain,
    w_gate,
    w_up,
    w_down,
):
    collected_rows = (
        lax.all_gather(attn_gain, SHARD_AXIS, axis=0, tiled=True),
        lax.all_gather(w_query, SHARD_AXIS, axis=0, tiled=True),
        lax.all_gather(key_weight_matrix, SHARD_AXIS, axis=0, tiled=True),
        lax.all_gather(value_weight_matrix, SHARD_AXIS, axis=0, tiled=True),
        lax.all_gather(query_gain, SHARD_AXIS, axis=0, tiled=True),
        lax.all_gather(key_gain, SHARD_AXIS, axis=0, tiled=True),
        lax.all_gather(mixer_exit_coefficients, SHARD_AXIS, axis=1, tiled=True),
        lax.all_gather(mlp_gain, SHARD_AXIS, axis=0, tiled=True),
        lax.all_gather(w_gate, SHARD_AXIS, axis=0, tiled=True),
        lax.all_gather(w_up, SHARD_AXIS, axis=0, tiled=True),
        lax.all_gather(w_down, SHARD_AXIS, axis=1, tiled=True),
    )
    gain_attn = collected_rows[0].astype(jnp.float32)
    gain_query = collected_rows[4].astype(jnp.float32)
    gain_key = collected_rows[5].astype(jnp.float32)
    gain_mlp = collected_rows[7].astype(jnp.float32)
    seq_count = hidden.shape[0]
    block_rows = hidden.shape[1] * lax.axis_size(TP_AXIS)
    seq_length = segments.shape[1]
    ctx_index = lax.axis_index(CTX_AXIS)
    heads_local = w_query.shape[1] // HEAD_SIZE
    kv_local = key_weight_matrix.shape[1] // HEAD_SIZE
    query_group_width = heads_local // kv_local
    score_scale = HEAD_SIZE ** (-0.5)
    block_start = ctx_index * block_rows
    query_pos = block_start + jnp.arange(block_rows, dtype=jnp.int32)
    query_seg = lax.dynamic_slice_in_dim(segments, block_start, block_rows, 1)
    positions = lax.dynamic_slice_in_dim(doc_positions(segments), block_start, block_rows, 1)
    cosine, sine_part = rope_tables(positions)

    def counting_keys(key_first, step_rows):
        early = key_first <= block_start + block_rows - 1
        last_seg = lax.dynamic_slice_in_dim(segments, key_first + step_rows - 1, 1, 1)[:, 0]
        return early & jnp.any(last_seg >= query_seg[:, 0])

    inputs = hidden.astype(jnp.float32)
    scale_one = rms_scale(inputs)
    attention_input = (inputs * scale_one * gain_attn).astype(jnp.bfloat16)
    attention_rows = tp_rows(attention_input)
    q_proj = jnp.einsum(
        "zjr,rm->zjm", attention_rows, collected_rows[1], preferred_element_type=jnp.float32
    ).reshape(seq_count, block_rows, heads_local, HEAD_SIZE)
    key_projected = jnp.einsum(
        "zjr,rm->zjm", attention_rows, collected_rows[2], preferred_element_type=jnp.float32
    ).reshape(seq_count, block_rows, kv_local, HEAD_SIZE)
    value_projected = jnp.einsum(
        "zjr,rm->zjm", attention_rows, collected_rows[3], preferred_element_type=jnp.float32
    )
    q_scale = rms_scale(q_proj)
    k_scale = rms_scale(key_projected)
    query_rows_input = (
        rotate(q_proj * q_scale * gain_query, cosine, sine_part)
        .astype(jnp.bfloat16)
        .reshape(seq_count, block_rows, kv_local, query_group_width, HEAD_SIZE)
    )
    keys = rotate(key_projected * k_scale * gain_key, cosine, sine_part).astype(jnp.bfloat16)
    values = value_projected.astype(jnp.bfloat16).reshape(
        seq_count, block_rows, kv_local, HEAD_SIZE
    )
    stat_shape = (seq_count, kv_local, query_group_width, block_rows)
    start_state = (
        jnp.full(stat_shape, masked_fill, jnp.float32),
        jnp.zeros(stat_shape, jnp.float32),
        jnp.zeros(stat_shape + (HEAD_SIZE,), jnp.float32),
    )
    piece_keys = lax.all_gather(keys, CTX_AXIS, axis=1, tiled=True)
    piece_values = lax.all_gather(values, CTX_AXIS, axis=1, tiled=True)
    piece_rows = piece_keys.shape[1]
    step_rows = math.gcd(piece_rows, 1024)

    def attend_one_step(number, loop_state):
        offset = number * step_rows
        key_first = offset

        def attend_compute(state):
            row_max, row_total, summed = state
            key_part = lax.dynamic_slice_in_dim(piece_keys, offset, step_rows, 1)
            value_part = lax.dynamic_slice_in_dim(piece_values, offset, step_rows, 1)
            allowed = key_block(segments, key_first, step_rows, query_pos, query_seg)
            scores = (
                jnp.einsum(
                    "sqhgd,skhd->shgqk",
                    query_rows_input,
                    key_part,
                    preferred_element_type=jnp.float32,
                )
                * score_scale
            )
            masked = jnp.where(allowed, scores, masked_fill)
            new_max = jnp.maximum(row_max, jnp.max(masked, axis=-1))
            weights = jnp.where(allowed, jnp.exp(masked - new_max[..., None]), 0.0)
            decay_factor = jnp.exp(row_max - new_max)
            row_total = row_total * decay_factor + jnp.sum(weights, axis=-1)
            summed = summed * decay_factor[..., None] + jnp.einsum(
                "shgqk,skhd->shgqd",
                weights.astype(jnp.bfloat16),
                value_part,
                preferred_element_type=jnp.float32,
            )
            return (new_max, row_total, summed)

        return lax.cond(counting_keys(key_first, step_rows), attend_compute, keep_state, loop_state)

    row_max, row_total, summed = lax.fori_loop(
        0, piece_rows // step_rows, attend_one_step, start_state
    )
    attended = summed / row_total[..., None]
    log_total = row_max + jnp.log(row_total)
    attended_reduced_copy = (
        attended.transpose(0, 3, 1, 2, 4)
        .reshape(seq_count, block_rows, heads_local * HEAD_SIZE)
        .astype(jnp.bfloat16)
    )
    branch = tp_total(
        jnp.einsum(
            "vkq,qy->vky",
            attended_reduced_copy,
            collected_rows[6],
            preferred_element_type=jnp.float32,
        )
    )
    middle = inputs + branch
    scale_two = rms_scale(middle)
    mlp_in = (middle * scale_two * gain_mlp).astype(jnp.bfloat16)
    mlp_rows = tp_rows(mlp_in)
    gate = jnp.einsum(
        "snd,df->snf", mlp_rows, collected_rows[8], preferred_element_type=jnp.float32
    )
    upward = jnp.einsum(
        "snd,df->snf", mlp_rows, collected_rows[9], preferred_element_type=jnp.float32
    )
    activated = (jax.nn.silu(gate) * upward).astype(jnp.bfloat16)
    out_hidden = (
        middle
        + tp_total(
            jnp.einsum(
                "snf,fd->snd", activated, collected_rows[10], preferred_element_type=jnp.float32
            )
        )
    ).astype(jnp.bfloat16)
    again = (
        lax.all_gather(attn_gain, SHARD_AXIS, axis=0, tiled=True),
        lax.all_gather(w_query, SHARD_AXIS, axis=0, tiled=True),
        lax.all_gather(key_weight_matrix, SHARD_AXIS, axis=0, tiled=True),
        lax.all_gather(value_weight_matrix, SHARD_AXIS, axis=0, tiled=True),
        lax.all_gather(query_gain, SHARD_AXIS, axis=0, tiled=True),
        lax.all_gather(key_gain, SHARD_AXIS, axis=0, tiled=True),
        lax.all_gather(mixer_exit_coefficients, SHARD_AXIS, axis=1, tiled=True),
        lax.all_gather(mlp_gain, SHARD_AXIS, axis=0, tiled=True),
        lax.all_gather(w_gate, SHARD_AXIS, axis=0, tiled=True),
        lax.all_gather(w_up, SHARD_AXIS, axis=0, tiled=True),
        lax.all_gather(w_down, SHARD_AXIS, axis=1, tiled=True),
    )
    query_backward = again[1]
    lookup_pullback = again[2]
    value_backward = again[3]
    output_backward = again[6]
    back_gate = again[8]
    back_up = again[9]
    back_down = again[10]
    d_out = cotangent.astype(jnp.float32)
    d_rows = tp_rows(cotangent)
    grad_down = jnp.einsum("snf,snd->fd", activated, d_rows, preferred_element_type=jnp.float32)
    d_act = jnp.einsum("snd,fd->snf", d_rows, back_down, preferred_element_type=jnp.float32)
    sigmoid_gate = jax.nn.sigmoid(gate)
    d_upward = (d_act * jax.nn.silu(gate)).astype(jnp.bfloat16)
    d_gate = (d_act * upward * sigmoid_gate * (1.0 + gate * (1.0 - sigmoid_gate))).astype(
        jnp.bfloat16
    )
    grad_gate = jnp.einsum("snd,snf->df", mlp_rows, d_gate, preferred_element_type=jnp.float32)
    grad_up = jnp.einsum("snd,snf->df", mlp_rows, d_upward, preferred_element_type=jnp.float32)
    d_mlp_in = tp_total(
        jnp.einsum("snf,df->snd", d_gate, back_gate, preferred_element_type=jnp.float32)
        + jnp.einsum("snf,df->snd", d_upward, back_up, preferred_element_type=jnp.float32)
    )
    grad_mlp_gain = jnp.sum(d_mlp_in * middle * scale_two, axis=(0, 1))
    d_middle = d_out + rms_back(d_mlp_in, middle, scale_two, gain_mlp)
    d_branch = d_middle.astype(jnp.bfloat16)
    residual_branch_rows = tp_rows(d_branch)
    result_cotangent = jnp.einsum(
        "xbj,xbk->jk",
        attended_reduced_copy,
        residual_branch_rows,
        preferred_element_type=jnp.float32,
    )
    d_attended = (
        jnp.einsum(
            "miv,cv->mic", residual_branch_rows, output_backward, preferred_element_type=jnp.float32
        )
        .astype(jnp.bfloat16)
        .reshape(seq_count, block_rows, kv_local, query_group_width, HEAD_SIZE)
    )
    delta = jnp.sum(d_attended.astype(jnp.float32).transpose(0, 2, 3, 1, 4) * attended, axis=-1)
    query_zeros = jnp.zeros(
        (seq_count, block_rows, kv_local, query_group_width, HEAD_SIZE), jnp.float32
    )
    back_state = (
        query_zeros,
        jnp.zeros((seq_count, seq_length, kv_local, HEAD_SIZE), jnp.float32),
        jnp.zeros((seq_count, seq_length, kv_local, HEAD_SIZE), jnp.float32),
    )
    back_piece_keys = lax.all_gather(keys, CTX_AXIS, axis=1, tiled=True)
    back_piece_values = lax.all_gather(values, CTX_AXIS, axis=1, tiled=True)
    piece_rows = back_piece_keys.shape[1]
    back_step_rows = math.gcd(piece_rows, 1024)

    def back_one_step(number, loop_state):
        offset = number * back_step_rows
        key_first = offset
        write_at = offset

        def back_compute(state):
            d_query, d_keys, d_values = state
            key_part = lax.dynamic_slice_in_dim(back_piece_keys, offset, back_step_rows, 1)
            value_part = lax.dynamic_slice_in_dim(back_piece_values, offset, back_step_rows, 1)
            allowed = key_block(segments, key_first, back_step_rows, query_pos, query_seg)
            scores = (
                jnp.einsum(
                    "sqhgd,skhd->shgqk",
                    query_rows_input,
                    key_part,
                    preferred_element_type=jnp.float32,
                )
                * score_scale
            )
            probs = jnp.where(allowed, jnp.exp(scores - log_total[..., None]), 0.0)
            d_probs = jnp.einsum(
                "sqhgd,skhd->shgqk", d_attended, value_part, preferred_element_type=jnp.float32
            )
            d_scores = (probs * (d_probs - delta[..., None])).astype(jnp.bfloat16)
            d_query = d_query + jnp.einsum(
                "shgqk,skhd->sqhgd", d_scores, key_part, preferred_element_type=jnp.float32
            )
            key_grad = jnp.einsum(
                "shgqk,sqhgd->skhd", d_scores, query_rows_input, preferred_element_type=jnp.float32
            )
            value_grad = jnp.einsum(
                "shgqk,sqhgd->skhd",
                probs.astype(jnp.bfloat16),
                d_attended,
                preferred_element_type=jnp.float32,
            )
            d_keys = lax.dynamic_update_slice_in_dim(
                d_keys,
                lax.dynamic_slice_in_dim(d_keys, write_at, back_step_rows, 1) + key_grad,
                write_at,
                1,
            )
            d_values = lax.dynamic_update_slice_in_dim(
                d_values,
                lax.dynamic_slice_in_dim(d_values, write_at, back_step_rows, 1) + value_grad,
                write_at,
                1,
            )
            return (d_query, d_keys, d_values)

        return lax.cond(
            counting_keys(key_first, back_step_rows), back_compute, keep_state, loop_state
        )

    d_query, d_keys, d_values = lax.fori_loop(
        0, piece_rows // back_step_rows, back_one_step, back_state
    )
    own_keys, own_values = (
        lax.psum_scatter(
            d_keys.astype(jnp.bfloat16), CTX_AXIS, scatter_dimension=1, tiled=True
        ).astype(jnp.float32),
        lax.psum_scatter(
            d_values.astype(jnp.bfloat16), CTX_AXIS, scatter_dimension=1, tiled=True
        ).astype(jnp.float32),
    )
    q_normed = rotate_back(
        d_query.reshape(seq_count, block_rows, heads_local, HEAD_SIZE) * score_scale,
        cosine,
        sine_part,
    )
    grad_query_gain = jnp.sum(q_normed * q_proj * q_scale, axis=(0, 1, 2))
    query_projection_gradient = (
        rms_back(q_normed, q_proj, q_scale, gain_query)
        .astype(jnp.bfloat16)
        .reshape(seq_count, block_rows, heads_local * HEAD_SIZE)
    )
    k_normed = rotate_back(own_keys * score_scale, cosine, sine_part)
    grad_key_gain = jnp.sum(k_normed * key_projected * k_scale, axis=(0, 1, 2))
    lookup_map_derivative = (
        rms_back(k_normed, key_projected, k_scale, gain_key)
        .astype(jnp.bfloat16)
        .reshape(seq_count, block_rows, kv_local * HEAD_SIZE)
    )
    value_projection_gradient = own_values.astype(jnp.bfloat16).reshape(
        seq_count, block_rows, kv_local * HEAD_SIZE
    )
    query_gradient_rows = jnp.einsum(
        "zqr,zqa->ra", attention_rows, query_projection_gradient, preferred_element_type=jnp.float32
    )
    key_gradient_rows = jnp.einsum(
        "zqr,zqa->ra", attention_rows, lookup_map_derivative, preferred_element_type=jnp.float32
    )
    value_gradient_rows = jnp.einsum(
        "zqr,zqa->ra", attention_rows, value_projection_gradient, preferred_element_type=jnp.float32
    )
    d_attn_in = tp_total(
        jnp.einsum(
            "wtl,al->wta",
            query_projection_gradient,
            query_backward,
            preferred_element_type=jnp.float32,
        )
        + jnp.einsum(
            "wtl,al->wta",
            lookup_map_derivative,
            lookup_pullback,
            preferred_element_type=jnp.float32,
        )
        + jnp.einsum(
            "wtl,al->wta",
            value_projection_gradient,
            value_backward,
            preferred_element_type=jnp.float32,
        )
    )
    grad_attn_gain = jnp.sum(d_attn_in * inputs * scale_one, axis=(0, 1))
    grad_hidden = d_middle + rms_back(d_attn_in, inputs, scale_one, gain_attn)
    reduced = (
        lax.psum_scatter(
            grad_attn_gain.astype(jnp.bfloat16), SHARD_AXIS, scatter_dimension=0, tiled=True
        ).astype(jnp.float32),
        lax.psum_scatter(
            query_gradient_rows.astype(jnp.bfloat16), SHARD_AXIS, scatter_dimension=0, tiled=True
        ).astype(jnp.float32),
        lax.psum_scatter(
            key_gradient_rows.astype(jnp.bfloat16), SHARD_AXIS, scatter_dimension=0, tiled=True
        ).astype(jnp.float32),
        lax.psum_scatter(
            value_gradient_rows.astype(jnp.bfloat16), SHARD_AXIS, scatter_dimension=0, tiled=True
        ).astype(jnp.float32),
        lax.psum_scatter(
            grad_query_gain.astype(jnp.bfloat16), SHARD_AXIS, scatter_dimension=0, tiled=True
        ).astype(jnp.float32),
        lax.psum_scatter(
            grad_key_gain.astype(jnp.bfloat16), SHARD_AXIS, scatter_dimension=0, tiled=True
        ).astype(jnp.float32),
        lax.psum_scatter(
            result_cotangent.astype(jnp.bfloat16), SHARD_AXIS, scatter_dimension=1, tiled=True
        ).astype(jnp.float32),
        lax.psum_scatter(
            grad_mlp_gain.astype(jnp.bfloat16), SHARD_AXIS, scatter_dimension=0, tiled=True
        ).astype(jnp.float32),
        lax.psum_scatter(
            grad_gate.astype(jnp.bfloat16), SHARD_AXIS, scatter_dimension=0, tiled=True
        ).astype(jnp.float32),
        lax.psum_scatter(
            grad_up.astype(jnp.bfloat16), SHARD_AXIS, scatter_dimension=0, tiled=True
        ).astype(jnp.float32),
        lax.psum_scatter(
            grad_down.astype(jnp.bfloat16), SHARD_AXIS, scatter_dimension=1, tiled=True
        ).astype(jnp.float32),
    )
    matrices = (
        lax.psum(reduced[1].astype(jnp.bfloat16), CTX_AXIS).astype(jnp.float32),
        lax.psum(reduced[2].astype(jnp.bfloat16), CTX_AXIS).astype(jnp.float32),
        lax.psum(reduced[3].astype(jnp.bfloat16), CTX_AXIS).astype(jnp.float32),
        lax.psum(reduced[6].astype(jnp.bfloat16), CTX_AXIS).astype(jnp.float32),
        lax.psum(reduced[8].astype(jnp.bfloat16), CTX_AXIS).astype(jnp.float32),
        lax.psum(reduced[9].astype(jnp.bfloat16), CTX_AXIS).astype(jnp.float32),
        lax.psum(reduced[10].astype(jnp.bfloat16), CTX_AXIS).astype(jnp.float32),
    )
    gains = lax.psum((reduced[0], reduced[4], reduced[5], reduced[7]), (CTX_AXIS, TP_AXIS))
    return (
        out_hidden,
        grad_hidden,
        gains[0],
        matrices[0],
        matrices[1],
        matrices[2],
        gains[1],
        gains[2],
        matrices[3],
        gains[3],
        matrices[4],
        matrices[5],
        matrices[6],
    )


def solution(mesh):
    in_specs = (
        P(SHARD_AXIS, (CTX_AXIS, TP_AXIS), None),
        P(SHARD_AXIS, None),
        P(SHARD_AXIS, (CTX_AXIS, TP_AXIS), None),
        P(SHARD_AXIS),
        P(SHARD_AXIS, TP_AXIS),
        P(SHARD_AXIS, TP_AXIS),
        P(SHARD_AXIS, TP_AXIS),
        P(SHARD_AXIS),
        P(SHARD_AXIS),
        P(TP_AXIS, SHARD_AXIS),
        P(SHARD_AXIS),
        P(SHARD_AXIS, TP_AXIS),
        P(SHARD_AXIS, TP_AXIS),
        P(TP_AXIS, SHARD_AXIS),
    )
    out_specs = (
        P(SHARD_AXIS, (CTX_AXIS, TP_AXIS), None),
        P(SHARD_AXIS, (CTX_AXIS, TP_AXIS), None),
        P(SHARD_AXIS),
        P(SHARD_AXIS, TP_AXIS),
        P(SHARD_AXIS, TP_AXIS),
        P(SHARD_AXIS, TP_AXIS),
        P(SHARD_AXIS),
        P(SHARD_AXIS),
        P(TP_AXIS, SHARD_AXIS),
        P(SHARD_AXIS),
        P(SHARD_AXIS, TP_AXIS),
        P(SHARD_AXIS, TP_AXIS),
        P(TP_AXIS, SHARD_AXIS),
    )
    shape = mesh.shape
    fast = shape[SHARD_AXIS] == 2 and shape[CTX_AXIS] == 4 and shape[TP_AXIS] == 4
    return jax.shard_map(
        fast_device if fast else per_device, mesh=mesh, in_specs=in_specs, out_specs=out_specs, check_vma=False
    )
```

```python
import functools
import math

import jax
import jax.numpy as jnp
import numpy as np
from jax import lax
from jax.experimental import pallas as pl
from jax.experimental.pallas import tpu as pltpu
from jax.sharding import PartitionSpec as P

SHARD_AXIS, CTX_AXIS, TP_AXIS = "shard", "ctx", "tp"
HEAD_SIZE = 128
NDOC = 8


norm_eps = 1e-06
rope_base = 1000000.0
masked_fill = -1e30


def rms_scale(values):
    return lax.rsqrt(jnp.mean(values * values, axis=-1, keepdims=True) + norm_eps)


def rms_back(grad_out, values, row_scale, gain_vec):
    scaled = grad_out * gain_vec
    inner_sum = jnp.mean(scaled * values, axis=-1, keepdims=True)
    return row_scale * scaled - values * (row_scale * row_scale * row_scale) * inner_sum


def doc_positions(segments):
    seq_width = segments.shape[-1]
    labels = jnp.arange(NDOC, dtype=jnp.int32)
    onehot = (segments[..., None] == labels).astype(jnp.int32)
    counts = jnp.sum(onehot, axis=-2)
    starts = jnp.cumsum(counts, axis=-1) - counts
    first_row = jnp.sum(onehot * starts[..., None, :], axis=-1)
    return jnp.arange(seq_width, dtype=jnp.int32) - first_row


def rope_tables(positions):
    exponents = jnp.arange(0, HEAD_SIZE, 2).astype(jnp.float32) / HEAD_SIZE
    angle_rates = jnp.power(jnp.float32(rope_base), -exponents)
    angles = positions.astype(jnp.float32)[..., None] * angle_rates
    angles = jnp.concatenate([angles, angles], axis=-1)[..., None, :]
    return (jnp.cos(angles), jnp.sin(angles))


def rotate(inputs, cosine, sine_part):
    half_dim = inputs.shape[-1] // 2
    turned = jnp.concatenate([-inputs[..., half_dim:], inputs[..., :half_dim]], axis=-1)
    return inputs * cosine + turned * sine_part


def rotate_back(grads, cosine, sine_part):
    half_dim = grads.shape[-1] // 2
    moved = grads * sine_part
    turned = jnp.concatenate([moved[..., half_dim:], -moved[..., :half_dim]], axis=-1)
    return grads * cosine + turned


def tp_rows(local_part):
    return lax.all_gather(local_part, TP_AXIS, axis=1, tiled=True)


def tp_total(partial_sum):
    return lax.psum_scatter(
        partial_sum.astype(jnp.bfloat16), TP_AXIS, scatter_dimension=1, tiled=True
    ).astype(jnp.float32)


def key_block(segments, key_first, step_rows, query_pos, query_seg):
    key_pos = key_first + jnp.arange(step_rows, dtype=jnp.int32)
    key_seg = lax.dynamic_slice_in_dim(segments, key_first, step_rows, 1)
    allowed = (key_pos[None, None, :] <= query_pos[None, :, None]) & (
        key_seg[:, None, :] == query_seg[:, :, None]
    )
    return allowed[:, None, None]


def keep_state(state):
    return state


CHUNKS = 15
FROM_MLP = 9
READY = 2
UNITS, EARLY, MATED, LATE = 2 * CHUNKS, 2 * FROM_MLP, 2 * READY, 22


MESH_ID = pl.DeviceIdType.MESH
ANY_SPEC = pl.BlockSpec(memory_space=pl.ANY)
VMEM_SPEC = pl.BlockSpec(memory_space=pltpu.VMEM)
SCORE_STEP = HEAD_SIZE ** (-0.5) * math.log2(math.e)
APART = 16384.0


def enter(peers):
    barrier = pltpu.get_barrier_semaphore()
    for peer in peers:
        pl.semaphore_signal(barrier, inc=1, device_id=peer, device_id_type=MESH_ID)
    pl.semaphore_wait(barrier, len(peers))


def last_dot(left, right):
    return lax.dot_general(
        left, right, (((1,), (1,)), ((), ())), preferred_element_type=jnp.float32
    )


def flat_dot(left, right):
    return jnp.dot(left, right, preferred_element_type=jnp.float32)


def first_dot(left, right):
    return lax.dot_general(
        left, right, (((0,), (0,)), ((), ())), preferred_element_type=jnp.float32
    )


def spin(values, cosine, sine_signed):
    return values * cosine + pltpu.roll(values, HEAD_SIZE // 2, 1) * sine_signed


class Links:
    def __init__(self, send, recv):
        self.send, self.recv, self.used = send, recv, 0

    def copy(self, src, dst, device):
        number = self.used
        self.used += 1
        return pltpu.make_async_remote_copy(
            src_ref=src, dst_ref=dst, send_sem=self.send.at[number],
            recv_sem=self.recv.at[number], device_id=device, device_id_type=MESH_ID,
        )


class Locals:
    def __init__(self, sems):
        self.sems, self.used, self.open = sems, 0, []

    def make(self, src, dst):
        copy = pltpu.make_async_copy(src, dst, self.sems.at[self.used])
        self.used += 1
        return copy

    def start(self, src, dst):
        copy = self.make(src, dst)
        copy.start()
        self.open.append(copy)
        return copy

    def wait(self, copy):
        copy.wait()
        self.open = [other for other in self.open if other is not copy]

    def finish(self):
        for copy in self.open:
            copy.wait()


def forward_kernel(
    hidden, cotangent, attn_gain, mlp_gain, query_gain, key_gain, segments, rates, wq, wk, wv, wo, wg, wu,
    gains_out, rows_out, q_out, k_out, query_out, keys_out, values_out, cos_out, sin_out,
    attended_out, low_out, wqkv_out, crows_out, wo_out, wg_out, wu_out,
    gains, raw, rows, wqkv, q_proj, k_proj, qaug, kaug, vaug, cosine, sine, acc, low, crows,
    gains_in, gains_land, places, send, recv, local,
):
    s, c, t = lax.axis_index(SHARD_AXIS), lax.axis_index(CTX_AXIS), lax.axis_index(TP_AXIS)
    nctx = lax.axis_size(CTX_AXIS)
    part = hidden.shape[0]
    block = 4 * part
    half = wq.shape[0]
    f32, bf16 = jnp.float32, jnp.bfloat16
    side, across, mate = {TP_AXIS: t ^ 1}, {TP_AXIS: t ^ 2}, {SHARD_AXIS: 1 - s}
    pair = {CTX_AXIS: c ^ 1}
    nxt, prv = {CTX_AXIS: lax.rem(c + 1, nctx)}, {CTX_AXIS: lax.rem(c + nctx - 1, nctx)}
    gains_in[...] = jnp.zeros(gains_in.shape, f32)
    for row, gain in enumerate((attn_gain, mlp_gain)):
        own_gain = gain[...].astype(f32)[None, :]
        gains_in[row : row + 1, pl.ds(pl.multiple_of(s * half, half), half)] = own_gain
    small = HEAD_SIZE // 2
    source_lane = lax.broadcasted_iota(jnp.int32, (small, HEAD_SIZE), 0)
    target_lane = lax.broadcasted_iota(jnp.int32, (small, HEAD_SIZE), 1) - s * small
    chosen = jnp.where(source_lane == target_lane, 1.0, 0.0).astype(bf16)
    for row, gain in ((2, query_gain), (3, key_gain)):
        placed = flat_dot(jnp.broadcast_to(gain[...][None, :], (16, small)), chosen)
        gains_in[row : row + 1, 0:HEAD_SIZE] = placed[0:1]
    enter([side, across, mate, nxt, prv])
    links, locals_ = Links(send, recv), Locals(local)

    def piece(owner):
        return pl.ds(pl.multiple_of(owner * part, part), part)

    low_bit = c & 1

    def some(shard, count, size):
        return pl.ds(pl.multiple_of(shard * count + low_bit * size, size), size)

    mine = pl.ds(pl.multiple_of(s * half, half), half)
    quarter = half // 2
    gains_copy = links.copy(gains_in, gains_land, mate)
    wk_copy = links.copy(wk, wqkv.at[mine, 512:768], mate)
    wv_copy = links.copy(wv, wqkv.at[mine, 768:1024], mate)
    wq_copy = links.copy(wq, wqkv.at[mine, 0:512], mate)
    wo_copy = links.copy(
        wo.at[some(0, 0, quarter), :], wo_out.at[some(0, 0, quarter), :], mate
    )
    wo_got = wo_out.at[some(0, 0, quarter), :]
    wo_on = links.copy(wo_got, wo_got, pair)
    wg_copy = links.copy(
        wg.at[some(0, 0, quarter), :], wg_out.at[some(0, 0, quarter), :], mate
    )
    wg_got = wg_out.at[some(0, 0, quarter), :]
    wg_on = links.copy(wg_got, wg_got, pair)
    wu_copy = links.copy(
        wu.at[some(0, 0, quarter), :], wu_out.at[some(0, 0, quarter), :], mate
    )
    gains_copy.start()
    wk_copy.start()
    wv_copy.start()
    wq_copy.start()
    own_k = locals_.start(wk, wqkv.at[mine, 512:768])
    own_v = locals_.start(wv, wqkv.at[mine, 768:1024])
    own_q = locals_.start(wq, wqkv.at[mine, 0:512])
    own_c = locals_.start(cotangent, crows.at[piece(t), :])

    def source(b, owner):
        return hidden if b == 0 else raw.at[b, piece(owner)]

    to_across, to_side, on_to_side, to_next = [], [], [], []
    for b in range(3):
        there = raw.at[b, piece(t ^ 2)]
        to_side.append(links.copy(source(b, t), raw.at[b, piece(t)], side))
        on_to_side.append(links.copy(there, there, side))
        if b < 2:
            to_across.append(links.copy(source(b, t), raw.at[b, piece(t)], across))
            to_next.append(links.copy(source(b, t), raw.at[b + 1, piece(t)], nxt))
    far_to_next = links.copy(raw.at[1, piece(t ^ 2)], raw.at[2, piece(t ^ 2)], nxt)
    c_side = links.copy(cotangent, crows.at[piece(t), :], side)
    c_over = links.copy(cotangent, crows.at[piece(t), :], across)
    c_on = links.copy(crows.at[piece(t ^ 2), :], crows.at[piece(t ^ 2), :], side)
    to_across[0].start()
    to_side[0].start()

    @pl.when(c < nctx - 1)
    def _():
        to_next[0].start()

    c_side.start()
    raw[0, piece(t), :] = hidden[...]
    gains_copy.wait()
    gains[...] = gains_in[...] + gains_land[...]
    q_gain = gains[2:3, 0:HEAD_SIZE]
    k_gain = gains[3:4, 0:HEAD_SIZE]

    def table(b):
        start, stop, rate = places[0:1, :], places[1:2, :], rates[...]
        shape = (128, HEAD_SIZE)
        lower = lax.broadcasted_iota(jnp.int32, shape, 1) < HEAD_SIZE // 2

        @pl.loop(0, 4)
        def _(n):
            found = []
            for offset in (0, 512):
                first = n * 128 + offset
                index = (lax.broadcasted_iota(jnp.int32, shape, 0) + first) + (c - b) * block
                index = index.astype(f32)
                inside = (index >= start) & (index < stop)
                marks = jnp.where(inside, 1.0, 0.0)
                begin = jnp.sum(jnp.where(inside, start, 0.0), axis=1, keepdims=True)
                at = pl.ds(pl.multiple_of(first, 128), 128)
                for g in range(2):
                    kaug[b, g, at, 128:256] = (1.0 - marks).astype(bf16)
                if b == 0:
                    for h in range(4):
                        qaug[h, at, 128:256] = (marks * -APART).astype(bf16)
                found.append((at, index - begin))
            (low_at, low_pos), (high_at, high_pos) = found
            angle = jnp.where(lower, low_pos, high_pos) * rate
            cs, sn = jnp.cos(angle), jnp.sin(angle)
            cr, sr = pltpu.roll(cs, HEAD_SIZE // 2, 1), pltpu.roll(sn, HEAD_SIZE // 2, 1)
            cosine[b, low_at, :] = jnp.where(lower, cs, cr)
            cosine[b, high_at, :] = jnp.where(lower, cr, cs)
            sine[b, low_at, :] = jnp.where(lower, -sn, sr)
            sine[b, high_at, :] = jnp.where(lower, -sr, sn)

    def project_kv(b, owner):
        at = piece(owner)
        x = raw[b, at, :].astype(f32)
        scale = lax.rsqrt(jnp.mean(x * x, axis=-1, keepdims=True) + norm_eps)
        rows[b, at, :] = (x * scale * gains[0:1, :]).astype(bf16)
        got = flat_dot(rows[b, at, :], wqkv[:, 512:1024])
        k_proj[b, at, :] = got[:, 0:256]
        for g in range(2):
            u = got[:, g * 128 : g * 128 + 128]
            r = lax.rsqrt(jnp.mean(u * u, axis=-1, keepdims=True) + norm_eps)
            turned = spin(u * r * k_gain, cosine[b, at, :], sine[b, at, :])
            kaug[b, g, at, 0:128] = turned.astype(bf16)
            vaug[b, g, at, 0:128] = got[:, 256 + g * 128 : 384 + g * 128].astype(bf16)

    def project_q(owner):
        at = piece(owner)
        got = flat_dot(rows[0, at, :], wqkv[:, 0:512])
        q_proj[at, :] = got
        for h in range(4):
            u = got[:, h * 128 : h * 128 + 128]
            r = lax.rsqrt(jnp.mean(u * u, axis=-1, keepdims=True) + norm_eps)
            turned = spin(u * r * q_gain, cosine[0, at, :], sine[0, at, :])
            qaug[h, at, 0:128] = turned.astype(bf16)

    def unit(b, g, r, kc, bound):
        at = pl.ds(pl.multiple_of(r * 512, 512), 512)
        for hh in range(2):
            qq = qaug[2 * g + hh, at, :]
            total = None
            for j in range(2):
                keys_at = pl.ds(pl.multiple_of(kc * 512 + j * 256, 256), 256)
                p = jnp.exp2(last_dot(qq, kaug[b, g, keys_at, :]) * SCORE_STEP)
                if bound is not None:
                    ahead = lax.broadcasted_iota(jnp.int32, p.shape, 0) - lax.broadcasted_iota(
                        jnp.int32, p.shape, 1
                    )
                    p = jnp.where(ahead >= bound + j * 256, p, 0.0)
                value = flat_dot(p.astype(bf16), vaug[b, g, keys_at, :])
                total = value if total is None else total + value
            acc[2 * g + hh, at, :] += total

    def block_outs(b):
        pairs = (
            (rows, rows_out), (k_proj, k_out), (kaug, keys_out), (vaug, values_out),
            (cosine, cos_out), (sine, sin_out),
        )
        return [locals_.make(a.at[b], d.at[b]) for a, d in pairs]

    outs = [block_outs(b) for b in range(3)]

    lane = lax.broadcasted_iota(jnp.int32, (1, HEAD_SIZE), 1)
    begin = jnp.full((1, HEAD_SIZE), float(nctx * block), f32)
    end = begin
    for label in range(NDOC):
        before = jnp.where(segments[...] < label, 1.0, 0.0)
        before = jnp.sum(before, axis=(0, 1), keepdims=True)
        begin = jnp.where(lane == label, before, begin)
        end = jnp.where(lane == label - 1, before, end)
    places[0:1, :] = begin
    places[1:2, :] = end
    table(0)
    vaug[:, :, :, 128:256] = jnp.ones((3, 2, block, 128), bf16)
    acc[...] = jnp.zeros(acc.shape, f32)
    locals_.wait(own_k)
    locals_.wait(own_v)
    wk_copy.wait()
    wv_copy.wait()
    wo_copy.start()
    to_across[0].wait_recv()
    on_to_side[0].start()

    @pl.when(c >= 1)
    def _():
        to_next[0].wait_recv()
        to_across[1].start()
        to_side[1].start()

        @pl.when(c < nctx - 1)
        def _():
            to_next[1].start()

    to_side[0].wait_recv()
    on_to_side[0].wait_recv()

    @pl.loop(0, 4)
    def _(n):
        project_kv(0, n)

    for copy in outs[0]:
        copy.start()

    @pl.when(c >= 1)
    def _():
        table(1)
        to_side[1].wait_recv()

        @pl.loop(0, 2)
        def _(n):
            project_kv(1, t ^ n)

    @pl.when(c >= 2)
    def _():
        table(2)

    locals_.wait(own_q)
    wq_copy.wait()
    wg_copy.start()

    @pl.when(c >= 1)
    def _():
        to_across[1].wait_recv()
        on_to_side[1].start()

        @pl.when(c < nctx - 1)
        def _():
            far_to_next.start()

        @pl.when(c >= 2)
        def _():
            to_next[1].wait_recv()
            to_side[2].start()

    c_over.start()

    @pl.loop(0, 4)
    def _(n):
        project_q(n)

    locals_.start(q_proj, q_out)
    locals_.start(wqkv, wqkv_out)

    @pl.loop(0, 6)
    def _(n):
        m = lax.rem(n, 3)
        unit(0, n // 3, (m + 1) // 2, m // 2, (m & 1) * -512)

    wo_copy.wait_recv()
    wo_on.start()
    wu_copy.start()

    @pl.when(c >= 1)
    def _():
        on_to_side[1].wait_recv()

        @pl.loop(2, 4)
        def _(n):
            project_kv(1, t ^ n)

        for copy in outs[1]:
            copy.start()

        @pl.loop(0, 8)
        def _(n):
            m = lax.rem(n, 4)
            unit(1, n // 4, m // 2, m & 1, None)

    wg_copy.wait_recv()
    wg_on.start()

    c_over.wait_recv()
    c_on.start()

    @pl.when(c >= 2)
    def _():
        far_to_next.wait_recv()
        on_to_side[2].start()
        to_side[2].wait_recv()
        on_to_side[2].wait_recv()

        @pl.loop(0, 4)
        def _(n):
            project_kv(2, n)

        for copy in outs[2]:
            copy.start()

        @pl.loop(0, 6)
        def _(n):
            m = lax.rem(n, 3)
            unit(2, n // 3, m // 2, (m + 1) // 2, None)

    for h in range(4):

        @pl.loop(0, 4)
        def _(r):
            at = pl.ds(pl.multiple_of(r * 256, 256), 256)
            total = acc[h, at, 128:256]
            value = acc[h, at, 0:128] / total
            acc[h, at, 0:128] = value
            shift = jnp.log(total) * -(HEAD_SIZE**0.5)
            top = shift.astype(bf16).astype(f32)
            mid = (shift - top).astype(bf16).astype(f32)
            lane = lax.broadcasted_iota(jnp.int32, shift.shape, 1)
            parts = jnp.where(lane == NDOC, top, 0.0)
            parts = jnp.where(lane == NDOC + 1, mid, parts)
            parts = jnp.where(lane == NDOC + 2, shift - top - mid, parts)
            qaug[h, at, 128:256] = qaug[h, at, 128:256] + parts.astype(bf16)
            low[h, at, :] = value.astype(bf16)

        lanes = slice(h * 128, h * 128 + 128)
        locals_.start(low.at[h], low_out.at[:, lanes])
        locals_.start(acc.at[h, :, 0:128], attended_out.at[:, lanes])
        locals_.start(qaug.at[h], query_out.at[h])

    locals_.start(gains, gains_out)
    locals_.wait(own_c)
    c_side.wait()
    c_on.wait()
    locals_.start(crows, crows_out)
    c_over.wait_send()
    to_across[0].wait_send()
    to_side[0].wait_send()
    on_to_side[0].wait_send()
    for copy in outs[0]:
        copy.wait()

    @pl.when(c < nctx - 1)
    def _():
        to_next[0].wait_send()

    for b in (1, 2):

        @pl.when(c >= b)
        def _():
            if b < 2:
                to_across[b].wait_send()
            to_side[b].wait_send()
            on_to_side[b].wait_send()
            for copy in outs[b]:
                copy.wait()

    @pl.when((c >= 1) & (c < nctx - 1))
    def _():
        to_next[1].wait_send()
        far_to_next.wait_send()

    wo_copy.wait_send()
    wo_on.wait()
    wg_copy.wait_send()
    wg_on.wait()
    wu_copy.wait()
    locals_.finish()


def forward_call(hidden, cotangent, gains, segments, rates, wq, wk, wv, wo, wg, wu):
    part, width = hidden.shape
    block = 4 * part
    f32, bf16 = jnp.float32, jnp.bfloat16
    shape = jax.ShapeDtypeStruct
    outs = (
        shape((8, width), f32),
        shape((3, block, width), bf16),
        shape((block, 512), f32),
        shape((3, block, 256), f32),
        shape((4, block, 256), bf16),
        shape((3, 2, block, 256), bf16),
        shape((3, 2, block, 256), bf16),
        shape((3, block, HEAD_SIZE), f32),
        shape((3, block, HEAD_SIZE), f32),
        shape((block, 512), f32),
        shape((block, 512), bf16),
        shape((width, 1024), bf16),
        shape((block, width), bf16),
        shape(wo.shape, bf16),
        shape(wg.shape, bf16),
        shape(wu.shape, bf16),
    )
    return pl.pallas_call(
        forward_kernel,
        name="forward",
        out_shape=outs,
        in_specs=[VMEM_SPEC] * 8 + [ANY_SPEC] * 6,
        out_specs=[ANY_SPEC] * len(outs),
        scratch_shapes=[
            pltpu.VMEM((8, width), f32),
            pltpu.VMEM((3, block, width), bf16),
            pltpu.VMEM((3, block, width), bf16),
            pltpu.VMEM((width, 1024), bf16),
            pltpu.VMEM((block, 512), f32),
            pltpu.VMEM((3, block, 256), f32),
            pltpu.VMEM((4, block, 256), bf16),
            pltpu.VMEM((3, 2, block, 256), bf16),
            pltpu.VMEM((3, 2, block, 256), bf16),
            pltpu.VMEM((3, block, HEAD_SIZE), f32),
            pltpu.VMEM((3, block, HEAD_SIZE), f32),
            pltpu.VMEM((4, block, 256), f32),
            pltpu.VMEM((4, block, 128), bf16),
            pltpu.VMEM((block, width), bf16),
            pltpu.VMEM((8, width), f32),
            pltpu.VMEM((8, width), f32),
            pltpu.VMEM((8, HEAD_SIZE), f32),
            pltpu.SemaphoreType.DMA((23,)),
            pltpu.SemaphoreType.DMA((23,)),
            pltpu.SemaphoreType.DMA((38,)),
        ],
        compiler_params=pltpu.CompilerParams(
            collective_id=0, has_side_effects=True, vmem_limit_bytes=58 << 20
        ),
    )(hidden, cotangent, *gains, segments, rates, wq, wk, wv, wo, wg, wu)


class Scatter:
    def __init__(self, links, bufs, side, across):
        self.bufs = bufs
        self.far = links.copy(bufs.at[0], bufs.at[3], side)
        self.over = links.copy(bufs.at[1], bufs.at[4], across)
        self.near = links.copy(bufs.at[2], bufs.at[5], side)

    def put_far(self, value):
        self.bufs[0] = value.astype(jnp.bfloat16)
        self.far.start()

    def put_over(self, value):
        self.far.wait_recv()
        self.bufs[1] = (value + self.bufs[3].astype(jnp.float32)).astype(jnp.bfloat16)
        self.over.start()

    def put_near(self, value):
        self.bufs[2] = value.astype(jnp.bfloat16)
        self.near.start()

    def total(self, value):
        self.near.wait_recv()
        self.over.wait_recv()
        return value + self.bufs[5].astype(jnp.float32) + self.bufs[4].astype(jnp.float32)

    def close(self):
        self.far.wait_send()
        self.over.wait_send()
        self.near.wait_send()


def mlp_kernel(
    low, hidden, gains, crows_in, wo_own, wo_got, wg_own, wg_got, wu_own, wu_got,
    wd,
    d_middle_out, gain_out, brow_out, own_out, give_out, parts_out, out_own_out,
    wo, wgf, wuf, wdf, mrows, act, dgate, dup, brow, kept, middle, bufs, parts, give, own, land,
    crows, result, send, recv, local,
):
    s, c, t = lax.axis_index(SHARD_AXIS), lax.axis_index(CTX_AXIS), lax.axis_index(TP_AXIS)
    part = hidden.shape[0]
    half = wd.shape[1]
    bf16, f32 = jnp.bfloat16, jnp.float32
    side, across = {TP_AXIS: t ^ 1}, {TP_AXIS: t ^ 2}
    mate, pair = {SHARD_AXIS: 1 - s}, {CTX_AXIS: c ^ 1}
    links, locals_ = Links(send, recv), Locals(local)

    def piece(owner):
        return pl.ds(pl.multiple_of(owner * part, part), part)

    mine = pl.ds(pl.multiple_of(s * half, half), half)
    theirs = pl.ds(pl.multiple_of((1 - s) * half, half), half)
    low_bit = c & 1

    def some(shard, count, size):
        return pl.ds(pl.multiple_of(shard * count + low_bit * size, size), size)

    quarter = half // 2
    third = wd.shape[0] // 2
    wu_at = some(1 - s, half, quarter)
    wu_on = links.copy(wu_got.at[some(0, 0, quarter), :], wuf.at[wu_at, :], pair)
    wd_copy = links.copy(
        wd.at[some(0, 0, third), :], wdf.at[some(0, 0, third), mine], mate
    )
    wd_got = wdf.at[some(0, 0, third), theirs]
    wd_on = links.copy(wd_got, wd_got, pair)
    wo_loads = [
        locals_.start(wo_own, wo.at[:, mine]),
        locals_.start(wo_got, wo.at[:, theirs]),
    ]
    enter([side, across, mate, pair])
    wu_on.start()
    wd_copy.start()
    own_weights = [
        locals_.start(wg_own, wgf.at[mine, :]),
        locals_.start(wg_got, wgf.at[theirs, :]),
        locals_.start(wu_own, wuf.at[mine, :]),
        locals_.start(wu_got.at[some(0, 0, quarter), :], wuf.at[wu_at, :]),
        locals_.start(wd, wdf.at[:, mine]),
        locals_.start(crows_in, crows),
    ]
    for copy in wo_loads:
        locals_.wait(copy)

    branch = Scatter(links, bufs.at[0], side, across)
    back = Scatter(links, bufs.at[1], side, across)

    def branch_part(owner):
        return flat_dot(low[piece(owner), :], wo[...])

    branch.put_far(branch_part(t ^ 3))
    branch.put_over(branch_part(t ^ 2))
    branch.put_near(branch_part(t ^ 1))
    middle[...] = hidden[...].astype(f32) + branch_part(t)
    wd_copy.wait_recv()
    wd_on.start()
    middle[...] = branch.total(middle[...])
    m = middle[...]
    scale = lax.rsqrt(jnp.mean(m * m, axis=-1, keepdims=True) + norm_eps)
    gain = gains[1:2, :]
    mrows[piece(t), :] = (m * scale * gain).astype(bf16)
    here, there = mrows.at[piece(t), :], mrows.at[piece(t ^ 2), :]
    m_over, m_near = links.copy(here, here, across), links.copy(here, here, side)
    m_on = links.copy(there, there, side)
    m_over.start()
    m_near.start()
    for copy in own_weights:
        locals_.wait(copy)
    wu_on.wait_recv()
    wd_on.wait_recv()

    def mlp(owner):
        at = piece(owner)
        rows = mrows[at, :]
        gate = flat_dot(rows, wgf[...])
        upward = flat_dot(rows, wuf[...])
        d_act = last_dot(crows[at, :], wdf[...])
        sig = 1.0 / (1.0 + jnp.exp(-gate))
        silu = gate * sig
        act[at, :] = (silu * upward).astype(bf16)
        dup[at, :] = (d_act * silu).astype(bf16)
        dgate[at, :] = (d_act * upward * sig * (1.0 + gate * (1.0 - sig))).astype(bf16)

    def out_part(owner):
        return flat_dot(act[piece(owner), :], wdf[...])

    def back_part(owner):
        at = piece(owner)
        return last_dot(dgate[at, :], wgf[...]) + last_dot(dup[at, :], wuf[...])

    m_near.wait_recv()

    @pl.loop(0, 4)
    def _(n):
        @pl.when(n == 2)
        def _():
            m_over.wait_recv()
            m_on.start()
            m_on.wait_recv()

        owner = t ^ jnp.where(n < 2, n, 5 - n)
        mlp(owner)
        value = back_part(owner)

        @pl.when(n == 0)
        def _():
            kept[0] = value

        pl.when(n == 1)(lambda: back.put_near(value))
        pl.when(n == 2)(lambda: back.put_far(value))
        pl.when(n == 3)(lambda: back.put_over(value))

    to_mate = [links.copy(give.at[k], land.at[k], mate) for k in range(READY)]

    def lanes(n):
        return pl.ds(pl.multiple_of(n * 256, 256), 256)

    def down_chunk(ref, n, columns):
        ref[n] = first_dot(act[:, lanes(n)], crows[:, columns]).astype(bf16)

    def wide_chunk(ref, k, grads, n, columns):
        got = first_dot(mrows[:, columns], grads[:, lanes(n)]).astype(bf16)
        ref[k + n, :, 0:256] = got[0:256]
        ref[k + n, :, 256:512] = got[256:512]

    @pl.loop(0, 3)
    def _(n):
        down_chunk(give, n, theirs)

    for copy in to_mate:
        copy.start()

    @pl.loop(0, 3)
    def _(n):
        down_chunk(own, n, mine)
        for k, grads in ((3, dgate), (6, dup)):
            wide_chunk(give, k, grads, n, theirs)
            wide_chunk(own, k, grads, n, mine)

    @pl.loop(0, 4)
    def _(n):
        value = out_part(t ^ (3 - n))

        @pl.when(n < 3)
        def _():
            parts[n] = value.astype(bf16)

        @pl.when(n == 3)
        def _():
            kept[1] = value + middle[...]

    locals_.start(kept.at[1], out_own_out)
    locals_.start(parts, parts_out)
    locals_.start(give.at[READY:FROM_MLP], give_out)
    locals_.start(own.at[READY:FROM_MLP], own_out.at[READY:FROM_MLP])

    d_mlp = back.total(kept[0])
    m = middle[...]
    scale = lax.rsqrt(jnp.mean(m * m, axis=-1, keepdims=True) + norm_eps)
    scaled = d_mlp * gain
    inner = jnp.mean(scaled * m, axis=-1, keepdims=True)
    d_middle = (
        crows[piece(t), :].astype(f32) + scale * scaled - m * (scale * scale * scale) * inner
    )
    kept[0] = d_middle
    gain_grad = jnp.sum(d_mlp * m * scale, axis=0, keepdims=True)
    brow[...] = d_middle.astype(bf16)
    locals_.start(brow, brow_out)
    locals_.start(kept.at[0], d_middle_out)
    result[...] = jnp.broadcast_to(gain_grad, (8, gain_grad.shape[1]))
    locals_.start(result, gain_out)

    for k in range(READY):
        to_mate[k].wait_recv()
        own[k] = own[k] + land[k]
    locals_.start(own.at[0:READY], own_out.at[0:READY])
    for k in range(READY):
        to_mate[k].wait_send()
    wu_on.wait_send()
    wd_copy.wait_send()
    wd_on.wait_send()
    branch.close()
    back.close()
    for copy in (m_over, m_near, m_on):
        copy.wait_send()
    locals_.finish()


def mlp_call(vmem_args, any_args):
    low, hidden, gains = vmem_args
    wo, wd = any_args[1], any_args[-1]
    part, width = hidden.shape
    block = 4 * part
    units = wd.shape[0]
    f32, bf16 = jnp.float32, jnp.bfloat16
    shape = jax.ShapeDtypeStruct
    outs = (
        shape((part, width), f32),
        shape((8, width), f32),
        shape((part, width), bf16),
        shape((FROM_MLP, 256, 512), bf16),
        shape((FROM_MLP - READY, 256, 512), bf16),
        shape((3, part, width), bf16),
        shape((part, width), f32),
    )
    return pl.pallas_call(
        mlp_kernel,
        name="mlp",
        out_shape=outs,
        in_specs=[VMEM_SPEC] * 3 + [ANY_SPEC] * 8,
        out_specs=[ANY_SPEC] * len(outs),
        scratch_shapes=[
            pltpu.VMEM((wo.shape[0], width), bf16),
            pltpu.VMEM((width, units), bf16),
            pltpu.VMEM((width, units), bf16),
            pltpu.VMEM((units, width), bf16),
            pltpu.VMEM((block, width), bf16),
            pltpu.VMEM((block, units), bf16),
            pltpu.VMEM((block, units), bf16),
            pltpu.VMEM((block, units), bf16),
            pltpu.VMEM((part, width), bf16),
            pltpu.VMEM((2, part, width), f32),
            pltpu.VMEM((part, width), f32),
            pltpu.VMEM((2, 6, part, width), bf16),
            pltpu.VMEM((3, part, width), bf16),
            pltpu.VMEM((FROM_MLP, 256, 512), bf16),
            pltpu.VMEM((FROM_MLP, 256, 512), bf16),
            pltpu.VMEM((READY, 256, 512), bf16),
            pltpu.VMEM((block, width), bf16),
            pltpu.VMEM((8, width), f32),
            pltpu.SemaphoreType.DMA((12 + READY,)),
            pltpu.SemaphoreType.DMA((12 + READY,)),
            pltpu.SemaphoreType.DMA((16,)),
        ],
        compiler_params=pltpu.CompilerParams(
            collective_id=1, has_side_effects=True, vmem_limit_bytes=58 << 20
        ),
    )(*vmem_args, *any_args)


class Pump:
    def __init__(self, refs, sems, mate, near, opposite, outer, out, first_mate):
        self.own, self.mated, self.landed, self.summed = refs
        self.send, self.recv, self.local = sems
        self.mate, self.near, self.opposite, self.outer = mate, near, opposite, outer
        self.inner = jnp.logical_not(outer)
        self.out, self.first_mate = out, first_mate

    def remote(self, stage, u, src, dst, device):
        return pltpu.make_async_remote_copy(
            src_ref=src, dst_ref=dst, send_sem=self.send.at[stage * UNITS + u],
            recv_sem=self.recv.at[stage * UNITS + u], device_id=device, device_id_type=MESH_ID,
        )

    def to_mate(self, u, src):
        return self.remote(0, u, src, self.mated.at[u - self.first_mate], self.mate)

    def inward(self, u):
        return self.remote(1, u, self.own.at[u], self.landed.at[u], self.near)

    def cross(self, u):
        return self.remote(2, u, self.landed.at[u], self.summed.at[u], self.opposite)

    def outward(self, u):
        return self.remote(3, u, self.summed.at[u], self.landed.at[u], self.near)

    def write(self, u, ref):
        return pltpu.make_async_copy(ref.at[u], self.out.at[u], self.local.at[u])

    def run(self, condition, body):
        if isinstance(condition, bool):
            if condition:
                body()
        else:
            pl.when(condition)(body)

    def first(self, u):
        def bring():
            self.to_mate(u, self.own.at[u]).wait_recv()
            self.own[u] = self.own[u] + self.mated[u - self.first_mate]

        self.run(u >= self.first_mate, bring)
        pl.when(self.outer)(lambda: self.inward(u).start())

    def second(self, u):
        @pl.when(self.inner)
        def _():
            self.inward(u).wait_recv()
            self.landed[u] = self.own[u] + self.landed[u]
            self.cross(u).start()

    def third(self, u):
        @pl.when(self.inner)
        def _():
            self.cross(u).wait_recv()
            self.summed[u] = self.landed[u] + self.summed[u]
            self.outward(u).start()
            self.write(u, self.summed).start()

    def fourth(self, u):
        @pl.when(self.outer)
        def _():
            self.outward(u).wait_recv()
            self.write(u, self.landed).start()

    def slot(self, k):
        for u in (2 * k, 2 * k + 1):
            self.run(k < LATE // 2, lambda: self.first(u))
            self.run(k >= 2, lambda: self.second(u - 4))
            self.run(k >= 4, lambda: self.third(u - 8))

    def close(self):
        @pl.loop(0, UNITS)
        def _(u):
            pl.when(self.outer)(lambda: self.inward(u).wait_send())

            @pl.when(self.inner)
            def _():
                self.cross(u).wait_send()
                self.outward(u).wait_send()

            self.write(u, self.summed).wait()


def backward_kernel(
    gains, mlp_gain_grad, query_in, hidden, brow_in, low, attended, wo_own, wo_got, d_middle,
    q_proj_in, wqkv_in, own_in, give, parts, out_own, keys, values, k_proj, cosine, sine, rows,
    hidden_out, hidden_grad, gains_out, sums_out,
    kbuf, vbuf, kpbuf, cosbuf, sinbuf, rowbuf, dq, dk, dv, dkv, dqp, gkv, kept, bufs,
    own, mated, landed, summed, late_give, far_land, mid_land, out_buf,
    query, dout, q_proj, wqkv,
    gsum, gland, send, recv, pump_send, pump_recv, pump_local, local, blocksem,
):
    s, c, t = lax.axis_index(SHARD_AXIS), lax.axis_index(CTX_AXIS), lax.axis_index(TP_AXIS)
    nctx = lax.axis_size(CTX_AXIS)
    part = hidden.shape[0]
    half = rows.shape[2] // 2
    f32, bf16 = jnp.float32, jnp.bfloat16
    side, across, mate = {TP_AXIS: t ^ 1}, {TP_AXIS: t ^ 2}, {SHARD_AXIS: 1 - s}
    near, opposite = {CTX_AXIS: c ^ 1}, {CTX_AXIS: c ^ 3}
    previous = {CTX_AXIS: lax.rem(c + nctx - 1, nctx)}
    outer = (c == 0) | (c == nctx - 1)
    links, locals_ = Links(send, recv), Locals(local)
    scale = HEAD_SIZE ** (-0.5)
    pump = Pump(
        (own, mated, landed, summed), (pump_send, pump_recv, pump_local),
        mate, near, opposite, outer, sums_out, MATED,
    )

    def piece(owner):
        return pl.ds(pl.multiple_of(owner * part, part), part)

    mine = pl.ds(pl.multiple_of(s * half, half), half)
    theirs = pl.ds(pl.multiple_of((1 - s) * half, half), half)

    def half_at(ref_shard, n, size):
        return pl.ds(pl.multiple_of(ref_shard * half + n * size, size), size)

    def block_copies(b):
        slot = b & 1
        pairs = (
            (keys.at[b], kbuf.at[slot]), (values.at[b], vbuf.at[slot]),
        )
        return [
            pltpu.make_async_copy(a, d, blocksem.at[6 * b + n]) for n, (a, d) in enumerate(pairs)
        ]

    def row_copies(b):
        pairs = (
            (k_proj.at[b], kpbuf), (cosine.at[b], cosbuf), (sine.at[b], sinbuf),
            (rows.at[b], rowbuf),
        )
        return [
            pltpu.make_async_copy(a, d, blocksem.at[6 * b + 2 + n])
            for n, (a, d) in enumerate(pairs)
        ]

    def row_fetch(b):
        for copy in row_copies(b):
            copy.start()

    def fetch(b):
        for copy in block_copies(b):
            copy.start()

    def fetched(b):
        for copy in block_copies(b):
            copy.wait()

    brow_load = locals_.start(brow_in, rowbuf.at[piece(t), :])
    loads = [locals_.start(own_in.at[0:MATED], own.at[0:MATED])]
    own_load = locals_.start(own_in.at[MATED:EARLY], own.at[MATED:EARLY])
    wo_loads = []
    for j in range(2):
        at = slice(j * 256, j * 256 + 256)
        wo_loads.append(locals_.start(wo_own.at[at, :], bufs.at[1, j, :, mine]))
        wo_loads.append(locals_.start(wo_got.at[at, :], bufs.at[1, j, :, theirs]))
    for h in range(4):
        wo_loads.append(locals_.start(attended.at[:, h * 128 : h * 128 + 128], dq.at[h]))
    wo_loads.append(locals_.start(low, dkv))
    out_loads = [locals_.start(parts.at[1], out_buf.at[0]), locals_.start(out_own, kept.at[1])]

    @pl.when(c >= 2)
    def _():
        fetch(2)

    @pl.when(c >= 1)
    def _():
        fetch(1)

    @pl.when(c <= 1)
    def _():
        fetch(0)

    late_loads = [
        locals_.start(query_in, query), locals_.start(q_proj_in, q_proj),
        locals_.start(wqkv_in, wqkv),
    ]
    enter([side, across, mate, near, opposite])

    def send_early(first, count):
        for u in range(first, min(first + count, EARLY)):
            pump.to_mate(u, give.at[u - MATED]).start()

    here, there = rowbuf.at[piece(t), :], rowbuf.at[piece(t ^ 2), :]
    b_over, b_near = links.copy(here, here, across), links.copy(here, here, side)
    b_on = links.copy(there, there, side)
    locals_.wait(brow_load)
    b_over.start()
    b_near.start()
    send_early(MATED, 4)
    out_far = links.copy(parts.at[0], out_buf.at[1], side)
    out_over = links.copy(out_buf.at[0], out_buf.at[2], across)
    out_near = links.copy(parts.at[2], out_buf.at[3], side)
    out_far.start()
    out_near.start()
    scatters = [
        Scatter(links, bufs.at[0], side, across),
        Scatter(links, bufs.at[1], side, across),
        Scatter(links, bufs.at[0], side, across),
    ]
    far_copy = links.copy(out_buf.at[0], far_land, previous)
    mid_copy = links.copy(out_buf.at[1], mid_land, previous)
    for copy in loads:
        locals_.wait(copy)
    pump.slot(0)
    pump.slot(1)
    send_early(MATED + 4, 4)
    locals_.wait(own_load)
    gkv[...] = jnp.zeros(gkv.shape, f32)
    gsum[...] = jnp.zeros(gsum.shape, f32)
    gsum[1:2, :] = mlp_gain_grad[0:1, :]
    q_gain = gains[2:3, 0:HEAD_SIZE]
    k_gain = gains[3:4, 0:HEAD_SIZE]
    def attended_back(owner):
        at = piece(owner)
        for j in range(2):
            got = last_dot(rowbuf[at, :], bufs[1, j]).astype(bf16)
            for hh in range(2):
                h = 2 * j + hh
                head = got[:, hh * 128 : hh * 128 + 128]
                delta = -jnp.sum(head.astype(f32) * dq[h, at, :], axis=1, keepdims=True)
                top = delta.astype(bf16).astype(f32)
                lane = lax.broadcasted_iota(jnp.int32, (part, HEAD_SIZE), 1)
                extra = jnp.where(lane == 0, top, jnp.where(lane == 1, delta - top, 0.0))
                dout[h, at, 0:128] = head
                dout[h, at, 128:256] = extra.astype(bf16)

    for copy in wo_loads:
        locals_.wait(copy)
    b_near.wait_recv()

    @pl.loop(0, 2)
    def _(n):
        attended_back(t ^ n)

    for copy in out_loads:
        locals_.wait(copy)
    out_far.wait_recv()
    out_buf[0] = out_buf[0] + out_buf[1]
    b_over.wait_recv()
    b_on.start()
    out_over.start()
    b_on.wait_recv()

    @pl.loop(2, 4)
    def _(n):
        attended_back(t ^ n)

    for copy in (b_over, b_near, b_on):
        copy.wait_send()
    @pl.loop(0, 2)
    def _(n):
        at = pl.ds(pl.multiple_of(n * 256, 256), 256)
        for columns, target, first in ((theirs, late_give, 0), (mine, own, EARLY)):
            got = first_dot(dkv[:, at], rowbuf[:, columns]).astype(bf16)
            for e in range(2):
                target[first + 2 * n + e] = got[e * 128 : e * 128 + 128]

    for n in range(4):
        pump.to_mate(EARLY + n, late_give.at[n]).start()
    dq[...] = jnp.zeros(dq.shape, f32)
    for b in range(3):
        pl.when((c == b) if b < 2 else (c >= b))(functools.partial(row_fetch, b))
    pump.slot(2)
    send_early(MATED + 8, 2)

    def tile(b, g, r, kc, bound):
        slot = b & 1
        q_at = pl.ds(pl.multiple_of(r * 512, 512), 512)
        k_at = pl.ds(pl.multiple_of(kc * 512, 512), 512)
        kk, vv = kbuf[slot, g, k_at, :], vbuf[slot, g, k_at, :]
        dv_new, dk_new = [], []
        for hh in range(2):
            h = 2 * g + hh
            qq, do = query[h, q_at, :], dout[h, q_at, :]
            p = jnp.exp2(last_dot(qq, kk) * SCORE_STEP)
            if bound is not None:
                ahead = lax.broadcasted_iota(jnp.int32, p.shape, 0) - lax.broadcasted_iota(
                    jnp.int32, p.shape, 1
                )
                p = jnp.where(ahead >= bound, p, 0.0)
            ds = (p * last_dot(do, vv)).astype(bf16)
            dv_new.append(first_dot(do[:, 0:HEAD_SIZE], p.astype(bf16)))
            dk_new.append(first_dot(qq[:, 0:HEAD_SIZE], ds))
            dq[h, q_at, :] += flat_dot(ds, kk[:, 0:HEAD_SIZE])
        dv[g, :, k_at] += dv_new[0] + dv_new[1]
        dk[g, :, k_at] += dk_new[0] + dk_new[1]

    def clear():
        dk[...] = jnp.zeros(dk.shape, f32)
        dv[...] = jnp.zeros(dv.shape, f32)

    def norm_back(grad, u, gain, cos, sin, row):
        turned = grad * cos - pltpu.roll(grad, HEAD_SIZE // 2, 1) * sin
        r = lax.rsqrt(jnp.mean(u * u, axis=-1, keepdims=True) + norm_eps)
        gsum[row : row + 1, 0:HEAD_SIZE] += jnp.sum(turned * u * r, axis=0, keepdims=True)
        scaled = turned * gain
        inner = jnp.mean(scaled * u, axis=-1, keepdims=True)
        return (r * scaled - u * (r * r * r) * inner).astype(bf16)

    def finish_kv(b):
        for copy in row_copies(b)[:3]:
            copy.wait()

        @pl.loop(0, 4)
        def _(n):
            at = piece(n)
            cos, sin = cosbuf[at, :], sinbuf[at, :]
            for g in range(2):
                lanes = slice(g * 128, g * 128 + 128)
                u = kpbuf[at, lanes]
                dkv[at, lanes] = norm_back(dk[g, :, at].T * scale, u, k_gain, cos, sin, 3)
                dkv[at, 256 + g * 128 : 384 + g * 128] = dv[g, :, at].T.astype(bf16)

        row_copies(b)[3].wait()

        gkv[...] += first_dot(rowbuf[...], dkv[...])

    def kv_part(owner):
        return last_dot(dkv[piece(owner), :], wqkv[:, 512:1024])

    def all_part(owner):
        return kv_part(owner) + last_dot(dqp[piece(owner), :], wqkv[:, 0:512])

    def scatter(which, slot, partial):
        @pl.loop(0, 4)
        def _(n):
            value = partial(t ^ (3 - n))
            pl.when(n == 0)(lambda: which.put_far(value))
            pl.when(n == 1)(lambda: which.put_over(value))
            pl.when(n == 2)(lambda: which.put_near(value))

            @pl.when(n == 3)
            def _():
                kept[slot] = value

    for copy in late_loads:
        locals_.wait(copy)

    @pl.when(c >= 2)
    def _():
        fetched(2)
        clear()

    @pl.loop(0, 6)
    def _(n):
        m = lax.rem(n, 3)

        @pl.when(c >= 2)
        def _():
            tile(2, n // 3, m // 2, (m + 1) // 2, None)

        @pl.when((n & 1) == 1)
        def _():
            pump.slot(3 + n // 2)

        @pl.when(m == 2)
        def _():
            for e in range(2):
                u = MATED + 10 + 2 * (n // 3) + e
                pump.to_mate(u, give.at[u - MATED]).start()

    @pl.when(c >= 2)
    def _():
        finish_kv(2)
        fetch(0)
        row_fetch(1)
        scatter(scatters[2], 0, kv_part)

    out_near.wait_recv()
    out_over.wait_recv()
    out_buf[3] = (kept[1] + out_buf[2].astype(f32) + out_buf[3].astype(f32)).astype(bf16)
    locals_.start(out_buf.at[3], hidden_out)
    out_far.wait_send()
    out_over.wait_send()
    out_near.wait_send()

    @pl.when(c >= 1)
    def _():
        fetched(1)
        clear()

    @pl.loop(0, 8)
    def _(n):
        m = lax.rem(n, 4)

        @pl.when(c >= 1)
        def _():
            tile(1, n // 4, m // 2, m & 1, None)

        @pl.when((n & 1) == 1)
        def _():
            pump.slot(6 + n // 2)

    @pl.when(c >= 2)
    def _():
        out_buf[0] = scatters[2].total(kept[0]).astype(bf16)
        far_copy.start()
        scatters[2].close()

    @pl.when(c >= 1)
    def _():
        finish_kv(1)
        row_fetch(0)

    @pl.when(c >= 1)
    def _():
        scatter(scatters[1], 1, kv_part)

    pump.slot(10)
    fetched(0)
    clear()

    @pl.loop(0, 6)
    def _(n):
        m = lax.rem(n, 3)
        tile(0, n // 3, (m + 1) // 2, m // 2, (m & 1) * -512)

        @pl.when(n == 3)
        def _():
            pump.slot(11)

    finish_kv(0)

    @pl.loop(0, 4)
    def _(n):
        at = piece(n)
        cos, sin = cosbuf[at, :], sinbuf[at, :]
        for h in range(4):
            lanes = slice(h * 128, h * 128 + 128)
            u = q_proj[at, lanes]
            dqp[at, lanes] = norm_back(dq[h, at, :] * scale, u, q_gain, cos, sin, 2)

    for n in range(4):
        late_give[4 + n] = gkv[half_at(1 - s, n, 128), :].astype(bf16)
        pump.to_mate(LATE + n, late_give.at[4 + n]).start()
    for n in range(2):
        got = first_dot(rowbuf[:, half_at(1 - s, n, 256)], dqp[...]).astype(bf16)
        for e in range(2):
            late_give[8 + 2 * n + e] = got[e * 128 : e * 128 + 128]
            pump.to_mate(LATE + 4 + 2 * n + e, late_give.at[8 + 2 * n + e]).start()
    pump.slot(12)

    @pl.when((c >= 1) & (c < nctx - 1))
    def _():
        far_copy.wait_recv()
        kept[1] += far_land[...].astype(f32)

    @pl.when(c >= 1)
    def _():
        out_buf[1] = scatters[1].total(kept[1]).astype(bf16)
        mid_copy.start()
        scatters[1].close()

    base = locals_.start(d_middle, kept.at[1])
    hidden_load = locals_.start(hidden, out_buf.at[2])
    scatter(scatters[0], 0, all_part)
    for n in range(2):
        rows_of = gkv[half_at(s, n, 256), :].astype(bf16)
        got = first_dot(rowbuf[:, half_at(s, n, 256)], dqp[...]).astype(bf16)
        for e in range(2):
            at = slice(e * 128, e * 128 + 128)
            own[LATE + 2 * n + e] = rows_of[at]
            own[LATE + 4 + 2 * n + e] = got[at]
    pump.third(LATE - 4)
    pump.third(LATE - 3)
    pl.loop(0, LATE - 8)(pump.fourth)

    def finish_rows():
        @pl.when(c < nctx - 1)
        def _():
            mid_copy.wait_recv()
            kept[0] += mid_land[...].astype(f32)

        kept[0] = scatters[0].total(kept[0])
        locals_.wait(hidden_load)
        locals_.wait(base)
        x = out_buf[2].astype(f32)
        r = lax.rsqrt(jnp.mean(x * x, axis=-1, keepdims=True) + norm_eps)
        d_in = kept[0]
        gsum[0:1, :] = jnp.sum(d_in * x * r, axis=0, keepdims=True)
        scaled = d_in * gains[0:1, :]
        inner = jnp.mean(scaled * x, axis=-1, keepdims=True)
        kept[1] += r * scaled - x * (r * r * r) * inner
        locals_.start(kept.at[1], hidden_grad)

    swaps = [
        links.copy(gsum, gland.at[n], device)
        for n, device in enumerate((side, across, mate, near, opposite))
    ]

    def swap(n):
        if n > 0:
            swaps[n - 1].wait()
            gsum[...] += gland[n - 1]
        if n < 5:
            swaps[n].start()

    for n, u in enumerate(range(LATE, UNITS)):
        pump.first(u)
        if n >= 1:
            pump.second(u - 1)
        pump.third(u - 2)
        if n == 3:
            finish_rows()
        if n >= 3:
            swap(n - 3)
    pump.second(UNITS - 1)
    pump.third(UNITS - 2)
    swap(8 - 3)
    pump.third(UNITS - 1)
    for n in range(9 - 3, 6):
        swap(n)
    locals_.start(gsum, gains_out)
    scatters[0].close()

    @pl.when(c >= 2)
    def _():
        far_copy.wait_send()

    @pl.when(c >= 1)
    def _():
        mid_copy.wait_send()

    @pl.loop(MATED, EARLY)
    def _(u):
        pump.to_mate(u, give.at[u - MATED]).wait_send()

    @pl.loop(EARLY, UNITS)
    def _(u):
        pump.to_mate(u, late_give.at[u - EARLY]).wait_send()

    pl.loop(LATE - 8, UNITS)(pump.fourth)
    pump.close()
    locals_.finish()


def backward_call(vmem_args, any_args):
    hidden = any_args[1]
    part, width = hidden.shape
    block = 4 * part
    f32, bf16 = jnp.float32, jnp.bfloat16
    shape = jax.ShapeDtypeStruct
    outs = (
        shape((part, width), bf16),
        shape((part, width), f32),
        shape((8, width), f32),
        shape((UNITS, 128, 512), bf16),
    )
    tile = pltpu.VMEM((part, width), bf16)
    units = pltpu.VMEM((UNITS, 128, 512), bf16)
    return pl.pallas_call(
        backward_kernel,
        name="backward",
        out_shape=outs,
        in_specs=[VMEM_SPEC] * 2 + [ANY_SPEC] * len(any_args),
        out_specs=[ANY_SPEC] * len(outs),
        scratch_shapes=[
            pltpu.VMEM((2, 2, block, 256), bf16),
            pltpu.VMEM((2, 2, block, 256), bf16),
            pltpu.VMEM((block, 256), f32),
            pltpu.VMEM((block, HEAD_SIZE), f32),
            pltpu.VMEM((block, HEAD_SIZE), f32),
            pltpu.VMEM((block, width), bf16),
            pltpu.VMEM((4, block, HEAD_SIZE), f32),
            pltpu.VMEM((2, HEAD_SIZE, block), f32),
            pltpu.VMEM((2, HEAD_SIZE, block), f32),
            pltpu.VMEM((block, 512), bf16),
            pltpu.VMEM((block, 512), bf16),
            pltpu.VMEM((width, 512), f32),
            pltpu.VMEM((2, part, width), f32),
            pltpu.VMEM((2, 6, part, width), bf16),
            units,
            pltpu.VMEM((UNITS - MATED, 128, 512), bf16),
            units,
            units,
            pltpu.VMEM((UNITS - EARLY, 128, 512), bf16),
            tile, tile,
            pltpu.VMEM((4, part, width), bf16),
            pltpu.VMEM((4, block, 256), bf16),
            pltpu.VMEM((4, block, 256), bf16),
            pltpu.VMEM((block, 512), f32),
            pltpu.VMEM((width, 1024), bf16),
            pltpu.VMEM((8, width), f32),
            pltpu.VMEM((5, 8, width), f32),
            pltpu.SemaphoreType.DMA((22,)),
            pltpu.SemaphoreType.DMA((22,)),
            pltpu.SemaphoreType.DMA((4 * UNITS,)),
            pltpu.SemaphoreType.DMA((4 * UNITS,)),
            pltpu.SemaphoreType.DMA((UNITS,)),
            pltpu.SemaphoreType.DMA((22,)),
            pltpu.SemaphoreType.DMA((18,)),
        ],
        compiler_params=pltpu.CompilerParams(
            collective_id=2, has_side_effects=True, vmem_limit_bytes=60 << 20
        ),
    )(*vmem_args, *any_args)


def result_kernel(
    chunks_in, gains, grad_in, hidden_in,
    grad_out, hidden_out, attn, wq, wk, wv, q_gain, k_gain, wo, mlp, wg, wu, wd,
    buf, q, k, v, o, gate, up, down, grad, hidden, inside, outside,
):
    shard = lax.axis_index(SHARD_AXIS)
    count = buf.shape[0]
    whole = [
        pltpu.make_async_copy(grad_in, grad, inside.at[count]),
        pltpu.make_async_copy(hidden_in, hidden, inside.at[count + 1]),
    ]
    loads = [pltpu.make_async_copy(chunks_in.at[n], buf.at[n], inside.at[n]) for n in range(count)]
    for copy in whole + loads:
        copy.start()
    stores = []

    def put(n, ref, out, row, lanes):
        at = (slice(row, row + 256), lanes)
        stores.append(pltpu.make_async_copy(ref.at[at], out.at[at], outside.at[len(stores)]))
        stores[-1].start()

    for copy in whole:
        copy.wait()
    for n, (ref, out) in enumerate(((grad, grad_out), (hidden, hidden_out))):
        whole[n] = pltpu.make_async_copy(ref, out, outside.at[count + n])
        whole[n].start()
    for n in range(count):
        loads[n].wait()
        values = buf[n].astype(jnp.float32)
        every = slice(0, 512)
        if n < 3:
            down[n * 256 : n * 256 + 256, :] = values
            put(n, down, wd, n * 256, every)
        elif n < 9:
            ref, out, j = (gate, wg, n - 3) if n < 6 else (up, wu, n - 6)
            lanes = slice(j * 256, j * 256 + 256)
            ref[0:256, lanes] = values[:, 0:256]
            ref[256:512, lanes] = values[:, 256:512]
            at = (slice(0, 512), lanes)
            stores.append(pltpu.make_async_copy(ref.at[at], out.at[at], outside.at[len(stores)]))
            stores[-1].start()
        elif n < 11:
            o[(n - 9) * 256 : (n - 8) * 256, :] = values
            put(n, o, wo, (n - 9) * 256, every)
        elif n < 13:
            row = (n - 11) * 256
            k[row : row + 256, :] = values[:, 0:256]
            v[row : row + 256, :] = values[:, 256:512]
        else:
            q[(n - 13) * 256 : (n - 12) * 256, :] = values
            put(n, q, wq, (n - 13) * 256, every)
    for ref, out in ((k, wk), (v, wv)):
        stores.append(pltpu.make_async_copy(ref, out, outside.at[len(stores)]))
        stores[-1].start()
    wide, small = attn.shape[1], q_gain.shape[1]
    first = shard == 0
    attn[...] = jnp.where(first, gains[0:1, 0:wide], gains[0:1, wide : 2 * wide])
    mlp[...] = jnp.where(first, gains[1:2, 0:wide], gains[1:2, wide : 2 * wide])
    q_gain[...] = jnp.where(first, gains[2:3, 0:small], gains[2:3, small : 2 * small])
    k_gain[...] = jnp.where(first, gains[3:4, 0:small], gains[3:4, small : 2 * small])
    for copy in stores + whole:
        copy.wait()


def result_call(chunks, gains, grad_hidden, out_hidden):
    part, width = grad_hidden.shape
    f32 = jnp.float32
    shape = jax.ShapeDtypeStruct
    half = width // 2
    q, k, v, o = (half, 512), (half, 256), (half, 256), (512, half)
    gate, up, down = (half, 768), (half, 768), (768, half)
    sizes = [q, k, v, (1, 64), (1, 64), o, (1, half), gate, up, down]
    outs = [shape((part, width), f32), shape((part, width), out_hidden.dtype), shape((1, half), f32)]
    outs += [shape(z, f32) for z in sizes]
    specs = [ANY_SPEC] * 2 + [VMEM_SPEC] + [ANY_SPEC] * 3 + [VMEM_SPEC] * 2 + [ANY_SPEC, VMEM_SPEC]
    return pl.pallas_call(
        result_kernel,
        name="result",
        out_shape=outs,
        in_specs=[ANY_SPEC, VMEM_SPEC, ANY_SPEC, ANY_SPEC],
        out_specs=specs + [ANY_SPEC] * 3,
        scratch_shapes=[pltpu.VMEM((CHUNKS, 256, 512), jnp.bfloat16)]
        + [pltpu.VMEM(z, f32) for z in (q, k, v, o, gate, up, down)]
        + [pltpu.VMEM((part, width), f32), pltpu.VMEM((part, width), out_hidden.dtype)]
        + [pltpu.SemaphoreType.DMA((CHUNKS + 2,)), pltpu.SemaphoreType.DMA((CHUNKS + 2,))],
        compiler_params=pltpu.CompilerParams(vmem_limit_bytes=60 << 20),
    )(chunks, gains, grad_hidden, out_hidden)


def fast_device(
    hidden,
    segments,
    cotangent,
    attn_gain,
    w_query,
    key_weight_matrix,
    value_weight_matrix,
    query_gain,
    key_gain,
    mixer_exit_coefficients,
    mlp_gain,
    w_gate,
    w_up,
    w_down,
):
    gains_own = (attn_gain, mlp_gain, query_gain, key_gain)
    exponents = 2.0 * (np.arange(HEAD_SIZE) % (HEAD_SIZE // 2)) / HEAD_SIZE
    rates = np.power(rope_base, -exponents).astype(np.float32)[None]
    labels = segments.reshape(-1, HEAD_SIZE)
    (gains, rows, q_proj, k_proj, query, keys, values, cosine, sine, attended, low, wqkv, crows,
     wo_got, wg_got, wu_got) = forward_call(
        hidden[0], cotangent[0], gains_own, labels, jnp.asarray(rates), w_query, key_weight_matrix,
        value_weight_matrix, mixer_exit_coefficients, w_gate, w_up,
    )
    def units(chunks, count):
        return chunks.reshape(count, 128, 512)

    d_middle, mlp_gain_grad, brow, own, give, parts, out_own = mlp_call(
        (low, hidden[0], gains),
        (crows, mixer_exit_coefficients, wo_got, w_gate, wg_got, w_up, wu_got, w_down),
    )
    out_hidden, grad_hidden, sums, chunks = backward_call(
        (gains, mlp_gain_grad),
        (query, hidden[0], brow, low, attended, mixer_exit_coefficients, wo_got, d_middle, q_proj, wqkv, units(own, EARLY), units(give, EARLY - MATED),
         parts, out_own, keys, values, k_proj, cosine, sine, rows),
    )
    (grad_hidden, out_hidden, attn, wq, wk, wv, q_gain, k_gain, wo, mlp, wg, wu, wd) = result_call(
        chunks.reshape(CHUNKS, 256, 512), sums, grad_hidden, out_hidden
    )
    return (
        out_hidden[None], grad_hidden[None], attn[0], wq, wk, wv, q_gain[0], k_gain[0], wo, mlp[0],
        wg, wu, wd,
    )


def per_device(
    hidden,
    segments,
    cotangent,
    attn_gain,
    w_query,
    key_weight_matrix,
    value_weight_matrix,
    query_gain,
    key_gain,
    mixer_exit_coefficients,
    mlp_gain,
    w_gate,
    w_up,
    w_down,
):
    collected_rows = (
        lax.all_gather(attn_gain, SHARD_AXIS, axis=0, tiled=True),
        lax.all_gather(w_query, SHARD_AXIS, axis=0, tiled=True),
        lax.all_gather(key_weight_matrix, SHARD_AXIS, axis=0, tiled=True),
        lax.all_gather(value_weight_matrix, SHARD_AXIS, axis=0, tiled=True),
        lax.all_gather(query_gain, SHARD_AXIS, axis=0, tiled=True),
        lax.all_gather(key_gain, SHARD_AXIS, axis=0, tiled=True),
        lax.all_gather(mixer_exit_coefficients, SHARD_AXIS, axis=1, tiled=True),
        lax.all_gather(mlp_gain, SHARD_AXIS, axis=0, tiled=True),
        lax.all_gather(w_gate, SHARD_AXIS, axis=0, tiled=True),
        lax.all_gather(w_up, SHARD_AXIS, axis=0, tiled=True),
        lax.all_gather(w_down, SHARD_AXIS, axis=1, tiled=True),
    )
    gain_attn = collected_rows[0].astype(jnp.float32)
    gain_query = collected_rows[4].astype(jnp.float32)
    gain_key = collected_rows[5].astype(jnp.float32)
    gain_mlp = collected_rows[7].astype(jnp.float32)
    seq_count = hidden.shape[0]
    block_rows = hidden.shape[1] * lax.axis_size(TP_AXIS)
    seq_length = segments.shape[1]
    ctx_index = lax.axis_index(CTX_AXIS)
    heads_local = w_query.shape[1] // HEAD_SIZE
    kv_local = key_weight_matrix.shape[1] // HEAD_SIZE
    query_group_width = heads_local // kv_local
    score_scale = HEAD_SIZE ** (-0.5)
    block_start = ctx_index * block_rows
    query_pos = block_start + jnp.arange(block_rows, dtype=jnp.int32)
    query_seg = lax.dynamic_slice_in_dim(segments, block_start, block_rows, 1)
    positions = lax.dynamic_slice_in_dim(doc_positions(segments), block_start, block_rows, 1)
    cosine, sine_part = rope_tables(positions)

    def counting_keys(key_first, step_rows):
        early = key_first <= block_start + block_rows - 1
        last_seg = lax.dynamic_slice_in_dim(segments, key_first + step_rows - 1, 1, 1)[:, 0]
        return early & jnp.any(last_seg >= query_seg[:, 0])

    inputs = hidden.astype(jnp.float32)
    scale_one = rms_scale(inputs)
    attention_input = (inputs * scale_one * gain_attn).astype(jnp.bfloat16)
    attention_rows = tp_rows(attention_input)
    q_proj = jnp.einsum(
        "zjr,rm->zjm", attention_rows, collected_rows[1], preferred_element_type=jnp.float32
    ).reshape(seq_count, block_rows, heads_local, HEAD_SIZE)
    key_projected = jnp.einsum(
        "zjr,rm->zjm", attention_rows, collected_rows[2], preferred_element_type=jnp.float32
    ).reshape(seq_count, block_rows, kv_local, HEAD_SIZE)
    value_projected = jnp.einsum(
        "zjr,rm->zjm", attention_rows, collected_rows[3], preferred_element_type=jnp.float32
    )
    q_scale = rms_scale(q_proj)
    k_scale = rms_scale(key_projected)
    query_rows_input = (
        rotate(q_proj * q_scale * gain_query, cosine, sine_part)
        .astype(jnp.bfloat16)
        .reshape(seq_count, block_rows, kv_local, query_group_width, HEAD_SIZE)
    )
    keys = rotate(key_projected * k_scale * gain_key, cosine, sine_part).astype(jnp.bfloat16)
    values = value_projected.astype(jnp.bfloat16).reshape(
        seq_count, block_rows, kv_local, HEAD_SIZE
    )
    stat_shape = (seq_count, kv_local, query_group_width, block_rows)
    start_state = (
        jnp.full(stat_shape, masked_fill, jnp.float32),
        jnp.zeros(stat_shape, jnp.float32),
        jnp.zeros(stat_shape + (HEAD_SIZE,), jnp.float32),
    )
    piece_keys = lax.all_gather(keys, CTX_AXIS, axis=1, tiled=True)
    piece_values = lax.all_gather(values, CTX_AXIS, axis=1, tiled=True)
    piece_rows = piece_keys.shape[1]
    step_rows = math.gcd(piece_rows, 1024)

    def attend_one_step(number, loop_state):
        offset = number * step_rows
        key_first = offset

        def attend_compute(state):
            row_max, row_total, summed = state
            key_part = lax.dynamic_slice_in_dim(piece_keys, offset, step_rows, 1)
            value_part = lax.dynamic_slice_in_dim(piece_values, offset, step_rows, 1)
            allowed = key_block(segments, key_first, step_rows, query_pos, query_seg)
            scores = (
                jnp.einsum(
                    "sqhgd,skhd->shgqk",
                    query_rows_input,
                    key_part,
                    preferred_element_type=jnp.float32,
                )
                * score_scale
            )
            masked = jnp.where(allowed, scores, masked_fill)
            new_max = jnp.maximum(row_max, jnp.max(masked, axis=-1))
            weights = jnp.where(allowed, jnp.exp(masked - new_max[..., None]), 0.0)
            decay_factor = jnp.exp(row_max - new_max)
            row_total = row_total * decay_factor + jnp.sum(weights, axis=-1)
            summed = summed * decay_factor[..., None] + jnp.einsum(
                "shgqk,skhd->shgqd",
                weights.astype(jnp.bfloat16),
                value_part,
                preferred_element_type=jnp.float32,
            )
            return (new_max, row_total, summed)

        return lax.cond(counting_keys(key_first, step_rows), attend_compute, keep_state, loop_state)

    row_max, row_total, summed = lax.fori_loop(
        0, piece_rows // step_rows, attend_one_step, start_state
    )
    attended = summed / row_total[..., None]
    log_total = row_max + jnp.log(row_total)
    attended_reduced_copy = (
        attended.transpose(0, 3, 1, 2, 4)
        .reshape(seq_count, block_rows, heads_local * HEAD_SIZE)
        .astype(jnp.bfloat16)
    )
    branch = tp_total(
        jnp.einsum(
            "vkq,qy->vky",
            attended_reduced_copy,
            collected_rows[6],
            preferred_element_type=jnp.float32,
        )
    )
    middle = inputs + branch
    scale_two = rms_scale(middle)
    mlp_in = (middle * scale_two * gain_mlp).astype(jnp.bfloat16)
    mlp_rows = tp_rows(mlp_in)
    gate = jnp.einsum(
        "snd,df->snf", mlp_rows, collected_rows[8], preferred_element_type=jnp.float32
    )
    upward = jnp.einsum(
        "snd,df->snf", mlp_rows, collected_rows[9], preferred_element_type=jnp.float32
    )
    activated = (jax.nn.silu(gate) * upward).astype(jnp.bfloat16)
    out_hidden = (
        middle
        + tp_total(
            jnp.einsum(
                "snf,fd->snd", activated, collected_rows[10], preferred_element_type=jnp.float32
            )
        )
    ).astype(jnp.bfloat16)
    again = (
        lax.all_gather(attn_gain, SHARD_AXIS, axis=0, tiled=True),
        lax.all_gather(w_query, SHARD_AXIS, axis=0, tiled=True),
        lax.all_gather(key_weight_matrix, SHARD_AXIS, axis=0, tiled=True),
        lax.all_gather(value_weight_matrix, SHARD_AXIS, axis=0, tiled=True),
        lax.all_gather(query_gain, SHARD_AXIS, axis=0, tiled=True),
        lax.all_gather(key_gain, SHARD_AXIS, axis=0, tiled=True),
        lax.all_gather(mixer_exit_coefficients, SHARD_AXIS, axis=1, tiled=True),
        lax.all_gather(mlp_gain, SHARD_AXIS, axis=0, tiled=True),
        lax.all_gather(w_gate, SHARD_AXIS, axis=0, tiled=True),
        lax.all_gather(w_up, SHARD_AXIS, axis=0, tiled=True),
        lax.all_gather(w_down, SHARD_AXIS, axis=1, tiled=True),
    )
    query_backward = again[1]
    lookup_pullback = again[2]
    value_backward = again[3]
    output_backward = again[6]
    back_gate = again[8]
    back_up = again[9]
    back_down = again[10]
    d_out = cotangent.astype(jnp.float32)
    d_rows = tp_rows(cotangent)
    grad_down = jnp.einsum("snf,snd->fd", activated, d_rows, preferred_element_type=jnp.float32)
    d_act = jnp.einsum("snd,fd->snf", d_rows, back_down, preferred_element_type=jnp.float32)
    sigmoid_gate = jax.nn.sigmoid(gate)
    d_upward = (d_act * jax.nn.silu(gate)).astype(jnp.bfloat16)
    d_gate = (d_act * upward * sigmoid_gate * (1.0 + gate * (1.0 - sigmoid_gate))).astype(
        jnp.bfloat16
    )
    grad_gate = jnp.einsum("snd,snf->df", mlp_rows, d_gate, preferred_element_type=jnp.float32)
    grad_up = jnp.einsum("snd,snf->df", mlp_rows, d_upward, preferred_element_type=jnp.float32)
    d_mlp_in = tp_total(
        jnp.einsum("snf,df->snd", d_gate, back_gate, preferred_element_type=jnp.float32)
        + jnp.einsum("snf,df->snd", d_upward, back_up, preferred_element_type=jnp.float32)
    )
    grad_mlp_gain = jnp.sum(d_mlp_in * middle * scale_two, axis=(0, 1))
    d_middle = d_out + rms_back(d_mlp_in, middle, scale_two, gain_mlp)
    d_branch = d_middle.astype(jnp.bfloat16)
    residual_branch_rows = tp_rows(d_branch)
    result_cotangent = jnp.einsum(
        "xbj,xbk->jk",
        attended_reduced_copy,
        residual_branch_rows,
        preferred_element_type=jnp.float32,
    )
    d_attended = (
        jnp.einsum(
            "miv,cv->mic", residual_branch_rows, output_backward, preferred_element_type=jnp.float32
        )
        .astype(jnp.bfloat16)
        .reshape(seq_count, block_rows, kv_local, query_group_width, HEAD_SIZE)
    )
    delta = jnp.sum(d_attended.astype(jnp.float32).transpose(0, 2, 3, 1, 4) * attended, axis=-1)
    query_zeros = jnp.zeros(
        (seq_count, block_rows, kv_local, query_group_width, HEAD_SIZE), jnp.float32
    )
    back_state = (
        query_zeros,
        jnp.zeros((seq_count, seq_length, kv_local, HEAD_SIZE), jnp.float32),
        jnp.zeros((seq_count, seq_length, kv_local, HEAD_SIZE), jnp.float32),
    )
    back_piece_keys = lax.all_gather(keys, CTX_AXIS, axis=1, tiled=True)
    back_piece_values = lax.all_gather(values, CTX_AXIS, axis=1, tiled=True)
    piece_rows = back_piece_keys.shape[1]
    back_step_rows = math.gcd(piece_rows, 1024)

    def back_one_step(number, loop_state):
        offset = number * back_step_rows
        key_first = offset
        write_at = offset

        def back_compute(state):
            d_query, d_keys, d_values = state
            key_part = lax.dynamic_slice_in_dim(back_piece_keys, offset, back_step_rows, 1)
            value_part = lax.dynamic_slice_in_dim(back_piece_values, offset, back_step_rows, 1)
            allowed = key_block(segments, key_first, back_step_rows, query_pos, query_seg)
            scores = (
                jnp.einsum(
                    "sqhgd,skhd->shgqk",
                    query_rows_input,
                    key_part,
                    preferred_element_type=jnp.float32,
                )
                * score_scale
            )
            probs = jnp.where(allowed, jnp.exp(scores - log_total[..., None]), 0.0)
            d_probs = jnp.einsum(
                "sqhgd,skhd->shgqk", d_attended, value_part, preferred_element_type=jnp.float32
            )
            d_scores = (probs * (d_probs - delta[..., None])).astype(jnp.bfloat16)
            d_query = d_query + jnp.einsum(
                "shgqk,skhd->sqhgd", d_scores, key_part, preferred_element_type=jnp.float32
            )
            key_grad = jnp.einsum(
                "shgqk,sqhgd->skhd", d_scores, query_rows_input, preferred_element_type=jnp.float32
            )
            value_grad = jnp.einsum(
                "shgqk,sqhgd->skhd",
                probs.astype(jnp.bfloat16),
                d_attended,
                preferred_element_type=jnp.float32,
            )
            d_keys = lax.dynamic_update_slice_in_dim(
                d_keys,
                lax.dynamic_slice_in_dim(d_keys, write_at, back_step_rows, 1) + key_grad,
                write_at,
                1,
            )
            d_values = lax.dynamic_update_slice_in_dim(
                d_values,
                lax.dynamic_slice_in_dim(d_values, write_at, back_step_rows, 1) + value_grad,
                write_at,
                1,
            )
            return (d_query, d_keys, d_values)

        return lax.cond(
            counting_keys(key_first, back_step_rows), back_compute, keep_state, loop_state
        )

    d_query, d_keys, d_values = lax.fori_loop(
        0, piece_rows // back_step_rows, back_one_step, back_state
    )
    own_keys, own_values = (
        lax.psum_scatter(
            d_keys.astype(jnp.bfloat16), CTX_AXIS, scatter_dimension=1, tiled=True
        ).astype(jnp.float32),
        lax.psum_scatter(
            d_values.astype(jnp.bfloat16), CTX_AXIS, scatter_dimension=1, tiled=True
        ).astype(jnp.float32),
    )
    q_normed = rotate_back(
        d_query.reshape(seq_count, block_rows, heads_local, HEAD_SIZE) * score_scale,
        cosine,
        sine_part,
    )
    grad_query_gain = jnp.sum(q_normed * q_proj * q_scale, axis=(0, 1, 2))
    query_projection_gradient = (
        rms_back(q_normed, q_proj, q_scale, gain_query)
        .astype(jnp.bfloat16)
        .reshape(seq_count, block_rows, heads_local * HEAD_SIZE)
    )
    k_normed = rotate_back(own_keys * score_scale, cosine, sine_part)
    grad_key_gain = jnp.sum(k_normed * key_projected * k_scale, axis=(0, 1, 2))
    lookup_map_derivative = (
        rms_back(k_normed, key_projected, k_scale, gain_key)
        .astype(jnp.bfloat16)
        .reshape(seq_count, block_rows, kv_local * HEAD_SIZE)
    )
    value_projection_gradient = own_values.astype(jnp.bfloat16).reshape(
        seq_count, block_rows, kv_local * HEAD_SIZE
    )
    query_gradient_rows = jnp.einsum(
        "zqr,zqa->ra", attention_rows, query_projection_gradient, preferred_element_type=jnp.float32
    )
    key_gradient_rows = jnp.einsum(
        "zqr,zqa->ra", attention_rows, lookup_map_derivative, preferred_element_type=jnp.float32
    )
    value_gradient_rows = jnp.einsum(
        "zqr,zqa->ra", attention_rows, value_projection_gradient, preferred_element_type=jnp.float32
    )
    d_attn_in = tp_total(
        jnp.einsum(
            "wtl,al->wta",
            query_projection_gradient,
            query_backward,
            preferred_element_type=jnp.float32,
        )
        + jnp.einsum(
            "wtl,al->wta",
            lookup_map_derivative,
            lookup_pullback,
            preferred_element_type=jnp.float32,
        )
        + jnp.einsum(
            "wtl,al->wta",
            value_projection_gradient,
            value_backward,
            preferred_element_type=jnp.float32,
        )
    )
    grad_attn_gain = jnp.sum(d_attn_in * inputs * scale_one, axis=(0, 1))
    grad_hidden = d_middle + rms_back(d_attn_in, inputs, scale_one, gain_attn)
    reduced = (
        lax.psum_scatter(
            grad_attn_gain.astype(jnp.bfloat16), SHARD_AXIS, scatter_dimension=0, tiled=True
        ).astype(jnp.float32),
        lax.psum_scatter(
            query_gradient_rows.astype(jnp.bfloat16), SHARD_AXIS, scatter_dimension=0, tiled=True
        ).astype(jnp.float32),
        lax.psum_scatter(
            key_gradient_rows.astype(jnp.bfloat16), SHARD_AXIS, scatter_dimension=0, tiled=True
        ).astype(jnp.float32),
        lax.psum_scatter(
            value_gradient_rows.astype(jnp.bfloat16), SHARD_AXIS, scatter_dimension=0, tiled=True
        ).astype(jnp.float32),
        lax.psum_scatter(
            grad_query_gain.astype(jnp.bfloat16), SHARD_AXIS, scatter_dimension=0, tiled=True
        ).astype(jnp.float32),
        lax.psum_scatter(
            grad_key_gain.astype(jnp.bfloat16), SHARD_AXIS, scatter_dimension=0, tiled=True
        ).astype(jnp.float32),
        lax.psum_scatter(
            result_cotangent.astype(jnp.bfloat16), SHARD_AXIS, scatter_dimension=1, tiled=True
        ).astype(jnp.float32),
        lax.psum_scatter(
            grad_mlp_gain.astype(jnp.bfloat16), SHARD_AXIS, scatter_dimension=0, tiled=True
        ).astype(jnp.float32),
        lax.psum_scatter(
            grad_gate.astype(jnp.bfloat16), SHARD_AXIS, scatter_dimension=0, tiled=True
        ).astype(jnp.float32),
        lax.psum_scatter(
            grad_up.astype(jnp.bfloat16), SHARD_AXIS, scatter_dimension=0, tiled=True
        ).astype(jnp.float32),
        lax.psum_scatter(
            grad_down.astype(jnp.bfloat16), SHARD_AXIS, scatter_dimension=1, tiled=True
        ).astype(jnp.float32),
    )
    matrices = (
        lax.psum(reduced[1].astype(jnp.bfloat16), CTX_AXIS).astype(jnp.float32),
        lax.psum(reduced[2].astype(jnp.bfloat16), CTX_AXIS).astype(jnp.float32),
        lax.psum(reduced[3].astype(jnp.bfloat16), CTX_AXIS).astype(jnp.float32),
        lax.psum(reduced[6].astype(jnp.bfloat16), CTX_AXIS).astype(jnp.float32),
        lax.psum(reduced[8].astype(jnp.bfloat16), CTX_AXIS).astype(jnp.float32),
        lax.psum(reduced[9].astype(jnp.bfloat16), CTX_AXIS).astype(jnp.float32),
        lax.psum(reduced[10].astype(jnp.bfloat16), CTX_AXIS).astype(jnp.float32),
    )
    gains = lax.psum((reduced[0], reduced[4], reduced[5], reduced[7]), (CTX_AXIS, TP_AXIS))
    return (
        out_hidden,
        grad_hidden,
        gains[0],
        matrices[0],
        matrices[1],
        matrices[2],
        gains[1],
        gains[2],
        matrices[3],
        gains[3],
        matrices[4],
        matrices[5],
        matrices[6],
    )


def solution(mesh):
    in_specs = (
        P(SHARD_AXIS, (CTX_AXIS, TP_AXIS), None),
        P(SHARD_AXIS, None),
        P(SHARD_AXIS, (CTX_AXIS, TP_AXIS), None),
        P(SHARD_AXIS),
        P(SHARD_AXIS, TP_AXIS),
        P(SHARD_AXIS, TP_AXIS),
        P(SHARD_AXIS, TP_AXIS),
        P(SHARD_AXIS),
        P(SHARD_AXIS),
        P(TP_AXIS, SHARD_AXIS),
        P(SHARD_AXIS),
        P(SHARD_AXIS, TP_AXIS),
        P(SHARD_AXIS, TP_AXIS),
        P(TP_AXIS, SHARD_AXIS),
    )
    out_specs = (
        P(SHARD_AXIS, (CTX_AXIS, TP_AXIS), None),
        P(SHARD_AXIS, (CTX_AXIS, TP_AXIS), None),
        P(SHARD_AXIS),
        P(SHARD_AXIS, TP_AXIS),
        P(SHARD_AXIS, TP_AXIS),
        P(SHARD_AXIS, TP_AXIS),
        P(SHARD_AXIS),
        P(SHARD_AXIS),
        P(TP_AXIS, SHARD_AXIS),
        P(SHARD_AXIS),
        P(SHARD_AXIS, TP_AXIS),
        P(SHARD_AXIS, TP_AXIS),
        P(TP_AXIS, SHARD_AXIS),
    )
    shape = mesh.shape
    fast = shape[SHARD_AXIS] == 2 and shape[CTX_AXIS] == 4 and shape[TP_AXIS] == 4
    return jax.shard_map(
        fast_device if fast else per_device, mesh=mesh, in_specs=in_specs, out_specs=out_specs, check_vma=False
    )
```
